32 devices in a mesh: fsdp: 2 (over x), cp: 4 (over y, core), seq: 4 (over z).
Axes of the slice: x: 2, y: 2, z: 4, core: 2. Of those that a mesh axis runs over, the one named last changes fastest.
Arguments:
- inputs: bfloat16 [6, 2048, 1536], P('fsdp', ('cp', 'seq')), may hold values from -6 to 6
- cotangent: bfloat16 [6, 2048, 1536], P('fsdp', ('cp', 'seq')), may hold values from -6 to 6
- span_order: int32 [6, 8], P('fsdp'), may hold values from 0 to 7, each once within a row
- adapter_ids: int32 [6], P('fsdp'), may hold values from 0 to 7
- first_gain: bfloat16 [1536], replicated, may hold values from 0.5 to 1.5
- second_gain: bfloat16 [1536], replicated, may hold values from 0.5 to 1.5
- query_weight: bfloat16 [1536, 1536], P(('fsdp', 'cp')), may hold values from -0.15625 to 0.15625
- key_weight: bfloat16 [1536, 256], P(('fsdp', 'cp')), may hold values from -0.15625 to 0.15625
- value_weight: bfloat16 [1536, 256], P(('fsdp', 'cp')), may hold values from -0.15625 to 0.15625
- output_weight: bfloat16 [1536, 1536], P(('fsdp', 'cp')), may hold values from -1.25 to 1.25
- gate_weight: bfloat16 [1536, 8960], P(('fsdp', 'cp')), may hold values from -0.15625 to 0.15625
- up_weight: bfloat16 [1536, 8960], P(('fsdp', 'cp')), may hold values from -0.15625 to 0.15625
- down_weight: bfloat16 [8960, 1536], P(('fsdp', 'cp')), may hold values from -0.0625 to 0.0625
- query_bias: bfloat16 [1536], replicated, may hold values from -1.796875 to 1.796875
- key_bias: bfloat16 [256], replicated, may hold values from -1.796875 to 1.796875
- value_bias: bfloat16 [256], replicated, may hold values from -0.59765625 to 0.59765625
- query_reduce_factors: bfloat16 [1536, 128], replicated, may hold values from -0.15625 to 0.15625
- query_lift_factors: bfloat16 [128, 1536], replicated, may hold values from -1.5 to 1.5
- key_reduce_factors: bfloat16 [1536, 128], replicated, may hold values from -0.15625 to 0.15625
- key_lift_factors: bfloat16 [128, 256], replicated, may hold values from -1.5 to 1.5
- value_reduce_factors: bfloat16 [1536, 128], replicated, may hold values from -0.15625 to 0.15625
- value_lift_factors: bfloat16 [128, 256], replicated, may hold values from -1.5 to 1.5
- output_reduce_factors: bfloat16 [1536, 128], replicated, may hold values from -1.25 to 1.25
- output_lift_factors: bfloat16 [128, 1536], replicated, may hold values from -1.5 to 1.5
- gate_reduce_factors: bfloat16 [1536, 128], replicated, may hold values from -0.15625 to 0.15625
- gate_lift_factors: bfloat16 [128, 8960], replicated, may hold values from -1.5 to 1.5
- upper_reduce_factors: bfloat16 [1536, 128], replicated, may hold values from -0.15625 to 0.15625
- upper_lift_factors: bfloat16 [128, 8960], replicated, may hold values from -1.5 to 1.5
- down_reduce_factors: bfloat16 [8960, 128], replicated, may hold values from -0.0625 to 0.0625
- down_lift_factors: bfloat16 [128, 1536], replicated, may hold values from -1.5 to 1.5
Outputs:
- outputs: bfloat16 [6, 2048, 1536], P('fsdp', ('cp', 'seq'))
- input_grad: float32 [6, 2048, 1536], P('fsdp', ('cp', 'seq'))
- query_shrink_grad: float32 [1536, 128], replicated
- query_expand_grad: float32 [128, 1536], replicated
- key_shrink_grad: float32 [1536, 128], replicated
- key_expand_grad: float32 [128, 256], replicated
- value_shrink_grad: float32 [1536, 128], replicated
- value_expand_grad: float32 [128, 256], replicated
- output_shrink_grad: float32 [1536, 128], replicated
- output_expand_grad: float32 [128, 1536], replicated
- gate_shrink_grad: float32 [1536, 128], replicated
- gate_expand_grad: float32 [128, 8960], replicated
- up_shrink_grad: float32 [1536, 128], replicated
- up_expand_grad: float32 [128, 8960], replicated
- down_shrink_grad: float32 [8960, 128], replicated
- down_expand_grad: float32 [128, 1536], replicated
The draws below stay inside these ranges and needn't reach their ends.
Inputs may be any that keep to these rules, and one draw needn't show every extreme that they name: `span_order`: each row is a permutation of the 8 block numbers.
All inputs are finite; a program needn't handle non-finite values.
Results may differ from the reference program's by a relative error of at most 0.018.
Values may be sent and summed in bfloat16 or wider, within the bound.
No kernel may reach another device: no remote copies, remote signals or barrier semaphores. Data moves between devices by JAX's collectives and lax.ppermute only.
A program may use at most 256 MiB of HBM per device.

```python
import math
import jax
import jax.numpy as jnp
from jax import lax

MODEL_DIMENSION = 1536
HEADS = 12
KV_HEADS = 2
HEAD_DIM = 128
FEEDFORWARD_UNITS = 8960
ADAPTER_RANK = 16
ADAPTERS = 8
LEN = 2048
SEQS = 6
SPANS = 8
KEY_VALUE_WIDTH = 256
ADAPTER_COLUMNS = 128
N_SEQ = 4


def draw_adapter_ids(key, part):
    key_one, key_two = jax.random.split(key)
    chosen = jax.random.randint(key_one, (SEQS,), 0, ADAPTERS)
    position = jax.random.randint(key_two, (), 0, SEQS)
    indices = jnp.arange(SEQS)
    chosen = jnp.where(indices == position, ADAPTERS - 1, chosen)
    return chosen.astype(jnp.int32)


def shard_levels(stream_key, extent, shards, low, largest):
    def one(dim, parts):
        draws = jax.random.uniform(jax.random.fold_in(jax.random.fold_in(stream_key, 6), dim), (parts,), jnp.float32, low / len(shards), largest / len(shards))
        return jnp.repeat(jnp.exp(draws), extent[dim] // parts).reshape((-1,) + (1,) * (len(extent) - dim - 1))

    gain = one(*shards[0])
    for cut in shards[1:]:
        gain = gain * one(*cut)
    return gain


def gaussian(rng, extent, deviation, bound, cuts=(), kind=jnp.bfloat16):
    entries = jax.random.normal(rng, extent, jnp.float32) * deviation
    if len(cuts) > 0:
        entries = shard_levels(rng, extent, cuts, -0.22, 0.18) * entries
    return jnp.clip(entries, min=-bound, max=bound).astype(kind)


def setup_inputs(seed: int = 0) -> dict:
    splits = jax.random.split(jax.random.key(seed), 31)
    return {
        "inputs": gaussian(splits[0], (SEQS, LEN, MODEL_DIMENSION), 1.0, 6.0, ((0, 2), (1, 16))),
        "cotangent": gaussian(splits[1], (SEQS, LEN, MODEL_DIMENSION), 1.0, 6.0, ((0, 2), (1, 16))),
        "span_order": jax.vmap(lambda own: jax.random.permutation(own, SPANS))(jax.random.split(splits[2], SEQS)).reshape((SEQS, SPANS)).astype(jnp.int32),
        "adapter_ids": draw_adapter_ids(jax.random.fold_in(splits[30], 71), 0),
        "first_gain": jnp.clip(1.0 + 0.1 * jax.random.normal(splits[4], (MODEL_DIMENSION,), jnp.float32), 0.5, 1.5).astype(jnp.bfloat16),
        "second_gain": jnp.clip(1.0 + 0.1 * jax.random.normal(splits[5], (MODEL_DIMENSION,), jnp.float32), 0.5, 1.5).astype(jnp.bfloat16),
        "query_weight": gaussian(splits[6], (MODEL_DIMENSION, MODEL_DIMENSION), MODEL_DIMENSION ** -0.5, 0.15625, ((0, 8),)),
        "key_weight": gaussian(splits[7], (MODEL_DIMENSION, KEY_VALUE_WIDTH), MODEL_DIMENSION ** -0.5, 0.15625, ((0, 8),)),
        "value_weight": gaussian(splits[8], (MODEL_DIMENSION, KEY_VALUE_WIDTH), MODEL_DIMENSION ** -0.5, 0.15625, ((0, 8),)),
        "output_weight": gaussian(splits[9], (MODEL_DIMENSION, MODEL_DIMENSION), (MODEL_DIMENSION // 64) ** -0.5, 1.25, ((0, 8),)),
        "gate_weight": gaussian(splits[10], (MODEL_DIMENSION, FEEDFORWARD_UNITS), MODEL_DIMENSION ** -0.5, 0.15625, ((0, 8),)),
        "up_weight": gaussian(splits[11], (MODEL_DIMENSION, FEEDFORWARD_UNITS), MODEL_DIMENSION ** -0.5, 0.15625, ((0, 8),)),
        "down_weight": gaussian(splits[12], (FEEDFORWARD_UNITS, MODEL_DIMENSION), FEEDFORWARD_UNITS ** -0.5, 0.0625, ((0, 8),)),
        "query_bias": gaussian(splits[13], (MODEL_DIMENSION,), 0.3, 1.796875),
        "key_bias": gaussian(splits[14], (KEY_VALUE_WIDTH,), 0.3, 1.796875),
        "value_bias": gaussian(splits[15], (KEY_VALUE_WIDTH,), 0.1, 0.59765625),
        "query_reduce_factors": gaussian(splits[16], (MODEL_DIMENSION, ADAPTER_COLUMNS), MODEL_DIMENSION ** -0.5, 0.15625),
        "query_lift_factors": gaussian(splits[17], (ADAPTER_COLUMNS, MODEL_DIMENSION), ADAPTER_RANK ** -0.5, 1.5),
        "key_reduce_factors": gaussian(splits[18], (MODEL_DIMENSION, ADAPTER_COLUMNS), MODEL_DIMENSION ** -0.5, 0.15625),
        "key_lift_factors": gaussian(splits[19], (ADAPTER_COLUMNS, KEY_VALUE_WIDTH), ADAPTER_RANK ** -0.5, 1.5),
        "value_reduce_factors": gaussian(splits[20], (MODEL_DIMENSION, ADAPTER_COLUMNS), MODEL_DIMENSION ** -0.5, 0.15625),
        "value_lift_factors": gaussian(splits[21], (ADAPTER_COLUMNS, KEY_VALUE_WIDTH), ADAPTER_RANK ** -0.5, 1.5),
        "output_reduce_factors": gaussian(splits[22], (MODEL_DIMENSION, ADAPTER_COLUMNS), (MODEL_DIMENSION // 64) ** -0.5, 1.25),
        "output_lift_factors": gaussian(splits[23], (ADAPTER_COLUMNS, MODEL_DIMENSION), ADAPTER_RANK ** -0.5, 1.5),
        "gate_reduce_factors": gaussian(splits[24], (MODEL_DIMENSION, ADAPTER_COLUMNS), MODEL_DIMENSION ** -0.5, 0.15625),
        "gate_lift_factors": gaussian(splits[25], (ADAPTER_COLUMNS, FEEDFORWARD_UNITS), ADAPTER_RANK ** -0.5, 1.5),
        "upper_reduce_factors": gaussian(splits[26], (MODEL_DIMENSION, ADAPTER_COLUMNS), MODEL_DIMENSION ** -0.5, 0.15625),
        "upper_lift_factors": gaussian(splits[27], (ADAPTER_COLUMNS, FEEDFORWARD_UNITS), ADAPTER_RANK ** -0.5, 1.5),
        "down_reduce_factors": gaussian(splits[28], (FEEDFORWARD_UNITS, ADAPTER_COLUMNS), FEEDFORWARD_UNITS ** -0.5, 0.0625),
        "down_lift_factors": gaussian(splits[29], (ADAPTER_COLUMNS, MODEL_DIMENSION), ADAPTER_RANK ** -0.5, 1.5),
    }


@jax.custom_vjp
def low(v):
    return lax.optimization_barrier(v.astype(jnp.bfloat16)).astype(jnp.float32)

@jax.custom_vjp
def low_back(v):
    return v

def low_keep(v):
    return (low(v), None)

def low_pass(kept, grad):
    return (grad,)

def back_keep(v):
    return (v, None)

def back_low(kept, grad):
    return (low(grad),)
low.defvjp(low_keep, low_pass)
low_back.defvjp(back_keep, back_low)
epsilon = 1e-06
adapter_scale = 0.5
rotary_base = 1000000.0
masked_score = -1e+30
highest = lax.Precision.HIGHEST

def matmul(matrix_a, matrix_b):
    return jnp.dot(matrix_a, matrix_b, precision=highest, preferred_element_type=jnp.float32)

def rotary_tables(positions):
    halfway = HEAD_DIM // 2
    frequency = jnp.exp(jnp.arange(halfway, dtype=jnp.float32) * (-2.0 * math.log(rotary_base) / HEAD_DIM))
    angles = positions.astype(jnp.float32)[..., None] * frequency
    angles = jnp.concatenate([angles, angles], axis=-1)
    return (jnp.cos(angles), jnp.sin(angles))

def rotate(values, cosine, sine_table):
    halfway = values.shape[-1] // 2
    turned = jnp.concatenate([-values[..., halfway:], values[..., :halfway]], axis=-1)
    return values * cosine + turned * sine_table

def rms_norm(values, scales):
    return values * lax.rsqrt(lax.optimization_barrier(jnp.mean(values * values, axis=-1, keepdims=True)) + epsilon) * scales

def adapter(inputs_low, shrink, expand, mixing):
    narrow = low_back(matmul(inputs_low, shrink))
    return matmul(low(narrow * mixing), expand)

def attention(queries, keys_all, values_all, positions):
    per_group = HEADS // N_SEQ
    block_rows = min(LEN, 512)
    num_blocks = LEN // block_rows
    grouped = queries.reshape(num_blocks, block_rows, N_SEQ, per_group, HEAD_DIM)
    query_pos = positions.reshape(num_blocks, block_rows)
    score_scale = 1.0 / math.sqrt(HEAD_DIM)

    def one_block(operand):
        query_blk, pos_blk = operand
        product = jnp.einsum('qgpd,kgd->gpqk', query_blk, keys_all, precision=highest)
        scores = low_back(product) * score_scale
        allowed = positions[None, None, None, :] <= pos_blk[None, None, :, None]
        scores = jnp.where(allowed, scores, masked_score)
        weights = low(jax.nn.softmax(scores, axis=-1))
        blended = jnp.einsum('gpqk,kgd->qgpd', weights, values_all, precision=highest)
        return blended.reshape(block_rows, HEADS * HEAD_DIM)
    blocks_out = lax.map(jax.checkpoint(one_block), (grouped, query_pos))
    return blocks_out.reshape(LEN, HEADS * HEAD_DIM)

def block_forward(tokens_f, adapters, frozen, mixing, positions):
    query_reduce_factors, query_lift_factors, key_reduce_factors, key_lift_factors, value_reduce_factors, value_lift_factors, output_reduce_factors, output_lift_factors, gate_reduce_factors, gate_lift_factors, upper_reduce_factors, upper_lift_factors, down_reduce_factors, down_lift_factors = adapters
    first_gain, second_gain, query_weight, key_weight, value_weight, output_weight, gate_weight, up_weight, down_weight, query_bias, key_bias, value_bias = frozen
    cosine, sine_table = rotary_tables(positions)
    cosine = cosine[:, None, :]
    sine_table = sine_table[:, None, :]
    repeat_by = N_SEQ // KV_HEADS
    normed = low(rms_norm(tokens_f, first_gain))
    query_rows = low_back(matmul(normed, query_weight) + query_bias + adapter(normed, query_reduce_factors, query_lift_factors, mixing))
    query_rows = low(low_back(rotate(query_rows.reshape(LEN, HEADS, HEAD_DIM), cosine, sine_table)))
    key_rows = low_back(matmul(normed, key_weight) + key_bias + adapter(normed, key_reduce_factors, key_lift_factors, mixing))
    key_rows = rotate(key_rows.reshape(LEN, KV_HEADS, HEAD_DIM), cosine, sine_table)
    key_rows = low(low_back(jnp.repeat(key_rows, repeat_by, axis=1)))
    value_rows = low_back(matmul(normed, value_weight) + value_bias + adapter(normed, value_reduce_factors, value_lift_factors, mixing))
    value_rows = low(low_back(jnp.repeat(value_rows.reshape(LEN, KV_HEADS, HEAD_DIM), repeat_by, axis=1)))
    attended = low(low_back(attention(query_rows, key_rows, value_rows, positions)))
    middle = tokens_f + low_back(matmul(attended, output_weight) + adapter(attended, output_reduce_factors, output_lift_factors, mixing))
    normed_two = low(rms_norm(middle, second_gain))
    gate_pre = low_back(matmul(normed_two, gate_weight) + adapter(normed_two, gate_reduce_factors, gate_lift_factors, mixing))
    upward = low_back(matmul(normed_two, up_weight) + adapter(normed_two, upper_reduce_factors, upper_lift_factors, mixing))
    hidden = low(jax.nn.silu(gate_pre) * upward)
    return middle + (matmul(hidden, down_weight) + adapter(hidden, down_reduce_factors, down_lift_factors, mixing))

def reference(inputs, cotangent, span_order, adapter_ids, first_gain, second_gain, query_weight, key_weight, value_weight, output_weight, gate_weight, up_weight, down_weight, query_bias, key_bias, value_bias, query_reduce_factors, query_lift_factors, key_reduce_factors, key_lift_factors, value_reduce_factors, value_lift_factors, output_reduce_factors, output_lift_factors, gate_reduce_factors, gate_lift_factors, upper_reduce_factors, upper_lift_factors, down_reduce_factors, down_lift_factors):
    frozen = tuple((element.astype(jnp.float32) for element in (first_gain, second_gain, query_weight, key_weight, value_weight, output_weight, gate_weight, up_weight, down_weight, query_bias, key_bias, value_bias)))
    adapters = tuple((element.astype(jnp.float32) for element in (query_reduce_factors, query_lift_factors, key_reduce_factors, key_lift_factors, value_reduce_factors, value_lift_factors, output_reduce_factors, output_lift_factors, gate_reduce_factors, gate_lift_factors, upper_reduce_factors, upper_lift_factors, down_reduce_factors, down_lift_factors)))
    span_len = LEN // SPANS
    row_index = jnp.arange(LEN, dtype=jnp.int32)
    column_count = jnp.arange(ADAPTER_COLUMNS, dtype=jnp.int32)

    def one_sequence(totals, operand):
        tokens, grad_rows, order_row, identity = operand
        positions = order_row[row_index // span_len] * span_len + row_index % span_len
        mixing = jnp.where(column_count // ADAPTER_RANK == identity, adapter_scale, 0.0).astype(jnp.float32)

        def forward(tokens_f, adapt_all):
            return block_forward(tokens_f, adapt_all, frozen, mixing, positions)
        result, pullback = jax.vjp(forward, tokens.astype(jnp.float32), adapters)
        grad_tokens, grad_adapt = pullback(grad_rows.astype(jnp.float32))
        totals = tuple((total_one + grad_one for total_one, grad_one in zip(totals, grad_adapt)))
        return (totals, (result.astype(jnp.bfloat16), grad_tokens))
    initial = tuple((jnp.zeros(element.shape, jnp.float32) for element in adapters))
    totals, (outputs, input_grad) = lax.scan(one_sequence, initial, (inputs, cotangent, span_order, adapter_ids))
    return (outputs, input_grad, totals[0], totals[1], totals[2], totals[3], totals[4], totals[5], totals[6], totals[7], totals[8], totals[9], totals[10], totals[11], totals[12], totals[13])
```

```python
import functools
import math

import jax
import jax.numpy as jnp
from jax import lax
from jax.experimental import pallas as pl
from jax.experimental.pallas import tpu as pltpu
from jax.sharding import PartitionSpec as P

HEAD_DIM = 128
ADAPTER_RANK = 16
epsilon = 1e-06
adapter_scale = 0.5
rotary_base = 1000000.0
masked_score = -1e30
PLANE = ("fsdp", "cp")
EVERY = ("fsdp", "cp", "seq")
BF = jnp.bfloat16
F32 = jnp.float32


def rotary_tables(positions):
    halfway = HEAD_DIM // 2
    frequency = jnp.exp(
        jnp.arange(halfway, dtype=jnp.float32) * (-2.0 * math.log(rotary_base) / HEAD_DIM)
    )
    angles = positions.astype(jnp.float32)[..., None] * frequency
    angles = jnp.concatenate([angles, angles], axis=-1)
    return (jnp.cos(angles), jnp.sin(angles))


def rotate(values, cosine, sine_table):
    halfway = values.shape[-1] // 2
    turned = jnp.concatenate([-values[..., halfway:], values[..., :halfway]], axis=-1)
    return values * cosine + turned * sine_table


def unrotate(gradient, cosine, sine_table):
    halfway = gradient.shape[-1] // 2
    scaled = gradient * sine_table
    turned = jnp.concatenate([scaled[..., halfway:], -scaled[..., :halfway]], axis=-1)
    return gradient * cosine + turned


def mm(left, right):
    return jnp.dot(left, right, preferred_element_type=jnp.float32)


def mm_nt(left, right):
    return lax.dot_general(
        left, right, (((1,), (1,)), ((), ())), preferred_element_type=jnp.float32
    )


def mm_tn(left, right):
    return lax.dot_general(
        left, right, (((0,), (0,)), ((), ())), preferred_element_type=jnp.float32
    )


def norm_forward(values, scales):
    return values * lax.rsqrt(jnp.mean(values * values, axis=-1, keepdims=True) + epsilon) * scales


def norm_backward(values, scales, gradient):
    inverse = lax.rsqrt(jnp.mean(values * values, axis=-1, keepdims=True) + epsilon)
    weighted = gradient * scales
    inner_sum = jnp.mean(weighted * values, axis=-1, keepdims=True)
    return inverse * weighted - values * (inverse * inverse * inverse) * inner_sum


def heads_to_rows(block):
    count = block.shape[1] // HEAD_DIM
    return jnp.concatenate(
        [block[:, HEAD_DIM * j : HEAD_DIM * (j + 1)] for j in range(count)], axis=0
    )


def rows_to_heads(rows, tokens):
    count = rows.shape[0] // tokens
    return jnp.concatenate([rows[tokens * j : tokens * (j + 1)] for j in range(count)], axis=1)


def attend_kernel(spans, span_len, tokens, info, q_ref, k_ref, v_ref, o_ref, lse_ref, m_ref, l_ref, acc_ref):
    seq = pl.program_id(0)
    seqs = pl.num_programs(0)
    own = info[seqs * spans + seq]
    shift = info[seqs * spans + seqs]
    scale = math.log2(math.e) / math.sqrt(HEAD_DIM)
    queries = heads_to_rows(q_ref[...])
    m_ref[...] = jnp.full(m_ref.shape, masked_score, F32)
    l_ref[...] = jnp.zeros(l_ref.shape, F32)
    acc_ref[...] = jnp.zeros(acc_ref.shape, F32)

    def update(j, masked):
        rows = pl.ds(pl.multiple_of(j * span_len, span_len), span_len)
        scores = mm_nt(k_ref[0, rows, :], queries) * scale
        if masked:
            key_at = lax.broadcasted_iota(jnp.int32, scores.shape, 0)
            query_at = shift + lax.rem(lax.broadcasted_iota(jnp.int32, scores.shape, 1), tokens)
            scores = jnp.where(key_at <= query_at, scores, masked_score)
        old = m_ref[...]
        top = jnp.maximum(old, jnp.max(scores, axis=0, keepdims=True))
        expo = jnp.exp2(scores - top)
        alpha = jnp.exp2(old - top)
        l_ref[...] = l_ref[...] * alpha + jnp.sum(expo, axis=0, keepdims=True)
        acc_ref[...] = acc_ref[...] * alpha + mm_tn(v_ref[0, rows, :], expo.astype(BF))
        m_ref[...] = top

    def step(j, carry):
        other = info[seq * spans + j]

        @pl.when(other < own)
        def _():
            update(j, False)

        @pl.when(other == own)
        def _():
            update(j, True)

        return carry

    lax.fori_loop(0, spans, step, 0)
    total = l_ref[...]
    out = jnp.transpose(acc_ref[...] / total)
    o_ref[...] = rows_to_heads(out.astype(BF), tokens)
    lse_ref[0] = jnp.broadcast_to(m_ref[...] + jnp.log2(total), lse_ref.shape[1:])


def attend(info, queries, pairs, seqs, spans, span_len):
    tokens = queries.shape[0] // seqs
    length = pairs.shape[1]
    kv_heads = pairs.shape[2] // (2 * HEAD_DIM)
    width = queries.shape[1] // kv_heads
    rows = tokens * (width // HEAD_DIM)
    grid_spec = pltpu.PrefetchScalarGridSpec(
        num_scalar_prefetch=1,
        grid=(seqs, kv_heads),
        in_specs=[
            pl.BlockSpec((tokens, width), lambda s, h, i: (s, h)),
            pl.BlockSpec((1, length, HEAD_DIM), lambda s, h, i: (s, 0, h)),
            pl.BlockSpec((1, length, HEAD_DIM), lambda s, h, i: (s, 0, kv_heads + h)),
        ],
        out_specs=[
            pl.BlockSpec((tokens, width), lambda s, h, i: (s, h)),
            pl.BlockSpec((1, 8, rows), lambda s, h, i: (s * kv_heads + h, 0, 0)),
        ],
        scratch_shapes=[pltpu.VMEM((1, rows), F32)] * 2 + [pltpu.VMEM((HEAD_DIM, rows), F32)],
    )
    work = seqs * kv_heads * rows * length
    return pl.pallas_call(
        functools.partial(attend_kernel, spans, span_len, tokens),
        grid_spec=grid_spec,
        out_shape=[
            jax.ShapeDtypeStruct(queries.shape, BF),
            jax.ShapeDtypeStruct((seqs * kv_heads, 8, rows), F32),
        ],
        name="attend",
        cost_estimate=pl.CostEstimate(
            flops=4 * work * HEAD_DIM, bytes_accessed=pairs.size * 2, transcendentals=work
        ),
    )(info, queries, pairs, pairs)


def attend_back_kernel(
    spans, span_len, tokens, kv_heads, info, q_ref, do_ref, o_ref, k_ref, v_ref, lse_ref, dq_ref, dkv_ref, acc_ref
):
    seq = pl.program_id(0)
    head = pl.program_id(1)
    seqs = pl.num_programs(0)
    own = info[seqs * spans + seq]
    shift = info[seqs * spans + seqs]
    root = 1.0 / math.sqrt(HEAD_DIM)
    scale = math.log2(math.e) * root
    queries = heads_to_rows(q_ref[...])
    grads = heads_to_rows(do_ref[...])
    results = heads_to_rows(o_ref[...])
    inner = jnp.sum(
        jnp.transpose(grads.astype(F32) * results.astype(F32)), axis=0, keepdims=True
    )
    lse = lse_ref[0, :1, :]
    acc_ref[...] = jnp.zeros(acc_ref.shape, F32)
    key_lane = pl.multiple_of(head * HEAD_DIM, HEAD_DIM)
    val_lane = pl.multiple_of((kv_heads + head) * HEAD_DIM, HEAD_DIM)

    def update(j, masked):
        rows = pl.ds(pl.multiple_of(j * span_len, span_len), span_len)
        keys = k_ref[0, rows, :]
        prob = jnp.exp2(mm_nt(keys, queries) * scale - lse)
        if masked:
            key_at = lax.broadcasted_iota(jnp.int32, prob.shape, 0)
            query_at = shift + lax.rem(lax.broadcasted_iota(jnp.int32, prob.shape, 1), tokens)
            prob = jnp.where(key_at <= query_at, prob, 0.0)
        prob_grad = mm_nt(v_ref[0, rows, :], grads)
        score_grad = (prob * (prob_grad - inner)).astype(BF)
        dkv_ref[0, rows, pl.ds(key_lane, HEAD_DIM)] = (mm(score_grad, queries) * root).astype(BF)
        dkv_ref[0, rows, pl.ds(val_lane, HEAD_DIM)] = mm(prob.astype(BF), grads).astype(BF)
        acc_ref[...] += mm_tn(score_grad, keys)

    def step(j, carry):
        other = info[seq * spans + j]

        @pl.when(other < own)
        def _():
            update(j, False)

        @pl.when(other == own)
        def _():
            update(j, True)

        @pl.when(other > own)
        def _():
            rows = pl.ds(pl.multiple_of(j * span_len, span_len), span_len)
            zero = jnp.zeros((span_len, HEAD_DIM), BF)
            dkv_ref[0, rows, pl.ds(key_lane, HEAD_DIM)] = zero
            dkv_ref[0, rows, pl.ds(val_lane, HEAD_DIM)] = zero

        return carry

    lax.fori_loop(0, spans, step, 0)
    dq_ref[...] = rows_to_heads((acc_ref[...] * root).astype(BF), tokens)


def attend_back(info, queries, grads, results, pairs, lse, seqs, spans, span_len):
    tokens = queries.shape[0] // seqs
    length = pairs.shape[1]
    kv_heads = pairs.shape[2] // (2 * HEAD_DIM)
    width = queries.shape[1] // kv_heads
    rows = tokens * (width // HEAD_DIM)
    grid_spec = pltpu.PrefetchScalarGridSpec(
        num_scalar_prefetch=1,
        grid=(seqs, kv_heads),
        in_specs=[
            pl.BlockSpec((tokens, width), lambda s, h, i: (s, h)),
            pl.BlockSpec((tokens, width), lambda s, h, i: (s, h)),
            pl.BlockSpec((tokens, width), lambda s, h, i: (s, h)),
            pl.BlockSpec((1, length, HEAD_DIM), lambda s, h, i: (s, 0, h)),
            pl.BlockSpec((1, length, HEAD_DIM), lambda s, h, i: (s, 0, kv_heads + h)),
            pl.BlockSpec((1, 8, rows), lambda s, h, i: (s * kv_heads + h, 0, 0)),
        ],
        out_specs=[
            pl.BlockSpec((tokens, width), lambda s, h, i: (s, h)),
            pl.BlockSpec((1, length, pairs.shape[2]), lambda s, h, i: (s, 0, 0)),
        ],
        scratch_shapes=[pltpu.VMEM((rows, HEAD_DIM), F32)],
    )
    work = seqs * kv_heads * rows * length
    return pl.pallas_call(
        functools.partial(attend_back_kernel, spans, span_len, tokens, kv_heads),
        grid_spec=grid_spec,
        out_shape=[
            jax.ShapeDtypeStruct(queries.shape, BF),
            jax.ShapeDtypeStruct(pairs.shape, BF),
        ],
        name="attend_back",
        cost_estimate=pl.CostEstimate(
            flops=10 * work * HEAD_DIM, bytes_accessed=pairs.size * 4, transcendentals=work
        ),
    )(info, queries, grads, results, pairs, pairs, lse)


def token_mask(tokens, lanes, seqs):
    row = lax.broadcasted_iota(jnp.int32, (tokens, lanes), 0) // (tokens // seqs)
    lane = lax.broadcasted_iota(jnp.int32, (tokens, lanes), 1) // ADAPTER_RANK
    return jnp.where(row == lane, adapter_scale, 0.0).astype(F32)


def feed_kernel(seqs, count, info, *refs):
    blocks = refs[:count]
    n2_ref, g0_ref, sgu_ref, ed_ref, wd_ref, eg_ref, eu_ref, sd_ref = refs[count : count + 8]
    peg_ref, peu_ref, psd_ref = refs[count + 8 : count + 11]
    out_ref, ng_ref, deg_ref, deu_ref, dsd_ref = refs[count + 11 : count + 16]
    acc_out, acc_ng, acc_nd, acc_bg, acc_bu, nar_g, nar_u, back_d, held, sems = refs[count + 16 :]
    chunk = pl.program_id(0)
    chunks = pl.num_programs(0)
    depth = blocks[0].shape[1]
    size = wd_ref.shape[0]

    def copies(at, slot):
        return [
            pltpu.make_async_copy(
                blocks[j].at[:, :, pl.ds(pl.multiple_of(at * size, 128), size)],
                held.at[slot, :, pl.ds(pl.multiple_of((info[0] ^ j) * depth, depth), depth), :],
                sems.at[slot, j],
            )
            for j in range(count)
        ]

    slot = lax.rem(chunk, 2)

    @pl.when(chunk == 0)
    def _():
        for copy in copies(chunk, slot):
            copy.start()

    @pl.when(chunk + 1 < chunks)
    def _():
        for copy in copies(chunk + 1, 1 - slot):
            copy.start()

    tokens = n2_ref.shape[0]
    model = n2_ref.shape[1]
    cols = sd_ref.shape[1]
    n2 = n2_ref[...]
    g0 = g0_ref[...]
    wg_ref = held.at[slot, 0]
    wu_ref = held.at[slot, 1]

    @pl.when(chunk == 0)
    def _():
        mix = token_mask(tokens, cols, seqs)
        narrow = mm(n2, sgu_ref[...])
        nar_g[...] = (narrow[:, :cols] * mix).astype(BF)
        nar_u[...] = (narrow[:, cols:] * mix).astype(BF)
        back_d[...] = (mm_nt(g0, ed_ref[...]) * mix).astype(BF)
        for acc in (acc_out, acc_ng, acc_nd, acc_bg, acc_bu):
            acc[...] = jnp.zeros(acc.shape, F32)

    for copy in copies(chunk, slot):
        copy.wait()
    narrow_g = nar_g[...]
    narrow_u = nar_u[...]
    narrow_b = back_d[...]
    gate = mm(n2, wg_ref[...]) + mm(narrow_g, eg_ref[...])
    upward = mm(n2, wu_ref[...]) + mm(narrow_u, eu_ref[...])
    sig = jax.nn.sigmoid(gate)
    act = gate * sig
    hidden = (act * upward).astype(BF)
    hidden_grad = mm_nt(g0, wd_ref[...]) + mm_nt(narrow_b, sd_ref[...])
    gate_grad = (hidden_grad * upward * (sig * (1.0 + gate * (1.0 - sig)))).astype(BF)
    up_grad = (hidden_grad * act).astype(BF)
    acc_out[...] += mm(hidden, wd_ref[...])
    acc_nd[...] += mm(hidden, sd_ref[...])
    acc_ng[...] += mm_nt(gate_grad, wg_ref[...]) + mm_nt(up_grad, wu_ref[...])
    acc_bg[...] += mm_nt(gate_grad, eg_ref[...])
    acc_bu[...] += mm_nt(up_grad, eu_ref[...])
    deg_ref[...] = peg_ref[...] + mm_tn(narrow_g, gate_grad)
    deu_ref[...] = peu_ref[...] + mm_tn(narrow_u, up_grad)
    dsd_ref[...] = psd_ref[...] + mm_tn(narrow_b, hidden)

    @pl.when(chunk == chunks - 1)
    def _():
        out_ref[:, :model] = acc_out[...].astype(BF)
        out_ref[:, model:] = jnp.concatenate([acc_nd[...], acc_nd[...]], axis=1).astype(BF)
        ng_ref[:, :model] = acc_ng[...].astype(BF)
        ng_ref[:, model:] = jnp.concatenate([acc_bg[...], acc_bu[...]], axis=1).astype(BF)


def feed(me, blocks, n2, g0, sgu, ed, wd, eg, eu, sd, previous, seqs, limit=768):
    tokens, model = n2.shape
    count = len(blocks)
    hidden = wd.shape[0]
    cols = ed.shape[0]
    size = max(c for c in range(128, limit + 1, 128) if hidden % c == 0)
    anywhere = pl.BlockSpec(memory_space=pl.ANY)
    whole = lambda a: pl.BlockSpec(
        a.shape, lambda h, i: (0,) * a.ndim, pipeline_mode=pl.Buffered(1)
    )
    part = lambda a: pl.BlockSpec((a.shape[0], size), lambda h, i: (0, h))
    tall = lambda a: pl.BlockSpec((size, a.shape[1]), lambda h, i: (h, 0))
    fixed = lambda c: pl.BlockSpec((tokens, c), lambda h, i: (0, 0))
    grads = jax.ShapeDtypeStruct((cols, hidden), F32)
    return pl.pallas_call(
        functools.partial(feed_kernel, seqs, count),
        grid_spec=pltpu.PrefetchScalarGridSpec(
            num_scalar_prefetch=1,
            grid=(hidden // size,),
            in_specs=[anywhere] * count
            + [whole(n2), whole(g0), whole(sgu), whole(ed), tall(wd)]
            + [part(eg), part(eu), tall(sd), part(grads), part(grads), part(grads)],
            out_specs=[fixed(model + 2 * cols), fixed(model + 2 * cols)] + [part(grads)] * 3,
            scratch_shapes=[
                pltpu.VMEM((tokens, model), F32),
                pltpu.VMEM((tokens, model), F32),
                pltpu.VMEM((tokens, cols), F32),
                pltpu.VMEM((tokens, cols), F32),
                pltpu.VMEM((tokens, cols), F32),
                pltpu.VMEM((tokens, cols), BF),
                pltpu.VMEM((tokens, cols), BF),
                pltpu.VMEM((tokens, cols), BF),
                pltpu.VMEM((2, 2, model, size), BF),
                pltpu.SemaphoreType.DMA((2, count)),
            ],
        ),
        out_shape=[
            jax.ShapeDtypeStruct((tokens, model + 2 * cols), BF),
            jax.ShapeDtypeStruct((tokens, model + 2 * cols), BF),
            grads, grads, grads,
        ],
        name="feed",
        cost_estimate=pl.CostEstimate(
            flops=12 * tokens * (model + cols) * hidden,
            bytes_accessed=6 * model * hidden,
            transcendentals=tokens * hidden,
        ),
    )(me.reshape(1).astype(jnp.int32), *blocks, n2, g0, sgu, ed, wd, eg, eu, sd, *previous)


def assemble_kernel(count, info, *refs):
    blocks = refs[:count]
    out_ref, held, blank, in_sem, out_sem = refs[count:]
    depth = blocks[0].shape[0]
    rest = out_ref.shape[0] - count * depth
    arrive = []
    leave = []
    for j in range(count):
        arrive.append(pltpu.make_async_copy(blocks[j], held.at[j], in_sem.at[j]))
        at = pl.multiple_of((info[0] ^ j) * depth, depth)
        leave.append(
            pltpu.make_async_copy(held.at[j], out_ref.at[pl.ds(at, depth), :], out_sem.at[j])
        )
    for copy in arrive:
        copy.start()
    if rest:
        blank[...] = jnp.zeros(blank.shape, BF)
        last = pltpu.make_async_copy(blank, out_ref.at[count * depth :, :], out_sem.at[count])
        last.start()
    for one, two in zip(arrive, leave):
        one.wait()
        two.start()
    for copy in leave:
        copy.wait()
    if rest:
        last.wait()


def assemble(index, blocks, rows):
    count = len(blocks)
    depth, lanes = blocks[0].shape
    anywhere = pl.BlockSpec(memory_space=pl.ANY)
    return pl.pallas_call(
        functools.partial(assemble_kernel, count),
        grid_spec=pltpu.PrefetchScalarGridSpec(
            num_scalar_prefetch=1,
            grid=(1,),
            in_specs=[anywhere] * count,
            out_specs=anywhere,
            scratch_shapes=[
                pltpu.VMEM((count, depth, lanes), BF),
                pltpu.VMEM((max(rows - count * depth, 16), lanes), BF),
                pltpu.SemaphoreType.DMA((count,)),
                pltpu.SemaphoreType.DMA((count + 1,)),
            ],
        ),
        out_shape=jax.ShapeDtypeStruct((rows, lanes), BF),
        name="assemble",
        cost_estimate=pl.CostEstimate(
            flops=0, bytes_accessed=4 * rows * lanes, transcendentals=0
        ),
    )(index.reshape(1).astype(jnp.int32), *blocks)


def expand_kernel(rank, hidden, padded, seq_n, early, kinds, both_ref, select_ref, *outs):
    pair = pl.program_id(0)
    select = select_ref[...]
    lanes = -(-hidden // 128) * 128
    width = both_ref.shape[2] - early
    for q in range(2):
        for i, out_ref in enumerate(outs[:3]):
            groups = []
            for f in range(2):
                at = i * padded
                left = lanes
                pieces = []
                while left:
                    z, low = divmod(at, width)
                    take = min(left, width - low)
                    device = pair * 4 * seq_n + (q * 2 + f) * seq_n + z
                    pieces.append(both_ref[device, :rank, early + low : early + low + take])
                    at += take
                    left -= take
                groups.append(jnp.concatenate(pieces, axis=1))
            rows = jnp.concatenate(groups, axis=0)
            if i < 2:
                out_ref[:, q * hidden : (q + 1) * hidden] = mm_tn(select, rows)[:, :hidden]
            else:
                out_ref[q * hidden : (q + 1) * hidden, :] = mm_tn(rows, select)[:hidden]

    @pl.when(pair == 0)
    def _():
        half = both_ref.shape[0] // 2
        for i, (out_ref, shrink) in enumerate(zip(outs[3:], kinds)):
            rows = jnp.concatenate(
                [
                    jnp.concatenate(
                        [both_ref[f * half + 2 * i + w, :rank, :early] for w in range(2)], axis=1
                    )
                    for f in range(2)
                ],
                axis=0,
            )
            out_ref[...] = mm_tn(rows, select) if shrink else mm_tn(select, rows)


def expand_all(both, select, rank, hidden, padded, seq_n, chips, early, kinds):
    cols = select.shape[1]
    model = 2 * early
    wide = lambda n: jax.ShapeDtypeStruct((cols, n), F32)
    tall = lambda n: jax.ShapeDtypeStruct((n, cols), F32)
    fixed = [tall(model) if shrink else wide(model) for shrink in kinds]
    return pl.pallas_call(
        functools.partial(expand_kernel, rank, hidden, padded, seq_n, early, kinds),
        grid=(chips // 2,),
        in_specs=[
            pl.BlockSpec(both.shape, lambda p: (0, 0, 0), pipeline_mode=pl.Buffered(1)),
            pl.BlockSpec(select.shape, lambda p: (0, 0)),
        ],
        out_specs=[
            pl.BlockSpec((cols, 2 * hidden), lambda p: (0, p)),
            pl.BlockSpec((cols, 2 * hidden), lambda p: (0, p)),
            pl.BlockSpec((2 * hidden, cols), lambda p: (p, 0)),
        ]
        + [pl.BlockSpec(one.shape, lambda p: (0, 0)) for one in fixed],
        out_shape=[wide(chips * hidden), wide(chips * hidden), tall(chips * hidden)] + fixed,
        name="expand",
        cost_estimate=pl.CostEstimate(
            flops=6 * cols * chips * hidden * select.shape[0],
            bytes_accessed=12 * cols * chips * hidden + both.size * 2,
            transcendentals=0,
        ),
    )(both, select)


def after(value, *needed):
    return lax.optimization_barrier((value, needed))[0]


def body(
    inputs, cotangent, span_order, adapter_ids, first_gain, second_gain,
    query_weight, key_weight, value_weight, output_weight, gate_weight, up_weight, down_weight,
    query_bias, key_bias, value_bias,
    query_reduce_factors, query_lift_factors, key_reduce_factors, key_lift_factors,
    value_reduce_factors, value_lift_factors, output_reduce_factors, output_lift_factors,
    gate_reduce_factors, gate_lift_factors, upper_reduce_factors, upper_lift_factors,
    down_reduce_factors, down_lift_factors,
):
    seq_n = lax.axis_size("seq")
    cp_n = lax.axis_size("cp")
    fsdp_n = lax.axis_size("fsdp")
    plane = fsdp_n * cp_n
    chips = plane // 2
    group = lax.axis_index("fsdp")
    me = group * cp_n + lax.axis_index("cp")
    chip = me // 2
    core = me % 2
    seqs, tok_rows, model = inputs.shape
    tokens = seqs * tok_rows
    cols = query_reduce_factors.shape[1]
    kv_width = key_weight.shape[1]
    length = tok_rows * seq_n * cp_n
    spans = span_order.shape[1]
    span_len = length // spans
    hidden_all = gate_weight.shape[1]
    hq = hidden_all // chips
    hp = -(-hq // 256) * 256
    pad = hp - hq
    rank = seqs * ADAPTER_RANK
    lanes = -(-rank // 64) * 64

    def swap(value, k):
        return lax.ppermute(value, PLANE, [(i, i ^ k) for i in range(plane)])

    first_row = (lax.axis_index("cp") * seq_n + lax.axis_index("seq")) * tok_rows
    own = lax.dynamic_slice_in_dim(span_order, first_row // span_len, 1, 1)[:, 0]
    shift = first_row % span_len
    info = jnp.concatenate([span_order.reshape(-1), own, shift.reshape(1)]).astype(jnp.int32)
    places = own[:, None] * span_len + shift + jnp.arange(tok_rows, dtype=jnp.int32)[None, :]
    cosine, sine_table = rotary_tables(places.reshape(tokens))
    cosine = cosine[:, None, :]
    sine_table = sine_table[:, None, :]
    lane = jnp.arange(lanes, dtype=jnp.int32)

    def chosen(ids):
        column = jnp.repeat(ids, ADAPTER_RANK) * ADAPTER_RANK + lane[:rank] % ADAPTER_RANK
        column = jnp.pad(column, (0, lanes - rank), constant_values=-1)
        return (jnp.arange(cols, dtype=jnp.int32)[:, None] == column[None, :]).astype(BF)

    ids_wide = jnp.broadcast_to(
        jnp.pad(adapter_ids, (0, -seqs % 8)).astype(F32)[:, None], (seqs + -seqs % 8, 128)
    )
    select = [chosen(adapter_ids)]
    for f in range(1, fsdp_n):
        select.append(chosen(swap(ids_wide, f * cp_n)[:seqs, 0].astype(jnp.int32)))
    mixing = token_mask(tokens, lanes, seqs)

    def shrink_of(value, f=0):
        return mm(value, select[f]).astype(BF)

    def expand_of(value, f=0):
        return mm_tn(select[f], value).astype(BF)

    w_kv = lax.all_gather(
        jnp.concatenate([key_weight, value_weight], axis=1), PLANE, axis=0, tiled=True
    )
    rows_q = [query_weight] + [swap(query_weight, 2 * k) for k in range(1, chips)]

    def by_chip(value):
        return jnp.stack(
            [
                jnp.pad(value[:, hq * c : hq * (c + 1)], ((0, 0), (0, pad)))
                for c in range(chips)
            ]
        )

    gate_up = jnp.stack([by_chip(gate_weight), by_chip(up_weight)], axis=1)
    depth = gate_weight.shape[0]
    parts = [lax.dynamic_index_in_dim(gate_up, chip ^ k, 0, keepdims=False) for k in range(chips)]

    resid_in = inputs.reshape(tokens, model).astype(F32)
    first_scales = first_gain.astype(F32)
    second_scales = second_gain.astype(F32)
    grad_low = cotangent.reshape(tokens, model)
    normed = norm_forward(resid_in, first_scales).astype(BF)
    w_kv, parts, rows_q = lax.optimization_barrier((w_kv, parts, rows_q))
    rows_o = [output_weight] + [swap(after(output_weight, rows_q), 2 * k) for k in range(1, chips)]
    crosses_cp = lambda k: 2 * k % cp_n != 0
    blocks = {
        k: swap(after(parts[k], rows_o), 2 * k) for k in range(1, chips) if not crosses_cp(k)
    }
    blocks[0] = parts[0]
    w_key = w_kv[:, :kv_width]
    w_value = w_kv[:, kv_width:]

    query_shrink, key_shrink, value_shrink, output_shrink, gate_shrink, up_shrink = [
        shrink_of(value)
        for value in (
            query_reduce_factors, key_reduce_factors, value_reduce_factors,
            output_reduce_factors, gate_reduce_factors, upper_reduce_factors,
        )
    ]
    query_expand, key_expand, value_expand, output_expand, down_expand = [
        expand_of(value)
        for value in (
            query_lift_factors, key_lift_factors, value_lift_factors,
            output_lift_factors, down_lift_factors,
        )
    ]

    def narrowed(value, shrink):
        return (mm(value, shrink) * mixing).astype(BF)

    key_narrow = narrowed(normed, key_shrink)
    value_narrow = narrowed(normed, value_shrink)
    key_pre = mm(normed, w_key) + key_bias.astype(F32) + mm(key_narrow, key_expand)
    value_low = (
        mm(normed, w_value) + value_bias.astype(F32) + mm(value_narrow, value_expand)
    ).astype(BF)
    key_rot = rotate(key_pre.reshape(tokens, -1, HEAD_DIM), cosine, sine_table).astype(BF)
    pair = jnp.concatenate([key_rot.reshape(tokens, kv_width), value_low], axis=1)
    pair_all = lax.all_gather(
        pair.reshape(seqs, tok_rows, 2 * kv_width), ("cp", "seq"), axis=1, tiled=True
    )

    def both_cores(rows):
        found = []
        for part in rows:
            found += [part, swap(part, 1)]
        return found

    w_query = assemble(me, after(both_cores(rows_q), pair), model)
    normed_later = after(normed, rows_o)
    query_narrow = narrowed(normed_later, query_shrink)
    query_pre = mm(normed_later, w_query) + query_bias.astype(F32) + mm(query_narrow, query_expand)
    query_rot = (
        rotate(query_pre.reshape(tokens, -1, HEAD_DIM), cosine, sine_table)
        .astype(BF)
        .reshape(tokens, model)
    )

    lift_g = lax.dynamic_index_in_dim(by_chip(gate_lift_factors), chip, 0, keepdims=False)
    lift_u = lax.dynamic_index_in_dim(by_chip(upper_lift_factors), chip, 0, keepdims=False)
    shrink_d = jnp.pad(
        lax.dynamic_slice_in_dim(down_reduce_factors, chip * hq, hq, 0), ((0, pad), (0, 0))
    )
    feed_factors = [
        (
            jnp.concatenate(
                [shrink_of(gate_reduce_factors, f), shrink_of(upper_reduce_factors, f)], axis=1
            ),
            expand_of(down_lift_factors, f),
            expand_of(lift_g, f),
            expand_of(lift_u, f),
            shrink_of(shrink_d, f),
        )
        for f in range(fsdp_n)
    ]

    down_rows = [down_weight, swap(after(down_weight, rows_o), 1)]
    w_output = assemble(me, after(both_cores(rows_o), query_rot), model)
    w_down = assemble(core, after(down_rows, query_rot), hp)
    query_rot = after(query_rot, [blocks[k] for k in blocks if k], w_output, w_down)
    for k in range(1, chips):
        if crosses_cp(k):
            blocks[k] = swap(after(parts[k], pair_all), 2 * k)
    blocks = [after(blocks[k], query_rot) for k in range(chips)]
    wide = []
    for part in blocks:
        wide += [part, swap(part, 1)]
    attended, lse = attend(info, query_rot, pair_all, seqs, spans, span_len)

    output_narrow = narrowed(attended, output_shrink)
    middle = resid_in + (mm(attended, w_output) + mm(output_narrow, output_expand))
    normed_two = norm_forward(middle, second_scales).astype(BF)

    g0_pieces = [grad_low] + [swap(after(grad_low, wide), 2 * k) for k in range(1, chips)]
    n2_pieces = [normed_two] + [swap(after(normed_two, wide), 2 * k) for k in range(1, chips)]
    if chips > 2:
        n2_pieces[1:3] = lax.optimization_barrier(n2_pieces[1:3])
    zero = jnp.zeros((lanes, hp), F32)
    sums = [(zero, zero, zero)] * fsdp_n
    out_raw = []
    grad_parts = []
    for k in range(chips):
        f = 2 * k // cp_n
        sgu, ed, eg, eu, sd = feed_factors[f]
        out_k, ng_k, *sums[f] = feed(
            me, wide, n2_pieces[k], g0_pieces[k], sgu, ed, w_down, eg, eu, sd, sums[f], seqs
        )
        out_raw.append(out_k)
        grad_parts.append(ng_k if k == 0 else swap(ng_k, 2 * k))

    grad_sum = grad_parts[0].astype(F32)
    for part in grad_parts[1:]:
        grad_sum = lax.optimization_barrier(grad_sum) + part.astype(F32)
    gate_back = (grad_sum[:, model : model + lanes] * mixing).astype(BF)
    up_back = (grad_sum[:, model + lanes :] * mixing).astype(BF)
    normed_two_grad = (
        grad_sum[:, :model] + mm_nt(gate_back, gate_shrink) + mm_nt(up_back, up_shrink)
    )
    middle_grad = grad_low.astype(F32) + norm_backward(middle, second_scales, normed_two_grad)
    middle_low = middle_grad.astype(BF)

    def narrowed_back(grad, expand):
        return (mm_nt(grad, expand) * mixing).astype(BF)

    output_back = narrowed_back(middle_low, output_expand)
    attended_grad = (mm_nt(middle_low, w_output) + mm_nt(output_back, output_shrink)).astype(BF)
    query_rot_grad, pair_part = attend_back(
        info, query_rot, attended_grad, attended, pair_all, lse, seqs, spans, span_len
    )

    out_raw = after(out_raw, grad_sum)
    out_parts = [part if k == 0 else swap(part, 2 * k) for k, part in enumerate(out_raw)]
    out_sum = sum(part.astype(F32) for part in out_parts)

    def pack(values, tiles):
        value = jnp.concatenate([value[:rank].astype(BF) for value in values], axis=1)
        return jnp.pad(value, ((0, 0), (0, -value.shape[1] % (128 * tiles))))

    sums = after(sums, attended_grad)
    stacked = jnp.stack([pack(sums[f], seq_n) for f in range(fsdp_n)])
    feed_wide = stacked.shape[2]

    def groups_of(parity):
        return jnp.stack(
            [
                lax.dynamic_index_in_dim(stacked, (2 * j + parity) ^ group, 0, keepdims=False)
                for j in range(fsdp_n // 2)
            ]
        )

    feed_half = groups_of(core).astype(F32) + swap(groups_of(1 - core), 1).astype(F32)
    feed_half = feed_half.reshape(fsdp_n // 2 * rank, seq_n, feed_wide // seq_n).astype(BF)
    feed_piece = lax.psum_scatter(
        feed_half.transpose(1, 0, 2), "seq", scatter_dimension=0, tiled=False
    )
    pair_grad = (
        lax.psum_scatter(
            after(pair_part, feed_piece, out_parts), ("cp", "seq"), scatter_dimension=1, tiled=True
        )
        .reshape(tokens, 2 * kv_width)
        .astype(F32)
    )

    down_narrow = (out_sum[:, model : model + lanes] * mixing).astype(BF)
    result = middle + (out_sum[:, :model] + mm(down_narrow, down_expand))
    outputs = result.astype(BF).reshape(seqs, tok_rows, model)

    query_grad = (
        unrotate(
            query_rot_grad.reshape(tokens, -1, HEAD_DIM).astype(F32), cosine, sine_table
        )
        .reshape(tokens, model)
        .astype(BF)
    )
    query_back = narrowed_back(query_grad, query_expand)
    query_in = mm_nt(query_grad, w_query) + mm_nt(query_back, query_shrink)

    def halves(value, index, exchange):
        span = 1
        while value.shape[0] > 1:
            split = value.reshape((value.shape[0] // 2, 2) + value.shape[1:])
            bit = index // span % 2
            keep = lax.dynamic_index_in_dim(split, bit, 1, keepdims=False)
            give = lax.dynamic_index_in_dim(split, 1 - bit, 1, keepdims=False)
            value = (keep.astype(F32) + exchange(give, span).astype(F32)).astype(BF)
            span *= 2
        return value[0]

    def swap_seq(value, k):
        return lax.ppermute(value, "seq", [(i, i ^ k) for i in range(seq_n)])

    ways = cp_n * seq_n
    cp_index = lax.axis_index("cp")
    early = pack(
        [
            mm_tn(output_back, attended),
            mm_tn(gate_back, normed_two),
            mm_tn(up_back, normed_two),
            mm_tn(output_narrow, middle_low),
            mm_tn(down_narrow, grad_low),
            mm_tn(query_back, normed),
            mm_tn(query_narrow, query_grad),
        ],
        ways,
    )
    early = early.reshape(rank, cp_n, seq_n, -1).transpose(1, 2, 0, 3)
    early = halves(early, cp_index, swap)
    early = halves(early, lax.axis_index("seq"), swap_seq)
    early_cols = early.shape[1]
    lines = feed_piece.shape[0]
    both = jnp.concatenate([jnp.pad(early, ((0, lines - rank), (0, 0))), feed_piece], axis=1)
    both = lax.all_gather(after(both, pair_grad), EVERY, axis=0, tiled=False)

    key_grad = (
        unrotate(pair_grad[:, :kv_width].reshape(tokens, -1, HEAD_DIM), cosine, sine_table)
        .reshape(tokens, kv_width)
        .astype(BF)
    )
    value_grad = pair_grad[:, kv_width:].astype(BF)
    key_back = narrowed_back(key_grad, key_expand)
    value_back = narrowed_back(value_grad, value_expand)

    late = pack(
        [
            mm_tn(key_back, normed),
            mm_tn(value_back, normed),
            mm_tn(key_narrow, key_grad),
            mm_tn(value_narrow, value_grad),
        ],
        cp_n,
    )
    late_wide = late.shape[1]
    late = late.reshape(rank, cp_n, late_wide // cp_n).transpose(1, 0, 2)
    late = halves(late, cp_index, swap)
    total = late.astype(F32)
    for k in range(1, seq_n):
        total = total + swap_seq(late, k).astype(F32)
    late = total.astype(BF)[None]
    for step in [span_k for span_k in (2**i for i in range(1, 30)) if span_k < plane] + [1]:
        late = jnp.concatenate([late, swap(late, step)], axis=0)

    normed_grad = (
        query_in
        + mm_nt(key_grad, w_key)
        + mm_nt(value_grad, w_value)
        + mm_nt(key_back, key_shrink)
        + mm_nt(value_back, value_shrink)
    )
    input_grad = middle_grad + norm_backward(resid_in, first_scales, normed_grad)

    came = [0]
    for step in [span_k for span_k in (2**i for i in range(1, 30)) if span_k < plane] + [1]:
        came = came + [c ^ step for c in came]
    inverse = [came.index(c) for c in range(plane)]
    late = jnp.take(
        late, jnp.asarray(inverse, jnp.int32)[jnp.arange(plane, dtype=jnp.int32) ^ me], axis=0
    )
    late = late.reshape(fsdp_n, cp_n, rank, late_wide // cp_n)
    late = late.transpose(0, 2, 1, 3).reshape(fsdp_n * rank, late_wide)

    order = jnp.arange(fsdp_n, dtype=jnp.int32) ^ group
    select_all = (
        jnp.take(jnp.stack(select), order, axis=0)[:, :, :rank]
        .transpose(0, 2, 1)
        .reshape(fsdp_n * rank, cols)
    )
    shrink_grad = lambda value: mm_tn(value, select_all)
    expand_grad = lambda value: mm_tn(select_all, value)

    late_of = lambda i: late[:, model * i : model * (i + 1)]
    tail_of = lambda i: late[:, model * 2 + kv_width * i : model * 2 + kv_width * (i + 1)]
    kinds = (True, True, True, False, False, True, False)
    if fsdp_n == 2 and 2 * hq % 128 == 0 and 2 * early_cols == model:
        expanded = expand_all(
            both, select_all, rank, hq, hp, seq_n, chips, early_cols, kinds
        )
    else:
        early_full = both[:, :rank, :early_cols].reshape(fsdp_n, ways, rank, early_cols)
        early_full = early_full.transpose(0, 2, 1, 3).reshape(fsdp_n * rank, ways * early_cols)
        feed_full = both[:, :, early_cols:].reshape(
            fsdp_n, cp_n // 2, 2, seq_n, fsdp_n // 2, rank, feed_wide // seq_n
        ).transpose(4, 2, 5, 0, 1, 3, 6)
        feed_full = feed_full.reshape(fsdp_n * rank, chips, feed_wide)
        expanded = []
        for i, shrink in enumerate((False, False, True) + kinds):
            if i < 3:
                rows = feed_full[:, :, i * hp : i * hp + hq].reshape(fsdp_n * rank, hidden_all)
            else:
                rows = early_full[:, model * (i - 3) : model * (i - 2)]
            expanded.append(shrink_grad(rows) if shrink else expand_grad(rows))

    return (
        outputs,
        input_grad.reshape(seqs, tok_rows, model),
        expanded[8],
        expanded[9],
        shrink_grad(late_of(0)),
        expand_grad(tail_of(0)),
        shrink_grad(late_of(1)),
        expand_grad(tail_of(1)),
        expanded[3],
        expanded[6],
        expanded[4],
        expanded[0],
        expanded[5],
        expanded[1],
        expanded[2],
        expanded[7],
    )


def solution(mesh):
    tokens_spec = P("fsdp", ("cp", "seq"), None)
    weight_spec = P(("fsdp", "cp"), None)
    placed = (
        (tokens_spec, tokens_spec, P("fsdp", None), P("fsdp"), P(), P())
        + (weight_spec,) * 7
        + (P(),) * 17
    )
    return jax.shard_map(
        body,
        mesh=mesh,
        in_specs=placed,
        out_specs=(tokens_spec, tokens_spec) + (P(),) * 14,
        check_vma=False,
    )
```

```python
import functools
import math

import jax
import jax.numpy as jnp
from jax import lax
from jax.experimental import pallas as pl
from jax.experimental.pallas import tpu as pltpu
from jax.sharding import PartitionSpec as P

HEAD_DIM = 128
ADAPTER_RANK = 16
epsilon = 1e-06
adapter_scale = 0.5
rotary_base = 1000000.0
masked_score = -1e30
PLANE = ("fsdp", "cp")
EVERY = ("fsdp", "cp", "seq")
BF = jnp.bfloat16
F32 = jnp.float32


def rotary_tables(positions):
    halfway = HEAD_DIM // 2
    frequency = jnp.exp(
        jnp.arange(halfway, dtype=jnp.float32) * (-2.0 * math.log(rotary_base) / HEAD_DIM)
    )
    angles = positions.astype(jnp.float32)[..., None] * frequency
    angles = jnp.concatenate([angles, angles], axis=-1)
    return (jnp.cos(angles), jnp.sin(angles))


def rotate(values, cosine, sine_table):
    halfway = values.shape[-1] // 2
    turned = jnp.concatenate([-values[..., halfway:], values[..., :halfway]], axis=-1)
    return values * cosine + turned * sine_table


def unrotate(gradient, cosine, sine_table):
    halfway = gradient.shape[-1] // 2
    scaled = gradient * sine_table
    turned = jnp.concatenate([scaled[..., halfway:], -scaled[..., :halfway]], axis=-1)
    return gradient * cosine + turned


def mm(left, right):
    return jnp.dot(left, right, preferred_element_type=jnp.float32)


def mm_nt(left, right):
    return lax.dot_general(
        left, right, (((1,), (1,)), ((), ())), preferred_element_type=jnp.float32
    )


def mm_tn(left, right):
    return lax.dot_general(
        left, right, (((0,), (0,)), ((), ())), preferred_element_type=jnp.float32
    )


def norm_forward(values, scales):
    return values * lax.rsqrt(jnp.mean(values * values, axis=-1, keepdims=True) + epsilon) * scales


def norm_backward(values, scales, gradient):
    inverse = lax.rsqrt(jnp.mean(values * values, axis=-1, keepdims=True) + epsilon)
    weighted = gradient * scales
    inner_sum = jnp.mean(weighted * values, axis=-1, keepdims=True)
    return inverse * weighted - values * (inverse * inverse * inverse) * inner_sum


def heads_to_rows(block):
    count = block.shape[1] // HEAD_DIM
    return jnp.concatenate(
        [block[:, HEAD_DIM * j : HEAD_DIM * (j + 1)] for j in range(count)], axis=0
    )


def rows_to_heads(rows, tokens):
    count = rows.shape[0] // tokens
    return jnp.concatenate([rows[tokens * j : tokens * (j + 1)] for j in range(count)], axis=1)


def attend_kernel(spans, span_len, tokens, info, q_ref, k_ref, v_ref, o_ref, lse_ref, m_ref, l_ref, acc_ref):
    seq = pl.program_id(0)
    seqs = pl.num_programs(0)
    own = info[seqs * spans + seq]
    shift = info[seqs * spans + seqs]
    scale = math.log2(math.e) / math.sqrt(HEAD_DIM)
    queries = heads_to_rows(q_ref[...])
    m_ref[...] = jnp.full(m_ref.shape, masked_score, F32)
    l_ref[...] = jnp.zeros(l_ref.shape, F32)
    acc_ref[...] = jnp.zeros(acc_ref.shape, F32)

    def update(j, masked):
        rows = pl.ds(pl.multiple_of(j * span_len, span_len), span_len)
        scores = mm_nt(k_ref[0, rows, :], queries) * scale
        if masked:
            key_at = lax.broadcasted_iota(jnp.int32, scores.shape, 0)
            query_at = shift + lax.rem(lax.broadcasted_iota(jnp.int32, scores.shape, 1), tokens)
            scores = jnp.where(key_at <= query_at, scores, masked_score)
        old = m_ref[...]
        top = jnp.maximum(old, jnp.max(scores, axis=0, keepdims=True))
        expo = jnp.exp2(scores - top)
        alpha = jnp.exp2(old - top)
        l_ref[...] = l_ref[...] * alpha + jnp.sum(expo, axis=0, keepdims=True)
        acc_ref[...] = acc_ref[...] * alpha + mm_tn(v_ref[0, rows, :], expo.astype(BF))
        m_ref[...] = top

    def step(j, carry):
        other = info[seq * spans + j]

        @pl.when(other < own)
        def _():
            update(j, False)

        @pl.when(other == own)
        def _():
            update(j, True)

        return carry

    lax.fori_loop(0, spans, step, 0)
    total = l_ref[...]
    out = jnp.transpose(acc_ref[...] / total)
    o_ref[...] = rows_to_heads(out.astype(BF), tokens)
    lse_ref[0] = jnp.broadcast_to(m_ref[...] + jnp.log2(total), lse_ref.shape[1:])


def attend(info, queries, pairs, seqs, spans, span_len):
    tokens = queries.shape[0] // seqs
    length = pairs.shape[1]
    kv_heads = pairs.shape[2] // (2 * HEAD_DIM)
    width = queries.shape[1] // kv_heads
    rows = tokens * (width // HEAD_DIM)
    grid_spec = pltpu.PrefetchScalarGridSpec(
        num_scalar_prefetch=1,
        grid=(seqs, kv_heads),
        in_specs=[
            pl.BlockSpec((tokens, width), lambda s, h, i: (s, h)),
            pl.BlockSpec((1, length, HEAD_DIM), lambda s, h, i: (s, 0, h)),
            pl.BlockSpec((1, length, HEAD_DIM), lambda s, h, i: (s, 0, kv_heads + h)),
        ],
        out_specs=[
            pl.BlockSpec((tokens, width), lambda s, h, i: (s, h)),
            pl.BlockSpec((1, 8, rows), lambda s, h, i: (s * kv_heads + h, 0, 0)),
        ],
        scratch_shapes=[pltpu.VMEM((1, rows), F32)] * 2 + [pltpu.VMEM((HEAD_DIM, rows), F32)],
    )
    work = seqs * kv_heads * rows * length
    return pl.pallas_call(
        functools.partial(attend_kernel, spans, span_len, tokens),
        grid_spec=grid_spec,
        out_shape=[
            jax.ShapeDtypeStruct(queries.shape, BF),
            jax.ShapeDtypeStruct((seqs * kv_heads, 8, rows), F32),
        ],
        name="attend",
        cost_estimate=pl.CostEstimate(
            flops=4 * work * HEAD_DIM, bytes_accessed=pairs.size * 2, transcendentals=work
        ),
    )(info, queries, pairs, pairs)


def attend_back_kernel(
    spans, span_len, tokens, kv_heads,
    info, q_ref, do_ref, o_ref, k_ref, v_ref, lse_ref, dq_ref, dkv_ref, acc_ref,
):
    seq = pl.program_id(0)
    head = pl.program_id(1)
    seqs = pl.num_programs(0)
    own = info[seqs * spans + seq]
    shift = info[seqs * spans + seqs]
    root = 1.0 / math.sqrt(HEAD_DIM)
    scale = math.log2(math.e) * root
    queries = heads_to_rows(q_ref[...])
    grads = heads_to_rows(do_ref[...])
    results = heads_to_rows(o_ref[...])
    inner = jnp.sum(
        jnp.transpose(grads.astype(F32) * results.astype(F32)), axis=0, keepdims=True
    )
    lse = lse_ref[0, :1, :]
    acc_ref[...] = jnp.zeros(acc_ref.shape, F32)
    key_lane = pl.multiple_of(head * HEAD_DIM, HEAD_DIM)
    val_lane = pl.multiple_of((kv_heads + head) * HEAD_DIM, HEAD_DIM)

    def store(j, key_grad, value_grad):
        rows = pl.ds(pl.multiple_of(j * span_len, span_len), span_len)
        dkv_ref[0, rows, pl.ds(key_lane, HEAD_DIM)] = key_grad
        dkv_ref[0, rows, pl.ds(val_lane, HEAD_DIM)] = value_grad

    def update(j, masked):
        rows = pl.ds(pl.multiple_of(j * span_len, span_len), span_len)
        keys = k_ref[0, rows, :]
        prob = jnp.exp2(mm_nt(keys, queries) * scale - lse)
        if masked:
            key_at = lax.broadcasted_iota(jnp.int32, prob.shape, 0)
            query_at = shift + lax.rem(lax.broadcasted_iota(jnp.int32, prob.shape, 1), tokens)
            prob = jnp.where(key_at <= query_at, prob, 0.0)
        prob_grad = mm_nt(v_ref[0, rows, :], grads)
        score_grad = (prob * (prob_grad - inner)).astype(BF)
        acc_ref[...] += mm_tn(score_grad, keys)
        store(
            j, (mm(score_grad, queries) * root).astype(BF), mm(prob.astype(BF), grads).astype(BF)
        )

    def step(j, carry):
        other = info[seq * spans + j]

        @pl.when(other < own)
        def _():
            update(j, False)

        @pl.when(other == own)
        def _():
            update(j, True)

        @pl.when(other > own)
        def _():
            zero = jnp.zeros((span_len, HEAD_DIM), BF)
            store(j, zero, zero)

        return carry

    lax.fori_loop(0, spans, step, 0)
    dq_ref[...] = rows_to_heads((acc_ref[...] * root).astype(BF), tokens)


def attend_back(info, queries, grads, results, pairs, lse, seqs, spans, span_len):
    tokens = queries.shape[0] // seqs
    length = pairs.shape[1]
    kv_heads = pairs.shape[2] // (2 * HEAD_DIM)
    width = queries.shape[1] // kv_heads
    rows = tokens * (width // HEAD_DIM)
    row = pl.BlockSpec((tokens, width), lambda s, h, i: (s, h))
    block = (1, length, pairs.shape[2])
    grid_spec = pltpu.PrefetchScalarGridSpec(
        num_scalar_prefetch=1,
        grid=(seqs, kv_heads),
        in_specs=[
            row,
            row,
            row,
            pl.BlockSpec((1, length, HEAD_DIM), lambda s, h, i: (s, 0, h)),
            pl.BlockSpec((1, length, HEAD_DIM), lambda s, h, i: (s, 0, kv_heads + h)),
            pl.BlockSpec((1, 8, rows), lambda s, h, i: (s * kv_heads + h, 0, 0)),
        ],
        out_specs=[row, pl.BlockSpec(block, lambda s, h, i: (s, 0, 0))],
        scratch_shapes=[pltpu.VMEM((rows, HEAD_DIM), F32)],
    )
    work = seqs * kv_heads * rows * length
    return pl.pallas_call(
        functools.partial(attend_back_kernel, spans, span_len, tokens, kv_heads),
        grid_spec=grid_spec,
        out_shape=[
            jax.ShapeDtypeStruct(queries.shape, BF),
            jax.ShapeDtypeStruct(pairs.shape, BF),
        ],
        name="attend_back",
        cost_estimate=pl.CostEstimate(
            flops=10 * work * HEAD_DIM, bytes_accessed=pairs.size * 4, transcendentals=work
        ),
    )(info, queries, grads, results, pairs, pairs, lse)


def turned(values, cosine, sine_signed):
    return values * cosine + pltpu.roll(values, HEAD_DIM // 2, axis=1) * sine_signed


def fetch_rows(index, blocks, out_ref, sems):
    depth = blocks[0].shape[0]
    return [
        pltpu.make_async_copy(
            block,
            out_ref.at[pl.ds(pl.multiple_of((index ^ j) * depth, depth), depth), :],
            sems.at[j],
        )
        for j, block in enumerate(blocks)
    ]


def keys_kernel(
    seqs, x_ref, gain_ref, w_ref, shrink_ref, ek_ref, ev_ref, bias_ref, cos_ref, sin_ref,
    normed_ref, nk_ref, nv_ref, pair_ref,
):
    tokens, width = pair_ref.shape
    kv = width // 2
    lanes = ek_ref.shape[0]
    normed = norm_forward(x_ref[...].astype(F32), gain_ref[...]).astype(BF)
    normed_ref[...] = normed
    mix = token_mask(tokens, lanes, seqs)
    narrow = mm(normed, shrink_ref[...])
    narrow_k = (narrow[:, :lanes] * mix).astype(BF)
    narrow_v = (narrow[:, lanes:] * mix).astype(BF)
    nk_ref[...] = narrow_k
    nv_ref[...] = narrow_v
    raw = mm(normed, w_ref[...]) + bias_ref[...]
    keys = raw[:, :kv] + mm(narrow_k, ek_ref[...])
    vals = raw[:, kv:] + mm(narrow_v, ev_ref[...])
    cosine = cos_ref[...]
    sine = sin_ref[...]
    for h in range(kv // HEAD_DIM):
        at = slice(h * HEAD_DIM, (h + 1) * HEAD_DIM)
        pair_ref[:, at] = turned(keys[:, at], cosine, sine).astype(BF)
    pair_ref[:, kv:] = vals.astype(BF)


def keys_values(x, gain, w_kv, shrink, expand_k, expand_v, bias, cosine, sine, seqs):
    tokens, model = x.shape
    lanes = expand_k.shape[0]
    low = lambda n: jax.ShapeDtypeStruct((tokens, n), BF)
    return pl.pallas_call(
        functools.partial(keys_kernel, seqs),
        out_shape=[low(model), low(lanes), low(lanes), low(w_kv.shape[1])],
        name="keys_values",
        cost_estimate=pl.CostEstimate(
            flops=2 * tokens * model * w_kv.shape[1],
            bytes_accessed=8 * tokens * model,
            transcendentals=tokens,
        ),
    )(x, gain, w_kv, shrink, expand_k, expand_v, bias, cosine, sine)


def queries_kernel(
    seqs, count, info, normed_ref, shrink_ref, eq_ref, bias_ref, cos_ref, sin_ref, *refs
):
    blocks = refs[:count]
    query_ref, narrow_ref, w_ref, sems = refs[count:]
    copies = fetch_rows(info[0], blocks, w_ref, sems)
    for copy in copies:
        copy.start()
    tokens, model = query_ref.shape
    lanes = eq_ref.shape[0]
    normed = normed_ref[...]
    narrow = (mm(normed, shrink_ref[...]) * token_mask(tokens, lanes, seqs)).astype(BF)
    narrow_ref[...] = narrow
    for copy in copies:
        copy.wait()
    cosine = cos_ref[...]
    sine = sin_ref[...]
    step = 2 * HEAD_DIM
    for c in range(0, model, step):
        raw = mm(normed, w_ref[:, c : c + step]) + bias_ref[:, c : c + step]
        raw = raw + mm(narrow, eq_ref[:, c : c + step])
        for h in range(0, step, HEAD_DIM):
            query_ref[:, c + h : c + h + HEAD_DIM] = turned(
                raw[:, h : h + HEAD_DIM], cosine, sine
            ).astype(BF)


def outputs_kernel(seqs, count, info, attended_ref, x_ref, gain_ref, shrink_ref, eo_ref, *refs):
    blocks = refs[:count]
    middle_ref, normed_ref, narrow_ref, w_ref, sems = refs[count:]
    copies = fetch_rows(info[0], blocks, w_ref, sems)
    for copy in copies:
        copy.start()
    tokens, model = middle_ref.shape
    lanes = eo_ref.shape[0]
    attended = attended_ref[...]
    narrow = (mm(attended, shrink_ref[...]) * token_mask(tokens, lanes, seqs)).astype(BF)
    narrow_ref[...] = narrow
    for copy in copies:
        copy.wait()
    middle = x_ref[...].astype(F32) + (mm(attended, w_ref[...]) + mm(narrow, eo_ref[...]))
    middle_ref[...] = middle
    normed_ref[...] = norm_forward(middle, gain_ref[...]).astype(BF)


def before_attention_kernel(
    seqs, most_ref, last_ref, grad_ref, middle_ref, gain_ref, gs_ref, us_ref, os_ref, oe_ref, w_ref,
    mg_ref, low_ref, gb_ref, ub_ref, ob_ref, ag_ref,
):
    tokens, model = mg_ref.shape
    lanes = oe_ref.shape[0]
    mix = token_mask(tokens, lanes, seqs)
    total = most_ref[...] + last_ref[...].astype(F32)
    gate_back = (total[:, model : model + lanes] * mix).astype(BF)
    up_back = (total[:, model + lanes :] * mix).astype(BF)
    gb_ref[...] = gate_back
    ub_ref[...] = up_back
    normed_grad = total[:, :model] + mm_nt(gate_back, gs_ref[...]) + mm_nt(up_back, us_ref[...])
    middle_grad = grad_ref[...].astype(F32) + norm_backward(
        middle_ref[...], gain_ref[...], normed_grad
    )
    mg_ref[...] = middle_grad
    low = middle_grad.astype(BF)
    low_ref[...] = low
    output_back = (mm_nt(low, oe_ref[...]) * mix).astype(BF)
    ob_ref[...] = output_back
    ag_ref[...] = (mm_nt(low, w_ref[...]) + mm_nt(output_back, os_ref[...])).astype(BF)


def before_attention(most, last, grad, middle, gain, gs, us, os, oe, w_output, seqs):
    tokens, model = middle.shape
    lanes = oe.shape[0]
    low = lambda n: jax.ShapeDtypeStruct((tokens, n), BF)
    return pl.pallas_call(
        functools.partial(before_attention_kernel, seqs),
        out_shape=[
            jax.ShapeDtypeStruct((tokens, model), F32),
            low(model), low(lanes), low(lanes), low(lanes), low(model),
        ],
        name="before_attention",
        cost_estimate=pl.CostEstimate(
            flops=2 * tokens * model * model, bytes_accessed=30 * tokens * model, transcendentals=0
        ),
    )(most, last, grad, middle, gain, gs, us, os, oe, w_output)


def last_grads_kernel(
    seqs, rank, info, pair_ref, cos_ref, sin_ref, ke_ref, ve_ref, normed_ref, nk_ref, nv_ref,
    kg_ref, vg_ref, kb_ref, vb_ref, late_ref, rows_ref,
):
    tokens, width = pair_ref.shape
    kv = width // 2
    lanes = ke_ref.shape[0]
    model = normed_ref.shape[1]
    mix = token_mask(tokens, lanes, seqs)
    cosine = cos_ref[...]
    sine = -sin_ref[...]
    for h in range(kv // HEAD_DIM):
        at = slice(h * HEAD_DIM, (h + 1) * HEAD_DIM)
        kg_ref[:, at] = turned(pair_ref[:, at].astype(F32), cosine, sine).astype(BF)
    vg_ref[...] = pair_ref[:, kv:]
    key_grad = kg_ref[...]
    value_grad = vg_ref[...]
    key_back = (mm_nt(key_grad, ke_ref[...]) * mix).astype(BF)
    value_back = (mm_nt(value_grad, ve_ref[...]) * mix).astype(BF)
    kb_ref[...] = key_back
    vb_ref[...] = value_back
    normed = normed_ref[...]
    rows_ref[:, :model] = mm_tn(key_back, normed)[:rank].astype(BF)
    rows_ref[:, model : 2 * model] = mm_tn(value_back, normed)[:rank].astype(BF)
    rows_ref[:, 2 * model : 2 * model + kv] = mm_tn(nk_ref[...], key_grad)[:rank].astype(BF)
    rows_ref[:, 2 * model + kv :] = mm_tn(nv_ref[...], value_grad)[:rank].astype(BF)
    parts = 2 * late_ref.shape[1]
    size = late_ref.shape[3]
    for p in range(parts):
        at = p ^ info[0]
        late_ref[lax.rem(at, 2), at // 2] = rows_ref[:, p * size : (p + 1) * size]


def last_grads(mine, pair_grad, cosine, sine, ke, ve, normed, nk, nv, seqs, rank, parts):
    tokens, width = pair_grad.shape
    lanes = ke.shape[0]
    model = normed.shape[1]
    low = lambda n: jax.ShapeDtypeStruct((tokens, n), BF)
    total = 2 * model + width
    operands = [pair_grad, cosine, sine, ke, ve, normed, nk, nv]
    results = [
        low(width // 2), low(width // 2), low(lanes), low(lanes),
        jax.ShapeDtypeStruct((2, parts // 2, rank, total // parts), BF),
    ]
    return pl.pallas_call(
        functools.partial(last_grads_kernel, seqs, rank),
        grid_spec=pltpu.PrefetchScalarGridSpec(
            num_scalar_prefetch=1,
            grid=(1,),
            in_specs=[pl.BlockSpec(a.shape, lambda g, i, n=a.ndim: (0,) * n) for a in operands],
            out_specs=[
                pl.BlockSpec(r.shape, lambda g, i, n=len(r.shape): (0,) * n) for r in results
            ],
            scratch_shapes=[pltpu.VMEM((rank, total), BF)],
        ),
        out_shape=results,
        name="last_grads",
        cost_estimate=pl.CostEstimate(
            flops=4 * tokens * model * 128, bytes_accessed=6 * tokens * model, transcendentals=0
        ),
    )(mine.reshape(1).astype(jnp.int32), *operands)


def with_blocks(kernel, name, seqs, index, blocks, operands, results):
    count = len(blocks)
    depth, lanes = blocks[0].shape
    inside = pl.BlockSpec(memory_space=pltpu.VMEM)
    results = list(results) + [jax.ShapeDtypeStruct((count * depth, lanes), BF)]
    return pl.pallas_call(
        functools.partial(kernel, seqs, count),
        grid_spec=pltpu.PrefetchScalarGridSpec(
            num_scalar_prefetch=1,
            grid=(1,),
            in_specs=[pl.BlockSpec(a.shape, lambda g, i, n=a.ndim: (0,) * n) for a in operands]
            + [pl.BlockSpec(memory_space=pl.ANY)] * count,
            out_specs=[pl.BlockSpec(r.shape, lambda g, i: (0, 0)) for r in results],
            scratch_shapes=[pltpu.SemaphoreType.DMA((count,))],
        ),
        out_shape=results,
        name=name,
        cost_estimate=pl.CostEstimate(
            flops=2 * operands[0].shape[0] * count * depth * lanes,
            bytes_accessed=4 * count * depth * lanes,
            transcendentals=0,
        ),
    )(index.reshape(1).astype(jnp.int32), *operands, *blocks)


def token_mask(tokens, lanes, seqs):
    row = lax.broadcasted_iota(jnp.int32, (tokens, lanes), 0) // (tokens // seqs)
    lane = lax.broadcasted_iota(jnp.int32, (tokens, lanes), 1) // ADAPTER_RANK
    return jnp.where(row == lane, adapter_scale, 0.0).astype(F32)


def feed_kernel(seqs, kinds, info, *refs):
    count = len(kinds)
    blocks = refs[:count]
    n2_ref, g0_ref, sgu_ref, ed_ref, wd_ref, eg_ref, eu_ref, sd_ref = refs[count : count + 8]
    peg_ref, peu_ref, psd_ref = refs[count + 8 : count + 11]
    out_ref, ng_ref, deg_ref, deu_ref, dsd_ref = refs[count + 11 : count + 16]
    acc_out, acc_ng, acc_nd, acc_bg, acc_bu, nar_g, nar_u, back_d, held, sems = refs[count + 16 :]
    chunk = pl.program_id(0)
    chunks = pl.num_programs(0)
    depth = blocks[0].shape[-2]
    size = wd_ref.shape[0]

    def copies(at, slot):
        found = []
        for n, (j, which) in enumerate(kinds):
            rows = pl.ds(pl.multiple_of((info[0] ^ j) * depth, depth), depth)
            lanes = pl.ds(pl.multiple_of(at * size, 128), size)
            if which is None:
                source, target = blocks[n].at[:, :, lanes], held.at[slot, :, rows, :]
            else:
                source, target = blocks[n].at[:, lanes], held.at[slot, info[1] ^ which, rows, :]
            found.append(pltpu.make_async_copy(source, target, sems.at[slot, n]))
        return found

    slot = lax.rem(chunk, 2)

    @pl.when(chunk == 0)
    def _():
        for copy in copies(chunk, slot):
            copy.start()

    @pl.when(chunk + 1 < chunks)
    def _():
        for copy in copies(chunk + 1, 1 - slot):
            copy.start()

    tokens = n2_ref.shape[0]
    model = n2_ref.shape[1]
    cols = sd_ref.shape[1]
    n2 = n2_ref[...]
    g0 = g0_ref[...]
    wg_ref = held.at[slot, 0]
    wu_ref = held.at[slot, 1]

    @pl.when(chunk == 0)
    def _():
        mix = token_mask(tokens, cols, seqs)
        narrow = mm(n2, sgu_ref[...])
        nar_g[...] = (narrow[:, :cols] * mix).astype(BF)
        nar_u[...] = (narrow[:, cols:] * mix).astype(BF)
        back_d[...] = (mm_nt(g0, ed_ref[...]) * mix).astype(BF)
        for acc in (acc_out, acc_ng, acc_nd, acc_bg, acc_bu):
            acc[...] = jnp.zeros(acc.shape, F32)

    for copy in copies(chunk, slot):
        copy.wait()
    narrow_g = nar_g[...]
    narrow_u = nar_u[...]
    narrow_b = back_d[...]
    gate = mm(n2, wg_ref[...]) + mm(narrow_g, eg_ref[...])
    upward = mm(n2, wu_ref[...]) + mm(narrow_u, eu_ref[...])
    sig = jax.nn.sigmoid(gate)
    act = gate * sig
    hidden = (act * upward).astype(BF)
    hidden_grad = mm_nt(g0, wd_ref[...]) + mm_nt(narrow_b, sd_ref[...])
    gate_grad = (hidden_grad * upward * (sig * (1.0 + gate * (1.0 - sig)))).astype(BF)
    up_grad = (hidden_grad * act).astype(BF)
    acc_out[...] += mm(hidden, wd_ref[...])
    acc_nd[...] += mm(hidden, sd_ref[...])
    acc_ng[...] += mm_nt(gate_grad, wg_ref[...]) + mm_nt(up_grad, wu_ref[...])
    acc_bg[...] += mm_nt(gate_grad, eg_ref[...])
    acc_bu[...] += mm_nt(up_grad, eu_ref[...])
    deg_ref[...] = peg_ref[...] + mm_tn(narrow_g, gate_grad)
    deu_ref[...] = peu_ref[...] + mm_tn(narrow_u, up_grad)
    dsd_ref[...] = psd_ref[...] + mm_tn(narrow_b, hidden)

    @pl.when(chunk == chunks - 1)
    def _():
        out_ref[:, :model] = acc_out[...].astype(BF)
        out_ref[:, model:] = jnp.concatenate([acc_nd[...], acc_nd[...]], axis=1).astype(BF)
        ng_ref[:, :model] = acc_ng[...].astype(BF)
        ng_ref[:, model:] = jnp.concatenate([acc_bg[...], acc_bu[...]], axis=1).astype(BF)


def feed(index, kinds, blocks, n2, g0, sgu, ed, wd, eg, eu, sd, previous, seqs, limit=768):
    tokens, model = n2.shape
    count = len(blocks)
    hidden = wd.shape[0]
    cols = ed.shape[0]
    size = max(c for c in range(128, limit + 1, 128) if hidden % c == 0)
    anywhere = pl.BlockSpec(memory_space=pl.ANY)
    whole = lambda a: pl.BlockSpec(
        a.shape, lambda h, i: (0,) * a.ndim, pipeline_mode=pl.Buffered(1)
    )
    part = lambda a: pl.BlockSpec((a.shape[0], size), lambda h, i: (0, h))
    tall = lambda a: pl.BlockSpec((size, a.shape[1]), lambda h, i: (h, 0))
    fixed = lambda c: pl.BlockSpec((tokens, c), lambda h, i: (0, 0))
    grads = jax.ShapeDtypeStruct((cols, hidden), F32)
    return pl.pallas_call(
        functools.partial(feed_kernel, seqs, tuple(kinds)),
        grid_spec=pltpu.PrefetchScalarGridSpec(
            num_scalar_prefetch=1,
            grid=(hidden // size,),
            in_specs=[anywhere] * count
            + [whole(n2), whole(g0), whole(sgu), whole(ed), tall(wd)]
            + [part(eg), part(eu), tall(sd), part(grads), part(grads), part(grads)],
            out_specs=[fixed(model + 2 * cols), fixed(model + 2 * cols)] + [part(grads)] * 3,
            scratch_shapes=[
                pltpu.VMEM((tokens, model), F32),
                pltpu.VMEM((tokens, model), F32),
                pltpu.VMEM((tokens, cols), F32),
                pltpu.VMEM((tokens, cols), F32),
                pltpu.VMEM((tokens, cols), F32),
                pltpu.VMEM((tokens, cols), BF),
                pltpu.VMEM((tokens, cols), BF),
                pltpu.VMEM((tokens, cols), BF),
                pltpu.VMEM((2, 2, model, size), BF),
                pltpu.SemaphoreType.DMA((2, count)),
            ],
        ),
        out_shape=[
            jax.ShapeDtypeStruct((tokens, model + 2 * cols), BF),
            jax.ShapeDtypeStruct((tokens, model + 2 * cols), BF),
            grads, grads, grads,
        ],
        name="feed",
        cost_estimate=pl.CostEstimate(
            flops=12 * tokens * (model + cols) * hidden,
            bytes_accessed=6 * model * hidden,
            transcendentals=tokens * hidden,
        ),
    )(index, *blocks, n2, g0, sgu, ed, wd, eg, eu, sd, *previous)


def assemble_kernel(count, info, *refs):
    blocks = refs[:count]
    out_ref, held, blank, in_sem, out_sem = refs[count:]
    depth = blocks[0].shape[0]
    rest = out_ref.shape[0] - count * depth
    arrive = []
    leave = []
    for j in range(count):
        arrive.append(pltpu.make_async_copy(blocks[j], held.at[j], in_sem.at[j]))
        at = pl.multiple_of((info[0] ^ j) * depth, depth)
        leave.append(
            pltpu.make_async_copy(held.at[j], out_ref.at[pl.ds(at, depth), :], out_sem.at[j])
        )
    for copy in arrive:
        copy.start()
    if rest:
        blank[...] = jnp.zeros(blank.shape, BF)
        last = pltpu.make_async_copy(blank, out_ref.at[count * depth :, :], out_sem.at[count])
        last.start()
    for one, two in zip(arrive, leave):
        one.wait()
        two.start()
    for copy in leave:
        copy.wait()
    if rest:
        last.wait()


def assemble(index, blocks, rows):
    count = len(blocks)
    depth, lanes = blocks[0].shape
    anywhere = pl.BlockSpec(memory_space=pl.ANY)
    return pl.pallas_call(
        functools.partial(assemble_kernel, count),
        grid_spec=pltpu.PrefetchScalarGridSpec(
            num_scalar_prefetch=1,
            grid=(1,),
            in_specs=[anywhere] * count,
            out_specs=anywhere,
            scratch_shapes=[
                pltpu.VMEM((count, depth, lanes), BF),
                pltpu.VMEM((max(rows - count * depth, 16), lanes), BF),
                pltpu.SemaphoreType.DMA((count,)),
                pltpu.SemaphoreType.DMA((count + 1,)),
            ],
        ),
        out_shape=jax.ShapeDtypeStruct((rows, lanes), BF),
        name="assemble",
        cost_estimate=pl.CostEstimate(
            flops=0, bytes_accessed=4 * rows * lanes, transcendentals=0
        ),
    )(index.reshape(1).astype(jnp.int32), *blocks)


def expand_kernel(rank, hidden, padded, seq_n, early, kinds, both_ref, select_ref, *outs):
    pair = pl.program_id(0)
    select = select_ref[...]
    lanes = -(-hidden // 128) * 128
    width = both_ref.shape[2] - early
    for q in range(2):
        for i, out_ref in enumerate(outs[:3]):
            groups = []
            for f in range(2):
                at = i * padded
                left = lanes
                pieces = []
                while left:
                    z, low = divmod(at, width)
                    take = min(left, width - low)
                    device = pair * 4 * seq_n + (q * 2 + f) * seq_n + z
                    pieces.append(both_ref[device, :rank, early + low : early + low + take])
                    at += take
                    left -= take
                groups.append(jnp.concatenate(pieces, axis=1))
            rows = jnp.concatenate(groups, axis=0)
            if i < 2:
                out_ref[:, q * hidden : (q + 1) * hidden] = mm_tn(select, rows)[:, :hidden]
            else:
                out_ref[q * hidden : (q + 1) * hidden, :] = mm_tn(rows, select)[:hidden]

    @pl.when(pair == 0)
    def _():
        half = both_ref.shape[0] // 2
        for i, (out_ref, shrink) in enumerate(zip(outs[3:], kinds)):
            rows = jnp.concatenate(
                [
                    jnp.concatenate(
                        [both_ref[f * half + 2 * i + w, :rank, :early] for w in range(2)], axis=1
                    )
                    for f in range(2)
                ],
                axis=0,
            )
            out_ref[...] = mm_tn(rows, select) if shrink else mm_tn(select, rows)


def expand_all(both, select, rank, hidden, padded, seq_n, chips, early, kinds):
    cols = select.shape[1]
    model = 2 * early
    wide = lambda n: jax.ShapeDtypeStruct((cols, n), F32)
    tall = lambda n: jax.ShapeDtypeStruct((n, cols), F32)
    fixed = [tall(model) if shrink else wide(model) for shrink in kinds]
    return pl.pallas_call(
        functools.partial(expand_kernel, rank, hidden, padded, seq_n, early, kinds),
        grid=(chips // 2,),
        in_specs=[
            pl.BlockSpec(both.shape, lambda p: (0, 0, 0), pipeline_mode=pl.Buffered(1)),
            pl.BlockSpec(select.shape, lambda p: (0, 0)),
        ],
        out_specs=[
            pl.BlockSpec((cols, 2 * hidden), lambda p: (0, p)),
            pl.BlockSpec((cols, 2 * hidden), lambda p: (0, p)),
            pl.BlockSpec((2 * hidden, cols), lambda p: (p, 0)),
        ]
        + [pl.BlockSpec(one.shape, lambda p: (0, 0)) for one in fixed],
        out_shape=[wide(chips * hidden), wide(chips * hidden), tall(chips * hidden)] + fixed,
        name="expand",
        cost_estimate=pl.CostEstimate(
            flops=6 * cols * chips * hidden * select.shape[0],
            bytes_accessed=12 * cols * chips * hidden,
            transcendentals=0,
        ),
    )(both, select)


def after(value, *needed):
    return lax.optimization_barrier((value, needed))[0]


def body(
    inputs, cotangent, span_order, adapter_ids, first_gain, second_gain,
    query_weight, key_weight, value_weight, output_weight, gate_weight, up_weight, down_weight,
    query_bias, key_bias, value_bias,
    query_reduce_factors, query_lift_factors, key_reduce_factors, key_lift_factors,
    value_reduce_factors, value_lift_factors, output_reduce_factors, output_lift_factors,
    gate_reduce_factors, gate_lift_factors, upper_reduce_factors, upper_lift_factors,
    down_reduce_factors, down_lift_factors,
):
    seq_n = lax.axis_size("seq")
    cp_n = lax.axis_size("cp")
    fsdp_n = lax.axis_size("fsdp")
    plane = fsdp_n * cp_n
    chips = plane // 2
    group = lax.axis_index("fsdp")
    me = group * cp_n + lax.axis_index("cp")
    chip = me // 2
    core = me % 2
    seqs, tok_rows, model = inputs.shape
    tokens = seqs * tok_rows
    cols = query_reduce_factors.shape[1]
    kv_width = key_weight.shape[1]
    length = tok_rows * seq_n * cp_n
    spans = span_order.shape[1]
    span_len = length // spans
    hidden_all = gate_weight.shape[1]
    hq = hidden_all // chips
    hp = -(-hq // 256) * 256
    pad = hp - hq
    rank = seqs * ADAPTER_RANK
    lanes = -(-rank // 64) * 64

    def swap(value, k):
        return lax.ppermute(value, PLANE, [(i, i ^ k) for i in range(plane)])

    def swap_seq(value, k):
        return lax.ppermute(value, "seq", [(i, i ^ k) for i in range(seq_n)])

    first_row = (lax.axis_index("cp") * seq_n + lax.axis_index("seq")) * tok_rows
    own = lax.dynamic_slice_in_dim(span_order, first_row // span_len, 1, 1)[:, 0]
    shift = first_row % span_len
    cp_index = lax.axis_index("cp")
    seq_index = lax.axis_index("seq")
    info = jnp.concatenate(
        [span_order.reshape(-1), own, jnp.stack([shift, cp_index])]
    ).astype(jnp.int32)
    places = own[:, None] * span_len + shift + jnp.arange(tok_rows, dtype=jnp.int32)[None, :]
    cosine, sine_table = rotary_tables(places.reshape(tokens))
    sine_signed = jnp.where(
        jnp.arange(HEAD_DIM, dtype=jnp.int32) < HEAD_DIM // 2, -sine_table, sine_table
    )
    flat_cosine = cosine
    cosine = cosine[:, None, :]
    sine_table = sine_table[:, None, :]
    lane = jnp.arange(lanes, dtype=jnp.int32)

    def chosen(ids):
        column = jnp.repeat(ids, ADAPTER_RANK) * ADAPTER_RANK + lane[:rank] % ADAPTER_RANK
        column = jnp.pad(column, (0, lanes - rank), constant_values=-1)
        return (jnp.arange(cols, dtype=jnp.int32)[:, None] == column[None, :]).astype(BF)

    ids_wide = jnp.broadcast_to(
        jnp.pad(adapter_ids, (0, -seqs % 8)).astype(F32)[:, None], (seqs + -seqs % 8, 128)
    )
    select = [chosen(adapter_ids)]
    for f in range(1, fsdp_n):
        select.append(chosen(swap(ids_wide, f * cp_n)[:seqs, 0].astype(jnp.int32)))
    mixing = token_mask(tokens, lanes, seqs)

    def shrink_of(value, f=0):
        return mm(value, select[f]).astype(BF)

    def expand_of(value, f=0):
        return mm_tn(select[f], value).astype(BF)

    w_kv = lax.all_gather(
        jnp.concatenate([key_weight, value_weight], axis=1), PLANE, axis=0, tiled=True
    )
    rows_q = [query_weight] + [swap(query_weight, 2 * k) for k in range(1, chips)]

    def by_chip(value):
        return jnp.stack(
            [
                jnp.pad(value[:, hq * c : hq * (c + 1)], ((0, 0), (0, pad)))
                for c in range(chips)
            ]
        )

    gate_up = jnp.stack([by_chip(gate_weight), by_chip(up_weight)], axis=1)
    depth = gate_weight.shape[0]
    parts = [lax.dynamic_index_in_dim(gate_up, chip ^ k, 0, keepdims=False) for k in range(chips)]

    low_in = inputs.reshape(tokens, model)
    resid_in = low_in.astype(F32)
    first_scales = first_gain.astype(F32)
    second_scales = second_gain.astype(F32)
    grad_low = cotangent.reshape(tokens, model)
    w_kv, parts, rows_q = lax.optimization_barrier((w_kv, parts, rows_q))
    rows_o = [output_weight] + [swap(after(output_weight, rows_q), 2 * k) for k in range(1, chips)]
    blocks = {}
    g0_pieces = {
        k: swap(after(grad_low, rows_q), 2 * k) for k in range(1, chips) if 2 * k % cp_n == 0
    }
    w_key = w_kv[:, :kv_width]
    w_value = w_kv[:, kv_width:]

    query_shrink, key_shrink, value_shrink, output_shrink, gate_shrink, up_shrink = [
        shrink_of(value)
        for value in (
            query_reduce_factors, key_reduce_factors, value_reduce_factors,
            output_reduce_factors, gate_reduce_factors, upper_reduce_factors,
        )
    ]
    query_expand, key_expand, value_expand, output_expand, down_expand = [
        expand_of(value)
        for value in (
            query_lift_factors, key_lift_factors, value_lift_factors,
            output_lift_factors, down_lift_factors,
        )
    ]

    def narrowed(value, shrink):
        return (mm(value, shrink) * mixing).astype(BF)

    normed, key_narrow, value_narrow, pair = keys_values(
        low_in, first_scales[None], w_kv, jnp.concatenate([key_shrink, value_shrink], axis=1),
        key_expand, value_expand,
        jnp.concatenate([key_bias, value_bias]).astype(F32)[None], flat_cosine, sine_signed, seqs,
    )
    pair_all = lax.all_gather(
        pair.reshape(seqs, tok_rows, 2 * kv_width), ("cp", "seq"), axis=1, tiled=True
    )

    def both_cores(rows):
        found = []
        for part in rows:
            found += [part, swap(part, 1)]
        return found

    query_rot, query_narrow, w_query = with_blocks(
        queries_kernel, "queries", seqs, me, after(both_cores(rows_q), pair),
        [
            after(normed, rows_o, g0_pieces), query_shrink, query_expand, query_bias.astype(F32)[None], flat_cosine,
            sine_signed,
        ],
        [
            jax.ShapeDtypeStruct((tokens, model), BF),
            jax.ShapeDtypeStruct((tokens, lanes), BF),
        ],
    )

    attended, lse = attend(info, query_rot, pair_all, seqs, spans, span_len)
    for k in range(1, chips):
        blocks[k] = swap(after(parts[k], pair_all, query_rot), 2 * k)
    late_lift = after(
        (gate_lift_factors, upper_lift_factors, down_reduce_factors), attended, blocks
    )
    lift_g = lax.dynamic_index_in_dim(by_chip(late_lift[0]), chip, 0, keepdims=False)
    lift_u = lax.dynamic_index_in_dim(by_chip(late_lift[1]), chip, 0, keepdims=False)
    shrink_d = jnp.pad(
        lax.dynamic_slice_in_dim(late_lift[2], chip * hq, hq, 0), ((0, pad), (0, 0))
    )
    feed_factors = [
        (
            jnp.concatenate(
                [shrink_of(gate_reduce_factors, f), shrink_of(upper_reduce_factors, f)], axis=1
            ),
            expand_of(down_lift_factors, f),
            expand_of(lift_g, f),
            expand_of(lift_u, f),
            shrink_of(shrink_d, f),
        )
        for f in range(fsdp_n)
    ]

    output_blocks = both_cores(after(rows_o, query_rot))
    down_rows = [down_weight, swap(after(down_weight, query_rot), 1)]
    w_down = assemble(core, after(down_rows, attended), hp)
    kinds = [(0, None), (1, None)]
    wide = [parts[0], swap(after(parts[0], query_rot), 1)]
    for k in range(1, chips):
        kinds += [(2 * k, None), (2 * k + 1, None)]
        wide += [blocks[k], swap(blocks[k], 1)]
    feed_index = jnp.stack([me, core]).astype(jnp.int32)

    middle, normed_two, output_narrow, w_output = with_blocks(
        outputs_kernel, "outputs", seqs, me, output_blocks,
        [attended, low_in, second_scales[None], output_shrink, output_expand],
        [
            jax.ShapeDtypeStruct((tokens, model), F32),
            jax.ShapeDtypeStruct((tokens, model), BF),
            jax.ShapeDtypeStruct((tokens, lanes), BF),
        ],
    )

    g0_pieces[0] = grad_low
    n2_pieces = [normed_two]
    for k in range(1, chips):
        if k < 3 and k not in g0_pieces:
            g0_pieces[k] = swap(after(grad_low, wide), 2 * k)
        if k < 3:
            n2_pieces.append(swap(after(normed_two, wide), 2 * k))
    if chips > 2:
        n2_pieces[1:3] = lax.optimization_barrier(n2_pieces[1:3])
    zero = jnp.zeros((lanes, hp), F32)
    sums = [(zero, zero, zero)] * fsdp_n
    out_raw = []
    grad_parts = []
    early_first = [0] + sorted(range(1, chips), key=lambda k: (k > 2, -k if k < 3 else k))
    for k in early_first:
        f = 2 * k // cp_n
        sgu, ed, eg, eu, sd = feed_factors[f]
        if len(out_raw) == 1:
            for other in range(3, chips):
                n2_pieces.append(swap(after(normed_two, out_raw[0]), 2 * other))
                g0_pieces[other] = swap(after(grad_low, out_raw[0]), 2 * other)
        if out_raw:
            sums[f] = after(sums[f], out_raw[-1])
        out_k, ng_k, *sums[f] = feed(
            feed_index, kinds, wide, n2_pieces[k], g0_pieces[k], sgu, ed, w_down, eg, eu, sd, sums[f], seqs
        )
        out_raw.append(out_k)
        grad_parts.append(ng_k if k == 0 else swap(ng_k, 2 * k))

    grad_most = grad_parts[0].astype(F32)
    for part in grad_parts[1:-1]:
        grad_most = lax.optimization_barrier(grad_most) + part.astype(F32)

    def pack(values, tiles):
        value = jnp.concatenate([value[:rank].astype(BF) for value in values], axis=1)
        return jnp.pad(value, ((0, 0), (0, -value.shape[1] % (128 * tiles))))

    middle_grad, middle_low, gate_back, up_back, output_back, attended_grad = before_attention(
        grad_most, grad_parts[-1], grad_low, middle, second_scales[None],
        gate_shrink, up_shrink, output_shrink, output_expand, w_output, seqs,
    )

    def narrowed_back(grad, expand):
        return (mm_nt(grad, expand) * mixing).astype(BF)

    out_raw = after(out_raw, middle_low)
    out_parts = [swap(part, 2 * k) if k else part for k, part in zip(early_first, out_raw)]
    query_rot_grad, pair_part = attend_back(
        info, query_rot, attended_grad, attended, pair_all, lse, seqs, spans, span_len
    )
    pair_grad = lax.psum_scatter(
        after(pair_part, out_parts[:3]), ("cp", "seq"), scatter_dimension=1, tiled=True
    ).reshape(tokens, 2 * kv_width)
    out_sum = sum(part.astype(F32) for part in out_parts)

    down_narrow = (out_sum[:, model : model + lanes] * mixing).astype(BF)
    result = middle + (out_sum[:, :model] + mm(down_narrow, down_expand))
    outputs = result.astype(BF).reshape(seqs, tok_rows, model)

    query_rot_grad, sums, middle_late, output_back, gate_back, up_back = after(
        (query_rot_grad, sums, middle_low, output_back, gate_back, up_back), out_parts[:3]
    )
    query_grad = (
        unrotate(
            query_rot_grad.reshape(tokens, -1, HEAD_DIM).astype(F32), cosine, sine_table
        )
        .reshape(tokens, model)
        .astype(BF)
    )
    query_back = narrowed_back(query_grad, query_expand)
    query_in = mm_nt(query_grad, w_query) + mm_nt(query_back, query_shrink)

    def halves(value, index, exchange):
        span = 1
        while value.shape[0] > 1:
            split = value.reshape((value.shape[0] // 2, 2) + value.shape[1:])
            bit = index // span % 2
            keep = lax.dynamic_index_in_dim(split, bit, 1, keepdims=False)
            give = lax.dynamic_index_in_dim(split, 1 - bit, 1, keepdims=False)
            value = (keep.astype(F32) + exchange(give, span).astype(F32)).astype(BF)
            span *= 2
        return value[0]

    stacked = jnp.stack([pack(sums[f], seq_n) for f in range(fsdp_n)])
    feed_wide = stacked.shape[2]

    def groups_of(parity):
        return jnp.stack(
            [
                lax.dynamic_index_in_dim(stacked, (2 * j + parity) ^ group, 0, keepdims=False)
                for j in range(fsdp_n // 2)
            ]
        )

    feed_half = groups_of(core).astype(F32) + swap(groups_of(1 - core), 1).astype(F32)
    feed_half = feed_half.reshape(fsdp_n // 2 * rank, seq_n, feed_wide // seq_n).astype(BF)
    feed_half = feed_half.transpose(1, 0, 2)
    feed_piece = halves(feed_half, seq_index, swap_seq)
    ways = cp_n * seq_n
    early = pack(
        [
            mm_tn(output_back, attended),
            mm_tn(gate_back, normed_two),
            mm_tn(up_back, normed_two),
            mm_tn(output_narrow, middle_late),
            mm_tn(down_narrow, grad_low),
            mm_tn(query_back, normed),
            mm_tn(query_narrow, query_grad),
        ],
        ways,
    )
    early = early.reshape(rank, cp_n, seq_n, -1).transpose(1, 2, 0, 3)
    early = halves(early, cp_index, swap)
    early = halves(early, seq_index, swap_seq)
    early_cols = early.shape[1]
    both = jnp.concatenate([jnp.pad(early, ((0, feed_piece.shape[0] - rank), (0, 0))), feed_piece], axis=1)
    both = lax.all_gather(after(both, pair_grad), EVERY, axis=0, tiled=False)

    key_grad, value_grad, key_back, value_back, late = last_grads(
        cp_index, pair_grad, flat_cosine, sine_signed, key_expand, value_expand, normed,
        key_narrow, value_narrow, seqs, rank, cp_n,
    )
    late_wide = late.shape[3] * cp_n
    total = late[0].astype(F32) + swap(late[1], 1).astype(F32)
    span = 2
    while span < cp_n:
        total = total[0::2] + swap(total[1::2].astype(BF), span).astype(F32)
        span *= 2
    late = total[0].astype(BF)
    total = late.astype(F32)
    for k in range(1, seq_n):
        total = total + swap_seq(late, k).astype(F32)
    late = total.astype(BF)[None]
    for step in [span_k for span_k in (2**i for i in range(1, 30)) if span_k < plane] + [1]:
        late = jnp.concatenate([late, swap(late, step)], axis=0)

    normed_grad = (
        query_in
        + mm_nt(key_grad, w_key)
        + mm_nt(value_grad, w_value)
        + mm_nt(key_back, key_shrink)
        + mm_nt(value_back, value_shrink)
    )
    input_grad = middle_grad + norm_backward(resid_in, first_scales, normed_grad)

    came = [0]
    for step in [span_k for span_k in (2**i for i in range(1, 30)) if span_k < plane] + [1]:
        came = came + [c ^ step for c in came]
    inverse = [came.index(c) for c in range(plane)]
    late = jnp.take(
        late, jnp.asarray(inverse, jnp.int32)[jnp.arange(plane, dtype=jnp.int32) ^ me], axis=0
    )
    late = late.reshape(fsdp_n, cp_n, rank, late_wide // cp_n)
    late = late.transpose(0, 2, 1, 3).reshape(fsdp_n * rank, late_wide)

    order = jnp.arange(fsdp_n, dtype=jnp.int32) ^ group
    select_all = (
        jnp.take(jnp.stack(select), order, axis=0)[:, :, :rank]
        .transpose(0, 2, 1)
        .reshape(fsdp_n * rank, cols)
    )
    shrink_grad = lambda value: mm_tn(value, select_all)
    expand_grad = lambda value: mm_tn(select_all, value)

    late_of = lambda i: late[:, model * i : model * (i + 1)]
    tail_of = lambda i: late[:, model * 2 + kv_width * i : model * 2 + kv_width * (i + 1)]
    order_kinds = (True, True, True, False, False, True, False)
    if fsdp_n == 2 and 2 * hq % 128 == 0 and 2 * early_cols == model:
        expanded = expand_all(
            both, select_all, rank, hq, hp, seq_n, chips, early_cols, order_kinds
        )
    else:
        early_full = both[:, :rank, :early_cols].reshape(fsdp_n, ways, rank, early_cols)
        early_full = early_full.transpose(0, 2, 1, 3).reshape(fsdp_n * rank, ways * early_cols)
        feed_full = both[:, :, early_cols:].reshape(
            fsdp_n, cp_n // 2, 2, seq_n, fsdp_n // 2, rank, feed_wide // seq_n
        ).transpose(4, 2, 5, 0, 1, 3, 6)
        feed_full = feed_full.reshape(fsdp_n * rank, chips, feed_wide)
        expanded = []
        for i, shrink in enumerate((False, False, True) + order_kinds):
            if i < 3:
                rows = feed_full[:, :, i * hp : i * hp + hq].reshape(fsdp_n * rank, hidden_all)
            else:
                rows = early_full[:, model * (i - 3) : model * (i - 2)]
            expanded.append(shrink_grad(rows) if shrink else expand_grad(rows))

    return (
        outputs,
        input_grad.reshape(seqs, tok_rows, model),
        expanded[8],
        expanded[9],
        shrink_grad(late_of(0)),
        expand_grad(tail_of(0)),
        shrink_grad(late_of(1)),
        expand_grad(tail_of(1)),
        expanded[3],
        expanded[6],
        expanded[4],
        expanded[0],
        expanded[5],
        expanded[1],
        expanded[2],
        expanded[7],
    )


def solution(mesh):
    tokens_spec = P("fsdp", ("cp", "seq"), None)
    weight_spec = P(("fsdp", "cp"), None)
    placed = (
        (tokens_spec, tokens_spec, P("fsdp", None), P("fsdp"), P(), P())
        + (weight_spec,) * 7
        + (P(),) * 17
    )
    return jax.shard_map(
        body,
        mesh=mesh,
        in_specs=placed,
        out_specs=(tokens_spec, tokens_spec) + (P(),) * 14,
        check_vma=False,
    )
```

```python
import functools
import math

import jax
import jax.numpy as jnp
from jax import lax
from jax.experimental import pallas as pl
from jax.experimental.pallas import tpu as pltpu
from jax.sharding import PartitionSpec as P

HEAD_DIM = 128
ADAPTER_RANK = 16
epsilon = 1e-06
adapter_scale = 0.5
rotary_base = 1000000.0
masked_score = -1e30
PLANE = ("fsdp", "cp")
EVERY = ("fsdp", "cp", "seq")
BF = jnp.bfloat16
F32 = jnp.float32


def rotary_tables(positions):
    halfway = HEAD_DIM // 2
    frequency = jnp.exp(
        jnp.arange(halfway, dtype=jnp.float32) * (-2.0 * math.log(rotary_base) / HEAD_DIM)
    )
    angles = positions.astype(jnp.float32)[..., None] * frequency
    angles = jnp.concatenate([angles, angles], axis=-1)
    return (jnp.cos(angles), jnp.sin(angles))


def rotate(values, cosine, sine_table):
    halfway = values.shape[-1] // 2
    turned = jnp.concatenate([-values[..., halfway:], values[..., :halfway]], axis=-1)
    return values * cosine + turned * sine_table


def unrotate(gradient, cosine, sine_table):
    halfway = gradient.shape[-1] // 2
    scaled = gradient * sine_table
    turned = jnp.concatenate([scaled[..., halfway:], -scaled[..., :halfway]], axis=-1)
    return gradient * cosine + turned


def mm(left, right):
    return jnp.dot(left, right, preferred_element_type=jnp.float32)


def mm_nt(left, right):
    return lax.dot_general(
        left, right, (((1,), (1,)), ((), ())), preferred_element_type=jnp.float32
    )


def mm_tn(left, right):
    return lax.dot_general(
        left, right, (((0,), (0,)), ((), ())), preferred_element_type=jnp.float32
    )


def norm_forward(values, scales):
    return values * lax.rsqrt(jnp.mean(values * values, axis=-1, keepdims=True) + epsilon) * scales


def norm_backward(values, scales, gradient):
    inverse = lax.rsqrt(jnp.mean(values * values, axis=-1, keepdims=True) + epsilon)
    weighted = gradient * scales
    inner_sum = jnp.mean(weighted * values, axis=-1, keepdims=True)
    return inverse * weighted - values * (inverse * inverse * inverse) * inner_sum


def heads_to_rows(block):
    count = block.shape[1] // HEAD_DIM
    return jnp.concatenate(
        [block[:, HEAD_DIM * j : HEAD_DIM * (j + 1)] for j in range(count)], axis=0
    )


def rows_to_heads(rows, tokens):
    count = rows.shape[0] // tokens
    return jnp.concatenate([rows[tokens * j : tokens * (j + 1)] for j in range(count)], axis=1)


def attend_kernel(spans, span_len, tokens, info, q_ref, k_ref, v_ref, o_ref, lse_ref, m_ref, l_ref, acc_ref):
    seq = pl.program_id(0)
    seqs = pl.num_programs(0)
    own = info[seqs * spans + seq]
    shift = info[seqs * spans + seqs]
    scale = math.log2(math.e) / math.sqrt(HEAD_DIM)
    queries = heads_to_rows(q_ref[...])
    m_ref[...] = jnp.full(m_ref.shape, masked_score, F32)
    l_ref[...] = jnp.zeros(l_ref.shape, F32)
    acc_ref[...] = jnp.zeros(acc_ref.shape, F32)

    def update(j, masked):
        rows = pl.ds(pl.multiple_of(j * span_len, span_len), span_len)
        scores = mm_nt(k_ref[0, rows, :], queries) * scale
        if masked:
            key_at = lax.broadcasted_iota(jnp.int32, scores.shape, 0)
            query_at = shift + lax.rem(lax.broadcasted_iota(jnp.int32, scores.shape, 1), tokens)
            scores = jnp.where(key_at <= query_at, scores, masked_score)
        old = m_ref[...]
        top = jnp.maximum(old, jnp.max(scores, axis=0, keepdims=True))
        expo = jnp.exp2(scores - top)
        alpha = jnp.exp2(old - top)
        l_ref[...] = l_ref[...] * alpha + jnp.sum(expo, axis=0, keepdims=True)
        acc_ref[...] = acc_ref[...] * alpha + mm_tn(v_ref[0, rows, :], expo.astype(BF))
        m_ref[...] = top

    def step(j, carry):
        other = info[seq * spans + j]

        @pl.when(other < own)
        def _():
            update(j, False)

        @pl.when(other == own)
        def _():
            update(j, True)

        return carry

    lax.fori_loop(0, spans, step, 0)
    total = l_ref[...]
    out = jnp.transpose(acc_ref[...] / total)
    o_ref[...] = rows_to_heads(out.astype(BF), tokens)
    lse_ref[0] = jnp.broadcast_to(m_ref[...] + jnp.log2(total), lse_ref.shape[1:])


def attend(info, queries, pairs, seqs, spans, span_len):
    tokens = queries.shape[0] // seqs
    length = pairs.shape[1]
    kv_heads = pairs.shape[2] // (2 * HEAD_DIM)
    width = queries.shape[1] // kv_heads
    rows = tokens * (width // HEAD_DIM)
    grid_spec = pltpu.PrefetchScalarGridSpec(
        num_scalar_prefetch=1,
        grid=(seqs, kv_heads),
        in_specs=[
            pl.BlockSpec((tokens, width), lambda s, h, i: (s, h)),
            pl.BlockSpec((1, length, HEAD_DIM), lambda s, h, i: (s, 0, h)),
            pl.BlockSpec((1, length, HEAD_DIM), lambda s, h, i: (s, 0, kv_heads + h)),
        ],
        out_specs=[
            pl.BlockSpec((tokens, width), lambda s, h, i: (s, h)),
            pl.BlockSpec((1, 8, rows), lambda s, h, i: (s * kv_heads + h, 0, 0)),
        ],
        scratch_shapes=[pltpu.VMEM((1, rows), F32)] * 2 + [pltpu.VMEM((HEAD_DIM, rows), F32)],
    )
    work = seqs * kv_heads * rows * length
    return pl.pallas_call(
        functools.partial(attend_kernel, spans, span_len, tokens),
        grid_spec=grid_spec,
        out_shape=[
            jax.ShapeDtypeStruct(queries.shape, BF),
            jax.ShapeDtypeStruct((seqs * kv_heads, 8, rows), F32),
        ],
        name="attend",
        cost_estimate=pl.CostEstimate(
            flops=4 * work * HEAD_DIM, bytes_accessed=pairs.size * 2, transcendentals=work
        ),
    )(info, queries, pairs, pairs)


def attend_back_kernel(
    spans, span_len, tokens, kv_heads,
    info, q_ref, do_ref, o_ref, k_ref, v_ref, lse_ref, dq_ref, dkv_ref, acc_ref,
):
    seq = pl.program_id(0)
    head = pl.program_id(1)
    seqs = pl.num_programs(0)
    own = info[seqs * spans + seq]
    shift = info[seqs * spans + seqs]
    root = 1.0 / math.sqrt(HEAD_DIM)
    scale = math.log2(math.e) * root
    queries = heads_to_rows(q_ref[...])
    grads = heads_to_rows(do_ref[...])
    results = heads_to_rows(o_ref[...])
    inner = jnp.sum(
        jnp.transpose(grads.astype(F32) * results.astype(F32)), axis=0, keepdims=True
    )
    lse = lse_ref[0, :1, :]
    acc_ref[...] = jnp.zeros(acc_ref.shape, F32)
    key_lane = pl.multiple_of(head * HEAD_DIM, HEAD_DIM)
    val_lane = pl.multiple_of((kv_heads + head) * HEAD_DIM, HEAD_DIM)

    def store(j, key_grad, value_grad):
        rows = pl.ds(pl.multiple_of(j * span_len, span_len), span_len)
        dkv_ref[0, rows, pl.ds(key_lane, HEAD_DIM)] = key_grad
        dkv_ref[0, rows, pl.ds(val_lane, HEAD_DIM)] = value_grad

    def update(j, masked):
        rows = pl.ds(pl.multiple_of(j * span_len, span_len), span_len)
        keys = k_ref[0, rows, :]
        prob = jnp.exp2(mm_nt(keys, queries) * scale - lse)
        if masked:
            key_at = lax.broadcasted_iota(jnp.int32, prob.shape, 0)
            query_at = shift + lax.rem(lax.broadcasted_iota(jnp.int32, prob.shape, 1), tokens)
            prob = jnp.where(key_at <= query_at, prob, 0.0)
        prob_grad = mm_nt(v_ref[0, rows, :], grads)
        score_grad = (prob * (prob_grad - inner)).astype(BF)
        acc_ref[...] += mm_tn(score_grad, keys)
        store(
            j, (mm(score_grad, queries) * root).astype(BF), mm(prob.astype(BF), grads).astype(BF)
        )

    def step(j, carry):
        other = info[seq * spans + j]

        @pl.when(other < own)
        def _():
            update(j, False)

        @pl.when(other == own)
        def _():
            update(j, True)

        @pl.when(other > own)
        def _():
            zero = jnp.zeros((span_len, HEAD_DIM), BF)
            store(j, zero, zero)

        return carry

    lax.fori_loop(0, spans, step, 0)
    dq_ref[...] = rows_to_heads((acc_ref[...] * root).astype(BF), tokens)


def attend_back(info, queries, grads, results, pairs, lse, seqs, spans, span_len):
    tokens = queries.shape[0] // seqs
    length = pairs.shape[1]
    kv_heads = pairs.shape[2] // (2 * HEAD_DIM)
    width = queries.shape[1] // kv_heads
    rows = tokens * (width // HEAD_DIM)
    row = pl.BlockSpec((tokens, width), lambda s, h, i: (s, h))
    block = (1, length, pairs.shape[2])
    grid_spec = pltpu.PrefetchScalarGridSpec(
        num_scalar_prefetch=1,
        grid=(seqs, kv_heads),
        in_specs=[
            row,
            row,
            row,
            pl.BlockSpec((1, length, HEAD_DIM), lambda s, h, i: (s, 0, h)),
            pl.BlockSpec((1, length, HEAD_DIM), lambda s, h, i: (s, 0, kv_heads + h)),
            pl.BlockSpec((1, 8, rows), lambda s, h, i: (s * kv_heads + h, 0, 0)),
        ],
        out_specs=[row, pl.BlockSpec(block, lambda s, h, i: (s, 0, 0))],
        scratch_shapes=[pltpu.VMEM((rows, HEAD_DIM), F32)],
    )
    work = seqs * kv_heads * rows * length
    return pl.pallas_call(
        functools.partial(attend_back_kernel, spans, span_len, tokens, kv_heads),
        grid_spec=grid_spec,
        out_shape=[
            jax.ShapeDtypeStruct(queries.shape, BF),
            jax.ShapeDtypeStruct(pairs.shape, BF),
        ],
        name="attend_back",
        cost_estimate=pl.CostEstimate(
            flops=10 * work * HEAD_DIM, bytes_accessed=pairs.size * 4, transcendentals=work
        ),
    )(info, queries, grads, results, pairs, pairs, lse)


def turned(values, cosine, sine_signed):
    return values * cosine + pltpu.roll(values, HEAD_DIM // 2, axis=1) * sine_signed


def fetch_rows(index, blocks, out_ref, sems):
    depth = blocks[0].shape[0]
    return [
        pltpu.make_async_copy(
            block,
            out_ref.at[pl.ds(pl.multiple_of((index ^ j) * depth, depth), depth), :],
            sems.at[j],
        )
        for j, block in enumerate(blocks)
    ]


def keys_kernel(
    seqs, x_ref, gain_ref, w_ref, shrink_ref, ek_ref, ev_ref, bias_ref, cos_ref, sin_ref,
    normed_ref, nk_ref, nv_ref, pair_ref,
):
    tokens, width = pair_ref.shape
    kv = width // 2
    lanes = ek_ref.shape[0]
    normed = norm_forward(x_ref[...].astype(F32), gain_ref[...]).astype(BF)
    normed_ref[...] = normed
    mix = token_mask(tokens, lanes, seqs)
    narrow = mm(normed, shrink_ref[...])
    narrow_k = (narrow[:, :lanes] * mix).astype(BF)
    narrow_v = (narrow[:, lanes:] * mix).astype(BF)
    nk_ref[...] = narrow_k
    nv_ref[...] = narrow_v
    raw = mm(normed, w_ref[...]) + bias_ref[...]
    keys = raw[:, :kv] + mm(narrow_k, ek_ref[...])
    vals = raw[:, kv:] + mm(narrow_v, ev_ref[...])
    cosine = cos_ref[...]
    sine = sin_ref[...]
    for h in range(kv // HEAD_DIM):
        at = slice(h * HEAD_DIM, (h + 1) * HEAD_DIM)
        pair_ref[:, at] = turned(keys[:, at], cosine, sine).astype(BF)
    pair_ref[:, kv:] = vals.astype(BF)


def keys_values(x, gain, w_kv, shrink, expand_k, expand_v, bias, cosine, sine, seqs):
    tokens, model = x.shape
    lanes = expand_k.shape[0]
    low = lambda n: jax.ShapeDtypeStruct((tokens, n), BF)
    return pl.pallas_call(
        functools.partial(keys_kernel, seqs),
        out_shape=[low(model), low(lanes), low(lanes), low(w_kv.shape[1])],
        name="keys_values",
        cost_estimate=pl.CostEstimate(
            flops=2 * tokens * model * w_kv.shape[1],
            bytes_accessed=8 * tokens * model,
            transcendentals=tokens,
        ),
    )(x, gain, w_kv, shrink, expand_k, expand_v, bias, cosine, sine)


def queries_kernel(
    seqs, count, info, normed_ref, shrink_ref, eq_ref, bias_ref, cos_ref, sin_ref, *refs
):
    blocks = refs[:count]
    query_ref, narrow_ref, w_ref, sems = refs[count:]
    copies = fetch_rows(info[0], blocks, w_ref, sems)
    for copy in copies:
        copy.start()
    tokens, model = query_ref.shape
    lanes = eq_ref.shape[0]
    normed = normed_ref[...]
    narrow = (mm(normed, shrink_ref[...]) * token_mask(tokens, lanes, seqs)).astype(BF)
    narrow_ref[...] = narrow
    for copy in copies:
        copy.wait()
    cosine = cos_ref[...]
    sine = sin_ref[...]
    step = 2 * HEAD_DIM
    for c in range(0, model, step):
        raw = mm(normed, w_ref[:, c : c + step]) + bias_ref[:, c : c + step]
        raw = raw + mm(narrow, eq_ref[:, c : c + step])
        for h in range(0, step, HEAD_DIM):
            query_ref[:, c + h : c + h + HEAD_DIM] = turned(
                raw[:, h : h + HEAD_DIM], cosine, sine
            ).astype(BF)


def outputs_kernel(seqs, count, info, attended_ref, x_ref, gain_ref, shrink_ref, eo_ref, *refs):
    blocks = refs[:count]
    middle_ref, normed_ref, narrow_ref, w_ref, sems = refs[count:]
    copies = fetch_rows(info[0], blocks, w_ref, sems)
    for copy in copies:
        copy.start()
    tokens, model = middle_ref.shape
    lanes = eo_ref.shape[0]
    attended = attended_ref[...]
    narrow = (mm(attended, shrink_ref[...]) * token_mask(tokens, lanes, seqs)).astype(BF)
    narrow_ref[...] = narrow
    for copy in copies:
        copy.wait()
    middle = x_ref[...].astype(F32) + (mm(attended, w_ref[...]) + mm(narrow, eo_ref[...]))
    middle_ref[...] = middle
    normed_ref[...] = norm_forward(middle, gain_ref[...]).astype(BF)


def before_attention_kernel(
    seqs, most_ref, last_ref, grad_ref, middle_ref, gain_ref, gs_ref, us_ref, os_ref, oe_ref, w_ref,
    mg_ref, low_ref, gb_ref, ub_ref, ob_ref, ag_ref,
):
    tokens, model = mg_ref.shape
    lanes = oe_ref.shape[0]
    mix = token_mask(tokens, lanes, seqs)
    total = most_ref[...] + last_ref[...].astype(F32)
    gate_back = (total[:, model : model + lanes] * mix).astype(BF)
    up_back = (total[:, model + lanes :] * mix).astype(BF)
    gb_ref[...] = gate_back
    ub_ref[...] = up_back
    normed_grad = total[:, :model] + mm_nt(gate_back, gs_ref[...]) + mm_nt(up_back, us_ref[...])
    middle_grad = grad_ref[...].astype(F32) + norm_backward(
        middle_ref[...], gain_ref[...], normed_grad
    )
    mg_ref[...] = middle_grad
    low = middle_grad.astype(BF)
    low_ref[...] = low
    output_back = (mm_nt(low, oe_ref[...]) * mix).astype(BF)
    ob_ref[...] = output_back
    ag_ref[...] = (mm_nt(low, w_ref[...]) + mm_nt(output_back, os_ref[...])).astype(BF)


def before_attention(most, last, grad, middle, gain, gs, us, os, oe, w_output, seqs):
    tokens, model = middle.shape
    lanes = oe.shape[0]
    low = lambda n: jax.ShapeDtypeStruct((tokens, n), BF)
    return pl.pallas_call(
        functools.partial(before_attention_kernel, seqs),
        out_shape=[
            jax.ShapeDtypeStruct((tokens, model), F32),
            low(model), low(lanes), low(lanes), low(lanes), low(model),
        ],
        name="before_attention",
        cost_estimate=pl.CostEstimate(
            flops=2 * tokens * model * model, bytes_accessed=30 * tokens * model, transcendentals=0
        ),
    )(most, last, grad, middle, gain, gs, us, os, oe, w_output)


def last_grads_kernel(
    seqs, rank, info, pair_ref, cos_ref, sin_ref, ke_ref, ve_ref, normed_ref, nk_ref, nv_ref,
    kg_ref, vg_ref, kb_ref, vb_ref, late_ref, rows_ref,
):
    tokens, width = pair_ref.shape
    kv = width // 2
    lanes = ke_ref.shape[0]
    model = normed_ref.shape[1]
    mix = token_mask(tokens, lanes, seqs)
    cosine = cos_ref[...]
    sine = -sin_ref[...]
    for h in range(kv // HEAD_DIM):
        at = slice(h * HEAD_DIM, (h + 1) * HEAD_DIM)
        kg_ref[:, at] = turned(pair_ref[:, at].astype(F32), cosine, sine).astype(BF)
    vg_ref[...] = pair_ref[:, kv:]
    key_grad = kg_ref[...]
    value_grad = vg_ref[...]
    key_back = (mm_nt(key_grad, ke_ref[...]) * mix).astype(BF)
    value_back = (mm_nt(value_grad, ve_ref[...]) * mix).astype(BF)
    kb_ref[...] = key_back
    vb_ref[...] = value_back
    normed = normed_ref[...]
    rows_ref[:, :model] = mm_tn(key_back, normed)[:rank].astype(BF)
    rows_ref[:, model : 2 * model] = mm_tn(value_back, normed)[:rank].astype(BF)
    rows_ref[:, 2 * model : 2 * model + kv] = mm_tn(nk_ref[...], key_grad)[:rank].astype(BF)
    rows_ref[:, 2 * model + kv :] = mm_tn(nv_ref[...], value_grad)[:rank].astype(BF)
    parts = 2 * late_ref.shape[1]
    size = late_ref.shape[3]
    for p in range(parts):
        at = p ^ info[0]
        late_ref[lax.rem(at, 2), at // 2] = rows_ref[:, p * size : (p + 1) * size]


def last_grads(mine, pair_grad, cosine, sine, ke, ve, normed, nk, nv, seqs, rank, parts):
    tokens, width = pair_grad.shape
    lanes = ke.shape[0]
    model = normed.shape[1]
    low = lambda n: jax.ShapeDtypeStruct((tokens, n), BF)
    total = 2 * model + width
    operands = [pair_grad, cosine, sine, ke, ve, normed, nk, nv]
    results = [
        low(width // 2), low(width // 2), low(lanes), low(lanes),
        jax.ShapeDtypeStruct((2, parts // 2, rank, total // parts), BF),
    ]
    return pl.pallas_call(
        functools.partial(last_grads_kernel, seqs, rank),
        grid_spec=pltpu.PrefetchScalarGridSpec(
            num_scalar_prefetch=1,
            grid=(1,),
            in_specs=[pl.BlockSpec(a.shape, lambda g, i, n=a.ndim: (0,) * n) for a in operands],
            out_specs=[
                pl.BlockSpec(r.shape, lambda g, i, n=len(r.shape): (0,) * n) for r in results
            ],
            scratch_shapes=[pltpu.VMEM((rank, total), BF)],
        ),
        out_shape=results,
        name="last_grads",
        cost_estimate=pl.CostEstimate(
            flops=4 * tokens * model * 128, bytes_accessed=6 * tokens * model, transcendentals=0
        ),
    )(mine.reshape(1).astype(jnp.int32), *operands)


def with_blocks(kernel, name, seqs, index, blocks, operands, results):
    count = len(blocks)
    depth, lanes = blocks[0].shape
    inside = pl.BlockSpec(memory_space=pltpu.VMEM)
    results = list(results) + [jax.ShapeDtypeStruct((count * depth, lanes), BF)]
    return pl.pallas_call(
        functools.partial(kernel, seqs, count),
        grid_spec=pltpu.PrefetchScalarGridSpec(
            num_scalar_prefetch=1,
            grid=(1,),
            in_specs=[pl.BlockSpec(a.shape, lambda g, i, n=a.ndim: (0,) * n) for a in operands]
            + [pl.BlockSpec(memory_space=pl.ANY)] * count,
            out_specs=[pl.BlockSpec(r.shape, lambda g, i: (0, 0)) for r in results],
            scratch_shapes=[pltpu.SemaphoreType.DMA((count,))],
        ),
        out_shape=results,
        name=name,
        cost_estimate=pl.CostEstimate(
            flops=2 * operands[0].shape[0] * count * depth * lanes,
            bytes_accessed=4 * count * depth * lanes,
            transcendentals=0,
        ),
    )(index.reshape(1).astype(jnp.int32), *operands, *blocks)


def token_mask(tokens, lanes, seqs):
    row = lax.broadcasted_iota(jnp.int32, (tokens, lanes), 0) // (tokens // seqs)
    lane = lax.broadcasted_iota(jnp.int32, (tokens, lanes), 1) // ADAPTER_RANK
    return jnp.where(row == lane, adapter_scale, 0.0).astype(F32)


def feed_kernel(seqs, kinds, info, *refs):
    count = len(kinds)
    blocks = refs[:count]
    n2_ref, g0_ref, sgu_ref, ed_ref, wd_ref, eg_ref, eu_ref, sd_ref = refs[count : count + 8]
    peg_ref, peu_ref, psd_ref = refs[count + 8 : count + 11]
    out_ref, ng_ref, deg_ref, deu_ref, dsd_ref = refs[count + 11 : count + 16]
    acc_out, acc_ng, acc_nd, acc_bg, acc_bu, nar_g, nar_u, back_d, held, sems = refs[count + 16 :]
    chunk = pl.program_id(0)
    chunks = pl.num_programs(0)
    depth = blocks[0].shape[-2]
    size = wd_ref.shape[0]

    def copies(at, slot):
        found = []
        for n, (j, which) in enumerate(kinds):
            rows = pl.ds(pl.multiple_of((info[0] ^ j) * depth, depth), depth)
            lanes = pl.ds(pl.multiple_of(at * size, 128), size)
            if which is None:
                source, target = blocks[n].at[:, :, lanes], held.at[slot, :, rows, :]
            else:
                source, target = blocks[n].at[:, lanes], held.at[slot, info[1] ^ which, rows, :]
            found.append(pltpu.make_async_copy(source, target, sems.at[slot, n]))
        return found

    slot = lax.rem(chunk, 2)

    @pl.when(chunk == 0)
    def _():
        for copy in copies(chunk, slot):
            copy.start()

    @pl.when(chunk + 1 < chunks)
    def _():
        for copy in copies(chunk + 1, 1 - slot):
            copy.start()

    tokens = n2_ref.shape[0]
    model = n2_ref.shape[1]
    cols = sd_ref.shape[1]
    n2 = n2_ref[...]
    g0 = g0_ref[...]
    wg_ref = held.at[slot, 0]
    wu_ref = held.at[slot, 1]

    @pl.when(chunk == 0)
    def _():
        mix = token_mask(tokens, cols, seqs)
        narrow = mm(n2, sgu_ref[...])
        nar_g[...] = (narrow[:, :cols] * mix).astype(BF)
        nar_u[...] = (narrow[:, cols:] * mix).astype(BF)
        back_d[...] = (mm_nt(g0, ed_ref[...]) * mix).astype(BF)
        for acc in (acc_out, acc_ng, acc_nd, acc_bg, acc_bu):
            acc[...] = jnp.zeros(acc.shape, F32)

    for copy in copies(chunk, slot):
        copy.wait()
    narrow_g = nar_g[...]
    narrow_u = nar_u[...]
    narrow_b = back_d[...]
    gate = mm(n2, wg_ref[...]) + mm(narrow_g, eg_ref[...])
    upward = mm(n2, wu_ref[...]) + mm(narrow_u, eu_ref[...])
    sig = jax.nn.sigmoid(gate)
    act = gate * sig
    hidden = (act * upward).astype(BF)
    hidden_grad = mm_nt(g0, wd_ref[...]) + mm_nt(narrow_b, sd_ref[...])
    gate_grad = (hidden_grad * upward * (sig * (1.0 + gate * (1.0 - sig)))).astype(BF)
    up_grad = (hidden_grad * act).astype(BF)
    acc_out[...] += mm(hidden, wd_ref[...])
    acc_nd[...] += mm(hidden, sd_ref[...])
    acc_ng[...] += mm_nt(gate_grad, wg_ref[...]) + mm_nt(up_grad, wu_ref[...])
    acc_bg[...] += mm_nt(gate_grad, eg_ref[...])
    acc_bu[...] += mm_nt(up_grad, eu_ref[...])
    deg_ref[...] = peg_ref[...] + mm_tn(narrow_g, gate_grad)
    deu_ref[...] = peu_ref[...] + mm_tn(narrow_u, up_grad)
    dsd_ref[...] = psd_ref[...] + mm_tn(narrow_b, hidden)

    @pl.when(chunk == chunks - 1)
    def _():
        out_ref[:, :model] = acc_out[...].astype(BF)
        out_ref[:, model:] = jnp.concatenate([acc_nd[...], acc_nd[...]], axis=1).astype(BF)
        ng_ref[:, :model] = acc_ng[...].astype(BF)
        ng_ref[:, model:] = jnp.concatenate([acc_bg[...], acc_bu[...]], axis=1).astype(BF)


def feed(index, kinds, blocks, n2, g0, sgu, ed, wd, eg, eu, sd, previous, seqs, limit=768):
    tokens, model = n2.shape
    count = len(blocks)
    hidden = wd.shape[0]
    cols = ed.shape[0]
    size = max(c for c in range(128, limit + 1, 128) if hidden % c == 0)
    anywhere = pl.BlockSpec(memory_space=pl.ANY)
    whole = lambda a: pl.BlockSpec(
        a.shape, lambda h, i: (0,) * a.ndim, pipeline_mode=pl.Buffered(1)
    )
    part = lambda a: pl.BlockSpec((a.shape[0], size), lambda h, i: (0, h))
    tall = lambda a: pl.BlockSpec((size, a.shape[1]), lambda h, i: (h, 0))
    fixed = lambda c: pl.BlockSpec((tokens, c), lambda h, i: (0, 0))
    grads = jax.ShapeDtypeStruct((cols, hidden), F32)
    return pl.pallas_call(
        functools.partial(feed_kernel, seqs, tuple(kinds)),
        grid_spec=pltpu.PrefetchScalarGridSpec(
            num_scalar_prefetch=1,
            grid=(hidden // size,),
            in_specs=[anywhere] * count
            + [whole(n2), whole(g0), whole(sgu), whole(ed), tall(wd)]
            + [part(eg), part(eu), tall(sd), part(grads), part(grads), part(grads)],
            out_specs=[fixed(model + 2 * cols), fixed(model + 2 * cols)] + [part(grads)] * 3,
            scratch_shapes=[
                pltpu.VMEM((tokens, model), F32),
                pltpu.VMEM((tokens, model), F32),
                pltpu.VMEM((tokens, cols), F32),
                pltpu.VMEM((tokens, cols), F32),
                pltpu.VMEM((tokens, cols), F32),
                pltpu.VMEM((tokens, cols), BF),
                pltpu.VMEM((tokens, cols), BF),
                pltpu.VMEM((tokens, cols), BF),
                pltpu.VMEM((2, 2, model, size), BF),
                pltpu.SemaphoreType.DMA((2, count)),
            ],
        ),
        out_shape=[
            jax.ShapeDtypeStruct((tokens, model + 2 * cols), BF),
            jax.ShapeDtypeStruct((tokens, model + 2 * cols), BF),
            grads, grads, grads,
        ],
        name="feed",
        cost_estimate=pl.CostEstimate(
            flops=12 * tokens * (model + cols) * hidden,
            bytes_accessed=6 * model * hidden,
            transcendentals=tokens * hidden,
        ),
    )(index, *blocks, n2, g0, sgu, ed, wd, eg, eu, sd, *previous)


def assemble_kernel(count, info, *refs):
    blocks = refs[:count]
    out_ref, held, blank, in_sem, out_sem = refs[count:]
    depth = blocks[0].shape[0]
    rest = out_ref.shape[0] - count * depth
    arrive = []
    leave = []
    for j in range(count):
        arrive.append(pltpu.make_async_copy(blocks[j], held.at[j], in_sem.at[j]))
        at = pl.multiple_of((info[0] ^ j) * depth, depth)
        leave.append(
            pltpu.make_async_copy(held.at[j], out_ref.at[pl.ds(at, depth), :], out_sem.at[j])
        )
    for copy in arrive:
        copy.start()
    if rest:
        blank[...] = jnp.zeros(blank.shape, BF)
        last = pltpu.make_async_copy(blank, out_ref.at[count * depth :, :], out_sem.at[count])
        last.start()
    for one, two in zip(arrive, leave):
        one.wait()
        two.start()
    for copy in leave:
        copy.wait()
    if rest:
        last.wait()


def assemble(index, blocks, rows):
    count = len(blocks)
    depth, lanes = blocks[0].shape
    anywhere = pl.BlockSpec(memory_space=pl.ANY)
    return pl.pallas_call(
        functools.partial(assemble_kernel, count),
        grid_spec=pltpu.PrefetchScalarGridSpec(
            num_scalar_prefetch=1,
            grid=(1,),
            in_specs=[anywhere] * count,
            out_specs=anywhere,
            scratch_shapes=[
                pltpu.VMEM((count, depth, lanes), BF),
                pltpu.VMEM((max(rows - count * depth, 16), lanes), BF),
                pltpu.SemaphoreType.DMA((count,)),
                pltpu.SemaphoreType.DMA((count + 1,)),
            ],
        ),
        out_shape=jax.ShapeDtypeStruct((rows, lanes), BF),
        name="assemble",
        cost_estimate=pl.CostEstimate(
            flops=0, bytes_accessed=4 * rows * lanes, transcendentals=0
        ),
    )(index.reshape(1).astype(jnp.int32), *blocks)


def expand_kernel(rank, hidden, padded, seq_n, early, kinds, both_ref, select_ref, *outs):
    pair = pl.program_id(0)
    select = select_ref[...]
    lanes = -(-hidden // 128) * 128
    width = both_ref.shape[2] - early
    for q in range(2):
        for i, out_ref in enumerate(outs[:3]):
            groups = []
            for f in range(2):
                at = i * padded
                left = lanes
                pieces = []
                while left:
                    z, low = divmod(at, width)
                    take = min(left, width - low)
                    device = pair * 4 * seq_n + (q * 2 + f) * seq_n + z
                    pieces.append(both_ref[device, :rank, early + low : early + low + take])
                    at += take
                    left -= take
                groups.append(jnp.concatenate(pieces, axis=1))
            rows = jnp.concatenate(groups, axis=0)
            if i < 2:
                out_ref[:, q * hidden : (q + 1) * hidden] = mm_tn(select, rows)[:, :hidden]
            else:
                out_ref[q * hidden : (q + 1) * hidden, :] = mm_tn(rows, select)[:hidden]

    @pl.when(pair == 0)
    def _():
        half = both_ref.shape[0] // 2
        for i, (out_ref, shrink) in enumerate(zip(outs[3:], kinds)):
            rows = jnp.concatenate(
                [
                    jnp.concatenate(
                        [both_ref[f * half + 2 * i + w, :rank, :early] for w in range(2)], axis=1
                    )
                    for f in range(2)
                ],
                axis=0,
            )
            out_ref[...] = mm_tn(rows, select) if shrink else mm_tn(select, rows)


def expand_all(both, select, rank, hidden, padded, seq_n, chips, early, kinds):
    cols = select.shape[1]
    model = 2 * early
    wide = lambda n: jax.ShapeDtypeStruct((cols, n), F32)
    tall = lambda n: jax.ShapeDtypeStruct((n, cols), F32)
    fixed = [tall(model) if shrink else wide(model) for shrink in kinds]
    return pl.pallas_call(
        functools.partial(expand_kernel, rank, hidden, padded, seq_n, early, kinds),
        grid=(chips // 2,),
        in_specs=[
            pl.BlockSpec(both.shape, lambda p: (0, 0, 0), pipeline_mode=pl.Buffered(1)),
            pl.BlockSpec(select.shape, lambda p: (0, 0)),
        ],
        out_specs=[
            pl.BlockSpec((cols, 2 * hidden), lambda p: (0, p)),
            pl.BlockSpec((cols, 2 * hidden), lambda p: (0, p)),
            pl.BlockSpec((2 * hidden, cols), lambda p: (p, 0)),
        ]
        + [pl.BlockSpec(one.shape, lambda p: (0, 0)) for one in fixed],
        out_shape=[wide(chips * hidden), wide(chips * hidden), tall(chips * hidden)] + fixed,
        name="expand",
        cost_estimate=pl.CostEstimate(
            flops=6 * cols * chips * hidden * select.shape[0],
            bytes_accessed=12 * cols * chips * hidden,
            transcendentals=0,
        ),
    )(both, select)


def after(value, *needed):
    return lax.optimization_barrier((value, needed))[0]


def body(
    inputs, cotangent, span_order, adapter_ids, first_gain, second_gain,
    query_weight, key_weight, value_weight, output_weight, gate_weight, up_weight, down_weight,
    query_bias, key_bias, value_bias,
    query_reduce_factors, query_lift_factors, key_reduce_factors, key_lift_factors,
    value_reduce_factors, value_lift_factors, output_reduce_factors, output_lift_factors,
    gate_reduce_factors, gate_lift_factors, upper_reduce_factors, upper_lift_factors,
    down_reduce_factors, down_lift_factors,
):
    seq_n = lax.axis_size("seq")
    cp_n = lax.axis_size("cp")
    fsdp_n = lax.axis_size("fsdp")
    plane = fsdp_n * cp_n
    chips = plane // 2
    group = lax.axis_index("fsdp")
    me = group * cp_n + lax.axis_index("cp")
    chip = me // 2
    core = me % 2
    seqs, tok_rows, model = inputs.shape
    tokens = seqs * tok_rows
    cols = query_reduce_factors.shape[1]
    kv_width = key_weight.shape[1]
    length = tok_rows * seq_n * cp_n
    spans = span_order.shape[1]
    span_len = length // spans
    hidden_all = gate_weight.shape[1]
    hq = hidden_all // chips
    hp = -(-hq // 256) * 256
    pad = hp - hq
    rank = seqs * ADAPTER_RANK
    lanes = -(-rank // 64) * 64

    def swap(value, k):
        return lax.ppermute(value, PLANE, [(i, i ^ k) for i in range(plane)])

    def swap_seq(value, k):
        return lax.ppermute(value, "seq", [(i, i ^ k) for i in range(seq_n)])

    first_row = (lax.axis_index("cp") * seq_n + lax.axis_index("seq")) * tok_rows
    own = lax.dynamic_slice_in_dim(span_order, first_row // span_len, 1, 1)[:, 0]
    shift = first_row % span_len
    cp_index = lax.axis_index("cp")
    seq_index = lax.axis_index("seq")
    info = jnp.concatenate(
        [span_order.reshape(-1), own, jnp.stack([shift, cp_index])]
    ).astype(jnp.int32)
    places = own[:, None] * span_len + shift + jnp.arange(tok_rows, dtype=jnp.int32)[None, :]
    cosine, sine_table = rotary_tables(places.reshape(tokens))
    sine_signed = jnp.where(
        jnp.arange(HEAD_DIM, dtype=jnp.int32) < HEAD_DIM // 2, -sine_table, sine_table
    )
    flat_cosine = cosine
    cosine = cosine[:, None, :]
    sine_table = sine_table[:, None, :]
    lane = jnp.arange(lanes, dtype=jnp.int32)

    def chosen(ids):
        column = jnp.repeat(ids, ADAPTER_RANK) * ADAPTER_RANK + lane[:rank] % ADAPTER_RANK
        column = jnp.pad(column, (0, lanes - rank), constant_values=-1)
        return (jnp.arange(cols, dtype=jnp.int32)[:, None] == column[None, :]).astype(BF)

    ids_wide = jnp.broadcast_to(
        jnp.pad(adapter_ids, (0, -seqs % 8)).astype(F32)[:, None], (seqs + -seqs % 8, 128)
    )
    select = [chosen(adapter_ids)]
    for f in range(1, fsdp_n):
        select.append(chosen(swap(ids_wide, f * cp_n)[:seqs, 0].astype(jnp.int32)))
    mixing = token_mask(tokens, lanes, seqs)

    def shrink_of(value, f=0):
        return mm(value, select[f]).astype(BF)

    def expand_of(value, f=0):
        return mm_tn(select[f], value).astype(BF)

    w_kv = lax.all_gather(
        jnp.concatenate([key_weight, value_weight], axis=1), PLANE, axis=0, tiled=True
    )
    rows_q = [query_weight] + [swap(query_weight, 2 * k) for k in range(1, chips)]

    def by_chip(value):
        return jnp.stack(
            [
                jnp.pad(value[:, hq * c : hq * (c + 1)], ((0, 0), (0, pad)))
                for c in range(chips)
            ]
        )

    gate_up = jnp.stack([by_chip(gate_weight), by_chip(up_weight)], axis=1)
    depth = gate_weight.shape[0]
    parts = [lax.dynamic_index_in_dim(gate_up, chip ^ k, 0, keepdims=False) for k in range(chips)]

    low_in = inputs.reshape(tokens, model)
    resid_in = low_in.astype(F32)
    first_scales = first_gain.astype(F32)
    second_scales = second_gain.astype(F32)
    grad_low = cotangent.reshape(tokens, model)
    w_kv, parts, rows_q = lax.optimization_barrier((w_kv, parts, rows_q))
    rows_o = [output_weight] + [swap(after(output_weight, rows_q), 2 * k) for k in range(1, chips)]
    blocks = {}
    g0_pieces = {
        k: swap(after(grad_low, rows_q), 2 * k) for k in range(1, chips) if 2 * k % cp_n == 0
    }
    w_key = w_kv[:, :kv_width]
    w_value = w_kv[:, kv_width:]

    query_shrink, key_shrink, value_shrink, output_shrink = [
        shrink_of(value)
        for value in (
            query_reduce_factors, key_reduce_factors, value_reduce_factors, output_reduce_factors,
        )
    ]
    query_expand, key_expand, value_expand, output_expand = [
        expand_of(value)
        for value in (
            query_lift_factors, key_lift_factors, value_lift_factors, output_lift_factors,
        )
    ]
    w_kv, output_shrink, output_expand, query_shrink, query_expand = lax.optimization_barrier(
        (w_kv, output_shrink, output_expand, query_shrink, query_expand)
    )

    def narrowed(value, shrink):
        return (mm(value, shrink) * mixing).astype(BF)

    normed, key_narrow, value_narrow, pair = keys_values(
        low_in, first_scales[None], w_kv, jnp.concatenate([key_shrink, value_shrink], axis=1),
        key_expand, value_expand,
        jnp.concatenate([key_bias, value_bias]).astype(F32)[None], flat_cosine, sine_signed, seqs,
    )
    pair_all = lax.all_gather(
        pair.reshape(seqs, tok_rows, 2 * kv_width), ("cp", "seq"), axis=1, tiled=True
    )

    def both_cores(rows):
        found = []
        for part in rows:
            found += [part, swap(part, 1)]
        return found

    late_lift = (
        gate_lift_factors, upper_lift_factors, down_reduce_factors, down_lift_factors,
        gate_reduce_factors, upper_reduce_factors,
    )
    gate_shrink, up_shrink = shrink_of(late_lift[4]), shrink_of(late_lift[5])
    down_expand = expand_of(late_lift[3])
    reduce_factors = [
        (
            jnp.concatenate([shrink_of(late_lift[4], f), shrink_of(late_lift[5], f)], axis=1),
            expand_of(late_lift[3], f),
        )
        for f in range(fsdp_n)
    ]
    query_rot, query_narrow, w_query = with_blocks(
        queries_kernel, "queries", seqs, me, after(both_cores(rows_q), pair),
        [
            after(normed, rows_o, g0_pieces, reduce_factors, gate_shrink, up_shrink, down_expand), query_shrink, query_expand, query_bias.astype(F32)[None], flat_cosine,
            sine_signed,
        ],
        [
            jax.ShapeDtypeStruct((tokens, model), BF),
            jax.ShapeDtypeStruct((tokens, lanes), BF),
        ],
    )

    attended, lse = attend(info, query_rot, pair_all, seqs, spans, span_len)
    for k in range(1, chips):
        blocks[k] = swap(after(parts[k], pair_all, query_rot), 2 * k)
    late_down, late_gate, late_up = after(
        (down_reduce_factors, gate_lift_factors, upper_lift_factors), attended, blocks
    )
    shrink_d = jnp.pad(
        lax.dynamic_slice_in_dim(late_down, chip * hq, hq, 0), ((0, pad), (0, 0))
    )
    lift_g = lax.dynamic_index_in_dim(by_chip(late_gate), chip, 0, keepdims=False)
    lift_u = lax.dynamic_index_in_dim(by_chip(late_up), chip, 0, keepdims=False)
    lift_factors = [(expand_of(lift_g, f), expand_of(lift_u, f)) for f in range(fsdp_n)]
    feed_factors = [
        reduce_factors[f] + lift_factors[f] + (shrink_of(shrink_d, f),) for f in range(fsdp_n)
    ]
    output_blocks = both_cores(after(rows_o, query_rot))
    down_rows = [down_weight, swap(after(down_weight, query_rot), 1)]
    w_down = assemble(core, after(down_rows, attended), hp)
    kinds = [(0, None), (1, None)]
    wide = [parts[0], swap(after(parts[0], query_rot), 1)]
    for k in range(1, chips):
        kinds += [(2 * k, None), (2 * k + 1, None)]
        wide += [blocks[k], swap(blocks[k], 1)]
    feed_index = jnp.stack([me, core]).astype(jnp.int32)

    middle, normed_two, output_narrow, w_output = with_blocks(
        outputs_kernel, "outputs", seqs, me, output_blocks,
        [attended, low_in, second_scales[None], output_shrink, output_expand],
        [
            jax.ShapeDtypeStruct((tokens, model), F32),
            jax.ShapeDtypeStruct((tokens, model), BF),
            jax.ShapeDtypeStruct((tokens, lanes), BF),
        ],
    )

    g0_pieces[0] = grad_low
    n2_pieces = [normed_two]
    for k in range(1, chips):
        if k < 3 and k not in g0_pieces:
            g0_pieces[k] = swap(after(grad_low, wide), 2 * k)
        if k < 3:
            n2_pieces.append(swap(after(normed_two, wide), 2 * k))
    if chips > 2:
        n2_pieces[1:3] = lax.optimization_barrier(n2_pieces[1:3])
    zero = jnp.zeros((lanes, hp), F32)
    sums = [(zero, zero, zero)] * fsdp_n
    out_raw = []
    grad_parts = []
    early_first = [0] + sorted(range(1, chips), key=lambda k: (k > 2, -k if k < 3 else k))
    for k in early_first:
        f = 2 * k // cp_n
        sgu, ed, eg, eu, sd = feed_factors[f]
        if len(out_raw) == 2 or (len(out_raw) == 1 and chips == 2):
            middle_row = tokens // 2
            for other in range(3, chips):
                for pieces in (n2_pieces, g0_pieces):
                    first, second = after((pieces[2], pieces[1]), out_raw[0])
                    if other == 3:
                        piece = jnp.concatenate(
                            [swap(first[:middle_row], 2), swap(second[middle_row:], 4)], axis=0
                        )
                    else:
                        piece = swap(after(pieces[0], out_raw[0]), 2 * other)
                    if pieces is n2_pieces:
                        n2_pieces.append(piece)
                    else:
                        g0_pieces[other] = piece
        if out_raw:
            sums[f] = after(sums[f], out_raw[-1])
        out_k, ng_k, *sums[f] = feed(
            feed_index, kinds, wide, n2_pieces[k], g0_pieces[k], sgu, ed, w_down, eg, eu, sd, sums[f], seqs
        )
        out_raw.append(out_k)
        grad_parts.append(ng_k if k == 0 else swap(ng_k, 2 * k))

    grad_most = grad_parts[0].astype(F32)
    for part in grad_parts[1:-1]:
        grad_most = lax.optimization_barrier(grad_most) + part.astype(F32)

    def pack(values, tiles):
        value = jnp.concatenate([value[:rank].astype(BF) for value in values], axis=1)
        return jnp.pad(value, ((0, 0), (0, -value.shape[1] % (128 * tiles))))

    middle_grad, middle_low, gate_back, up_back, output_back, attended_grad = before_attention(
        grad_most, grad_parts[-1], grad_low, middle, second_scales[None],
        gate_shrink, up_shrink, output_shrink, output_expand, w_output, seqs,
    )

    def narrowed_back(grad, expand):
        return (mm_nt(grad, expand) * mixing).astype(BF)

    out_raw = after(out_raw, middle_low)
    out_parts = [swap(part, 2 * k) if k else part for k, part in zip(early_first[:3], out_raw)]
    query_rot_grad, pair_part = attend_back(
        info, query_rot, attended_grad, attended, pair_all, lse, seqs, spans, span_len
    )
    out_parts += [
        swap(after(part, pair_part), 2 * k) for k, part in zip(early_first[3:], out_raw[3:])
    ]
    pair_grad = lax.psum_scatter(
        after(pair_part, out_parts[:3]), ("cp", "seq"), scatter_dimension=1, tiled=True
    ).reshape(tokens, 2 * kv_width)
    out_sum = sum(part.astype(F32) for part in out_parts)

    down_narrow = (out_sum[:, model : model + lanes] * mixing).astype(BF)
    result = middle + (out_sum[:, :model] + mm(down_narrow, down_expand))
    outputs = result.astype(BF).reshape(seqs, tok_rows, model)

    query_rot_grad, sums, middle_late, output_back, gate_back, up_back = after(
        (query_rot_grad, sums, middle_low, output_back, gate_back, up_back), out_parts[:3]
    )
    cosine, sine_table = after((cosine, sine_table), pair_part)
    query_grad = (
        unrotate(
            query_rot_grad.reshape(tokens, -1, HEAD_DIM).astype(F32), cosine, sine_table
        )
        .reshape(tokens, model)
        .astype(BF)
    )
    query_back = narrowed_back(query_grad, query_expand)
    query_in = mm_nt(query_grad, w_query) + mm_nt(query_back, query_shrink)

    def halves(value, index, exchange):
        span = 1
        while value.shape[0] > 1:
            split = value.reshape((value.shape[0] // 2, 2) + value.shape[1:])
            bit = index // span % 2
            keep = lax.dynamic_index_in_dim(split, bit, 1, keepdims=False)
            give = lax.dynamic_index_in_dim(split, 1 - bit, 1, keepdims=False)
            value = (keep.astype(F32) + exchange(give, span).astype(F32)).astype(BF)
            span *= 2
        return value[0]

    stacked = jnp.stack([pack(sums[f], seq_n) for f in range(fsdp_n)])
    feed_wide = stacked.shape[2]

    def groups_of(parity):
        return jnp.stack(
            [
                lax.dynamic_index_in_dim(stacked, (2 * j + parity) ^ group, 0, keepdims=False)
                for j in range(fsdp_n // 2)
            ]
        )

    feed_half = groups_of(core).astype(F32) + swap(groups_of(1 - core), 1).astype(F32)
    feed_half = feed_half.reshape(fsdp_n // 2 * rank, seq_n, feed_wide // seq_n).astype(BF)
    feed_half = feed_half.transpose(1, 0, 2)
    feed_piece = halves(feed_half, seq_index, swap_seq)
    ways = cp_n * seq_n
    early = pack(
        [
            mm_tn(output_back, attended),
            mm_tn(gate_back, normed_two),
            mm_tn(up_back, normed_two),
            mm_tn(output_narrow, middle_late),
            mm_tn(down_narrow, grad_low),
            mm_tn(query_back, normed),
            mm_tn(query_narrow, query_grad),
        ],
        ways,
    )
    early = early.reshape(rank, cp_n, seq_n, -1).transpose(1, 2, 0, 3)
    early = halves(early, cp_index, swap)
    early = halves(early, seq_index, swap_seq)
    early_cols = early.shape[1]
    both = jnp.concatenate([jnp.pad(early, ((0, feed_piece.shape[0] - rank), (0, 0))), feed_piece], axis=1)
    both = lax.all_gather(after(both, pair_grad), EVERY, axis=0, tiled=False)

    key_grad, value_grad, key_back, value_back, late = last_grads(
        cp_index, pair_grad, flat_cosine, sine_signed, key_expand, value_expand, normed,
        key_narrow, value_narrow, seqs, rank, cp_n,
    )
    late_wide = late.shape[3] * cp_n
    total = late[0].astype(F32) + swap(late[1], 1).astype(F32)
    span = 2
    while span < cp_n:
        total = total[0::2] + swap(total[1::2].astype(BF), span).astype(F32)
        span *= 2
    late = total[0].astype(BF)
    total = late.astype(F32)
    for k in range(1, seq_n):
        total = total + swap_seq(late, k).astype(F32)
    late = total.astype(BF)[None]
    for step in [span_k for span_k in (2**i for i in range(1, 30)) if span_k < plane] + [1]:
        late = jnp.concatenate([late, swap(late, step)], axis=0)

    normed_grad = (
        query_in
        + mm_nt(key_grad, w_key)
        + mm_nt(value_grad, w_value)
        + mm_nt(key_back, key_shrink)
        + mm_nt(value_back, value_shrink)
    )
    input_grad = middle_grad + norm_backward(resid_in, first_scales, normed_grad)

    came = [0]
    for step in [span_k for span_k in (2**i for i in range(1, 30)) if span_k < plane] + [1]:
        came = came + [c ^ step for c in came]
    inverse = [came.index(c) for c in range(plane)]
    late = jnp.take(
        late, jnp.asarray(inverse, jnp.int32)[jnp.arange(plane, dtype=jnp.int32) ^ me], axis=0
    )
    late = late.reshape(fsdp_n, cp_n, rank, late_wide // cp_n)
    late = late.transpose(0, 2, 1, 3).reshape(fsdp_n * rank, late_wide)

    order = jnp.arange(fsdp_n, dtype=jnp.int32) ^ group
    select_all = (
        jnp.take(jnp.stack(select), order, axis=0)[:, :, :rank]
        .transpose(0, 2, 1)
        .reshape(fsdp_n * rank, cols)
    )
    shrink_grad = lambda value: mm_tn(value, select_all)
    expand_grad = lambda value: mm_tn(select_all, value)

    late_of = lambda i: late[:, model * i : model * (i + 1)]
    tail_of = lambda i: late[:, model * 2 + kv_width * i : model * 2 + kv_width * (i + 1)]
    order_kinds = (True, True, True, False, False, True, False)
    if fsdp_n == 2 and 2 * hq % 128 == 0 and 2 * early_cols == model:
        expanded = expand_all(
            both, select_all, rank, hq, hp, seq_n, chips, early_cols, order_kinds
        )
    else:
        early_full = both[:, :rank, :early_cols].reshape(fsdp_n, ways, rank, early_cols)
        early_full = early_full.transpose(0, 2, 1, 3).reshape(fsdp_n * rank, ways * early_cols)
        feed_full = both[:, :, early_cols:].reshape(
            fsdp_n, cp_n // 2, 2, seq_n, fsdp_n // 2, rank, feed_wide // seq_n
        ).transpose(4, 2, 5, 0, 1, 3, 6)
        feed_full = feed_full.reshape(fsdp_n * rank, chips, feed_wide)
        expanded = []
        for i, shrink in enumerate((False, False, True) + order_kinds):
            if i < 3:
                rows = feed_full[:, :, i * hp : i * hp + hq].reshape(fsdp_n * rank, hidden_all)
            else:
                rows = early_full[:, model * (i - 3) : model * (i - 2)]
            expanded.append(shrink_grad(rows) if shrink else expand_grad(rows))

    return (
        outputs,
        input_grad.reshape(seqs, tok_rows, model),
        expanded[8],
        expanded[9],
        shrink_grad(late_of(0)),
        expand_grad(tail_of(0)),
        shrink_grad(late_of(1)),
        expand_grad(tail_of(1)),
        expanded[3],
        expanded[6],
        expanded[4],
        expanded[0],
        expanded[5],
        expanded[1],
        expanded[2],
        expanded[7],
    )


def solution(mesh):
    tokens_spec = P("fsdp", ("cp", "seq"), None)
    weight_spec = P(("fsdp", "cp"), None)
    placed = (
        (tokens_spec, tokens_spec, P("fsdp", None), P("fsdp"), P(), P())
        + (weight_spec,) * 7
        + (P(),) * 17
    )
    return jax.shard_map(
        body,
        mesh=mesh,
        in_specs=placed,
        out_specs=(tokens_spec, tokens_spec) + (P(),) * 14,
        check_vma=False,
    )
```

```python
import functools
import math

import jax
import jax.numpy as jnp
from jax import lax
from jax.experimental import pallas as pl
from jax.experimental.pallas import tpu as pltpu
from jax.sharding import PartitionSpec as P

HEAD_DIM = 128
ADAPTER_RANK = 16
epsilon = 1e-06
adapter_scale = 0.5
rotary_base = 1000000.0
masked_score = -1e30
PLANE = ("fsdp", "cp")
EVERY = ("fsdp", "cp", "seq")
BF = jnp.bfloat16
F32 = jnp.float32


def rotary_tables(positions):
    halfway = HEAD_DIM // 2
    frequency = jnp.exp(
        jnp.arange(halfway, dtype=jnp.float32) * (-2.0 * math.log(rotary_base) / HEAD_DIM)
    )
    angles = positions.astype(jnp.float32)[..., None] * frequency
    angles = jnp.concatenate([angles, angles], axis=-1)
    return (jnp.cos(angles), jnp.sin(angles))


def rotate(values, cosine, sine_table):
    halfway = values.shape[-1] // 2
    turned = jnp.concatenate([-values[..., halfway:], values[..., :halfway]], axis=-1)
    return values * cosine + turned * sine_table


def unrotate(gradient, cosine, sine_table):
    halfway = gradient.shape[-1] // 2
    scaled = gradient * sine_table
    turned = jnp.concatenate([scaled[..., halfway:], -scaled[..., :halfway]], axis=-1)
    return gradient * cosine + turned


def mm(left, right):
    return jnp.dot(left, right, preferred_element_type=jnp.float32)


def mm_nt(left, right):
    return lax.dot_general(
        left, right, (((1,), (1,)), ((), ())), preferred_element_type=jnp.float32
    )


def mm_tn(left, right):
    return lax.dot_general(
        left, right, (((0,), (0,)), ((), ())), preferred_element_type=jnp.float32
    )


def norm_forward(values, scales):
    return values * lax.rsqrt(jnp.mean(values * values, axis=-1, keepdims=True) + epsilon) * scales


def norm_backward(values, scales, gradient):
    inverse = lax.rsqrt(jnp.mean(values * values, axis=-1, keepdims=True) + epsilon)
    weighted = gradient * scales
    inner_sum = jnp.mean(weighted * values, axis=-1, keepdims=True)
    return inverse * weighted - values * (inverse * inverse * inverse) * inner_sum


def heads_to_rows(block):
    count = block.shape[1] // HEAD_DIM
    return jnp.concatenate(
        [block[:, HEAD_DIM * j : HEAD_DIM * (j + 1)] for j in range(count)], axis=0
    )


def rows_to_heads(rows, tokens):
    count = rows.shape[0] // tokens
    return jnp.concatenate([rows[tokens * j : tokens * (j + 1)] for j in range(count)], axis=1)


def attend_kernel(spans, span_len, tokens, info, q_ref, k_ref, v_ref, o_ref, lse_ref, m_ref, l_ref, acc_ref):
    seq = pl.program_id(0)
    seqs = pl.num_programs(0)
    own = info[seqs * spans + seq]
    shift = info[seqs * spans + seqs]
    scale = math.log2(math.e) / math.sqrt(HEAD_DIM)
    queries = heads_to_rows(q_ref[...])
    m_ref[...] = jnp.full(m_ref.shape, masked_score, F32)
    l_ref[...] = jnp.zeros(l_ref.shape, F32)
    acc_ref[...] = jnp.zeros(acc_ref.shape, F32)

    def update(j, masked):
        rows = pl.ds(pl.multiple_of(j * span_len, span_len), span_len)
        scores = mm_nt(k_ref[0, rows, :], queries) * scale
        if masked:
            key_at = lax.broadcasted_iota(jnp.int32, scores.shape, 0)
            query_at = shift + lax.rem(lax.broadcasted_iota(jnp.int32, scores.shape, 1), tokens)
            scores = jnp.where(key_at <= query_at, scores, masked_score)
        old = m_ref[...]
        top = jnp.maximum(old, jnp.max(scores, axis=0, keepdims=True))
        expo = jnp.exp2(scores - top)
        alpha = jnp.exp2(old - top)
        l_ref[...] = l_ref[...] * alpha + jnp.sum(expo, axis=0, keepdims=True)
        acc_ref[...] = acc_ref[...] * alpha + mm_tn(v_ref[0, rows, :], expo.astype(BF))
        m_ref[...] = top

    def step(j, carry):
        other = info[seq * spans + j]

        @pl.when(other < own)
        def _():
            update(j, False)

        @pl.when(other == own)
        def _():
            update(j, True)

        return carry

    lax.fori_loop(0, spans, step, 0)
    total = l_ref[...]
    out = jnp.transpose(acc_ref[...] / total)
    o_ref[...] = rows_to_heads(out.astype(BF), tokens)
    lse_ref[0] = jnp.broadcast_to(m_ref[...] + jnp.log2(total), lse_ref.shape[1:])


def attend(info, queries, pairs, seqs, spans, span_len):
    tokens = queries.shape[0] // seqs
    length = pairs.shape[1]
    kv_heads = pairs.shape[2] // (2 * HEAD_DIM)
    width = queries.shape[1] // kv_heads
    rows = tokens * (width // HEAD_DIM)
    grid_spec = pltpu.PrefetchScalarGridSpec(
        num_scalar_prefetch=1,
        grid=(seqs, kv_heads),
        in_specs=[
            pl.BlockSpec((tokens, width), lambda s, h, i: (s, h)),
            pl.BlockSpec((1, length, HEAD_DIM), lambda s, h, i: (s, 0, h)),
            pl.BlockSpec((1, length, HEAD_DIM), lambda s, h, i: (s, 0, kv_heads + h)),
        ],
        out_specs=[
            pl.BlockSpec((tokens, width), lambda s, h, i: (s, h)),
            pl.BlockSpec((1, 8, rows), lambda s, h, i: (s * kv_heads + h, 0, 0)),
        ],
        scratch_shapes=[pltpu.VMEM((1, rows), F32)] * 2 + [pltpu.VMEM((HEAD_DIM, rows), F32)],
    )
    work = seqs * kv_heads * rows * length
    return pl.pallas_call(
        functools.partial(attend_kernel, spans, span_len, tokens),
        grid_spec=grid_spec,
        out_shape=[
            jax.ShapeDtypeStruct(queries.shape, BF),
            jax.ShapeDtypeStruct((seqs * kv_heads, 8, rows), F32),
        ],
        name="attend",
        cost_estimate=pl.CostEstimate(
            flops=4 * work * HEAD_DIM, bytes_accessed=pairs.size * 2, transcendentals=work
        ),
    )(info, queries, pairs, pairs)


def attend_back_kernel(
    spans, span_len, tokens, kv_heads,
    info, q_ref, do_ref, o_ref, k_ref, v_ref, lse_ref, dq_ref, dkv_ref, acc_ref,
):
    seq = pl.program_id(0)
    head = pl.program_id(1)
    seqs = pl.num_programs(0)
    own = info[seqs * spans + seq]
    shift = info[seqs * spans + seqs]
    root = 1.0 / math.sqrt(HEAD_DIM)
    scale = math.log2(math.e) * root
    queries = heads_to_rows(q_ref[...])
    grads = heads_to_rows(do_ref[...])
    results = heads_to_rows(o_ref[...])
    inner = jnp.sum(
        jnp.transpose(grads.astype(F32) * results.astype(F32)), axis=0, keepdims=True
    )
    lse = lse_ref[0, :1, :]
    acc_ref[...] = jnp.zeros(acc_ref.shape, F32)
    key_lane = pl.multiple_of(head * HEAD_DIM, HEAD_DIM)
    val_lane = pl.multiple_of((kv_heads + head) * HEAD_DIM, HEAD_DIM)

    def store(j, key_grad, value_grad):
        rows = pl.ds(pl.multiple_of(j * span_len, span_len), span_len)
        dkv_ref[0, rows, pl.ds(key_lane, HEAD_DIM)] = key_grad
        dkv_ref[0, rows, pl.ds(val_lane, HEAD_DIM)] = value_grad

    def update(j, masked):
        rows = pl.ds(pl.multiple_of(j * span_len, span_len), span_len)
        keys = k_ref[0, rows, :]
        prob = jnp.exp2(mm_nt(keys, queries) * scale - lse)
        if masked:
            key_at = lax.broadcasted_iota(jnp.int32, prob.shape, 0)
            query_at = shift + lax.rem(lax.broadcasted_iota(jnp.int32, prob.shape, 1), tokens)
            prob = jnp.where(key_at <= query_at, prob, 0.0)
        prob_grad = mm_nt(v_ref[0, rows, :], grads)
        score_grad = (prob * (prob_grad - inner)).astype(BF)
        acc_ref[...] += mm_tn(score_grad, keys)
        store(
            j, (mm(score_grad, queries) * root).astype(BF), mm(prob.astype(BF), grads).astype(BF)
        )

    def step(j, carry):
        other = info[seq * spans + j]

        @pl.when(other < own)
        def _():
            update(j, False)

        @pl.when(other == own)
        def _():
            update(j, True)

        @pl.when(other > own)
        def _():
            zero = jnp.zeros((span_len, HEAD_DIM), BF)
            store(j, zero, zero)

        return carry

    lax.fori_loop(0, spans, step, 0)
    dq_ref[...] = rows_to_heads((acc_ref[...] * root).astype(BF), tokens)


def attend_back(info, queries, grads, results, pairs, lse, seqs, spans, span_len):
    tokens = queries.shape[0] // seqs
    length = pairs.shape[1]
    kv_heads = pairs.shape[2] // (2 * HEAD_DIM)
    width = queries.shape[1] // kv_heads
    rows = tokens * (width // HEAD_DIM)
    row = pl.BlockSpec((tokens, width), lambda s, h, i: (s, h))
    block = (1, length, pairs.shape[2])
    grid_spec = pltpu.PrefetchScalarGridSpec(
        num_scalar_prefetch=1,
        grid=(seqs, kv_heads),
        in_specs=[
            row,
            row,
            row,
            pl.BlockSpec((1, length, HEAD_DIM), lambda s, h, i: (s, 0, h)),
            pl.BlockSpec((1, length, HEAD_DIM), lambda s, h, i: (s, 0, kv_heads + h)),
            pl.BlockSpec((1, 8, rows), lambda s, h, i: (s * kv_heads + h, 0, 0)),
        ],
        out_specs=[row, pl.BlockSpec(block, lambda s, h, i: (s, 0, 0))],
        scratch_shapes=[pltpu.VMEM((rows, HEAD_DIM), F32)],
    )
    work = seqs * kv_heads * rows * length
    return pl.pallas_call(
        functools.partial(attend_back_kernel, spans, span_len, tokens, kv_heads),
        grid_spec=grid_spec,
        out_shape=[
            jax.ShapeDtypeStruct(queries.shape, BF),
            jax.ShapeDtypeStruct(pairs.shape, BF),
        ],
        name="attend_back",
        cost_estimate=pl.CostEstimate(
            flops=10 * work * HEAD_DIM, bytes_accessed=pairs.size * 4, transcendentals=work
        ),
    )(info, queries, grads, results, pairs, pairs, lse)


def turned(values, cosine, sine_signed):
    return values * cosine + pltpu.roll(values, HEAD_DIM // 2, axis=1) * sine_signed


def fetch_rows(index, blocks, out_ref, sems):
    depth = blocks[0].shape[0]
    return [
        pltpu.make_async_copy(
            block,
            out_ref.at[pl.ds(pl.multiple_of((index ^ j) * depth, depth), depth), :],
            sems.at[j],
        )
        for j, block in enumerate(blocks)
    ]


def keys_kernel(
    seqs, x_ref, gain_ref, w_ref, shrink_ref, ek_ref, ev_ref, bias_ref, cos_ref, sin_ref,
    normed_ref, nk_ref, nv_ref, pair_ref,
):
    tokens, width = pair_ref.shape
    kv = width // 2
    lanes = ek_ref.shape[0]
    normed = norm_forward(x_ref[...].astype(F32), gain_ref[...]).astype(BF)
    normed_ref[...] = normed
    mix = token_mask(tokens, lanes, seqs)
    narrow = mm(normed, shrink_ref[...])
    narrow_k = (narrow[:, :lanes] * mix).astype(BF)
    narrow_v = (narrow[:, lanes:] * mix).astype(BF)
    nk_ref[...] = narrow_k
    nv_ref[...] = narrow_v
    raw = mm(normed, w_ref[...]) + bias_ref[...]
    keys = raw[:, :kv] + mm(narrow_k, ek_ref[...])
    vals = raw[:, kv:] + mm(narrow_v, ev_ref[...])
    cosine = cos_ref[...]
    sine = sin_ref[...]
    for h in range(kv // HEAD_DIM):
        at = slice(h * HEAD_DIM, (h + 1) * HEAD_DIM)
        pair_ref[:, at] = turned(keys[:, at], cosine, sine).astype(BF)
    pair_ref[:, kv:] = vals.astype(BF)


def keys_values(x, gain, w_kv, shrink, expand_k, expand_v, bias, cosine, sine, seqs):
    tokens, model = x.shape
    lanes = expand_k.shape[0]
    low = lambda n: jax.ShapeDtypeStruct((tokens, n), BF)
    return pl.pallas_call(
        functools.partial(keys_kernel, seqs),
        out_shape=[low(model), low(lanes), low(lanes), low(w_kv.shape[1])],
        name="keys_values",
        cost_estimate=pl.CostEstimate(
            flops=2 * tokens * model * w_kv.shape[1],
            bytes_accessed=8 * tokens * model,
            transcendentals=tokens,
        ),
    )(x, gain, w_kv, shrink, expand_k, expand_v, bias, cosine, sine)


def queries_kernel(
    seqs, count, info, normed_ref, shrink_ref, eq_ref, bias_ref, cos_ref, sin_ref, *refs
):
    blocks = refs[:count]
    query_ref, narrow_ref, w_ref, sems = refs[count:]
    copies = fetch_rows(info[0], blocks, w_ref, sems)
    for copy in copies:
        copy.start()
    tokens, model = query_ref.shape
    lanes = eq_ref.shape[0]
    normed = normed_ref[...]
    narrow = (mm(normed, shrink_ref[...]) * token_mask(tokens, lanes, seqs)).astype(BF)
    narrow_ref[...] = narrow
    for copy in copies:
        copy.wait()
    cosine = cos_ref[...]
    sine = sin_ref[...]
    step = 2 * HEAD_DIM
    for c in range(0, model, step):
        raw = mm(normed, w_ref[:, c : c + step]) + bias_ref[:, c : c + step]
        raw = raw + mm(narrow, eq_ref[:, c : c + step])
        for h in range(0, step, HEAD_DIM):
            query_ref[:, c + h : c + h + HEAD_DIM] = turned(
                raw[:, h : h + HEAD_DIM], cosine, sine
            ).astype(BF)


def outputs_kernel(seqs, count, info, attended_ref, x_ref, gain_ref, shrink_ref, eo_ref, *refs):
    blocks = refs[:count]
    middle_ref, normed_ref, top_ref, bottom_ref, narrow_ref, w_ref, sems = refs[count:]
    copies = fetch_rows(info[0], blocks, w_ref, sems)
    for copy in copies:
        copy.start()
    tokens, model = middle_ref.shape
    lanes = eo_ref.shape[0]
    attended = attended_ref[...]
    narrow = (mm(attended, shrink_ref[...]) * token_mask(tokens, lanes, seqs)).astype(BF)
    narrow_ref[...] = narrow
    for copy in copies:
        copy.wait()
    middle = x_ref[...].astype(F32) + (mm(attended, w_ref[...]) + mm(narrow, eo_ref[...]))
    middle_ref[...] = middle
    normed = norm_forward(middle, gain_ref[...]).astype(BF)
    normed_ref[...] = normed
    top_ref[...] = normed[: tokens // 2]
    bottom_ref[...] = normed[tokens // 2 :]


def before_attention_kernel(
    seqs, most_ref, last_ref, grad_ref, middle_ref, gain_ref, gs_ref, us_ref, os_ref, oe_ref, w_ref,
    mg_ref, low_ref, gb_ref, ub_ref, ob_ref, ag_ref,
):
    tokens, model = mg_ref.shape
    lanes = oe_ref.shape[0]
    mix = token_mask(tokens, lanes, seqs)
    total = most_ref[...] + last_ref[...].astype(F32)
    gate_back = (total[:, model : model + lanes] * mix).astype(BF)
    up_back = (total[:, model + lanes :] * mix).astype(BF)
    gb_ref[...] = gate_back
    ub_ref[...] = up_back
    normed_grad = total[:, :model] + mm_nt(gate_back, gs_ref[...]) + mm_nt(up_back, us_ref[...])
    middle_grad = grad_ref[...].astype(F32) + norm_backward(
        middle_ref[...], gain_ref[...], normed_grad
    )
    mg_ref[...] = middle_grad
    low = middle_grad.astype(BF)
    low_ref[...] = low
    output_back = (mm_nt(low, oe_ref[...]) * mix).astype(BF)
    ob_ref[...] = output_back
    ag_ref[...] = (mm_nt(low, w_ref[...]) + mm_nt(output_back, os_ref[...])).astype(BF)


def before_attention(most, last, grad, middle, gain, gs, us, os, oe, w_output, seqs):
    tokens, model = middle.shape
    lanes = oe.shape[0]
    low = lambda n: jax.ShapeDtypeStruct((tokens, n), BF)
    return pl.pallas_call(
        functools.partial(before_attention_kernel, seqs),
        out_shape=[
            jax.ShapeDtypeStruct((tokens, model), F32),
            low(model), low(lanes), low(lanes), low(lanes), low(model),
        ],
        name="before_attention",
        cost_estimate=pl.CostEstimate(
            flops=2 * tokens * model * model, bytes_accessed=30 * tokens * model, transcendentals=0
        ),
    )(most, last, grad, middle, gain, gs, us, os, oe, w_output)


def last_grads_kernel(
    seqs, rank, info, pair_ref, cos_ref, sin_ref, ke_ref, ve_ref, normed_ref, nk_ref, nv_ref,
    kg_ref, vg_ref, kb_ref, vb_ref, late_ref, rows_ref,
):
    tokens, width = pair_ref.shape
    kv = width // 2
    lanes = ke_ref.shape[0]
    model = normed_ref.shape[1]
    mix = token_mask(tokens, lanes, seqs)
    cosine = cos_ref[...]
    sine = -sin_ref[...]
    for h in range(kv // HEAD_DIM):
        at = slice(h * HEAD_DIM, (h + 1) * HEAD_DIM)
        kg_ref[:, at] = turned(pair_ref[:, at].astype(F32), cosine, sine).astype(BF)
    vg_ref[...] = pair_ref[:, kv:]
    key_grad = kg_ref[...]
    value_grad = vg_ref[...]
    key_back = (mm_nt(key_grad, ke_ref[...]) * mix).astype(BF)
    value_back = (mm_nt(value_grad, ve_ref[...]) * mix).astype(BF)
    kb_ref[...] = key_back
    vb_ref[...] = value_back
    normed = normed_ref[...]
    rows_ref[:, :model] = mm_tn(key_back, normed)[:rank].astype(BF)
    rows_ref[:, model : 2 * model] = mm_tn(value_back, normed)[:rank].astype(BF)
    rows_ref[:, 2 * model : 2 * model + kv] = mm_tn(nk_ref[...], key_grad)[:rank].astype(BF)
    rows_ref[:, 2 * model + kv :] = mm_tn(nv_ref[...], value_grad)[:rank].astype(BF)
    parts = 2 * late_ref.shape[1]
    size = late_ref.shape[3]
    for p in range(parts):
        at = p ^ info[0]
        late_ref[lax.rem(at, 2), at // 2] = rows_ref[:, p * size : (p + 1) * size]


def last_grads(mine, pair_grad, cosine, sine, ke, ve, normed, nk, nv, seqs, rank, parts):
    tokens, width = pair_grad.shape
    lanes = ke.shape[0]
    model = normed.shape[1]
    low = lambda n: jax.ShapeDtypeStruct((tokens, n), BF)
    total = 2 * model + width
    operands = [pair_grad, cosine, sine, ke, ve, normed, nk, nv]
    results = [
        low(width // 2), low(width // 2), low(lanes), low(lanes),
        jax.ShapeDtypeStruct((2, parts // 2, rank, total // parts), BF),
    ]
    return pl.pallas_call(
        functools.partial(last_grads_kernel, seqs, rank),
        grid_spec=pltpu.PrefetchScalarGridSpec(
            num_scalar_prefetch=1,
            grid=(1,),
            in_specs=[pl.BlockSpec(a.shape, lambda g, i, n=a.ndim: (0,) * n) for a in operands],
            out_specs=[
                pl.BlockSpec(r.shape, lambda g, i, n=len(r.shape): (0,) * n) for r in results
            ],
            scratch_shapes=[pltpu.VMEM((rank, total), BF)],
        ),
        out_shape=results,
        name="last_grads",
        cost_estimate=pl.CostEstimate(
            flops=4 * tokens * model * 128, bytes_accessed=6 * tokens * model, transcendentals=0
        ),
    )(mine.reshape(1).astype(jnp.int32), *operands)


def with_blocks(kernel, name, seqs, index, blocks, operands, results):
    count = len(blocks)
    depth, lanes = blocks[0].shape
    inside = pl.BlockSpec(memory_space=pltpu.VMEM)
    results = list(results) + [jax.ShapeDtypeStruct((count * depth, lanes), BF)]
    return pl.pallas_call(
        functools.partial(kernel, seqs, count),
        grid_spec=pltpu.PrefetchScalarGridSpec(
            num_scalar_prefetch=1,
            grid=(1,),
            in_specs=[pl.BlockSpec(a.shape, lambda g, i, n=a.ndim: (0,) * n) for a in operands]
            + [pl.BlockSpec(memory_space=pl.ANY)] * count,
            out_specs=[pl.BlockSpec(r.shape, lambda g, i: (0, 0)) for r in results],
            scratch_shapes=[pltpu.SemaphoreType.DMA((count,))],
        ),
        out_shape=results,
        name=name,
        cost_estimate=pl.CostEstimate(
            flops=2 * operands[0].shape[0] * count * depth * lanes,
            bytes_accessed=4 * count * depth * lanes,
            transcendentals=0,
        ),
    )(index.reshape(1).astype(jnp.int32), *operands, *blocks)


def token_mask(tokens, lanes, seqs):
    row = lax.broadcasted_iota(jnp.int32, (tokens, lanes), 0) // (tokens // seqs)
    lane = lax.broadcasted_iota(jnp.int32, (tokens, lanes), 1) // ADAPTER_RANK
    return jnp.where(row == lane, adapter_scale, 0.0).astype(F32)


def feed_kernel(seqs, kinds, info, *refs):
    count = len(kinds)
    blocks = refs[:count]
    top_ref, bottom_ref, grad_top_ref, grad_bottom_ref = refs[count : count + 4]
    count += 4
    sgu_ref, ed_ref, wd_ref, eg_ref, eu_ref, sd_ref = refs[count : count + 6]
    peg_ref, peu_ref, psd_ref = refs[count + 6 : count + 9]
    out_ref, ng_ref, deg_ref, deu_ref, dsd_ref = refs[count + 9 : count + 14]
    acc_out, acc_ng, acc_nd, acc_bg, acc_bu, nar_g, nar_u, back_d, held, sems = refs[count + 14 :]
    chunk = pl.program_id(0)
    chunks = pl.num_programs(0)
    depth = blocks[0].shape[-2]
    size = wd_ref.shape[0]

    def copies(at, slot):
        found = []
        for n, (j, which) in enumerate(kinds):
            rows = pl.ds(pl.multiple_of((info[0] ^ j) * depth, depth), depth)
            lanes = pl.ds(pl.multiple_of(at * size, 128), size)
            if which is None:
                source, target = blocks[n].at[:, :, lanes], held.at[slot, :, rows, :]
            else:
                source, target = blocks[n].at[:, lanes], held.at[slot, info[1] ^ which, rows, :]
            found.append(pltpu.make_async_copy(source, target, sems.at[slot, n]))
        return found

    slot = lax.rem(chunk, 2)

    @pl.when(chunk == 0)
    def _():
        for copy in copies(chunk, slot):
            copy.start()

    @pl.when(chunk + 1 < chunks)
    def _():
        for copy in copies(chunk + 1, 1 - slot):
            copy.start()

    tokens = out_ref.shape[0]
    model = top_ref.shape[1]
    cols = sd_ref.shape[1]
    n2 = jnp.concatenate([top_ref[...], bottom_ref[...]], axis=0)
    g0 = jnp.concatenate([grad_top_ref[...], grad_bottom_ref[...]], axis=0)
    wg_ref = held.at[slot, 0]
    wu_ref = held.at[slot, 1]

    @pl.when(chunk == 0)
    def _():
        mix = token_mask(tokens, cols, seqs)
        narrow = mm(n2, sgu_ref[...])
        nar_g[...] = (narrow[:, :cols] * mix).astype(BF)
        nar_u[...] = (narrow[:, cols:] * mix).astype(BF)
        back_d[...] = (mm_nt(g0, ed_ref[...]) * mix).astype(BF)
        for acc in (acc_out, acc_ng, acc_nd, acc_bg, acc_bu):
            acc[...] = jnp.zeros(acc.shape, F32)

    for copy in copies(chunk, slot):
        copy.wait()
    narrow_g = nar_g[...]
    narrow_u = nar_u[...]
    narrow_b = back_d[...]
    gate = mm(n2, wg_ref[...]) + mm(narrow_g, eg_ref[...])
    upward = mm(n2, wu_ref[...]) + mm(narrow_u, eu_ref[...])
    sig = jax.nn.sigmoid(gate)
    act = gate * sig
    hidden = (act * upward).astype(BF)
    hidden_grad = mm_nt(g0, wd_ref[...]) + mm_nt(narrow_b, sd_ref[...])
    gate_grad = (hidden_grad * upward * (sig * (1.0 + gate * (1.0 - sig)))).astype(BF)
    up_grad = (hidden_grad * act).astype(BF)
    acc_out[...] += mm(hidden, wd_ref[...])
    acc_nd[...] += mm(hidden, sd_ref[...])
    acc_ng[...] += mm_nt(gate_grad, wg_ref[...]) + mm_nt(up_grad, wu_ref[...])
    acc_bg[...] += mm_nt(gate_grad, eg_ref[...])
    acc_bu[...] += mm_nt(up_grad, eu_ref[...])
    deg_ref[...] = peg_ref[...] + mm_tn(narrow_g, gate_grad)
    deu_ref[...] = peu_ref[...] + mm_tn(narrow_u, up_grad)
    dsd_ref[...] = psd_ref[...] + mm_tn(narrow_b, hidden)

    @pl.when(chunk == chunks - 1)
    def _():
        out_ref[:, :model] = acc_out[...].astype(BF)
        out_ref[:, model:] = jnp.concatenate([acc_nd[...], acc_nd[...]], axis=1).astype(BF)
        ng_ref[:, :model] = acc_ng[...].astype(BF)
        ng_ref[:, model:] = jnp.concatenate([acc_bg[...], acc_bu[...]], axis=1).astype(BF)


def feed(index, kinds, blocks, n2, g0, sgu, ed, wd, eg, eu, sd, previous, seqs, limit=768):
    tokens, model = 2 * n2[0].shape[0], n2[0].shape[1]
    count = len(blocks)
    hidden = wd.shape[0]
    cols = ed.shape[0]
    size = max(c for c in range(128, limit + 1, 128) if hidden % c == 0)
    anywhere = pl.BlockSpec(memory_space=pl.ANY)
    whole = lambda a: pl.BlockSpec(
        a.shape, lambda h, i: (0,) * a.ndim, pipeline_mode=pl.Buffered(1)
    )
    part = lambda a: pl.BlockSpec((a.shape[0], size), lambda h, i: (0, h))
    tall = lambda a: pl.BlockSpec((size, a.shape[1]), lambda h, i: (h, 0))
    fixed = lambda c: pl.BlockSpec((tokens, c), lambda h, i: (0, 0))
    grads = jax.ShapeDtypeStruct((cols, hidden), F32)
    return pl.pallas_call(
        functools.partial(feed_kernel, seqs, tuple(kinds)),
        grid_spec=pltpu.PrefetchScalarGridSpec(
            num_scalar_prefetch=1,
            grid=(hidden // size,),
            in_specs=[anywhere] * count
            + [whole(n2[0]), whole(n2[1]), whole(g0[0]), whole(g0[1]), whole(sgu), whole(ed), tall(wd)]
            + [part(eg), part(eu), tall(sd), part(grads), part(grads), part(grads)],
            out_specs=[fixed(model + 2 * cols), fixed(model + 2 * cols)] + [part(grads)] * 3,
            scratch_shapes=[
                pltpu.VMEM((tokens, model), F32),
                pltpu.VMEM((tokens, model), F32),
                pltpu.VMEM((tokens, cols), F32),
                pltpu.VMEM((tokens, cols), F32),
                pltpu.VMEM((tokens, cols), F32),
                pltpu.VMEM((tokens, cols), BF),
                pltpu.VMEM((tokens, cols), BF),
                pltpu.VMEM((tokens, cols), BF),
                pltpu.VMEM((2, 2, model, size), BF),
                pltpu.SemaphoreType.DMA((2, count)),
            ],
        ),
        out_shape=[
            jax.ShapeDtypeStruct((tokens, model + 2 * cols), BF),
            jax.ShapeDtypeStruct((tokens, model + 2 * cols), BF),
            grads, grads, grads,
        ],
        name="feed",
        cost_estimate=pl.CostEstimate(
            flops=12 * tokens * (model + cols) * hidden,
            bytes_accessed=6 * model * hidden,
            transcendentals=tokens * hidden,
        ),
    )(index, *blocks, *n2, *g0, sgu, ed, wd, eg, eu, sd, *previous)


def assemble_kernel(count, info, *refs):
    blocks = refs[:count]
    out_ref, held, blank, in_sem, out_sem = refs[count:]
    depth = blocks[0].shape[0]
    rest = out_ref.shape[0] - count * depth
    arrive = []
    leave = []
    for j in range(count):
        arrive.append(pltpu.make_async_copy(blocks[j], held.at[j], in_sem.at[j]))
        at = pl.multiple_of((info[0] ^ j) * depth, depth)
        leave.append(
            pltpu.make_async_copy(held.at[j], out_ref.at[pl.ds(at, depth), :], out_sem.at[j])
        )
    for copy in arrive:
        copy.start()
    if rest:
        blank[...] = jnp.zeros(blank.shape, BF)
        last = pltpu.make_async_copy(blank, out_ref.at[count * depth :, :], out_sem.at[count])
        last.start()
    for one, two in zip(arrive, leave):
        one.wait()
        two.start()
    for copy in leave:
        copy.wait()
    if rest:
        last.wait()


def assemble(index, blocks, rows):
    count = len(blocks)
    depth, lanes = blocks[0].shape
    anywhere = pl.BlockSpec(memory_space=pl.ANY)
    return pl.pallas_call(
        functools.partial(assemble_kernel, count),
        grid_spec=pltpu.PrefetchScalarGridSpec(
            num_scalar_prefetch=1,
            grid=(1,),
            in_specs=[anywhere] * count,
            out_specs=anywhere,
            scratch_shapes=[
                pltpu.VMEM((count, depth, lanes), BF),
                pltpu.VMEM((max(rows - count * depth, 16), lanes), BF),
                pltpu.SemaphoreType.DMA((count,)),
                pltpu.SemaphoreType.DMA((count + 1,)),
            ],
        ),
        out_shape=jax.ShapeDtypeStruct((rows, lanes), BF),
        name="assemble",
        cost_estimate=pl.CostEstimate(
            flops=0, bytes_accessed=4 * rows * lanes, transcendentals=0
        ),
    )(index.reshape(1).astype(jnp.int32), *blocks)


def expand_kernel(rank, hidden, padded, seq_n, early, kinds, both_ref, select_ref, *outs):
    pair = pl.program_id(0)
    select = select_ref[...]
    lanes = -(-hidden // 128) * 128
    width = both_ref.shape[2] - early
    for q in range(2):
        for i, out_ref in enumerate(outs[:3]):
            groups = []
            for f in range(2):
                at = i * padded
                left = lanes
                pieces = []
                while left:
                    z, low = divmod(at, width)
                    take = min(left, width - low)
                    device = pair * 4 * seq_n + (q * 2 + f) * seq_n + z
                    pieces.append(both_ref[device, :rank, early + low : early + low + take])
                    at += take
                    left -= take
                groups.append(jnp.concatenate(pieces, axis=1))
            rows = jnp.concatenate(groups, axis=0)
            if i < 2:
                out_ref[:, q * hidden : (q + 1) * hidden] = mm_tn(select, rows)[:, :hidden]
            else:
                out_ref[q * hidden : (q + 1) * hidden, :] = mm_tn(rows, select)[:hidden]

    @pl.when(pair == 0)
    def _():
        half = both_ref.shape[0] // 2
        for i, (out_ref, shrink) in enumerate(zip(outs[3:], kinds)):
            rows = jnp.concatenate(
                [
                    jnp.concatenate(
                        [both_ref[f * half + 2 * i + w, :rank, :early] for w in range(2)], axis=1
                    )
                    for f in range(2)
                ],
                axis=0,
            )
            out_ref[...] = mm_tn(rows, select) if shrink else mm_tn(select, rows)


def expand_all(both, select, rank, hidden, padded, seq_n, chips, early, kinds):
    cols = select.shape[1]
    model = 2 * early
    wide = lambda n: jax.ShapeDtypeStruct((cols, n), F32)
    tall = lambda n: jax.ShapeDtypeStruct((n, cols), F32)
    fixed = [tall(model) if shrink else wide(model) for shrink in kinds]
    return pl.pallas_call(
        functools.partial(expand_kernel, rank, hidden, padded, seq_n, early, kinds),
        grid=(chips // 2,),
        in_specs=[
            pl.BlockSpec(both.shape, lambda p: (0, 0, 0), pipeline_mode=pl.Buffered(1)),
            pl.BlockSpec(select.shape, lambda p: (0, 0)),
        ],
        out_specs=[
            pl.BlockSpec((cols, 2 * hidden), lambda p: (0, p)),
            pl.BlockSpec((cols, 2 * hidden), lambda p: (0, p)),
            pl.BlockSpec((2 * hidden, cols), lambda p: (p, 0)),
        ]
        + [pl.BlockSpec(one.shape, lambda p: (0, 0)) for one in fixed],
        out_shape=[wide(chips * hidden), wide(chips * hidden), tall(chips * hidden)] + fixed,
        name="expand",
        cost_estimate=pl.CostEstimate(
            flops=6 * cols * chips * hidden * select.shape[0],
            bytes_accessed=12 * cols * chips * hidden,
            transcendentals=0,
        ),
    )(both, select)


def after(value, *needed):
    return lax.optimization_barrier((value, needed))[0]


def body(
    inputs, cotangent, span_order, adapter_ids, first_gain, second_gain,
    query_weight, key_weight, value_weight, output_weight, gate_weight, up_weight, down_weight,
    query_bias, key_bias, value_bias,
    query_reduce_factors, query_lift_factors, key_reduce_factors, key_lift_factors,
    value_reduce_factors, value_lift_factors, output_reduce_factors, output_lift_factors,
    gate_reduce_factors, gate_lift_factors, upper_reduce_factors, upper_lift_factors,
    down_reduce_factors, down_lift_factors,
):
    seq_n = lax.axis_size("seq")
    cp_n = lax.axis_size("cp")
    fsdp_n = lax.axis_size("fsdp")
    plane = fsdp_n * cp_n
    chips = plane // 2
    group = lax.axis_index("fsdp")
    me = group * cp_n + lax.axis_index("cp")
    chip = me // 2
    core = me % 2
    seqs, tok_rows, model = inputs.shape
    tokens = seqs * tok_rows
    cols = query_reduce_factors.shape[1]
    kv_width = key_weight.shape[1]
    length = tok_rows * seq_n * cp_n
    spans = span_order.shape[1]
    span_len = length // spans
    hidden_all = gate_weight.shape[1]
    hq = hidden_all // chips
    hp = -(-hq // 256) * 256
    pad = hp - hq
    rank = seqs * ADAPTER_RANK
    lanes = -(-rank // 64) * 64

    def swap(value, k):
        return lax.ppermute(value, PLANE, [(i, i ^ k) for i in range(plane)])

    def swap_seq(value, k):
        return lax.ppermute(value, "seq", [(i, i ^ k) for i in range(seq_n)])

    first_row = (lax.axis_index("cp") * seq_n + lax.axis_index("seq")) * tok_rows
    own = lax.dynamic_slice_in_dim(span_order, first_row // span_len, 1, 1)[:, 0]
    shift = first_row % span_len
    cp_index = lax.axis_index("cp")
    seq_index = lax.axis_index("seq")
    info = jnp.concatenate(
        [span_order.reshape(-1), own, jnp.stack([shift, cp_index])]
    ).astype(jnp.int32)
    places = own[:, None] * span_len + shift + jnp.arange(tok_rows, dtype=jnp.int32)[None, :]
    cosine, sine_table = rotary_tables(places.reshape(tokens))
    sine_signed = jnp.where(
        jnp.arange(HEAD_DIM, dtype=jnp.int32) < HEAD_DIM // 2, -sine_table, sine_table
    )
    flat_cosine = cosine
    cosine = cosine[:, None, :]
    sine_table = sine_table[:, None, :]
    lane = jnp.arange(lanes, dtype=jnp.int32)

    def chosen(ids):
        column = jnp.repeat(ids, ADAPTER_RANK) * ADAPTER_RANK + lane[:rank] % ADAPTER_RANK
        column = jnp.pad(column, (0, lanes - rank), constant_values=-1)
        return (jnp.arange(cols, dtype=jnp.int32)[:, None] == column[None, :]).astype(BF)

    ids_wide = jnp.broadcast_to(
        jnp.pad(adapter_ids, (0, -seqs % 8)).astype(F32)[:, None], (seqs + -seqs % 8, 128)
    )
    select = [chosen(adapter_ids)]
    for f in range(1, fsdp_n):
        select.append(chosen(swap(ids_wide, f * cp_n)[:seqs, 0].astype(jnp.int32)))
    mixing = token_mask(tokens, lanes, seqs)

    def shrink_of(value, f=0):
        return mm(value, select[f]).astype(BF)

    def expand_of(value, f=0):
        return mm_tn(select[f], value).astype(BF)

    w_kv = lax.all_gather(
        jnp.concatenate([key_weight, value_weight], axis=1), PLANE, axis=0, tiled=True
    )
    rows_q = [query_weight] + [swap(query_weight, 2 * k) for k in range(1, chips)]

    def by_chip(value):
        return jnp.stack(
            [
                jnp.pad(value[:, hq * c : hq * (c + 1)], ((0, 0), (0, pad)))
                for c in range(chips)
            ]
        )

    gate_up = jnp.stack([by_chip(gate_weight), by_chip(up_weight)], axis=1)
    depth = gate_weight.shape[0]
    parts = [lax.dynamic_index_in_dim(gate_up, chip ^ k, 0, keepdims=False) for k in range(chips)]

    low_in = inputs.reshape(tokens, model)
    resid_in = low_in.astype(F32)
    first_scales = first_gain.astype(F32)
    second_scales = second_gain.astype(F32)
    grad_low = cotangent.reshape(tokens, model)
    w_kv, parts, rows_q = lax.optimization_barrier((w_kv, parts, rows_q))
    rows_o = [output_weight] + [swap(after(output_weight, rows_q), 2 * k) for k in range(1, chips)]
    blocks = {}
    w_key = w_kv[:, :kv_width]
    w_value = w_kv[:, kv_width:]

    query_shrink, key_shrink, value_shrink, output_shrink = [
        shrink_of(value)
        for value in (
            query_reduce_factors, key_reduce_factors, value_reduce_factors, output_reduce_factors,
        )
    ]
    query_expand, key_expand, value_expand, output_expand = [
        expand_of(value)
        for value in (
            query_lift_factors, key_lift_factors, value_lift_factors, output_lift_factors,
        )
    ]
    grad_halves = (grad_low[: tokens // 2], grad_low[tokens // 2 :])
    w_kv, output_shrink, output_expand, query_shrink, query_expand, grad_halves = (
        lax.optimization_barrier(
            (w_kv, output_shrink, output_expand, query_shrink, query_expand, grad_halves)
        )
    )

    def swap_both(pair, k):
        return tuple(swap(half, k) for half in pair)

    g0_pieces = {
        k: swap_both(after(grad_halves, rows_q), 2 * k) for k in range(1, chips) if 2 * k % cp_n == 0
    }

    def narrowed(value, shrink):
        return (mm(value, shrink) * mixing).astype(BF)

    normed, key_narrow, value_narrow, pair = keys_values(
        low_in, first_scales[None], w_kv, jnp.concatenate([key_shrink, value_shrink], axis=1),
        key_expand, value_expand,
        jnp.concatenate([key_bias, value_bias]).astype(F32)[None], flat_cosine, sine_signed, seqs,
    )
    pair_all = lax.all_gather(
        pair.reshape(seqs, tok_rows, 2 * kv_width), ("cp", "seq"), axis=1, tiled=True
    )

    def both_cores(rows):
        found = []
        for part in rows:
            found += [part, swap(part, 1)]
        return found

    late_lift = (
        gate_lift_factors, upper_lift_factors, down_reduce_factors, down_lift_factors,
        gate_reduce_factors, upper_reduce_factors,
    )
    gate_shrink, up_shrink = shrink_of(late_lift[4]), shrink_of(late_lift[5])
    down_expand = expand_of(late_lift[3])
    reduce_factors = [
        (
            jnp.concatenate([shrink_of(late_lift[4], f), shrink_of(late_lift[5], f)], axis=1),
            expand_of(late_lift[3], f),
        )
        for f in range(fsdp_n)
    ]
    late_down, late_gate, late_up = down_reduce_factors, gate_lift_factors, upper_lift_factors
    shrink_d = jnp.pad(
        lax.dynamic_slice_in_dim(late_down, chip * hq, hq, 0), ((0, pad), (0, 0))
    )
    lift_g = lax.dynamic_index_in_dim(by_chip(late_gate), chip, 0, keepdims=False)
    lift_u = lax.dynamic_index_in_dim(by_chip(late_up), chip, 0, keepdims=False)
    lift_factors = [(expand_of(lift_g, f), expand_of(lift_u, f)) for f in range(fsdp_n)]
    feed_factors = [
        reduce_factors[f] + lift_factors[f] + (shrink_of(shrink_d, f),) for f in range(fsdp_n)
    ]
    query_rot, query_narrow, w_query = with_blocks(
        queries_kernel, "queries", seqs, me, after(both_cores(rows_q), pair),
        [
            after(normed, rows_o, g0_pieces, feed_factors, gate_shrink, up_shrink, down_expand), query_shrink, query_expand, query_bias.astype(F32)[None], flat_cosine,
            sine_signed,
        ],
        [
            jax.ShapeDtypeStruct((tokens, model), BF),
            jax.ShapeDtypeStruct((tokens, lanes), BF),
        ],
    )

    down_rows = [down_weight, swap(after(down_weight, query_rot), 1)]
    w_down = assemble(core, after(down_rows, query_rot), hp)
    attended, lse = attend(info, after(query_rot, w_down), pair_all, seqs, spans, span_len)
    for k in range(1, chips):
        blocks[k] = swap(after(parts[k], pair_all, query_rot), 2 * k)
    output_blocks = both_cores(after(rows_o, query_rot))
    middle, normed_two, normed_top, normed_bottom, output_narrow, w_output = with_blocks(
        outputs_kernel, "outputs", seqs, me, output_blocks,
        [attended, low_in, second_scales[None], output_shrink, output_expand],
        [
            jax.ShapeDtypeStruct((tokens, model), F32),
            jax.ShapeDtypeStruct((tokens, model), BF),
            jax.ShapeDtypeStruct((tokens // 2, model), BF),
            jax.ShapeDtypeStruct((tokens // 2, model), BF),
            jax.ShapeDtypeStruct((tokens, lanes), BF),
        ],
    )

    kinds = [(0, None), (1, None)]
    wide = [parts[0], swap(after(parts[0], query_rot), 1)]
    for k in range(1, chips):
        kinds += [(2 * k, None), (2 * k + 1, None)]
        wide += [blocks[k], swap(after(blocks[k], middle), 1)]
    feed_index = jnp.stack([me, core]).astype(jnp.int32)

    g0_pieces[0] = grad_halves
    normed_halves = (normed_top, normed_bottom)
    n2_pieces = [normed_halves]
    for k in range(1, chips):
        if k < 3:
            n2_pieces.append(swap_both(after(normed_halves, wide), 2 * k))
    if chips > 2:
        n2_pieces[1:3] = lax.optimization_barrier(n2_pieces[1:3])
    zero = jnp.zeros((lanes, hp), F32)
    sums = [(zero, zero, zero)] * fsdp_n
    out_raw = []
    grad_parts = []
    early_first = [0] + sorted(range(1, chips), key=lambda k: (k > 2, -k if k < 3 else k))
    for k in early_first:
        f = 2 * k // cp_n
        sgu, ed, eg, eu, sd = feed_factors[f]
        if len(out_raw) == 1:
            for other in range(1, min(chips, 3)):
                if other not in g0_pieces:
                    g0_pieces[other] = swap_both(after(grad_halves, out_raw[0]), 2 * other)
        if len(out_raw) == 2:
            for other in range(3, chips):
                for pieces in (n2_pieces, g0_pieces):
                    first, second, own_pair = after((pieces[2], pieces[1], pieces[0]), out_raw[-1])
                    if other == 3:
                        piece = (swap(first[0], 2), swap(second[1], 4))
                    else:
                        piece = swap_both(own_pair, 2 * other)
                    if pieces is n2_pieces:
                        n2_pieces.append(piece)
                    else:
                        g0_pieces[other] = piece
        if out_raw:
            sums[f] = after(sums[f], out_raw[-1])
        out_k, ng_k, *sums[f] = feed(
            feed_index, kinds, wide, n2_pieces[k], g0_pieces[k], sgu, ed, w_down, eg, eu, sd, sums[f], seqs
        )
        out_raw.append(out_k)
        grad_parts.append(ng_k if k == 0 else swap(ng_k, 2 * k))

    grad_most = grad_parts[0].astype(F32)
    for part in grad_parts[1:-1]:
        grad_most = lax.optimization_barrier(grad_most) + part.astype(F32)

    def pack(values, tiles):
        value = jnp.concatenate([value[:rank].astype(BF) for value in values], axis=1)
        return jnp.pad(value, ((0, 0), (0, -value.shape[1] % (128 * tiles))))

    middle_grad, middle_low, gate_back, up_back, output_back, attended_grad = before_attention(
        grad_most, grad_parts[-1], grad_low, middle, second_scales[None],
        gate_shrink, up_shrink, output_shrink, output_expand, w_output, seqs,
    )

    def narrowed_back(grad, expand):
        return (mm_nt(grad, expand) * mixing).astype(BF)

    out_raw = after(out_raw, middle_low)
    out_parts = [swap(part, 2 * k) if k else part for k, part in zip(early_first[:3], out_raw)]
    query_rot_grad, pair_part = attend_back(
        info, query_rot, attended_grad, attended, pair_all, lse, seqs, spans, span_len
    )
    out_parts += [
        swap(after(part, pair_part), 2 * k) for k, part in zip(early_first[3:], out_raw[3:])
    ]
    pair_grad = lax.psum_scatter(
        after(pair_part, out_parts[:3]), ("cp", "seq"), scatter_dimension=1, tiled=True
    ).reshape(tokens, 2 * kv_width)
    out_sum = sum(part.astype(F32) for part in out_parts)

    down_narrow = (out_sum[:, model : model + lanes] * mixing).astype(BF)
    result = middle + (out_sum[:, :model] + mm(down_narrow, down_expand))
    outputs = result.astype(BF).reshape(seqs, tok_rows, model)

    query_rot_grad, sums, middle_late, output_back, gate_back, up_back = after(
        (query_rot_grad, sums, middle_low, output_back, gate_back, up_back), out_parts[:3]
    )
    cosine, sine_table = after((cosine, sine_table), pair_part)
    query_grad = (
        unrotate(
            query_rot_grad.reshape(tokens, -1, HEAD_DIM).astype(F32), cosine, sine_table
        )
        .reshape(tokens, model)
        .astype(BF)
    )
    query_back = narrowed_back(query_grad, query_expand)
    query_in = mm_nt(query_grad, w_query) + mm_nt(query_back, query_shrink)

    def halves(value, index, exchange):
        span = 1
        while value.shape[0] > 1:
            split = value.reshape((value.shape[0] // 2, 2) + value.shape[1:])
            bit = index // span % 2
            keep = lax.dynamic_index_in_dim(split, bit, 1, keepdims=False)
            give = lax.dynamic_index_in_dim(split, 1 - bit, 1, keepdims=False)
            value = (keep.astype(F32) + exchange(give, span).astype(F32)).astype(BF)
            span *= 2
        return value[0]

    stacked = jnp.stack([pack(sums[f], seq_n) for f in range(fsdp_n)])
    feed_wide = stacked.shape[2]

    def groups_of(parity):
        return jnp.stack(
            [
                lax.dynamic_index_in_dim(stacked, (2 * j + parity) ^ group, 0, keepdims=False)
                for j in range(fsdp_n // 2)
            ]
        )

    feed_half = groups_of(core).astype(F32) + swap(groups_of(1 - core), 1).astype(F32)
    feed_half = feed_half.reshape(fsdp_n // 2 * rank, seq_n, feed_wide // seq_n).astype(BF)
    feed_half = feed_half.transpose(1, 0, 2)
    feed_piece = halves(feed_half, seq_index, swap_seq)
    ways = cp_n * seq_n
    early = pack(
        [
            mm_tn(output_back, attended),
            mm_tn(gate_back, normed_two),
            mm_tn(up_back, normed_two),
            mm_tn(output_narrow, middle_late),
            mm_tn(down_narrow, grad_low),
            mm_tn(query_back, normed),
            mm_tn(query_narrow, query_grad),
        ],
        ways,
    )
    early = early.reshape(rank, cp_n, seq_n, -1).transpose(1, 2, 0, 3)
    early = halves(early, cp_index, swap)
    early = halves(early, seq_index, swap_seq)
    early_cols = early.shape[1]
    both = jnp.concatenate([jnp.pad(early, ((0, feed_piece.shape[0] - rank), (0, 0))), feed_piece], axis=1)
    both = lax.all_gather(after(both, pair_grad), EVERY, axis=0, tiled=False)

    key_grad, value_grad, key_back, value_back, late = last_grads(
        cp_index, pair_grad, flat_cosine, sine_signed, key_expand, value_expand, normed,
        key_narrow, value_narrow, seqs, rank, cp_n,
    )
    late_wide = late.shape[3] * cp_n
    total = late[0].astype(F32) + swap(late[1], 1).astype(F32)
    span = 2
    while span < cp_n:
        total = total[0::2] + swap(total[1::2].astype(BF), span).astype(F32)
        span *= 2
    late = total[0].astype(BF)
    total = late.astype(F32)
    for k in range(1, seq_n):
        total = total + swap_seq(late, k).astype(F32)
    late = total.astype(BF)[None]
    for step in [span_k for span_k in (2**i for i in range(1, 30)) if span_k < plane] + [1]:
        late = jnp.concatenate([late, swap(late, step)], axis=0)

    normed_grad = (
        query_in
        + mm_nt(key_grad, w_key)
        + mm_nt(value_grad, w_value)
        + mm_nt(key_back, key_shrink)
        + mm_nt(value_back, value_shrink)
    )
    input_grad = middle_grad + norm_backward(resid_in, first_scales, normed_grad)

    came = [0]
    for step in [span_k for span_k in (2**i for i in range(1, 30)) if span_k < plane] + [1]:
        came = came + [c ^ step for c in came]
    inverse = [came.index(c) for c in range(plane)]
    late = jnp.take(
        late, jnp.asarray(inverse, jnp.int32)[jnp.arange(plane, dtype=jnp.int32) ^ me], axis=0
    )
    late = late.reshape(fsdp_n, cp_n, rank, late_wide // cp_n)
    late = late.transpose(0, 2, 1, 3).reshape(fsdp_n * rank, late_wide)

    order = jnp.arange(fsdp_n, dtype=jnp.int32) ^ group
    select_all = (
        jnp.take(jnp.stack(select), order, axis=0)[:, :, :rank]
        .transpose(0, 2, 1)
        .reshape(fsdp_n * rank, cols)
    )
    shrink_grad = lambda value: mm_tn(value, select_all)
    expand_grad = lambda value: mm_tn(select_all, value)

    late_of = lambda i: late[:, model * i : model * (i + 1)]
    tail_of = lambda i: late[:, model * 2 + kv_width * i : model * 2 + kv_width * (i + 1)]
    order_kinds = (True, True, True, False, False, True, False)
    if fsdp_n == 2 and 2 * hq % 128 == 0 and 2 * early_cols == model:
        expanded = expand_all(
            both, select_all, rank, hq, hp, seq_n, chips, early_cols, order_kinds
        )
    else:
        early_full = both[:, :rank, :early_cols].reshape(fsdp_n, ways, rank, early_cols)
        early_full = early_full.transpose(0, 2, 1, 3).reshape(fsdp_n * rank, ways * early_cols)
        feed_full = both[:, :, early_cols:].reshape(
            fsdp_n, cp_n // 2, 2, seq_n, fsdp_n // 2, rank, feed_wide // seq_n
        ).transpose(4, 2, 5, 0, 1, 3, 6)
        feed_full = feed_full.reshape(fsdp_n * rank, chips, feed_wide)
        expanded = []
        for i, shrink in enumerate((False, False, True) + order_kinds):
            if i < 3:
                rows = feed_full[:, :, i * hp : i * hp + hq].reshape(fsdp_n * rank, hidden_all)
            else:
                rows = early_full[:, model * (i - 3) : model * (i - 2)]
            expanded.append(shrink_grad(rows) if shrink else expand_grad(rows))

    return (
        outputs,
        input_grad.reshape(seqs, tok_rows, model),
        expanded[8],
        expanded[9],
        shrink_grad(late_of(0)),
        expand_grad(tail_of(0)),
        shrink_grad(late_of(1)),
        expand_grad(tail_of(1)),
        expanded[3],
        expanded[6],
        expanded[4],
        expanded[0],
        expanded[5],
        expanded[1],
        expanded[2],
        expanded[7],
    )


def solution(mesh):
    tokens_spec = P("fsdp", ("cp", "seq"), None)
    weight_spec = P(("fsdp", "cp"), None)
    placed = (
        (tokens_spec, tokens_spec, P("fsdp", None), P("fsdp"), P(), P())
        + (weight_spec,) * 7
        + (P(),) * 17
    )
    return jax.shard_map(
        body,
        mesh=mesh,
        in_specs=placed,
        out_specs=(tokens_spec, tokens_spec) + (P(),) * 14,
        check_vma=False,
    )
```

```python
import functools
import math

import jax
import jax.numpy as jnp
from jax import lax
from jax.experimental import pallas as pl
from jax.experimental.pallas import tpu as pltpu
from jax.sharding import PartitionSpec as P

HEAD_DIM = 128
ADAPTER_RANK = 16
epsilon = 1e-06
adapter_scale = 0.5
rotary_base = 1000000.0
masked_score = -1e30
PLANE = ("fsdp", "cp")
EVERY = ("fsdp", "cp", "seq")
BF = jnp.bfloat16
F32 = jnp.float32


def rotary_tables(positions):
    halfway = HEAD_DIM // 2
    frequency = jnp.exp(
        jnp.arange(halfway, dtype=jnp.float32) * (-2.0 * math.log(rotary_base) / HEAD_DIM)
    )
    angles = positions.astype(jnp.float32)[..., None] * frequency
    angles = jnp.concatenate([angles, angles], axis=-1)
    return (jnp.cos(angles), jnp.sin(angles))


def rotate(values, cosine, sine_table):
    halfway = values.shape[-1] // 2
    turned = jnp.concatenate([-values[..., halfway:], values[..., :halfway]], axis=-1)
    return values * cosine + turned * sine_table


def unrotate(gradient, cosine, sine_table):
    halfway = gradient.shape[-1] // 2
    scaled = gradient * sine_table
    turned = jnp.concatenate([scaled[..., halfway:], -scaled[..., :halfway]], axis=-1)
    return gradient * cosine + turned


def mm(left, right):
    return jnp.dot(left, right, preferred_element_type=jnp.float32)


def mm_nt(left, right):
    return lax.dot_general(
        left, right, (((1,), (1,)), ((), ())), preferred_element_type=jnp.float32
    )


def mm_tn(left, right):
    return lax.dot_general(
        left, right, (((0,), (0,)), ((), ())), preferred_element_type=jnp.float32
    )


def norm_forward(values, scales):
    return values * lax.rsqrt(jnp.mean(values * values, axis=-1, keepdims=True) + epsilon) * scales


def norm_backward(values, scales, gradient):
    inverse = lax.rsqrt(jnp.mean(values * values, axis=-1, keepdims=True) + epsilon)
    weighted = gradient * scales
    inner_sum = jnp.mean(weighted * values, axis=-1, keepdims=True)
    return inverse * weighted - values * (inverse * inverse * inverse) * inner_sum


def heads_to_rows(block):
    count = block.shape[1] // HEAD_DIM
    return jnp.concatenate(
        [block[:, HEAD_DIM * j : HEAD_DIM * (j + 1)] for j in range(count)], axis=0
    )


def rows_to_heads(rows, tokens):
    count = rows.shape[0] // tokens
    return jnp.concatenate([rows[tokens * j : tokens * (j + 1)] for j in range(count)], axis=1)


def attend_kernel(spans, span_len, tokens, info, q_ref, k_ref, v_ref, o_ref, lse_ref, m_ref, l_ref, acc_ref):
    seq = pl.program_id(0)
    seqs = pl.num_programs(0)
    own = info[seqs * spans + seq]
    shift = info[seqs * spans + seqs]
    scale = math.log2(math.e) / math.sqrt(HEAD_DIM)
    queries = heads_to_rows(q_ref[...])
    m_ref[...] = jnp.full(m_ref.shape, masked_score, F32)
    l_ref[...] = jnp.zeros(l_ref.shape, F32)
    acc_ref[...] = jnp.zeros(acc_ref.shape, F32)

    def update(j, masked):
        rows = pl.ds(pl.multiple_of(j * span_len, span_len), span_len)
        scores = mm_nt(k_ref[0, rows, :], queries) * scale
        if masked:
            key_at = lax.broadcasted_iota(jnp.int32, scores.shape, 0)
            query_at = shift + lax.rem(lax.broadcasted_iota(jnp.int32, scores.shape, 1), tokens)
            scores = jnp.where(key_at <= query_at, scores, masked_score)
        old = m_ref[...]
        top = jnp.maximum(old, jnp.max(scores, axis=0, keepdims=True))
        expo = jnp.exp2(scores - top)
        alpha = jnp.exp2(old - top)
        l_ref[...] = l_ref[...] * alpha + jnp.sum(expo, axis=0, keepdims=True)
        acc_ref[...] = acc_ref[...] * alpha + mm_tn(v_ref[0, rows, :], expo.astype(BF))
        m_ref[...] = top

    def step(j, carry):
        other = info[seq * spans + j]

        @pl.when(other < own)
        def _():
            update(j, False)

        @pl.when(other == own)
        def _():
            update(j, True)

        return carry

    lax.fori_loop(0, spans, step, 0)
    total = l_ref[...]
    out = jnp.transpose(acc_ref[...] / total)
    o_ref[...] = rows_to_heads(out.astype(BF), tokens)
    lse_ref[0] = jnp.broadcast_to(m_ref[...] + jnp.log2(total), lse_ref.shape[1:])


def attend(info, queries, pairs, seqs, spans, span_len):
    tokens = queries.shape[0] // seqs
    length = pairs.shape[1]
    kv_heads = pairs.shape[2] // (2 * HEAD_DIM)
    width = queries.shape[1] // kv_heads
    rows = tokens * (width // HEAD_DIM)
    grid_spec = pltpu.PrefetchScalarGridSpec(
        num_scalar_prefetch=1,
        grid=(seqs, kv_heads),
        in_specs=[
            pl.BlockSpec((tokens, width), lambda s, h, i: (s, h)),
            pl.BlockSpec((1, length, HEAD_DIM), lambda s, h, i: (s, 0, h)),
            pl.BlockSpec((1, length, HEAD_DIM), lambda s, h, i: (s, 0, kv_heads + h)),
        ],
        out_specs=[
            pl.BlockSpec((tokens, width), lambda s, h, i: (s, h)),
            pl.BlockSpec((1, 8, rows), lambda s, h, i: (s * kv_heads + h, 0, 0)),
        ],
        scratch_shapes=[pltpu.VMEM((1, rows), F32)] * 2 + [pltpu.VMEM((HEAD_DIM, rows), F32)],
    )
    work = seqs * kv_heads * rows * length
    return pl.pallas_call(
        functools.partial(attend_kernel, spans, span_len, tokens),
        grid_spec=grid_spec,
        out_shape=[
            jax.ShapeDtypeStruct(queries.shape, BF),
            jax.ShapeDtypeStruct((seqs * kv_heads, 8, rows), F32),
        ],
        name="attend",
        cost_estimate=pl.CostEstimate(
            flops=4 * work * HEAD_DIM, bytes_accessed=pairs.size * 2, transcendentals=work
        ),
    )(info, queries, pairs, pairs)


def attend_back_kernel(
    spans, span_len, tokens, kv_heads,
    info, q_ref, do_ref, o_ref, k_ref, v_ref, lse_ref, dq_ref, dkv_ref, acc_ref,
):
    seq = pl.program_id(0)
    head = pl.program_id(1)
    seqs = pl.num_programs(0)
    own = info[seqs * spans + seq]
    shift = info[seqs * spans + seqs]
    root = 1.0 / math.sqrt(HEAD_DIM)
    scale = math.log2(math.e) * root
    queries = heads_to_rows(q_ref[...])
    grads = heads_to_rows(do_ref[...])
    results = heads_to_rows(o_ref[...])
    inner = jnp.sum(
        jnp.transpose(grads.astype(F32) * results.astype(F32)), axis=0, keepdims=True
    )
    lse = lse_ref[0, :1, :]
    acc_ref[...] = jnp.zeros(acc_ref.shape, F32)
    key_lane = pl.multiple_of(head * HEAD_DIM, HEAD_DIM)
    val_lane = pl.multiple_of((kv_heads + head) * HEAD_DIM, HEAD_DIM)

    def store(j, key_grad, value_grad):
        rows = pl.ds(pl.multiple_of(j * span_len, span_len), span_len)
        dkv_ref[0, rows, pl.ds(key_lane, HEAD_DIM)] = key_grad
        dkv_ref[0, rows, pl.ds(val_lane, HEAD_DIM)] = value_grad

    def update(j, masked):
        rows = pl.ds(pl.multiple_of(j * span_len, span_len), span_len)
        keys = k_ref[0, rows, :]
        prob = jnp.exp2(mm_nt(keys, queries) * scale - lse)
        if masked:
            key_at = lax.broadcasted_iota(jnp.int32, prob.shape, 0)
            query_at = shift + lax.rem(lax.broadcasted_iota(jnp.int32, prob.shape, 1), tokens)
            prob = jnp.where(key_at <= query_at, prob, 0.0)
        prob_grad = mm_nt(v_ref[0, rows, :], grads)
        score_grad = (prob * (prob_grad - inner)).astype(BF)
        acc_ref[...] += mm_tn(score_grad, keys)
        store(
            j, (mm(score_grad, queries) * root).astype(BF), mm(prob.astype(BF), grads).astype(BF)
        )

    def step(j, carry):
        other = info[seq * spans + j]

        @pl.when(other < own)
        def _():
            update(j, False)

        @pl.when(other == own)
        def _():
            update(j, True)

        @pl.when(other > own)
        def _():
            zero = jnp.zeros((span_len, HEAD_DIM), BF)
            store(j, zero, zero)

        return carry

    lax.fori_loop(0, spans, step, 0)
    dq_ref[...] = rows_to_heads((acc_ref[...] * root).astype(BF), tokens)


def attend_back(info, queries, grads, results, pairs, lse, seqs, spans, span_len):
    tokens = queries.shape[0] // seqs
    length = pairs.shape[1]
    kv_heads = pairs.shape[2] // (2 * HEAD_DIM)
    width = queries.shape[1] // kv_heads
    rows = tokens * (width // HEAD_DIM)
    row = pl.BlockSpec((tokens, width), lambda s, h, i: (s, h))
    block = (1, length, pairs.shape[2])
    grid_spec = pltpu.PrefetchScalarGridSpec(
        num_scalar_prefetch=1,
        grid=(seqs, kv_heads),
        in_specs=[
            row,
            row,
            row,
            pl.BlockSpec((1, length, HEAD_DIM), lambda s, h, i: (s, 0, h)),
            pl.BlockSpec((1, length, HEAD_DIM), lambda s, h, i: (s, 0, kv_heads + h)),
            pl.BlockSpec((1, 8, rows), lambda s, h, i: (s * kv_heads + h, 0, 0)),
        ],
        out_specs=[row, pl.BlockSpec(block, lambda s, h, i: (s, 0, 0))],
        scratch_shapes=[pltpu.VMEM((rows, HEAD_DIM), F32)],
    )
    work = seqs * kv_heads * rows * length
    return pl.pallas_call(
        functools.partial(attend_back_kernel, spans, span_len, tokens, kv_heads),
        grid_spec=grid_spec,
        out_shape=[
            jax.ShapeDtypeStruct(queries.shape, BF),
            jax.ShapeDtypeStruct(pairs.shape, BF),
        ],
        name="attend_back",
        cost_estimate=pl.CostEstimate(
            flops=10 * work * HEAD_DIM, bytes_accessed=pairs.size * 4, transcendentals=work
        ),
    )(info, queries, grads, results, pairs, pairs, lse)


def turned(values, cosine, sine_signed):
    return values * cosine + pltpu.roll(values, HEAD_DIM // 2, axis=1) * sine_signed


def fetch_rows(index, blocks, out_ref, sems):
    depth = blocks[0].shape[0]
    return [
        pltpu.make_async_copy(
            block,
            out_ref.at[pl.ds(pl.multiple_of((index ^ j) * depth, depth), depth), :],
            sems.at[j],
        )
        for j, block in enumerate(blocks)
    ]


def keys_kernel(
    seqs, x_ref, gain_ref, w_ref, shrink_ref, ek_ref, ev_ref, bias_ref, cos_ref, sin_ref,
    normed_ref, nk_ref, nv_ref, pair_ref,
):
    tokens, width = pair_ref.shape
    kv = width // 2
    lanes = ek_ref.shape[0]
    normed = norm_forward(x_ref[...].astype(F32), gain_ref[...]).astype(BF)
    normed_ref[...] = normed
    mix = token_mask(tokens, lanes, seqs)
    narrow = mm(normed, shrink_ref[...])
    narrow_k = (narrow[:, :lanes] * mix).astype(BF)
    narrow_v = (narrow[:, lanes:] * mix).astype(BF)
    nk_ref[...] = narrow_k
    nv_ref[...] = narrow_v
    raw = mm(normed, w_ref[...]) + bias_ref[...]
    keys = raw[:, :kv] + mm(narrow_k, ek_ref[...])
    vals = raw[:, kv:] + mm(narrow_v, ev_ref[...])
    cosine = cos_ref[...]
    sine = sin_ref[...]
    for h in range(kv // HEAD_DIM):
        at = slice(h * HEAD_DIM, (h + 1) * HEAD_DIM)
        pair_ref[:, at] = turned(keys[:, at], cosine, sine).astype(BF)
    pair_ref[:, kv:] = vals.astype(BF)


def keys_values(x, gain, w_kv, shrink, expand_k, expand_v, bias, cosine, sine, seqs):
    tokens, model = x.shape
    lanes = expand_k.shape[0]
    low = lambda n: jax.ShapeDtypeStruct((tokens, n), BF)
    return pl.pallas_call(
        functools.partial(keys_kernel, seqs),
        out_shape=[low(model), low(lanes), low(lanes), low(w_kv.shape[1])],
        name="keys_values",
        cost_estimate=pl.CostEstimate(
            flops=2 * tokens * model * w_kv.shape[1],
            bytes_accessed=8 * tokens * model,
            transcendentals=tokens,
        ),
    )(x, gain, w_kv, shrink, expand_k, expand_v, bias, cosine, sine)


def queries_kernel(
    seqs, count, info, normed_ref, shrink_ref, eq_ref, bias_ref, cos_ref, sin_ref, *refs
):
    blocks = refs[:count]
    query_ref, narrow_ref, w_ref, sems = refs[count:]
    copies = fetch_rows(info[0], blocks, w_ref, sems)
    for copy in copies:
        copy.start()
    tokens, model = query_ref.shape
    lanes = eq_ref.shape[0]
    normed = normed_ref[...]
    narrow = (mm(normed, shrink_ref[...]) * token_mask(tokens, lanes, seqs)).astype(BF)
    narrow_ref[...] = narrow
    for copy in copies:
        copy.wait()
    cosine = cos_ref[...]
    sine = sin_ref[...]
    step = 2 * HEAD_DIM
    for c in range(0, model, step):
        raw = mm(normed, w_ref[:, c : c + step]) + bias_ref[:, c : c + step]
        raw = raw + mm(narrow, eq_ref[:, c : c + step])
        for h in range(0, step, HEAD_DIM):
            query_ref[:, c + h : c + h + HEAD_DIM] = turned(
                raw[:, h : h + HEAD_DIM], cosine, sine
            ).astype(BF)


def outputs_kernel(seqs, count, info, attended_ref, x_ref, gain_ref, shrink_ref, eo_ref, *refs):
    blocks = refs[:count]
    middle_ref, normed_ref, top_ref, bottom_ref, narrow_ref, w_ref, sems = refs[count:]
    copies = fetch_rows(info[0], blocks, w_ref, sems)
    for copy in copies:
        copy.start()
    tokens, model = middle_ref.shape
    lanes = eo_ref.shape[0]
    attended = attended_ref[...]
    narrow = (mm(attended, shrink_ref[...]) * token_mask(tokens, lanes, seqs)).astype(BF)
    narrow_ref[...] = narrow
    for copy in copies:
        copy.wait()
    middle = x_ref[...].astype(F32) + (mm(attended, w_ref[...]) + mm(narrow, eo_ref[...]))
    middle_ref[...] = middle
    normed = norm_forward(middle, gain_ref[...]).astype(BF)
    normed_ref[...] = normed
    top_ref[...] = normed[: tokens // 2]
    bottom_ref[...] = normed[tokens // 2 :]


def before_attention_kernel(
    seqs, most_ref, last_ref, grad_ref, middle_ref, gain_ref, gs_ref, us_ref, os_ref, oe_ref, w_ref,
    mg_ref, low_ref, gb_ref, ub_ref, ob_ref, ag_ref,
):
    tokens, model = mg_ref.shape
    lanes = oe_ref.shape[0]
    mix = token_mask(tokens, lanes, seqs)
    total = most_ref[...] + last_ref[...].astype(F32)
    gate_back = (total[:, model : model + lanes] * mix).astype(BF)
    up_back = (total[:, model + lanes :] * mix).astype(BF)
    gb_ref[...] = gate_back
    ub_ref[...] = up_back
    normed_grad = total[:, :model] + mm_nt(gate_back, gs_ref[...]) + mm_nt(up_back, us_ref[...])
    middle_grad = grad_ref[...].astype(F32) + norm_backward(
        middle_ref[...], gain_ref[...], normed_grad
    )
    mg_ref[...] = middle_grad
    low = middle_grad.astype(BF)
    low_ref[...] = low
    output_back = (mm_nt(low, oe_ref[...]) * mix).astype(BF)
    ob_ref[...] = output_back
    ag_ref[...] = (mm_nt(low, w_ref[...]) + mm_nt(output_back, os_ref[...])).astype(BF)


def before_attention(most, last, grad, middle, gain, gs, us, os, oe, w_output, seqs):
    tokens, model = middle.shape
    lanes = oe.shape[0]
    low = lambda n: jax.ShapeDtypeStruct((tokens, n), BF)
    return pl.pallas_call(
        functools.partial(before_attention_kernel, seqs),
        out_shape=[
            jax.ShapeDtypeStruct((tokens, model), F32),
            low(model), low(lanes), low(lanes), low(lanes), low(model),
        ],
        name="before_attention",
        cost_estimate=pl.CostEstimate(
            flops=2 * tokens * model * model, bytes_accessed=30 * tokens * model, transcendentals=0
        ),
    )(most, last, grad, middle, gain, gs, us, os, oe, w_output)


def last_grads_kernel(
    seqs, rank, info, pair_ref, cos_ref, sin_ref, ke_ref, ve_ref, normed_ref, nk_ref, nv_ref,
    kg_ref, vg_ref, kb_ref, vb_ref, late_ref, rows_ref,
):
    tokens, width = pair_ref.shape
    kv = width // 2
    lanes = ke_ref.shape[0]
    model = normed_ref.shape[1]
    mix = token_mask(tokens, lanes, seqs)
    cosine = cos_ref[...]
    sine = -sin_ref[...]
    for h in range(kv // HEAD_DIM):
        at = slice(h * HEAD_DIM, (h + 1) * HEAD_DIM)
        kg_ref[:, at] = turned(pair_ref[:, at].astype(F32), cosine, sine).astype(BF)
    vg_ref[...] = pair_ref[:, kv:]
    key_grad = kg_ref[...]
    value_grad = vg_ref[...]
    key_back = (mm_nt(key_grad, ke_ref[...]) * mix).astype(BF)
    value_back = (mm_nt(value_grad, ve_ref[...]) * mix).astype(BF)
    kb_ref[...] = key_back
    vb_ref[...] = value_back
    normed = normed_ref[...]
    rows_ref[:, :model] = mm_tn(key_back, normed)[:rank].astype(BF)
    rows_ref[:, model : 2 * model] = mm_tn(value_back, normed)[:rank].astype(BF)
    rows_ref[:, 2 * model : 2 * model + kv] = mm_tn(nk_ref[...], key_grad)[:rank].astype(BF)
    rows_ref[:, 2 * model + kv :] = mm_tn(nv_ref[...], value_grad)[:rank].astype(BF)
    parts = 2 * late_ref.shape[1]
    size = late_ref.shape[3]
    for p in range(parts):
        at = p ^ info[0]
        late_ref[lax.rem(at, 2), at // 2] = rows_ref[:, p * size : (p + 1) * size]


def last_grads(mine, pair_grad, cosine, sine, ke, ve, normed, nk, nv, seqs, rank, parts):
    tokens, width = pair_grad.shape
    lanes = ke.shape[0]
    model = normed.shape[1]
    low = lambda n: jax.ShapeDtypeStruct((tokens, n), BF)
    total = 2 * model + width
    operands = [pair_grad, cosine, sine, ke, ve, normed, nk, nv]
    results = [
        low(width // 2), low(width // 2), low(lanes), low(lanes),
        jax.ShapeDtypeStruct((2, parts // 2, rank, total // parts), BF),
    ]
    return pl.pallas_call(
        functools.partial(last_grads_kernel, seqs, rank),
        grid_spec=pltpu.PrefetchScalarGridSpec(
            num_scalar_prefetch=1,
            grid=(1,),
            in_specs=[pl.BlockSpec(a.shape, lambda g, i, n=a.ndim: (0,) * n) for a in operands],
            out_specs=[
                pl.BlockSpec(r.shape, lambda g, i, n=len(r.shape): (0,) * n) for r in results
            ],
            scratch_shapes=[pltpu.VMEM((rank, total), BF)],
        ),
        out_shape=results,
        name="last_grads",
        cost_estimate=pl.CostEstimate(
            flops=4 * tokens * model * 128, bytes_accessed=6 * tokens * model, transcendentals=0
        ),
    )(mine.reshape(1).astype(jnp.int32), *operands)


def with_blocks(kernel, name, seqs, index, blocks, operands, results):
    count = len(blocks)
    depth, lanes = blocks[0].shape
    inside = pl.BlockSpec(memory_space=pltpu.VMEM)
    results = list(results) + [jax.ShapeDtypeStruct((count * depth, lanes), BF)]
    return pl.pallas_call(
        functools.partial(kernel, seqs, count),
        grid_spec=pltpu.PrefetchScalarGridSpec(
            num_scalar_prefetch=1,
            grid=(1,),
            in_specs=[pl.BlockSpec(a.shape, lambda g, i, n=a.ndim: (0,) * n) for a in operands]
            + [pl.BlockSpec(memory_space=pl.ANY)] * count,
            out_specs=[pl.BlockSpec(r.shape, lambda g, i: (0, 0)) for r in results],
            scratch_shapes=[pltpu.SemaphoreType.DMA((count,))],
        ),
        out_shape=results,
        name=name,
        cost_estimate=pl.CostEstimate(
            flops=2 * operands[0].shape[0] * count * depth * lanes,
            bytes_accessed=4 * count * depth * lanes,
            transcendentals=0,
        ),
    )(index.reshape(1).astype(jnp.int32), *operands, *blocks)


def token_mask(tokens, lanes, seqs):
    row = lax.broadcasted_iota(jnp.int32, (tokens, lanes), 0) // (tokens // seqs)
    lane = lax.broadcasted_iota(jnp.int32, (tokens, lanes), 1) // ADAPTER_RANK
    return jnp.where(row == lane, adapter_scale, 0.0).astype(F32)


def feed_kernel(seqs, kinds, info, *refs):
    count = len(kinds)
    blocks = refs[:count]
    top_ref, bottom_ref, grad_top_ref, grad_bottom_ref = refs[count : count + 4]
    count += 4
    sgu_ref, ed_ref, wd_ref, eg_ref, eu_ref, sd_ref = refs[count : count + 6]
    peg_ref, peu_ref, psd_ref = refs[count + 6 : count + 9]
    out_ref, ng_ref, deg_ref, deu_ref, dsd_ref = refs[count + 9 : count + 14]
    acc_out, acc_ng, acc_nd, acc_bg, acc_bu, nar_g, nar_u, back_d, held, sems = refs[count + 14 :]
    chunk = pl.program_id(0)
    chunks = pl.num_programs(0)
    depth = blocks[0].shape[-2]
    size = wd_ref.shape[0]

    def copies(at, slot):
        found = []
        for n, (j, which) in enumerate(kinds):
            rows = pl.ds(pl.multiple_of((info[0] ^ j) * depth, depth), depth)
            lanes = pl.ds(pl.multiple_of(at * size, 128), size)
            if which is None:
                source, target = blocks[n].at[:, :, lanes], held.at[slot, :, rows, :]
            else:
                source, target = blocks[n].at[:, lanes], held.at[slot, info[1] ^ which, rows, :]
            found.append(pltpu.make_async_copy(source, target, sems.at[slot, n]))
        return found

    slot = lax.rem(chunk, 2)

    @pl.when(chunk == 0)
    def _():
        for copy in copies(chunk, slot):
            copy.start()

    @pl.when(chunk + 1 < chunks)
    def _():
        for copy in copies(chunk + 1, 1 - slot):
            copy.start()

    tokens = out_ref.shape[0]
    model = top_ref.shape[1]
    cols = sd_ref.shape[1]
    n2 = jnp.concatenate([top_ref[...], bottom_ref[...]], axis=0)
    g0 = jnp.concatenate([grad_top_ref[...], grad_bottom_ref[...]], axis=0)
    wg_ref = held.at[slot, 0]
    wu_ref = held.at[slot, 1]

    @pl.when(chunk == 0)
    def _():
        mix = token_mask(tokens, cols, seqs)
        narrow = mm(n2, sgu_ref[...])
        nar_g[...] = (narrow[:, :cols] * mix).astype(BF)
        nar_u[...] = (narrow[:, cols:] * mix).astype(BF)
        back_d[...] = (mm_nt(g0, ed_ref[...]) * mix).astype(BF)
        for acc in (acc_out, acc_ng, acc_nd, acc_bg, acc_bu):
            acc[...] = jnp.zeros(acc.shape, F32)

    for copy in copies(chunk, slot):
        copy.wait()
    narrow_g = nar_g[...]
    narrow_u = nar_u[...]
    narrow_b = back_d[...]
    gate = mm(n2, wg_ref[...]) + mm(narrow_g, eg_ref[...])
    upward = mm(n2, wu_ref[...]) + mm(narrow_u, eu_ref[...])
    sig = jax.nn.sigmoid(gate)
    act = gate * sig
    hidden = (act * upward).astype(BF)
    hidden_grad = mm_nt(g0, wd_ref[...]) + mm_nt(narrow_b, sd_ref[...])
    gate_grad = (hidden_grad * upward * (sig * (1.0 + gate * (1.0 - sig)))).astype(BF)
    up_grad = (hidden_grad * act).astype(BF)
    acc_out[...] += mm(hidden, wd_ref[...])
    acc_nd[...] += mm(hidden, sd_ref[...])
    acc_ng[...] += mm_nt(gate_grad, wg_ref[...]) + mm_nt(up_grad, wu_ref[...])
    acc_bg[...] += mm_nt(gate_grad, eg_ref[...])
    acc_bu[...] += mm_nt(up_grad, eu_ref[...])
    deg_ref[...] = peg_ref[...] + mm_tn(narrow_g, gate_grad)
    deu_ref[...] = peu_ref[...] + mm_tn(narrow_u, up_grad)
    dsd_ref[...] = psd_ref[...] + mm_tn(narrow_b, hidden)

    @pl.when(chunk == chunks - 1)
    def _():
        out_ref[:, :model] = acc_out[...].astype(BF)
        out_ref[:, model:] = jnp.concatenate([acc_nd[...], acc_nd[...]], axis=1).astype(BF)
        ng_ref[:, :model] = acc_ng[...].astype(BF)
        ng_ref[:, model:] = jnp.concatenate([acc_bg[...], acc_bu[...]], axis=1).astype(BF)


def feed(index, kinds, blocks, n2, g0, sgu, ed, wd, eg, eu, sd, previous, seqs, limit=768):
    tokens, model = 2 * n2[0].shape[0], n2[0].shape[1]
    count = len(blocks)
    hidden = wd.shape[0]
    cols = ed.shape[0]
    size = max(c for c in range(128, limit + 1, 128) if hidden % c == 0)
    anywhere = pl.BlockSpec(memory_space=pl.ANY)
    whole = lambda a: pl.BlockSpec(
        a.shape, lambda h, i: (0,) * a.ndim, pipeline_mode=pl.Buffered(1)
    )
    part = lambda a: pl.BlockSpec((a.shape[0], size), lambda h, i: (0, h))
    tall = lambda a: pl.BlockSpec((size, a.shape[1]), lambda h, i: (h, 0))
    fixed = lambda c: pl.BlockSpec((tokens, c), lambda h, i: (0, 0))
    grads = jax.ShapeDtypeStruct((cols, hidden), F32)
    return pl.pallas_call(
        functools.partial(feed_kernel, seqs, tuple(kinds)),
        grid_spec=pltpu.PrefetchScalarGridSpec(
            num_scalar_prefetch=1,
            grid=(hidden // size,),
            in_specs=[anywhere] * count
            + [whole(n2[0]), whole(n2[1]), whole(g0[0]), whole(g0[1]), whole(sgu), whole(ed), tall(wd)]
            + [part(eg), part(eu), tall(sd), part(grads), part(grads), part(grads)],
            out_specs=[fixed(model + 2 * cols), fixed(model + 2 * cols)] + [part(grads)] * 3,
            scratch_shapes=[
                pltpu.VMEM((tokens, model), F32),
                pltpu.VMEM((tokens, model), F32),
                pltpu.VMEM((tokens, cols), F32),
                pltpu.VMEM((tokens, cols), F32),
                pltpu.VMEM((tokens, cols), F32),
                pltpu.VMEM((tokens, cols), BF),
                pltpu.VMEM((tokens, cols), BF),
                pltpu.VMEM((tokens, cols), BF),
                pltpu.VMEM((2, 2, model, size), BF),
                pltpu.SemaphoreType.DMA((2, count)),
            ],
        ),
        out_shape=[
            jax.ShapeDtypeStruct((tokens, model + 2 * cols), BF),
            jax.ShapeDtypeStruct((tokens, model + 2 * cols), BF),
            grads, grads, grads,
        ],
        name="feed",
        cost_estimate=pl.CostEstimate(
            flops=12 * tokens * (model + cols) * hidden,
            bytes_accessed=6 * model * hidden,
            transcendentals=tokens * hidden,
        ),
    )(index, *blocks, *n2, *g0, sgu, ed, wd, eg, eu, sd, *previous)


def assemble_kernel(count, info, *refs):
    blocks = refs[:count]
    out_ref, held, blank, in_sem, out_sem = refs[count:]
    depth = blocks[0].shape[0]
    rest = out_ref.shape[0] - count * depth
    arrive = []
    leave = []
    for j in range(count):
        arrive.append(pltpu.make_async_copy(blocks[j], held.at[j], in_sem.at[j]))
        at = pl.multiple_of((info[0] ^ j) * depth, depth)
        leave.append(
            pltpu.make_async_copy(held.at[j], out_ref.at[pl.ds(at, depth), :], out_sem.at[j])
        )
    for copy in arrive:
        copy.start()
    if rest:
        blank[...] = jnp.zeros(blank.shape, BF)
        last = pltpu.make_async_copy(blank, out_ref.at[count * depth :, :], out_sem.at[count])
        last.start()
    for one, two in zip(arrive, leave):
        one.wait()
        two.start()
    for copy in leave:
        copy.wait()
    if rest:
        last.wait()


def assemble(index, blocks, rows):
    count = len(blocks)
    depth, lanes = blocks[0].shape
    anywhere = pl.BlockSpec(memory_space=pl.ANY)
    return pl.pallas_call(
        functools.partial(assemble_kernel, count),
        grid_spec=pltpu.PrefetchScalarGridSpec(
            num_scalar_prefetch=1,
            grid=(1,),
            in_specs=[anywhere] * count,
            out_specs=anywhere,
            scratch_shapes=[
                pltpu.VMEM((count, depth, lanes), BF),
                pltpu.VMEM((max(rows - count * depth, 16), lanes), BF),
                pltpu.SemaphoreType.DMA((count,)),
                pltpu.SemaphoreType.DMA((count + 1,)),
            ],
        ),
        out_shape=jax.ShapeDtypeStruct((rows, lanes), BF),
        name="assemble",
        cost_estimate=pl.CostEstimate(
            flops=0, bytes_accessed=4 * rows * lanes, transcendentals=0
        ),
    )(index.reshape(1).astype(jnp.int32), *blocks)


def expand_kernel(rank, hidden, padded, seq_n, early, kinds, both_ref, select_ref, *outs):
    pair = pl.program_id(0)
    select = select_ref[...]
    lanes = -(-hidden // 128) * 128
    width = both_ref.shape[2] - early
    for q in range(2):
        for i, out_ref in enumerate(outs[:3]):
            groups = []
            for f in range(2):
                at = i * padded
                left = lanes
                pieces = []
                while left:
                    z, low = divmod(at, width)
                    take = min(left, width - low)
                    device = pair * 4 * seq_n + (q * 2 + f) * seq_n + z
                    pieces.append(both_ref[device, :rank, early + low : early + low + take])
                    at += take
                    left -= take
                groups.append(jnp.concatenate(pieces, axis=1))
            rows = jnp.concatenate(groups, axis=0)
            if i < 2:
                out_ref[:, q * hidden : (q + 1) * hidden] = mm_tn(select, rows)[:, :hidden]
            else:
                out_ref[q * hidden : (q + 1) * hidden, :] = mm_tn(rows, select)[:hidden]

    @pl.when(pair == 0)
    def _():
        half = both_ref.shape[0] // 2
        for i, (out_ref, shrink) in enumerate(zip(outs[3:], kinds)):
            rows = jnp.concatenate(
                [
                    jnp.concatenate(
                        [both_ref[f * half + 2 * i + w, :rank, :early] for w in range(2)], axis=1
                    )
                    for f in range(2)
                ],
                axis=0,
            )
            out_ref[...] = mm_tn(rows, select) if shrink else mm_tn(select, rows)


def expand_all(both, select, rank, hidden, padded, seq_n, chips, early, kinds):
    cols = select.shape[1]
    model = 2 * early
    wide = lambda n: jax.ShapeDtypeStruct((cols, n), F32)
    tall = lambda n: jax.ShapeDtypeStruct((n, cols), F32)
    fixed = [tall(model) if shrink else wide(model) for shrink in kinds]
    return pl.pallas_call(
        functools.partial(expand_kernel, rank, hidden, padded, seq_n, early, kinds),
        grid=(chips // 2,),
        in_specs=[
            pl.BlockSpec(both.shape, lambda p: (0, 0, 0), pipeline_mode=pl.Buffered(1)),
            pl.BlockSpec(select.shape, lambda p: (0, 0)),
        ],
        out_specs=[
            pl.BlockSpec((cols, 2 * hidden), lambda p: (0, p)),
            pl.BlockSpec((cols, 2 * hidden), lambda p: (0, p)),
            pl.BlockSpec((2 * hidden, cols), lambda p: (p, 0)),
        ]
        + [pl.BlockSpec(one.shape, lambda p: (0, 0)) for one in fixed],
        out_shape=[wide(chips * hidden), wide(chips * hidden), tall(chips * hidden)] + fixed,
        name="expand",
        cost_estimate=pl.CostEstimate(
            flops=6 * cols * chips * hidden * select.shape[0],
            bytes_accessed=12 * cols * chips * hidden,
            transcendentals=0,
        ),
    )(both, select)


def after(value, *needed):
    return lax.optimization_barrier((value, needed))[0]


def body(
    inputs, cotangent, span_order, adapter_ids, first_gain, second_gain,
    query_weight, key_weight, value_weight, output_weight, gate_weight, up_weight, down_weight,
    query_bias, key_bias, value_bias,
    query_reduce_factors, query_lift_factors, key_reduce_factors, key_lift_factors,
    value_reduce_factors, value_lift_factors, output_reduce_factors, output_lift_factors,
    gate_reduce_factors, gate_lift_factors, upper_reduce_factors, upper_lift_factors,
    down_reduce_factors, down_lift_factors,
):
    seq_n = lax.axis_size("seq")
    cp_n = lax.axis_size("cp")
    fsdp_n = lax.axis_size("fsdp")
    plane = fsdp_n * cp_n
    chips = plane // 2
    group = lax.axis_index("fsdp")
    me = group * cp_n + lax.axis_index("cp")
    chip = me // 2
    core = me % 2
    seqs, tok_rows, model = inputs.shape
    tokens = seqs * tok_rows
    cols = query_reduce_factors.shape[1]
    kv_width = key_weight.shape[1]
    length = tok_rows * seq_n * cp_n
    spans = span_order.shape[1]
    span_len = length // spans
    hidden_all = gate_weight.shape[1]
    hq = hidden_all // chips
    hp = -(-hq // 256) * 256
    pad = hp - hq
    rank = seqs * ADAPTER_RANK
    lanes = -(-rank // 64) * 64

    def swap(value, k):
        return lax.ppermute(value, PLANE, [(i, i ^ k) for i in range(plane)])

    def swap_seq(value, k):
        return lax.ppermute(value, "seq", [(i, i ^ k) for i in range(seq_n)])

    first_row = (lax.axis_index("cp") * seq_n + lax.axis_index("seq")) * tok_rows
    own = lax.dynamic_slice_in_dim(span_order, first_row // span_len, 1, 1)[:, 0]
    shift = first_row % span_len
    cp_index = lax.axis_index("cp")
    seq_index = lax.axis_index("seq")
    info = jnp.concatenate(
        [span_order.reshape(-1), own, jnp.stack([shift, cp_index])]
    ).astype(jnp.int32)
    places = own[:, None] * span_len + shift + jnp.arange(tok_rows, dtype=jnp.int32)[None, :]
    cosine, sine_table = rotary_tables(places.reshape(tokens))
    sine_signed = jnp.where(
        jnp.arange(HEAD_DIM, dtype=jnp.int32) < HEAD_DIM // 2, -sine_table, sine_table
    )
    flat_cosine = cosine
    cosine = cosine[:, None, :]
    sine_table = sine_table[:, None, :]
    lane = jnp.arange(lanes, dtype=jnp.int32)

    def chosen(ids):
        column = jnp.repeat(ids, ADAPTER_RANK) * ADAPTER_RANK + lane[:rank] % ADAPTER_RANK
        column = jnp.pad(column, (0, lanes - rank), constant_values=-1)
        return (jnp.arange(cols, dtype=jnp.int32)[:, None] == column[None, :]).astype(BF)

    ids_wide = jnp.broadcast_to(
        jnp.pad(adapter_ids, (0, -seqs % 8)).astype(F32)[:, None], (seqs + -seqs % 8, 128)
    )
    select = [chosen(adapter_ids)]
    for f in range(1, fsdp_n):
        select.append(chosen(swap(ids_wide, f * cp_n)[:seqs, 0].astype(jnp.int32)))
    mixing = token_mask(tokens, lanes, seqs)

    def shrink_of(value, f=0):
        return mm(value, select[f]).astype(BF)

    def expand_of(value, f=0):
        return mm_tn(select[f], value).astype(BF)

    w_kv = lax.all_gather(
        jnp.concatenate([key_weight, value_weight], axis=1), PLANE, axis=0, tiled=True
    )
    rows_q = [query_weight] + [swap(query_weight, 2 * k) for k in range(1, chips)]

    def by_chip(value):
        return jnp.stack(
            [
                jnp.pad(value[:, hq * c : hq * (c + 1)], ((0, 0), (0, pad)))
                for c in range(chips)
            ]
        )

    gate_up = jnp.stack([by_chip(gate_weight), by_chip(up_weight)], axis=1)
    depth = gate_weight.shape[0]
    parts = [lax.dynamic_index_in_dim(gate_up, chip ^ k, 0, keepdims=False) for k in range(chips)]

    low_in = inputs.reshape(tokens, model)
    resid_in = low_in.astype(F32)
    first_scales = first_gain.astype(F32)
    second_scales = second_gain.astype(F32)
    grad_low = cotangent.reshape(tokens, model)
    w_kv, parts, rows_q = lax.optimization_barrier((w_kv, parts, rows_q))
    rows_o = [output_weight] + [swap(after(output_weight, rows_q), 2 * k) for k in range(1, chips)]
    blocks = {}
    w_key = w_kv[:, :kv_width]
    w_value = w_kv[:, kv_width:]

    query_shrink, key_shrink, value_shrink, output_shrink = [
        shrink_of(value)
        for value in (
            query_reduce_factors, key_reduce_factors, value_reduce_factors, output_reduce_factors,
        )
    ]
    query_expand, key_expand, value_expand, output_expand = [
        expand_of(value)
        for value in (
            query_lift_factors, key_lift_factors, value_lift_factors, output_lift_factors,
        )
    ]
    grad_halves = (grad_low[: tokens // 2], grad_low[tokens // 2 :])
    w_kv, output_shrink, output_expand, query_shrink, query_expand, grad_halves = (
        lax.optimization_barrier(
            (w_kv, output_shrink, output_expand, query_shrink, query_expand, grad_halves)
        )
    )

    def swap_both(pair, k):
        return tuple(swap(half, k) for half in pair)

    g0_pieces = {
        k: swap_both(after(grad_halves, rows_q), 2 * k) for k in range(1, chips) if 2 * k % cp_n == 0
    }

    def narrowed(value, shrink):
        return (mm(value, shrink) * mixing).astype(BF)

    normed, key_narrow, value_narrow, pair = keys_values(
        low_in, first_scales[None], w_kv, jnp.concatenate([key_shrink, value_shrink], axis=1),
        key_expand, value_expand,
        jnp.concatenate([key_bias, value_bias]).astype(F32)[None], flat_cosine, sine_signed, seqs,
    )
    pair_all = lax.all_gather(
        pair.reshape(seqs, tok_rows, 2 * kv_width), ("cp", "seq"), axis=1, tiled=True
    )

    def both_cores(rows):
        found = []
        for part in rows:
            found += [part, swap(part, 1)]
        return found

    query_rot, query_narrow, w_query = with_blocks(
        queries_kernel, "queries", seqs, me, after(both_cores(rows_q), pair),
        [
            after(normed, rows_o, g0_pieces), query_shrink, query_expand, query_bias.astype(F32)[None], flat_cosine,
            sine_signed,
        ],
        [
            jax.ShapeDtypeStruct((tokens, model), BF),
            jax.ShapeDtypeStruct((tokens, lanes), BF),
        ],
    )

    late_lift = after(
        (
        gate_lift_factors, upper_lift_factors, down_reduce_factors, down_lift_factors,
        gate_reduce_factors, upper_reduce_factors,
        ),
        query_rot,
    )
    gate_shrink, up_shrink = shrink_of(late_lift[4]), shrink_of(late_lift[5])
    down_expand = expand_of(late_lift[3])
    reduce_factors = [
        (
            jnp.concatenate([shrink_of(late_lift[4], f), shrink_of(late_lift[5], f)], axis=1),
            expand_of(late_lift[3], f),
        )
        for f in range(fsdp_n)
    ]
    late_down, late_gate, late_up = late_lift[2], late_lift[0], late_lift[1]
    shrink_d = jnp.pad(
        lax.dynamic_slice_in_dim(late_down, chip * hq, hq, 0), ((0, pad), (0, 0))
    )
    lift_g = lax.dynamic_index_in_dim(by_chip(late_gate), chip, 0, keepdims=False)
    lift_u = lax.dynamic_index_in_dim(by_chip(late_up), chip, 0, keepdims=False)
    lift_factors = [(expand_of(lift_g, f), expand_of(lift_u, f)) for f in range(fsdp_n)]
    feed_factors = [
        reduce_factors[f] + lift_factors[f] + (shrink_of(shrink_d, f),) for f in range(fsdp_n)
    ]
    down_rows = [down_weight, swap(after(down_weight, query_rot), 1)]
    w_down = assemble(core, after(down_rows, query_rot), hp)
    attended, lse = attend(
        info, after(query_rot, w_down, feed_factors, gate_shrink, up_shrink, down_expand),
        pair_all, seqs, spans, span_len,
    )
    for k in range(1, chips):
        blocks[k] = swap(after(parts[k], rows_o), 2 * k)
    output_blocks = both_cores(after(rows_o, query_rot))
    middle, normed_two, normed_top, normed_bottom, output_narrow, w_output = with_blocks(
        outputs_kernel, "outputs", seqs, me, output_blocks,
        [attended, low_in, second_scales[None], output_shrink, output_expand],
        [
            jax.ShapeDtypeStruct((tokens, model), F32),
            jax.ShapeDtypeStruct((tokens, model), BF),
            jax.ShapeDtypeStruct((tokens // 2, model), BF),
            jax.ShapeDtypeStruct((tokens // 2, model), BF),
            jax.ShapeDtypeStruct((tokens, lanes), BF),
        ],
    )

    kinds = [(0, None), (1, None)]
    wide = [parts[0], swap(after(parts[0], query_rot), 1)]
    for k in range(1, chips):
        kinds += [(2 * k, None), (2 * k + 1, None)]
        wide += [blocks[k], swap(after(blocks[k], middle), 1)]
    feed_index = jnp.stack([me, core]).astype(jnp.int32)

    g0_pieces[0] = grad_halves
    normed_halves = (normed_top, normed_bottom)
    n2_pieces = [normed_halves]
    for k in range(1, chips):
        if k < 3:
            n2_pieces.append(swap_both(after(normed_halves, wide), 2 * k))
    if chips > 2:
        n2_pieces[1:3] = lax.optimization_barrier(n2_pieces[1:3])
    zero = jnp.zeros((lanes, hp), F32)
    sums = [(zero, zero, zero)] * fsdp_n
    out_raw = []
    grad_parts = []
    early_first = [0] + sorted(range(1, chips), key=lambda k: (k > 2, -k if k < 3 else k))
    for k in early_first:
        f = 2 * k // cp_n
        sgu, ed, eg, eu, sd = feed_factors[f]
        if len(out_raw) == 1:
            for other in range(1, min(chips, 3)):
                if other not in g0_pieces:
                    g0_pieces[other] = swap_both(after(grad_halves, out_raw[0]), 2 * other)
        if len(out_raw) == 2:
            for other in range(3, chips):
                for pieces in (n2_pieces, g0_pieces):
                    first, second, own_pair = after((pieces[2], pieces[1], pieces[0]), out_raw[-1])
                    if other == 3:
                        piece = (swap(first[0], 2), swap(second[1], 4))
                    else:
                        piece = swap_both(own_pair, 2 * other)
                    if pieces is n2_pieces:
                        n2_pieces.append(piece)
                    else:
                        g0_pieces[other] = piece
        if out_raw:
            sums[f] = after(sums[f], out_raw[-1])
        out_k, ng_k, *sums[f] = feed(
            feed_index, kinds, wide, n2_pieces[k], g0_pieces[k], sgu, ed, w_down, eg, eu, sd, sums[f], seqs
        )
        out_raw.append(out_k)
        grad_parts.append(ng_k if k == 0 else swap(ng_k, 2 * k))

    grad_most = grad_parts[0].astype(F32)
    for part in grad_parts[1:-1]:
        grad_most = lax.optimization_barrier(grad_most) + part.astype(F32)

    def pack(values, tiles):
        value = jnp.concatenate([value[:rank].astype(BF) for value in values], axis=1)
        return jnp.pad(value, ((0, 0), (0, -value.shape[1] % (128 * tiles))))

    middle_grad, middle_low, gate_back, up_back, output_back, attended_grad = before_attention(
        grad_most, grad_parts[-1], grad_low, middle, second_scales[None],
        gate_shrink, up_shrink, output_shrink, output_expand, w_output, seqs,
    )

    def narrowed_back(grad, expand):
        return (mm_nt(grad, expand) * mixing).astype(BF)

    out_raw = after(out_raw, middle_low)
    out_parts = [swap(part, 2 * k) if k else part for k, part in zip(early_first[:3], out_raw)]
    query_rot_grad, pair_part = attend_back(
        info, query_rot, attended_grad, attended, pair_all, lse, seqs, spans, span_len
    )
    out_parts += [
        swap(after(part, pair_part), 2 * k) for k, part in zip(early_first[3:], out_raw[3:])
    ]
    pair_grad = lax.psum_scatter(
        after(pair_part, out_parts[:3]), ("cp", "seq"), scatter_dimension=1, tiled=True
    ).reshape(tokens, 2 * kv_width)
    out_sum = sum(part.astype(F32) for part in out_parts)

    down_narrow = (out_sum[:, model : model + lanes] * mixing).astype(BF)
    result = middle + (out_sum[:, :model] + mm(down_narrow, down_expand))
    outputs = result.astype(BF).reshape(seqs, tok_rows, model)

    query_rot_grad, sums, middle_late, output_back, gate_back, up_back = after(
        (query_rot_grad, sums, middle_low, output_back, gate_back, up_back), out_parts[:3]
    )
    cosine, sine_table = after((cosine, sine_table), pair_part)
    query_grad = (
        unrotate(
            query_rot_grad.reshape(tokens, -1, HEAD_DIM).astype(F32), cosine, sine_table
        )
        .reshape(tokens, model)
        .astype(BF)
    )
    query_back = narrowed_back(query_grad, query_expand)
    query_in = mm_nt(query_grad, w_query) + mm_nt(query_back, query_shrink)

    def halves(value, index, exchange):
        span = 1
        while value.shape[0] > 1:
            split = value.reshape((value.shape[0] // 2, 2) + value.shape[1:])
            bit = index // span % 2
            keep = lax.dynamic_index_in_dim(split, bit, 1, keepdims=False)
            give = lax.dynamic_index_in_dim(split, 1 - bit, 1, keepdims=False)
            value = (keep.astype(F32) + exchange(give, span).astype(F32)).astype(BF)
            span *= 2
        return value[0]

    stacked = jnp.stack([pack(sums[f], seq_n) for f in range(fsdp_n)])
    feed_wide = stacked.shape[2]

    def groups_of(parity):
        return jnp.stack(
            [
                lax.dynamic_index_in_dim(stacked, (2 * j + parity) ^ group, 0, keepdims=False)
                for j in range(fsdp_n // 2)
            ]
        )

    feed_half = groups_of(core).astype(F32) + swap(groups_of(1 - core), 1).astype(F32)
    feed_half = feed_half.reshape(fsdp_n // 2 * rank, seq_n, feed_wide // seq_n).astype(BF)
    feed_half = feed_half.transpose(1, 0, 2)
    feed_piece = halves(feed_half, seq_index, swap_seq)
    ways = cp_n * seq_n
    early = pack(
        [
            mm_tn(output_back, attended),
            mm_tn(gate_back, normed_two),
            mm_tn(up_back, normed_two),
            mm_tn(output_narrow, middle_late),
            mm_tn(down_narrow, grad_low),
            mm_tn(query_back, normed),
            mm_tn(query_narrow, query_grad),
        ],
        ways,
    )
    early = early.reshape(rank, cp_n, seq_n, -1).transpose(1, 2, 0, 3)
    early = halves(early, cp_index, swap)
    early = halves(early, seq_index, swap_seq)
    early_cols = early.shape[1]
    both = jnp.concatenate([jnp.pad(early, ((0, feed_piece.shape[0] - rank), (0, 0))), feed_piece], axis=1)
    both = lax.all_gather(after(both, pair_grad), EVERY, axis=0, tiled=False)

    key_grad, value_grad, key_back, value_back, late = last_grads(
        cp_index, pair_grad, flat_cosine, sine_signed, key_expand, value_expand, normed,
        key_narrow, value_narrow, seqs, rank, cp_n,
    )
    late_wide = late.shape[3] * cp_n
    total = late[0].astype(F32) + swap(late[1], 1).astype(F32)
    span = 2
    while span < cp_n:
        total = total[0::2] + swap(total[1::2].astype(BF), span).astype(F32)
        span *= 2
    late = total[0].astype(BF)
    total = late.astype(F32)
    for k in range(1, seq_n):
        total = total + swap_seq(late, k).astype(F32)
    late = total.astype(BF)[None]
    for step in [span_k for span_k in (2**i for i in range(1, 30)) if span_k < plane] + [1]:
        late = jnp.concatenate([late, swap(late, step)], axis=0)

    normed_grad = (
        query_in
        + mm_nt(key_grad, w_key)
        + mm_nt(value_grad, w_value)
        + mm_nt(key_back, key_shrink)
        + mm_nt(value_back, value_shrink)
    )
    input_grad = middle_grad + norm_backward(resid_in, first_scales, normed_grad)

    came = [0]
    for step in [span_k for span_k in (2**i for i in range(1, 30)) if span_k < plane] + [1]:
        came = came + [c ^ step for c in came]
    inverse = [came.index(c) for c in range(plane)]
    late = jnp.take(
        late, jnp.asarray(inverse, jnp.int32)[jnp.arange(plane, dtype=jnp.int32) ^ me], axis=0
    )
    late = late.reshape(fsdp_n, cp_n, rank, late_wide // cp_n)
    late = late.transpose(0, 2, 1, 3).reshape(fsdp_n * rank, late_wide)

    order = jnp.arange(fsdp_n, dtype=jnp.int32) ^ group
    select_all = (
        jnp.take(jnp.stack(select), order, axis=0)[:, :, :rank]
        .transpose(0, 2, 1)
        .reshape(fsdp_n * rank, cols)
    )
    shrink_grad = lambda value: mm_tn(value, select_all)
    expand_grad = lambda value: mm_tn(select_all, value)

    late_of = lambda i: late[:, model * i : model * (i + 1)]
    tail_of = lambda i: late[:, model * 2 + kv_width * i : model * 2 + kv_width * (i + 1)]
    order_kinds = (True, True, True, False, False, True, False)
    if fsdp_n == 2 and 2 * hq % 128 == 0 and 2 * early_cols == model:
        expanded = expand_all(
            both, select_all, rank, hq, hp, seq_n, chips, early_cols, order_kinds
        )
    else:
        early_full = both[:, :rank, :early_cols].reshape(fsdp_n, ways, rank, early_cols)
        early_full = early_full.transpose(0, 2, 1, 3).reshape(fsdp_n * rank, ways * early_cols)
        feed_full = both[:, :, early_cols:].reshape(
            fsdp_n, cp_n // 2, 2, seq_n, fsdp_n // 2, rank, feed_wide // seq_n
        ).transpose(4, 2, 5, 0, 1, 3, 6)
        feed_full = feed_full.reshape(fsdp_n * rank, chips, feed_wide)
        expanded = []
        for i, shrink in enumerate((False, False, True) + order_kinds):
            if i < 3:
                rows = feed_full[:, :, i * hp : i * hp + hq].reshape(fsdp_n * rank, hidden_all)
            else:
                rows = early_full[:, model * (i - 3) : model * (i - 2)]
            expanded.append(shrink_grad(rows) if shrink else expand_grad(rows))

    return (
        outputs,
        input_grad.reshape(seqs, tok_rows, model),
        expanded[8],
        expanded[9],
        shrink_grad(late_of(0)),
        expand_grad(tail_of(0)),
        shrink_grad(late_of(1)),
        expand_grad(tail_of(1)),
        expanded[3],
        expanded[6],
        expanded[4],
        expanded[0],
        expanded[5],
        expanded[1],
        expanded[2],
        expanded[7],
    )


def solution(mesh):
    tokens_spec = P("fsdp", ("cp", "seq"), None)
    weight_spec = P(("fsdp", "cp"), None)
    placed = (
        (tokens_spec, tokens_spec, P("fsdp", None), P("fsdp"), P(), P())
        + (weight_spec,) * 7
        + (P(),) * 17
    )
    return jax.shard_map(
        body,
        mesh=mesh,
        in_specs=placed,
        out_specs=(tokens_spec, tokens_spec) + (P(),) * 14,
        check_vma=False,
    )
```

```python
import functools
import math

import jax
import jax.numpy as jnp
from jax import lax
from jax.experimental import pallas as pl
from jax.experimental.pallas import tpu as pltpu
from jax.sharding import PartitionSpec as P

HEAD_DIM = 128
ADAPTER_RANK = 16
epsilon = 1e-06
adapter_scale = 0.5
rotary_base = 1000000.0
masked_score = -1e30
PLANE = ("fsdp", "cp")
EVERY = ("fsdp", "cp", "seq")
BF = jnp.bfloat16
F32 = jnp.float32


def rotary_tables(positions):
    halfway = HEAD_DIM // 2
    frequency = jnp.exp(
        jnp.arange(halfway, dtype=jnp.float32) * (-2.0 * math.log(rotary_base) / HEAD_DIM)
    )
    angles = positions.astype(jnp.float32)[..., None] * frequency
    angles = jnp.concatenate([angles, angles], axis=-1)
    return (jnp.cos(angles), jnp.sin(angles))


def rotate(values, cosine, sine_table):
    halfway = values.shape[-1] // 2
    turned = jnp.concatenate([-values[..., halfway:], values[..., :halfway]], axis=-1)
    return values * cosine + turned * sine_table


def unrotate(gradient, cosine, sine_table):
    halfway = gradient.shape[-1] // 2
    scaled = gradient * sine_table
    turned = jnp.concatenate([scaled[..., halfway:], -scaled[..., :halfway]], axis=-1)
    return gradient * cosine + turned


def mm(left, right):
    return jnp.dot(left, right, preferred_element_type=jnp.float32)


def mm_nt(left, right):
    return lax.dot_general(
        left, right, (((1,), (1,)), ((), ())), preferred_element_type=jnp.float32
    )


def mm_tn(left, right):
    return lax.dot_general(
        left, right, (((0,), (0,)), ((), ())), preferred_element_type=jnp.float32
    )


def norm_forward(values, scales):
    return values * lax.rsqrt(jnp.mean(values * values, axis=-1, keepdims=True) + epsilon) * scales


def norm_backward(values, scales, gradient):
    inverse = lax.rsqrt(jnp.mean(values * values, axis=-1, keepdims=True) + epsilon)
    weighted = gradient * scales
    inner_sum = jnp.mean(weighted * values, axis=-1, keepdims=True)
    return inverse * weighted - values * (inverse * inverse * inverse) * inner_sum


def heads_to_rows(block):
    count = block.shape[1] // HEAD_DIM
    return jnp.concatenate(
        [block[:, HEAD_DIM * j : HEAD_DIM * (j + 1)] for j in range(count)], axis=0
    )


def rows_to_heads(rows, tokens):
    count = rows.shape[0] // tokens
    return jnp.concatenate([rows[tokens * j : tokens * (j + 1)] for j in range(count)], axis=1)


def attend_kernel(spans, span_len, tokens, info, q_ref, k_ref, v_ref, o_ref, lse_ref, m_ref, l_ref, acc_ref):
    seq = pl.program_id(0)
    seqs = pl.num_programs(0)
    own = info[seqs * spans + seq]
    shift = info[seqs * spans + seqs]
    scale = math.log2(math.e) / math.sqrt(HEAD_DIM)
    queries = heads_to_rows(q_ref[...])
    m_ref[...] = jnp.full(m_ref.shape, masked_score, F32)
    l_ref[...] = jnp.zeros(l_ref.shape, F32)
    acc_ref[...] = jnp.zeros(acc_ref.shape, F32)

    def update(j, masked):
        rows = pl.ds(pl.multiple_of(j * span_len, span_len), span_len)
        scores = mm_nt(k_ref[0, rows, :], queries) * scale
        if masked:
            key_at = lax.broadcasted_iota(jnp.int32, scores.shape, 0)
            query_at = shift + lax.rem(lax.broadcasted_iota(jnp.int32, scores.shape, 1), tokens)
            scores = jnp.where(key_at <= query_at, scores, masked_score)
        old = m_ref[...]
        top = jnp.maximum(old, jnp.max(scores, axis=0, keepdims=True))
        expo = jnp.exp2(scores - top)
        alpha = jnp.exp2(old - top)
        l_ref[...] = l_ref[...] * alpha + jnp.sum(expo, axis=0, keepdims=True)
        acc_ref[...] = acc_ref[...] * alpha + mm_tn(v_ref[0, rows, :], expo.astype(BF))
        m_ref[...] = top

    def step(j, carry):
        other = info[seq * spans + j]

        @pl.when(other < own)
        def _():
            update(j, False)

        @pl.when(other == own)
        def _():
            update(j, True)

        return carry

    lax.fori_loop(0, spans, step, 0)
    total = l_ref[...]
    out = jnp.transpose(acc_ref[...] / total)
    o_ref[...] = rows_to_heads(out.astype(BF), tokens)
    lse_ref[0] = jnp.broadcast_to(m_ref[...] + jnp.log2(total), lse_ref.shape[1:])


def attend(info, queries, pairs, seqs, spans, span_len):
    tokens = queries.shape[0] // seqs
    length = pairs.shape[1]
    kv_heads = pairs.shape[2] // (2 * HEAD_DIM)
    width = queries.shape[1] // kv_heads
    rows = tokens * (width // HEAD_DIM)
    grid_spec = pltpu.PrefetchScalarGridSpec(
        num_scalar_prefetch=1,
        grid=(seqs, kv_heads),
        in_specs=[
            pl.BlockSpec((tokens, width), lambda s, h, i: (s, h)),
            pl.BlockSpec((1, length, HEAD_DIM), lambda s, h, i: (s, 0, h)),
            pl.BlockSpec((1, length, HEAD_DIM), lambda s, h, i: (s, 0, kv_heads + h)),
        ],
        out_specs=[
            pl.BlockSpec((tokens, width), lambda s, h, i: (s, h)),
            pl.BlockSpec((1, 8, rows), lambda s, h, i: (s * kv_heads + h, 0, 0)),
        ],
        scratch_shapes=[pltpu.VMEM((1, rows), F32)] * 2 + [pltpu.VMEM((HEAD_DIM, rows), F32)],
    )
    work = seqs * kv_heads * rows * length
    return pl.pallas_call(
        functools.partial(attend_kernel, spans, span_len, tokens),
        grid_spec=grid_spec,
        out_shape=[
            jax.ShapeDtypeStruct(queries.shape, BF),
            jax.ShapeDtypeStruct((seqs * kv_heads, 8, rows), F32),
        ],
        name="attend",
        cost_estimate=pl.CostEstimate(
            flops=4 * work * HEAD_DIM, bytes_accessed=pairs.size * 2, transcendentals=work
        ),
    )(info, queries, pairs, pairs)


def attend_back_kernel(
    spans, span_len, tokens, kv_heads,
    info, q_ref, do_ref, o_ref, k_ref, v_ref, lse_ref, dq_ref, dkv_ref, acc_ref,
):
    seq = pl.program_id(0)
    head = pl.program_id(1)
    seqs = pl.num_programs(0)
    own = info[seqs * spans + seq]
    shift = info[seqs * spans + seqs]
    root = 1.0 / math.sqrt(HEAD_DIM)
    scale = math.log2(math.e) * root
    queries = heads_to_rows(q_ref[...])
    grads = heads_to_rows(do_ref[...])
    results = heads_to_rows(o_ref[...])
    inner = jnp.sum(
        jnp.transpose(grads.astype(F32) * results.astype(F32)), axis=0, keepdims=True
    )
    lse = lse_ref[0, :1, :]
    acc_ref[...] = jnp.zeros(acc_ref.shape, F32)
    key_lane = pl.multiple_of(head * HEAD_DIM, HEAD_DIM)
    val_lane = pl.multiple_of((kv_heads + head) * HEAD_DIM, HEAD_DIM)

    def store(j, key_grad, value_grad):
        rows = pl.ds(pl.multiple_of(j * span_len, span_len), span_len)
        dkv_ref[0, rows, pl.ds(key_lane, HEAD_DIM)] = key_grad
        dkv_ref[0, rows, pl.ds(val_lane, HEAD_DIM)] = value_grad

    def update(j, masked):
        rows = pl.ds(pl.multiple_of(j * span_len, span_len), span_len)
        keys = k_ref[0, rows, :]
        prob = jnp.exp2(mm_nt(keys, queries) * scale - lse)
        if masked:
            key_at = lax.broadcasted_iota(jnp.int32, prob.shape, 0)
            query_at = shift + lax.rem(lax.broadcasted_iota(jnp.int32, prob.shape, 1), tokens)
            prob = jnp.where(key_at <= query_at, prob, 0.0)
        prob_grad = mm_nt(v_ref[0, rows, :], grads)
        score_grad = (prob * (prob_grad - inner)).astype(BF)
        acc_ref[...] += mm_tn(score_grad, keys)
        store(
            j, (mm(score_grad, queries) * root).astype(BF), mm(prob.astype(BF), grads).astype(BF)
        )

    def step(j, carry):
        other = info[seq * spans + j]

        @pl.when(other < own)
        def _():
            update(j, False)

        @pl.when(other == own)
        def _():
            update(j, True)

        @pl.when(other > own)
        def _():
            zero = jnp.zeros((span_len, HEAD_DIM), BF)
            store(j, zero, zero)

        return carry

    lax.fori_loop(0, spans, step, 0)
    dq_ref[...] = rows_to_heads((acc_ref[...] * root).astype(BF), tokens)


def attend_back(info, queries, grads, results, pairs, lse, seqs, spans, span_len):
    tokens = queries.shape[0] // seqs
    length = pairs.shape[1]
    kv_heads = pairs.shape[2] // (2 * HEAD_DIM)
    width = queries.shape[1] // kv_heads
    rows = tokens * (width // HEAD_DIM)
    row = pl.BlockSpec((tokens, width), lambda s, h, i: (s, h))
    block = (1, length, pairs.shape[2])
    grid_spec = pltpu.PrefetchScalarGridSpec(
        num_scalar_prefetch=1,
        grid=(seqs, kv_heads),
        in_specs=[
            row,
            row,
            row,
            pl.BlockSpec((1, length, HEAD_DIM), lambda s, h, i: (s, 0, h)),
            pl.BlockSpec((1, length, HEAD_DIM), lambda s, h, i: (s, 0, kv_heads + h)),
            pl.BlockSpec((1, 8, rows), lambda s, h, i: (s * kv_heads + h, 0, 0)),
        ],
        out_specs=[row, pl.BlockSpec(block, lambda s, h, i: (s, 0, 0))],
        scratch_shapes=[pltpu.VMEM((rows, HEAD_DIM), F32)],
    )
    work = seqs * kv_heads * rows * length
    return pl.pallas_call(
        functools.partial(attend_back_kernel, spans, span_len, tokens, kv_heads),
        grid_spec=grid_spec,
        out_shape=[
            jax.ShapeDtypeStruct(queries.shape, BF),
            jax.ShapeDtypeStruct(pairs.shape, BF),
        ],
        name="attend_back",
        cost_estimate=pl.CostEstimate(
            flops=10 * work * HEAD_DIM, bytes_accessed=pairs.size * 4, transcendentals=work
        ),
    )(info, queries, grads, results, pairs, pairs, lse)


def turned(values, cosine, sine_signed):
    return values * cosine + pltpu.roll(values, HEAD_DIM // 2, axis=1) * sine_signed


def fetch_rows(index, blocks, out_ref, sems):
    depth = blocks[0].shape[0]
    return [
        pltpu.make_async_copy(
            block,
            out_ref.at[pl.ds(pl.multiple_of((index ^ j) * depth, depth), depth), :],
            sems.at[j],
        )
        for j, block in enumerate(blocks)
    ]


def keys_kernel(
    seqs, x_ref, gain_ref, w_ref, shrink_ref, ek_ref, ev_ref, bias_ref, cos_ref, sin_ref,
    normed_ref, nk_ref, nv_ref, pair_ref,
):
    tokens, width = pair_ref.shape
    kv = width // 2
    lanes = ek_ref.shape[0]
    normed = norm_forward(x_ref[...].astype(F32), gain_ref[...]).astype(BF)
    normed_ref[...] = normed
    mix = token_mask(tokens, lanes, seqs)
    narrow = mm(normed, shrink_ref[...])
    narrow_k = (narrow[:, :lanes] * mix).astype(BF)
    narrow_v = (narrow[:, lanes:] * mix).astype(BF)
    nk_ref[...] = narrow_k
    nv_ref[...] = narrow_v
    raw = mm(normed, w_ref[...]) + bias_ref[...]
    keys = raw[:, :kv] + mm(narrow_k, ek_ref[...])
    vals = raw[:, kv:] + mm(narrow_v, ev_ref[...])
    cosine = cos_ref[...]
    sine = sin_ref[...]
    for h in range(kv // HEAD_DIM):
        at = slice(h * HEAD_DIM, (h + 1) * HEAD_DIM)
        pair_ref[:, at] = turned(keys[:, at], cosine, sine).astype(BF)
    pair_ref[:, kv:] = vals.astype(BF)


def keys_values(x, gain, w_kv, shrink, expand_k, expand_v, bias, cosine, sine, seqs):
    tokens, model = x.shape
    lanes = expand_k.shape[0]
    low = lambda n: jax.ShapeDtypeStruct((tokens, n), BF)
    return pl.pallas_call(
        functools.partial(keys_kernel, seqs),
        out_shape=[low(model), low(lanes), low(lanes), low(w_kv.shape[1])],
        name="keys_values",
        cost_estimate=pl.CostEstimate(
            flops=2 * tokens * model * w_kv.shape[1],
            bytes_accessed=8 * tokens * model,
            transcendentals=tokens,
        ),
    )(x, gain, w_kv, shrink, expand_k, expand_v, bias, cosine, sine)


def queries_kernel(
    seqs, count, info, normed_ref, shrink_ref, eq_ref, bias_ref, cos_ref, sin_ref, *refs
):
    blocks = refs[:count]
    query_ref, narrow_ref, w_ref, sems = refs[count:]
    copies = fetch_rows(info[0], blocks, w_ref, sems)
    for copy in copies:
        copy.start()
    tokens, model = query_ref.shape
    lanes = eq_ref.shape[0]
    normed = normed_ref[...]
    narrow = (mm(normed, shrink_ref[...]) * token_mask(tokens, lanes, seqs)).astype(BF)
    narrow_ref[...] = narrow
    for copy in copies:
        copy.wait()
    cosine = cos_ref[...]
    sine = sin_ref[...]
    step = 2 * HEAD_DIM
    for c in range(0, model, step):
        raw = mm(normed, w_ref[:, c : c + step]) + bias_ref[:, c : c + step]
        raw = raw + mm(narrow, eq_ref[:, c : c + step])
        for h in range(0, step, HEAD_DIM):
            query_ref[:, c + h : c + h + HEAD_DIM] = turned(
                raw[:, h : h + HEAD_DIM], cosine, sine
            ).astype(BF)


def outputs_kernel(seqs, count, info, attended_ref, x_ref, gain_ref, shrink_ref, eo_ref, *refs):
    blocks = refs[:count]
    middle_ref, normed_ref, top_ref, bottom_ref, narrow_ref, w_ref, sems = refs[count:]
    copies = fetch_rows(info[0], blocks, w_ref, sems)
    for copy in copies:
        copy.start()
    tokens, model = middle_ref.shape
    lanes = eo_ref.shape[0]
    attended = attended_ref[...]
    narrow = (mm(attended, shrink_ref[...]) * token_mask(tokens, lanes, seqs)).astype(BF)
    narrow_ref[...] = narrow
    for copy in copies:
        copy.wait()
    middle = x_ref[...].astype(F32) + (mm(attended, w_ref[...]) + mm(narrow, eo_ref[...]))
    middle_ref[...] = middle
    normed = norm_forward(middle, gain_ref[...]).astype(BF)
    normed_ref[...] = normed
    top_ref[...] = normed[: tokens // 2]
    bottom_ref[...] = normed[tokens // 2 :]


def before_attention_kernel(
    seqs, count, *refs
):
    grad_ref, middle_ref, gain_ref, gs_ref, us_ref, os_ref, oe_ref, w_ref = refs[count : count + 8]
    mg_ref, low_ref, gb_ref, ub_ref, ob_ref, ag_ref = refs[count + 8 :]
    tokens, model = mg_ref.shape
    lanes = oe_ref.shape[0]
    mix = token_mask(tokens, lanes, seqs)
    total = sum(ref[...].astype(F32) for ref in refs[:count])
    gate_back = (total[:, model : model + lanes] * mix).astype(BF)
    up_back = (total[:, model + lanes :] * mix).astype(BF)
    gb_ref[...] = gate_back
    ub_ref[...] = up_back
    normed_grad = total[:, :model] + mm_nt(gate_back, gs_ref[...]) + mm_nt(up_back, us_ref[...])
    middle_grad = grad_ref[...].astype(F32) + norm_backward(
        middle_ref[...], gain_ref[...], normed_grad
    )
    mg_ref[...] = middle_grad
    low = middle_grad.astype(BF)
    low_ref[...] = low
    output_back = (mm_nt(low, oe_ref[...]) * mix).astype(BF)
    ob_ref[...] = output_back
    ag_ref[...] = (mm_nt(low, w_ref[...]) + mm_nt(output_back, os_ref[...])).astype(BF)


def before_attention(parts, grad, middle, gain, gs, us, os, oe, w_output, seqs):
    tokens, model = middle.shape
    lanes = oe.shape[0]
    low = lambda n: jax.ShapeDtypeStruct((tokens, n), BF)
    return pl.pallas_call(
        functools.partial(before_attention_kernel, seqs, len(parts)),
        out_shape=[
            jax.ShapeDtypeStruct((tokens, model), F32),
            low(model), low(lanes), low(lanes), low(lanes), low(model),
        ],
        name="before_attention",
        cost_estimate=pl.CostEstimate(
            flops=2 * tokens * model * model, bytes_accessed=30 * tokens * model, transcendentals=0
        ),
    )(*parts, grad, middle, gain, gs, us, os, oe, w_output)


def last_grads_kernel(
    seqs, rank, info, pair_ref, cos_ref, sin_ref, ke_ref, ve_ref, normed_ref, nk_ref, nv_ref,
    kg_ref, vg_ref, kb_ref, vb_ref, late_ref, rows_ref,
):
    tokens, width = pair_ref.shape
    kv = width // 2
    lanes = ke_ref.shape[0]
    model = normed_ref.shape[1]
    mix = token_mask(tokens, lanes, seqs)
    cosine = cos_ref[...]
    sine = -sin_ref[...]
    for h in range(kv // HEAD_DIM):
        at = slice(h * HEAD_DIM, (h + 1) * HEAD_DIM)
        kg_ref[:, at] = turned(pair_ref[:, at].astype(F32), cosine, sine).astype(BF)
    vg_ref[...] = pair_ref[:, kv:]
    key_grad = kg_ref[...]
    value_grad = vg_ref[...]
    key_back = (mm_nt(key_grad, ke_ref[...]) * mix).astype(BF)
    value_back = (mm_nt(value_grad, ve_ref[...]) * mix).astype(BF)
    kb_ref[...] = key_back
    vb_ref[...] = value_back
    normed = normed_ref[...]
    rows_ref[:, :model] = mm_tn(key_back, normed)[:rank].astype(BF)
    rows_ref[:, model : 2 * model] = mm_tn(value_back, normed)[:rank].astype(BF)
    rows_ref[:, 2 * model : 2 * model + kv] = mm_tn(nk_ref[...], key_grad)[:rank].astype(BF)
    rows_ref[:, 2 * model + kv :] = mm_tn(nv_ref[...], value_grad)[:rank].astype(BF)
    parts = 2 * late_ref.shape[1]
    size = late_ref.shape[3]
    for p in range(parts):
        at = p ^ info[0]
        late_ref[lax.rem(at, 2), at // 2] = rows_ref[:, p * size : (p + 1) * size]


def last_grads(mine, pair_grad, cosine, sine, ke, ve, normed, nk, nv, seqs, rank, parts):
    tokens, width = pair_grad.shape
    lanes = ke.shape[0]
    model = normed.shape[1]
    low = lambda n: jax.ShapeDtypeStruct((tokens, n), BF)
    total = 2 * model + width
    operands = [pair_grad, cosine, sine, ke, ve, normed, nk, nv]
    results = [
        low(width // 2), low(width // 2), low(lanes), low(lanes),
        jax.ShapeDtypeStruct((2, parts // 2, rank, total // parts), BF),
    ]
    return pl.pallas_call(
        functools.partial(last_grads_kernel, seqs, rank),
        grid_spec=pltpu.PrefetchScalarGridSpec(
            num_scalar_prefetch=1,
            grid=(1,),
            in_specs=[pl.BlockSpec(a.shape, lambda g, i, n=a.ndim: (0,) * n) for a in operands],
            out_specs=[
                pl.BlockSpec(r.shape, lambda g, i, n=len(r.shape): (0,) * n) for r in results
            ],
            scratch_shapes=[pltpu.VMEM((rank, total), BF)],
        ),
        out_shape=results,
        name="last_grads",
        cost_estimate=pl.CostEstimate(
            flops=4 * tokens * model * 128, bytes_accessed=6 * tokens * model, transcendentals=0
        ),
    )(mine.reshape(1).astype(jnp.int32), *operands)


def with_blocks(kernel, name, seqs, index, blocks, operands, results):
    count = len(blocks)
    depth, lanes = blocks[0].shape
    inside = pl.BlockSpec(memory_space=pltpu.VMEM)
    results = list(results) + [jax.ShapeDtypeStruct((count * depth, lanes), BF)]
    return pl.pallas_call(
        functools.partial(kernel, seqs, count),
        grid_spec=pltpu.PrefetchScalarGridSpec(
            num_scalar_prefetch=1,
            grid=(1,),
            in_specs=[pl.BlockSpec(a.shape, lambda g, i, n=a.ndim: (0,) * n) for a in operands]
            + [pl.BlockSpec(memory_space=pl.ANY)] * count,
            out_specs=[pl.BlockSpec(r.shape, lambda g, i: (0, 0)) for r in results],
            scratch_shapes=[pltpu.SemaphoreType.DMA((count,))],
        ),
        out_shape=results,
        name=name,
        cost_estimate=pl.CostEstimate(
            flops=2 * operands[0].shape[0] * count * depth * lanes,
            bytes_accessed=4 * count * depth * lanes,
            transcendentals=0,
        ),
    )(index.reshape(1).astype(jnp.int32), *operands, *blocks)


def token_mask(tokens, lanes, seqs):
    row = lax.broadcasted_iota(jnp.int32, (tokens, lanes), 0) // (tokens // seqs)
    lane = lax.broadcasted_iota(jnp.int32, (tokens, lanes), 1) // ADAPTER_RANK
    return jnp.where(row == lane, adapter_scale, 0.0).astype(F32)


def feed_kernel(seqs, kinds, info, *refs):
    count = len(kinds)
    blocks = refs[:count]
    top_ref, bottom_ref, grad_top_ref, grad_bottom_ref = refs[count : count + 4]
    count += 4
    sgu_ref, ed_ref, wd_ref, eg_ref, eu_ref, sd_ref = refs[count : count + 6]
    peg_ref, peu_ref, psd_ref = refs[count + 6 : count + 9]
    out_ref, ng_ref, deg_ref, deu_ref, dsd_ref = refs[count + 9 : count + 14]
    acc_out, acc_ng, acc_nd, acc_bg, acc_bu, nar_g, nar_u, back_d, held, sems = refs[count + 14 :]
    chunk = pl.program_id(0)
    chunks = pl.num_programs(0)
    depth = blocks[0].shape[-2]
    size = wd_ref.shape[0]

    def copies(at, slot):
        found = []
        for n, (j, which) in enumerate(kinds):
            rows = pl.ds(pl.multiple_of((info[0] ^ j) * depth, depth), depth)
            lanes = pl.ds(pl.multiple_of(at * size, 128), size)
            if which is None:
                source, target = blocks[n].at[:, :, lanes], held.at[slot, :, rows, :]
            else:
                source, target = blocks[n].at[:, lanes], held.at[slot, info[1] ^ which, rows, :]
            found.append(pltpu.make_async_copy(source, target, sems.at[slot, n]))
        return found

    slot = lax.rem(chunk, 2)

    @pl.when(chunk == 0)
    def _():
        for copy in copies(chunk, slot):
            copy.start()

    @pl.when(chunk + 1 < chunks)
    def _():
        for copy in copies(chunk + 1, 1 - slot):
            copy.start()

    tokens = out_ref.shape[0]
    model = top_ref.shape[1]
    cols = sd_ref.shape[1]
    n2 = jnp.concatenate([top_ref[...], bottom_ref[...]], axis=0)
    g0 = jnp.concatenate([grad_top_ref[...], grad_bottom_ref[...]], axis=0)
    wg_ref = held.at[slot, 0]
    wu_ref = held.at[slot, 1]

    @pl.when(chunk == 0)
    def _():
        mix = token_mask(tokens, cols, seqs)
        narrow = mm(n2, sgu_ref[...])
        nar_g[...] = (narrow[:, :cols] * mix).astype(BF)
        nar_u[...] = (narrow[:, cols:] * mix).astype(BF)
        back_d[...] = (mm_nt(g0, ed_ref[...]) * mix).astype(BF)
        for acc in (acc_out, acc_ng, acc_nd, acc_bg, acc_bu):
            acc[...] = jnp.zeros(acc.shape, F32)

    for copy in copies(chunk, slot):
        copy.wait()
    narrow_g = nar_g[...]
    narrow_u = nar_u[...]
    narrow_b = back_d[...]
    gate = mm(n2, wg_ref[...]) + mm(narrow_g, eg_ref[...])
    upward = mm(n2, wu_ref[...]) + mm(narrow_u, eu_ref[...])
    sig = jax.nn.sigmoid(gate)
    act = gate * sig
    hidden = (act * upward).astype(BF)
    hidden_grad = mm_nt(g0, wd_ref[...]) + mm_nt(narrow_b, sd_ref[...])
    gate_grad = (hidden_grad * upward * (sig * (1.0 + gate * (1.0 - sig)))).astype(BF)
    up_grad = (hidden_grad * act).astype(BF)
    acc_out[...] += mm(hidden, wd_ref[...])
    acc_nd[...] += mm(hidden, sd_ref[...])
    acc_ng[...] += mm_nt(gate_grad, wg_ref[...]) + mm_nt(up_grad, wu_ref[...])
    acc_bg[...] += mm_nt(gate_grad, eg_ref[...])
    acc_bu[...] += mm_nt(up_grad, eu_ref[...])
    deg_ref[...] = peg_ref[...] + mm_tn(narrow_g, gate_grad)
    deu_ref[...] = peu_ref[...] + mm_tn(narrow_u, up_grad)
    dsd_ref[...] = psd_ref[...] + mm_tn(narrow_b, hidden)

    @pl.when(chunk == chunks - 1)
    def _():
        out_ref[:, :model] = acc_out[...].astype(BF)
        out_ref[:, model:] = jnp.concatenate([acc_nd[...], acc_nd[...]], axis=1).astype(BF)
        ng_ref[:, :model] = acc_ng[...].astype(BF)
        ng_ref[:, model:] = jnp.concatenate([acc_bg[...], acc_bu[...]], axis=1).astype(BF)


def feed(index, kinds, blocks, n2, g0, sgu, ed, wd, eg, eu, sd, previous, seqs, limit=768):
    tokens, model = 2 * n2[0].shape[0], n2[0].shape[1]
    count = len(blocks)
    hidden = wd.shape[0]
    cols = ed.shape[0]
    size = max(c for c in range(128, limit + 1, 128) if hidden % c == 0)
    anywhere = pl.BlockSpec(memory_space=pl.ANY)
    whole = lambda a: pl.BlockSpec(
        a.shape, lambda h, i: (0,) * a.ndim, pipeline_mode=pl.Buffered(1)
    )
    part = lambda a: pl.BlockSpec((a.shape[0], size), lambda h, i: (0, h))
    tall = lambda a: pl.BlockSpec((size, a.shape[1]), lambda h, i: (h, 0))
    fixed = lambda c: pl.BlockSpec((tokens, c), lambda h, i: (0, 0))
    grads = jax.ShapeDtypeStruct((cols, hidden), F32)
    return pl.pallas_call(
        functools.partial(feed_kernel, seqs, tuple(kinds)),
        grid_spec=pltpu.PrefetchScalarGridSpec(
            num_scalar_prefetch=1,
            grid=(hidden // size,),
            in_specs=[anywhere] * count
            + [whole(n2[0]), whole(n2[1]), whole(g0[0]), whole(g0[1]), whole(sgu), whole(ed), tall(wd)]
            + [part(eg), part(eu), tall(sd), part(grads), part(grads), part(grads)],
            out_specs=[fixed(model + 2 * cols), fixed(model + 2 * cols)] + [part(grads)] * 3,
            scratch_shapes=[
                pltpu.VMEM((tokens, model), F32),
                pltpu.VMEM((tokens, model), F32),
                pltpu.VMEM((tokens, cols), F32),
                pltpu.VMEM((tokens, cols), F32),
                pltpu.VMEM((tokens, cols), F32),
                pltpu.VMEM((tokens, cols), BF),
                pltpu.VMEM((tokens, cols), BF),
                pltpu.VMEM((tokens, cols), BF),
                pltpu.VMEM((2, 2, model, size), BF),
                pltpu.SemaphoreType.DMA((2, count)),
            ],
        ),
        out_shape=[
            jax.ShapeDtypeStruct((tokens, model + 2 * cols), BF),
            jax.ShapeDtypeStruct((tokens, model + 2 * cols), BF),
            grads, grads, grads,
        ],
        name="feed",
        cost_estimate=pl.CostEstimate(
            flops=12 * tokens * (model + cols) * hidden,
            bytes_accessed=6 * model * hidden,
            transcendentals=tokens * hidden,
        ),
    )(index, *blocks, *n2, *g0, sgu, ed, wd, eg, eu, sd, *previous)


def assemble_kernel(count, info, *refs):
    blocks = refs[:count]
    out_ref, held, blank, in_sem, out_sem = refs[count:]
    depth = blocks[0].shape[0]
    rest = out_ref.shape[0] - count * depth
    arrive = []
    leave = []
    for j in range(count):
        arrive.append(pltpu.make_async_copy(blocks[j], held.at[j], in_sem.at[j]))
        at = pl.multiple_of((info[0] ^ j) * depth, depth)
        leave.append(
            pltpu.make_async_copy(held.at[j], out_ref.at[pl.ds(at, depth), :], out_sem.at[j])
        )
    for copy in arrive:
        copy.start()
    if rest:
        blank[...] = jnp.zeros(blank.shape, BF)
        last = pltpu.make_async_copy(blank, out_ref.at[count * depth :, :], out_sem.at[count])
        last.start()
    for one, two in zip(arrive, leave):
        one.wait()
        two.start()
    for copy in leave:
        copy.wait()
    if rest:
        last.wait()


def assemble(index, blocks, rows):
    count = len(blocks)
    depth, lanes = blocks[0].shape
    anywhere = pl.BlockSpec(memory_space=pl.ANY)
    return pl.pallas_call(
        functools.partial(assemble_kernel, count),
        grid_spec=pltpu.PrefetchScalarGridSpec(
            num_scalar_prefetch=1,
            grid=(1,),
            in_specs=[anywhere] * count,
            out_specs=anywhere,
            scratch_shapes=[
                pltpu.VMEM((count, depth, lanes), BF),
                pltpu.VMEM((max(rows - count * depth, 16), lanes), BF),
                pltpu.SemaphoreType.DMA((count,)),
                pltpu.SemaphoreType.DMA((count + 1,)),
            ],
        ),
        out_shape=jax.ShapeDtypeStruct((rows, lanes), BF),
        name="assemble",
        cost_estimate=pl.CostEstimate(
            flops=0, bytes_accessed=4 * rows * lanes, transcendentals=0
        ),
    )(index.reshape(1).astype(jnp.int32), *blocks)


def expand_kernel(rank, hidden, padded, seq_n, early, kinds, both_ref, select_ref, *outs):
    pair = pl.program_id(0)
    select = select_ref[...]
    lanes = -(-hidden // 128) * 128
    width = both_ref.shape[2] - early
    for q in range(2):
        for i, out_ref in enumerate(outs[:3]):
            groups = []
            for f in range(2):
                at = i * padded
                left = lanes
                pieces = []
                while left:
                    z, low = divmod(at, width)
                    take = min(left, width - low)
                    device = pair * 4 * seq_n + (q * 2 + f) * seq_n + z
                    pieces.append(both_ref[device, :rank, early + low : early + low + take])
                    at += take
                    left -= take
                groups.append(jnp.concatenate(pieces, axis=1))
            rows = jnp.concatenate(groups, axis=0)
            if i < 2:
                out_ref[:, q * hidden : (q + 1) * hidden] = mm_tn(select, rows)[:, :hidden]
            else:
                out_ref[q * hidden : (q + 1) * hidden, :] = mm_tn(rows, select)[:hidden]

    @pl.when(pair == 0)
    def _():
        half = both_ref.shape[0] // 2
        for i, (out_ref, shrink) in enumerate(zip(outs[3:], kinds)):
            rows = jnp.concatenate(
                [
                    jnp.concatenate(
                        [both_ref[f * half + 2 * i + w, :rank, :early] for w in range(2)], axis=1
                    )
                    for f in range(2)
                ],
                axis=0,
            )
            out_ref[...] = mm_tn(rows, select) if shrink else mm_tn(select, rows)


def expand_all(both, select, rank, hidden, padded, seq_n, chips, early, kinds):
    cols = select.shape[1]
    model = 2 * early
    wide = lambda n: jax.ShapeDtypeStruct((cols, n), F32)
    tall = lambda n: jax.ShapeDtypeStruct((n, cols), F32)
    fixed = [tall(model) if shrink else wide(model) for shrink in kinds]
    return pl.pallas_call(
        functools.partial(expand_kernel, rank, hidden, padded, seq_n, early, kinds),
        grid=(chips // 2,),
        in_specs=[
            pl.BlockSpec(both.shape, lambda p: (0, 0, 0), pipeline_mode=pl.Buffered(1)),
            pl.BlockSpec(select.shape, lambda p: (0, 0)),
        ],
        out_specs=[
            pl.BlockSpec((cols, 2 * hidden), lambda p: (0, p)),
            pl.BlockSpec((cols, 2 * hidden), lambda p: (0, p)),
            pl.BlockSpec((2 * hidden, cols), lambda p: (p, 0)),
        ]
        + [pl.BlockSpec(one.shape, lambda p: (0, 0)) for one in fixed],
        out_shape=[wide(chips * hidden), wide(chips * hidden), tall(chips * hidden)] + fixed,
        name="expand",
        cost_estimate=pl.CostEstimate(
            flops=6 * cols * chips * hidden * select.shape[0],
            bytes_accessed=12 * cols * chips * hidden,
            transcendentals=0,
        ),
    )(both, select)


def after(value, *needed):
    return lax.optimization_barrier((value, needed))[0]


def body(
    inputs, cotangent, span_order, adapter_ids, first_gain, second_gain,
    query_weight, key_weight, value_weight, output_weight, gate_weight, up_weight, down_weight,
    query_bias, key_bias, value_bias,
    query_reduce_factors, query_lift_factors, key_reduce_factors, key_lift_factors,
    value_reduce_factors, value_lift_factors, output_reduce_factors, output_lift_factors,
    gate_reduce_factors, gate_lift_factors, upper_reduce_factors, upper_lift_factors,
    down_reduce_factors, down_lift_factors,
):
    seq_n = lax.axis_size("seq")
    cp_n = lax.axis_size("cp")
    fsdp_n = lax.axis_size("fsdp")
    plane = fsdp_n * cp_n
    chips = plane // 2
    group = lax.axis_index("fsdp")
    me = group * cp_n + lax.axis_index("cp")
    chip = me // 2
    core = me % 2
    seqs, tok_rows, model = inputs.shape
    tokens = seqs * tok_rows
    cols = query_reduce_factors.shape[1]
    kv_width = key_weight.shape[1]
    length = tok_rows * seq_n * cp_n
    spans = span_order.shape[1]
    span_len = length // spans
    hidden_all = gate_weight.shape[1]
    hq = hidden_all // chips
    hp = -(-hq // 256) * 256
    pad = hp - hq
    rank = seqs * ADAPTER_RANK
    lanes = -(-rank // 64) * 64

    def swap(value, k):
        return lax.ppermute(value, PLANE, [(i, i ^ k) for i in range(plane)])

    def swap_seq(value, k):
        return lax.ppermute(value, "seq", [(i, i ^ k) for i in range(seq_n)])

    first_row = (lax.axis_index("cp") * seq_n + lax.axis_index("seq")) * tok_rows
    own = lax.dynamic_slice_in_dim(span_order, first_row // span_len, 1, 1)[:, 0]
    shift = first_row % span_len
    cp_index = lax.axis_index("cp")
    seq_index = lax.axis_index("seq")
    info = jnp.concatenate(
        [span_order.reshape(-1), own, jnp.stack([shift, cp_index])]
    ).astype(jnp.int32)
    places = own[:, None] * span_len + shift + jnp.arange(tok_rows, dtype=jnp.int32)[None, :]
    cosine, sine_table = rotary_tables(places.reshape(tokens))
    sine_signed = jnp.where(
        jnp.arange(HEAD_DIM, dtype=jnp.int32) < HEAD_DIM // 2, -sine_table, sine_table
    )
    flat_cosine = cosine
    cosine = cosine[:, None, :]
    sine_table = sine_table[:, None, :]
    lane = jnp.arange(lanes, dtype=jnp.int32)

    def chosen(ids):
        column = jnp.repeat(ids, ADAPTER_RANK) * ADAPTER_RANK + lane[:rank] % ADAPTER_RANK
        column = jnp.pad(column, (0, lanes - rank), constant_values=-1)
        return (jnp.arange(cols, dtype=jnp.int32)[:, None] == column[None, :]).astype(BF)

    ids_wide = jnp.broadcast_to(
        jnp.pad(adapter_ids, (0, -seqs % 8)).astype(F32)[:, None], (seqs + -seqs % 8, 128)
    )
    select = [chosen(adapter_ids)]
    for f in range(1, fsdp_n):
        select.append(chosen(swap(ids_wide, f * cp_n)[:seqs, 0].astype(jnp.int32)))
    mixing = token_mask(tokens, lanes, seqs)

    def shrink_of(value, f=0):
        return mm(value, select[f]).astype(BF)

    def expand_of(value, f=0):
        return mm_tn(select[f], value).astype(BF)

    w_kv = lax.all_gather(
        jnp.concatenate([key_weight, value_weight], axis=1), PLANE, axis=0, tiled=True
    )
    rows_q = [query_weight] + [swap(query_weight, 2 * k) for k in range(1, chips)]

    def by_chip(value):
        return jnp.stack(
            [
                jnp.pad(value[:, hq * c : hq * (c + 1)], ((0, 0), (0, pad)))
                for c in range(chips)
            ]
        )

    gate_up = jnp.stack([by_chip(gate_weight), by_chip(up_weight)], axis=1)
    depth = gate_weight.shape[0]
    parts = [lax.dynamic_index_in_dim(gate_up, chip ^ k, 0, keepdims=False) for k in range(chips)]

    low_in = inputs.reshape(tokens, model)
    resid_in = low_in.astype(F32)
    first_scales = first_gain.astype(F32)
    second_scales = second_gain.astype(F32)
    grad_low = cotangent.reshape(tokens, model)
    w_kv, parts, rows_q = lax.optimization_barrier((w_kv, parts, rows_q))
    rows_o = [output_weight] + [swap(after(output_weight, rows_q), 2 * k) for k in range(1, chips)]
    blocks = {}
    w_key = w_kv[:, :kv_width]
    w_value = w_kv[:, kv_width:]

    query_shrink, key_shrink, value_shrink, output_shrink = [
        shrink_of(value)
        for value in (
            query_reduce_factors, key_reduce_factors, value_reduce_factors, output_reduce_factors,
        )
    ]
    query_expand, key_expand, value_expand, output_expand = [
        expand_of(value)
        for value in (
            query_lift_factors, key_lift_factors, value_lift_factors, output_lift_factors,
        )
    ]
    grad_halves = (grad_low[: tokens // 2], grad_low[tokens // 2 :])
    w_kv, output_shrink, output_expand, query_shrink, query_expand, grad_halves = (
        lax.optimization_barrier(
            (w_kv, output_shrink, output_expand, query_shrink, query_expand, grad_halves)
        )
    )

    def swap_both(pair, k):
        return tuple(swap(half, k) for half in pair)

    g0_pieces = {
        k: swap_both(after(grad_halves, rows_q), 2 * k) for k in range(1, chips) if 2 * k % cp_n == 0
    }

    def narrowed(value, shrink):
        return (mm(value, shrink) * mixing).astype(BF)

    normed, key_narrow, value_narrow, pair = keys_values(
        low_in, first_scales[None], w_kv, jnp.concatenate([key_shrink, value_shrink], axis=1),
        key_expand, value_expand,
        jnp.concatenate([key_bias, value_bias]).astype(F32)[None], flat_cosine, sine_signed, seqs,
    )
    pair_all = lax.all_gather(
        pair.reshape(seqs, tok_rows, 2 * kv_width), ("cp", "seq"), axis=1, tiled=True
    )

    def both_cores(rows):
        found = []
        for part in rows:
            found += [part, swap(part, 1)]
        return found

    query_rot, query_narrow, w_query = with_blocks(
        queries_kernel, "queries", seqs, me, after(both_cores(rows_q), pair),
        [
            after(normed, rows_o, g0_pieces), query_shrink, query_expand, query_bias.astype(F32)[None], flat_cosine,
            sine_signed,
        ],
        [
            jax.ShapeDtypeStruct((tokens, model), BF),
            jax.ShapeDtypeStruct((tokens, lanes), BF),
        ],
    )

    late_lift = after(
        (
        gate_lift_factors, upper_lift_factors, down_reduce_factors, down_lift_factors,
        gate_reduce_factors, upper_reduce_factors,
        ),
        query_rot,
    )
    gate_shrink, up_shrink = shrink_of(late_lift[4]), shrink_of(late_lift[5])
    down_expand = expand_of(late_lift[3])
    reduce_factors = [
        (
            jnp.concatenate([shrink_of(late_lift[4], f), shrink_of(late_lift[5], f)], axis=1),
            expand_of(late_lift[3], f),
        )
        for f in range(fsdp_n)
    ]
    late_down, late_gate, late_up = late_lift[2], late_lift[0], late_lift[1]
    shrink_d = jnp.pad(
        lax.dynamic_slice_in_dim(late_down, chip * hq, hq, 0), ((0, pad), (0, 0))
    )
    lift_g = lax.dynamic_index_in_dim(by_chip(late_gate), chip, 0, keepdims=False)
    lift_u = lax.dynamic_index_in_dim(by_chip(late_up), chip, 0, keepdims=False)
    lift_factors = [(expand_of(lift_g, f), expand_of(lift_u, f)) for f in range(fsdp_n)]
    feed_factors = [
        reduce_factors[f] + lift_factors[f] + (shrink_of(shrink_d, f),) for f in range(fsdp_n)
    ]
    down_rows = [down_weight, swap(after(down_weight, query_rot), 1)]
    w_down = assemble(core, after(down_rows, query_rot), hp)
    attended, lse = attend(
        info, after(query_rot, w_down, feed_factors, gate_shrink, up_shrink, down_expand),
        pair_all, seqs, spans, span_len,
    )
    for k in range(1, chips):
        blocks[k] = swap(after(parts[k], rows_o), 2 * k)
    output_blocks = both_cores(after(rows_o, query_rot))
    middle, normed_two, normed_top, normed_bottom, output_narrow, w_output = with_blocks(
        outputs_kernel, "outputs", seqs, me, output_blocks,
        [attended, low_in, second_scales[None], output_shrink, output_expand],
        [
            jax.ShapeDtypeStruct((tokens, model), F32),
            jax.ShapeDtypeStruct((tokens, model), BF),
            jax.ShapeDtypeStruct((tokens // 2, model), BF),
            jax.ShapeDtypeStruct((tokens // 2, model), BF),
            jax.ShapeDtypeStruct((tokens, lanes), BF),
        ],
    )

    kinds = [(0, None), (1, None)]
    wide = [parts[0], swap(after(parts[0], query_rot), 1)]
    for k in range(1, chips):
        kinds += [(2 * k, None), (2 * k + 1, None)]
        wide += [blocks[k], swap(after(blocks[k], middle), 1)]
    feed_index = jnp.stack([me, core]).astype(jnp.int32)

    g0_pieces[0] = grad_halves
    normed_halves = (normed_top, normed_bottom)
    n2_pieces = [normed_halves]
    for k in range(1, chips):
        if k < 3:
            n2_pieces.append(swap_both(after(normed_halves, wide), 2 * k))
            if k not in g0_pieces:
                g0_pieces[k] = swap_both(after(grad_halves, wide), 2 * k)
    zero = jnp.zeros((lanes, hp), F32)
    sums = [(zero, zero, zero)] * fsdp_n
    out_raw = []
    grad_parts = []
    early_first = sorted(range(1, chips), key=lambda k: (k > 2, -k if k < 3 else k)) + [0]
    for k in early_first:
        f = 2 * k // cp_n
        sgu, ed, eg, eu, sd = feed_factors[f]
        if len(out_raw) == 1:
            for other in range(3, chips):
                for pieces in (n2_pieces, g0_pieces):
                    first, second, own_pair = after((pieces[2], pieces[1], pieces[0]), out_raw[-1])
                    if other == 3:
                        piece = (swap(first[0], 2), swap(second[1], 4))
                    else:
                        piece = swap_both(own_pair, 2 * other)
                    if pieces is n2_pieces:
                        n2_pieces.append(piece)
                    else:
                        g0_pieces[other] = piece
        if out_raw:
            sums[f] = after(sums[f], out_raw[-1], [] if k else grad_parts[:-1])
        out_k, ng_k, *sums[f] = feed(
            feed_index, kinds, wide, n2_pieces[k], g0_pieces[k], sgu, ed, w_down, eg, eu, sd, sums[f], seqs
        )
        out_raw.append(out_k)
        grad_parts.append(ng_k if k == 0 else swap(ng_k, 2 * k))

    def pack(values, tiles):
        value = jnp.concatenate([value[:rank].astype(BF) for value in values], axis=1)
        return jnp.pad(value, ((0, 0), (0, -value.shape[1] % (128 * tiles))))

    middle_grad, middle_low, gate_back, up_back, output_back, attended_grad = before_attention(
        grad_parts, grad_low, middle, second_scales[None],
        gate_shrink, up_shrink, output_shrink, output_expand, w_output, seqs,
    )

    def narrowed_back(grad, expand):
        return (mm_nt(grad, expand) * mixing).astype(BF)

    out_raw = after(out_raw, middle_low)
    out_of = dict(zip(early_first, out_raw))
    out_parts = [out_of[0]] + [swap(out_of[k], 2 * k) for k in range(1, min(chips, 3))]
    query_rot_grad, pair_part = attend_back(
        info, query_rot, attended_grad, attended, pair_all, lse, seqs, spans, span_len
    )
    out_parts += [
        swap(after(out_of[k], pair_part), 2 * k) for k in range(3, chips)
    ]
    pair_grad = lax.psum_scatter(
        after(pair_part, out_parts[:3]), ("cp", "seq"), scatter_dimension=1, tiled=True
    ).reshape(tokens, 2 * kv_width)
    out_sum = sum(part.astype(F32) for part in out_parts)

    down_narrow = (out_sum[:, model : model + lanes] * mixing).astype(BF)
    result = middle + (out_sum[:, :model] + mm(down_narrow, down_expand))
    outputs = result.astype(BF).reshape(seqs, tok_rows, model)

    query_rot_grad, sums, middle_late, output_back, gate_back, up_back = after(
        (query_rot_grad, sums, middle_low, output_back, gate_back, up_back), out_parts[:3]
    )
    cosine, sine_table = after((cosine, sine_table), pair_part)
    query_grad = (
        unrotate(
            query_rot_grad.reshape(tokens, -1, HEAD_DIM).astype(F32), cosine, sine_table
        )
        .reshape(tokens, model)
        .astype(BF)
    )
    query_back = narrowed_back(query_grad, query_expand)
    query_in = mm_nt(query_grad, w_query) + mm_nt(query_back, query_shrink)

    def halves(value, index, exchange):
        span = 1
        while value.shape[0] > 1:
            split = value.reshape((value.shape[0] // 2, 2) + value.shape[1:])
            bit = index // span % 2
            keep = lax.dynamic_index_in_dim(split, bit, 1, keepdims=False)
            give = lax.dynamic_index_in_dim(split, 1 - bit, 1, keepdims=False)
            value = (keep.astype(F32) + exchange(give, span).astype(F32)).astype(BF)
            span *= 2
        return value[0]

    stacked = jnp.stack([pack(sums[f], seq_n) for f in range(fsdp_n)])
    feed_wide = stacked.shape[2]

    def groups_of(parity):
        return jnp.stack(
            [
                lax.dynamic_index_in_dim(stacked, (2 * j + parity) ^ group, 0, keepdims=False)
                for j in range(fsdp_n // 2)
            ]
        )

    feed_half = groups_of(core).astype(F32) + swap(groups_of(1 - core), 1).astype(F32)
    feed_half = feed_half.reshape(fsdp_n // 2 * rank, seq_n, feed_wide // seq_n).astype(BF)
    feed_half = feed_half.transpose(1, 0, 2)
    feed_piece = halves(feed_half, seq_index, swap_seq)
    ways = cp_n * seq_n
    early = pack(
        [
            mm_tn(output_back, attended),
            mm_tn(gate_back, normed_two),
            mm_tn(up_back, normed_two),
            mm_tn(output_narrow, middle_late),
            mm_tn(down_narrow, grad_low),
            mm_tn(query_back, normed),
            mm_tn(query_narrow, query_grad),
        ],
        ways,
    )
    early = early.reshape(rank, cp_n, seq_n, -1).transpose(1, 2, 0, 3)
    early = halves(early, cp_index, swap)
    early = halves(early, seq_index, swap_seq)
    early_cols = early.shape[1]
    both = jnp.concatenate([jnp.pad(early, ((0, feed_piece.shape[0] - rank), (0, 0))), feed_piece], axis=1)
    both = lax.all_gather(after(both, pair_grad), EVERY, axis=0, tiled=False)

    key_grad, value_grad, key_back, value_back, late = last_grads(
        cp_index, pair_grad, flat_cosine, sine_signed, key_expand, value_expand, normed,
        key_narrow, value_narrow, seqs, rank, cp_n,
    )
    late_wide = late.shape[3] * cp_n
    total = late[0].astype(F32) + swap(late[1], 1).astype(F32)
    span = 2
    while span < cp_n:
        total = total[0::2] + swap(total[1::2].astype(BF), span).astype(F32)
        span *= 2
    late = total[0].astype(BF)
    total = late.astype(F32)
    for k in range(1, seq_n):
        total = total + swap_seq(late, k).astype(F32)
    late = total.astype(BF)[None]
    for step in [span_k for span_k in (2**i for i in range(1, 30)) if span_k < plane] + [1]:
        late = jnp.concatenate([late, swap(late, step)], axis=0)

    normed_grad = (
        query_in
        + mm_nt(key_grad, w_key)
        + mm_nt(value_grad, w_value)
        + mm_nt(key_back, key_shrink)
        + mm_nt(value_back, value_shrink)
    )
    input_grad = middle_grad + norm_backward(resid_in, first_scales, normed_grad)

    came = [0]
    for step in [span_k for span_k in (2**i for i in range(1, 30)) if span_k < plane] + [1]:
        came = came + [c ^ step for c in came]
    inverse = [came.index(c) for c in range(plane)]
    late = jnp.take(
        late, jnp.asarray(inverse, jnp.int32)[jnp.arange(plane, dtype=jnp.int32) ^ me], axis=0
    )
    late = late.reshape(fsdp_n, cp_n, rank, late_wide // cp_n)
    late = late.transpose(0, 2, 1, 3).reshape(fsdp_n * rank, late_wide)

    order = jnp.arange(fsdp_n, dtype=jnp.int32) ^ group
    select_all = (
        jnp.take(jnp.stack(select), order, axis=0)[:, :, :rank]
        .transpose(0, 2, 1)
        .reshape(fsdp_n * rank, cols)
    )
    shrink_grad = lambda value: mm_tn(value, select_all)
    expand_grad = lambda value: mm_tn(select_all, value)

    late_of = lambda i: late[:, model * i : model * (i + 1)]
    tail_of = lambda i: late[:, model * 2 + kv_width * i : model * 2 + kv_width * (i + 1)]
    order_kinds = (True, True, True, False, False, True, False)
    if fsdp_n == 2 and 2 * hq % 128 == 0 and 2 * early_cols == model:
        expanded = expand_all(
            both, select_all, rank, hq, hp, seq_n, chips, early_cols, order_kinds
        )
    else:
        early_full = both[:, :rank, :early_cols].reshape(fsdp_n, ways, rank, early_cols)
        early_full = early_full.transpose(0, 2, 1, 3).reshape(fsdp_n * rank, ways * early_cols)
        feed_full = both[:, :, early_cols:].reshape(
            fsdp_n, cp_n // 2, 2, seq_n, fsdp_n // 2, rank, feed_wide // seq_n
        ).transpose(4, 2, 5, 0, 1, 3, 6)
        feed_full = feed_full.reshape(fsdp_n * rank, chips, feed_wide)
        expanded = []
        for i, shrink in enumerate((False, False, True) + order_kinds):
            if i < 3:
                rows = feed_full[:, :, i * hp : i * hp + hq].reshape(fsdp_n * rank, hidden_all)
            else:
                rows = early_full[:, model * (i - 3) : model * (i - 2)]
            expanded.append(shrink_grad(rows) if shrink else expand_grad(rows))

    return (
        outputs,
        input_grad.reshape(seqs, tok_rows, model),
        expanded[8],
        expanded[9],
        shrink_grad(late_of(0)),
        expand_grad(tail_of(0)),
        shrink_grad(late_of(1)),
        expand_grad(tail_of(1)),
        expanded[3],
        expanded[6],
        expanded[4],
        expanded[0],
        expanded[5],
        expanded[1],
        expanded[2],
        expanded[7],
    )


def solution(mesh):
    tokens_spec = P("fsdp", ("cp", "seq"), None)
    weight_spec = P(("fsdp", "cp"), None)
    placed = (
        (tokens_spec, tokens_spec, P("fsdp", None), P("fsdp"), P(), P())
        + (weight_spec,) * 7
        + (P(),) * 17
    )
    return jax.shard_map(
        body,
        mesh=mesh,
        in_specs=placed,
        out_specs=(tokens_spec, tokens_spec) + (P(),) * 14,
        check_vma=False,
    )
```

```python
import functools
import math

import jax
import jax.numpy as jnp
from jax import lax
from jax.experimental import pallas as pl
from jax.experimental.pallas import tpu as pltpu
from jax.sharding import PartitionSpec as P

HEAD_DIM = 128
ADAPTER_RANK = 16
epsilon = 1e-06
adapter_scale = 0.5
rotary_base = 1000000.0
masked_score = -1e30
PLANE = ("fsdp", "cp")
EVERY = ("fsdp", "cp", "seq")
BF = jnp.bfloat16
F32 = jnp.float32


def rotary_tables(positions):
    halfway = HEAD_DIM // 2
    frequency = jnp.exp(
        jnp.arange(halfway, dtype=jnp.float32) * (-2.0 * math.log(rotary_base) / HEAD_DIM)
    )
    angles = positions.astype(jnp.float32)[..., None] * frequency
    angles = jnp.concatenate([angles, angles], axis=-1)
    return (jnp.cos(angles), jnp.sin(angles))


def rotate(values, cosine, sine_table):
    halfway = values.shape[-1] // 2
    turned = jnp.concatenate([-values[..., halfway:], values[..., :halfway]], axis=-1)
    return values * cosine + turned * sine_table


def unrotate(gradient, cosine, sine_table):
    halfway = gradient.shape[-1] // 2
    scaled = gradient * sine_table
    turned = jnp.concatenate([scaled[..., halfway:], -scaled[..., :halfway]], axis=-1)
    return gradient * cosine + turned


def mm(left, right):
    return jnp.dot(left, right, preferred_element_type=jnp.float32)


def mm_nt(left, right):
    return lax.dot_general(
        left, right, (((1,), (1,)), ((), ())), preferred_element_type=jnp.float32
    )


def mm_tn(left, right):
    return lax.dot_general(
        left, right, (((0,), (0,)), ((), ())), preferred_element_type=jnp.float32
    )


def norm_forward(values, scales):
    return values * lax.rsqrt(jnp.mean(values * values, axis=-1, keepdims=True) + epsilon) * scales


def norm_backward(values, scales, gradient):
    inverse = lax.rsqrt(jnp.mean(values * values, axis=-1, keepdims=True) + epsilon)
    weighted = gradient * scales
    inner_sum = jnp.mean(weighted * values, axis=-1, keepdims=True)
    return inverse * weighted - values * (inverse * inverse * inverse) * inner_sum


def heads_to_rows(block):
    count = block.shape[1] // HEAD_DIM
    return jnp.concatenate(
        [block[:, HEAD_DIM * j : HEAD_DIM * (j + 1)] for j in range(count)], axis=0
    )


def rows_to_heads(rows, tokens):
    count = rows.shape[0] // tokens
    return jnp.concatenate([rows[tokens * j : tokens * (j + 1)] for j in range(count)], axis=1)


def attend_kernel(spans, span_len, tokens, info, q_ref, k_ref, v_ref, o_ref, lse_ref, m_ref, l_ref, acc_ref):
    seq = pl.program_id(0)
    seqs = pl.num_programs(0)
    own = info[seqs * spans + seq]
    shift = info[seqs * spans + seqs]
    scale = math.log2(math.e) / math.sqrt(HEAD_DIM)
    queries = heads_to_rows(q_ref[...])
    m_ref[...] = jnp.full(m_ref.shape, masked_score, F32)
    l_ref[...] = jnp.zeros(l_ref.shape, F32)
    acc_ref[...] = jnp.zeros(acc_ref.shape, F32)

    def update(j, masked):
        rows = pl.ds(pl.multiple_of(j * span_len, span_len), span_len)
        scores = mm_nt(k_ref[0, rows, :], queries) * scale
        if masked:
            key_at = lax.broadcasted_iota(jnp.int32, scores.shape, 0)
            query_at = shift + lax.rem(lax.broadcasted_iota(jnp.int32, scores.shape, 1), tokens)
            scores = jnp.where(key_at <= query_at, scores, masked_score)
        old = m_ref[...]
        top = jnp.maximum(old, jnp.max(scores, axis=0, keepdims=True))
        expo = jnp.exp2(scores - top)
        alpha = jnp.exp2(old - top)
        l_ref[...] = l_ref[...] * alpha + jnp.sum(expo, axis=0, keepdims=True)
        acc_ref[...] = acc_ref[...] * alpha + mm_tn(v_ref[0, rows, :], expo.astype(BF))
        m_ref[...] = top

    def step(j, carry):
        other = info[seq * spans + j]

        @pl.when(other < own)
        def _():
            update(j, False)

        @pl.when(other == own)
        def _():
            update(j, True)

        return carry

    lax.fori_loop(0, spans, step, 0)
    total = l_ref[...]
    out = jnp.transpose(acc_ref[...] / total)
    o_ref[...] = rows_to_heads(out.astype(BF), tokens)
    lse_ref[0] = jnp.broadcast_to(m_ref[...] + jnp.log2(total), lse_ref.shape[1:])


def attend(info, queries, pairs, seqs, spans, span_len):
    tokens = queries.shape[0] // seqs
    length = pairs.shape[1]
    kv_heads = pairs.shape[2] // (2 * HEAD_DIM)
    width = queries.shape[1] // kv_heads
    rows = tokens * (width // HEAD_DIM)
    grid_spec = pltpu.PrefetchScalarGridSpec(
        num_scalar_prefetch=1,
        grid=(seqs, kv_heads),
        in_specs=[
            pl.BlockSpec((tokens, width), lambda s, h, i: (s, h)),
            pl.BlockSpec((1, length, HEAD_DIM), lambda s, h, i: (s, 0, h)),
            pl.BlockSpec((1, length, HEAD_DIM), lambda s, h, i: (s, 0, kv_heads + h)),
        ],
        out_specs=[
            pl.BlockSpec((tokens, width), lambda s, h, i: (s, h)),
            pl.BlockSpec((1, 8, rows), lambda s, h, i: (s * kv_heads + h, 0, 0)),
        ],
        scratch_shapes=[pltpu.VMEM((1, rows), F32)] * 2 + [pltpu.VMEM((HEAD_DIM, rows), F32)],
    )
    work = seqs * kv_heads * rows * length
    return pl.pallas_call(
        functools.partial(attend_kernel, spans, span_len, tokens),
        grid_spec=grid_spec,
        out_shape=[
            jax.ShapeDtypeStruct(queries.shape, BF),
            jax.ShapeDtypeStruct((seqs * kv_heads, 8, rows), F32),
        ],
        name="attend",
        cost_estimate=pl.CostEstimate(
            flops=4 * work * HEAD_DIM, bytes_accessed=pairs.size * 2, transcendentals=work
        ),
    )(info, queries, pairs, pairs)


def attend_back_kernel(
    spans, span_len, tokens, kv_heads,
    info, q_ref, do_ref, o_ref, k_ref, v_ref, lse_ref, dq_ref, dkv_ref, acc_ref,
):
    seq = pl.program_id(0)
    head = pl.program_id(1)
    seqs = pl.num_programs(0)
    own = info[seqs * spans + seq]
    shift = info[seqs * spans + seqs]
    root = 1.0 / math.sqrt(HEAD_DIM)
    scale = math.log2(math.e) * root
    queries = heads_to_rows(q_ref[...])
    grads = heads_to_rows(do_ref[...])
    results = heads_to_rows(o_ref[...])
    inner = jnp.sum(
        jnp.transpose(grads.astype(F32) * results.astype(F32)), axis=0, keepdims=True
    )
    lse = lse_ref[0, :1, :]
    acc_ref[...] = jnp.zeros(acc_ref.shape, F32)
    key_lane = pl.multiple_of(head * HEAD_DIM, HEAD_DIM)
    val_lane = pl.multiple_of((kv_heads + head) * HEAD_DIM, HEAD_DIM)

    def store(j, key_grad, value_grad):
        rows = pl.ds(pl.multiple_of(j * span_len, span_len), span_len)
        dkv_ref[0, rows, pl.ds(key_lane, HEAD_DIM)] = key_grad
        dkv_ref[0, rows, pl.ds(val_lane, HEAD_DIM)] = value_grad

    def update(j, masked):
        rows = pl.ds(pl.multiple_of(j * span_len, span_len), span_len)
        keys = k_ref[0, rows, :]
        prob = jnp.exp2(mm_nt(keys, queries) * scale - lse)
        if masked:
            key_at = lax.broadcasted_iota(jnp.int32, prob.shape, 0)
            query_at = shift + lax.rem(lax.broadcasted_iota(jnp.int32, prob.shape, 1), tokens)
            prob = jnp.where(key_at <= query_at, prob, 0.0)
        prob_grad = mm_nt(v_ref[0, rows, :], grads)
        score_grad = (prob * (prob_grad - inner)).astype(BF)
        acc_ref[...] += mm_tn(score_grad, keys)
        store(
            j, (mm(score_grad, queries) * root).astype(BF), mm(prob.astype(BF), grads).astype(BF)
        )

    def step(j, carry):
        other = info[seq * spans + j]

        @pl.when(other < own)
        def _():
            update(j, False)

        @pl.when(other == own)
        def _():
            update(j, True)

        @pl.when(other > own)
        def _():
            zero = jnp.zeros((span_len, HEAD_DIM), BF)
            store(j, zero, zero)

        return carry

    lax.fori_loop(0, spans, step, 0)
    dq_ref[...] = rows_to_heads((acc_ref[...] * root).astype(BF), tokens)


def attend_back(info, queries, grads, results, pairs, lse, seqs, spans, span_len):
    tokens = queries.shape[0] // seqs
    length = pairs.shape[1]
    kv_heads = pairs.shape[2] // (2 * HEAD_DIM)
    width = queries.shape[1] // kv_heads
    rows = tokens * (width // HEAD_DIM)
    row = pl.BlockSpec((tokens, width), lambda s, h, i: (s, h))
    block = (1, length, pairs.shape[2])
    grid_spec = pltpu.PrefetchScalarGridSpec(
        num_scalar_prefetch=1,
        grid=(seqs, kv_heads),
        in_specs=[
            row,
            row,
            row,
            pl.BlockSpec((1, length, HEAD_DIM), lambda s, h, i: (s, 0, h)),
            pl.BlockSpec((1, length, HEAD_DIM), lambda s, h, i: (s, 0, kv_heads + h)),
            pl.BlockSpec((1, 8, rows), lambda s, h, i: (s * kv_heads + h, 0, 0)),
        ],
        out_specs=[row, pl.BlockSpec(block, lambda s, h, i: (s, 0, 0))],
        scratch_shapes=[pltpu.VMEM((rows, HEAD_DIM), F32)],
    )
    work = seqs * kv_heads * rows * length
    return pl.pallas_call(
        functools.partial(attend_back_kernel, spans, span_len, tokens, kv_heads),
        grid_spec=grid_spec,
        out_shape=[
            jax.ShapeDtypeStruct(queries.shape, BF),
            jax.ShapeDtypeStruct(pairs.shape, BF),
        ],
        name="attend_back",
        cost_estimate=pl.CostEstimate(
            flops=10 * work * HEAD_DIM, bytes_accessed=pairs.size * 4, transcendentals=work
        ),
    )(info, queries, grads, results, pairs, pairs, lse)


def turned(values, cosine, sine_signed):
    return values * cosine + pltpu.roll(values, HEAD_DIM // 2, axis=1) * sine_signed


def fetch_rows(index, blocks, out_ref, sems):
    depth = blocks[0].shape[0]
    return [
        pltpu.make_async_copy(
            block,
            out_ref.at[pl.ds(pl.multiple_of((index ^ j) * depth, depth), depth), :],
            sems.at[j],
        )
        for j, block in enumerate(blocks)
    ]


def keys_kernel(
    seqs, x_ref, gain_ref, w_ref, shrink_ref, ek_ref, ev_ref, bias_ref, cos_ref, sin_ref,
    normed_ref, nk_ref, nv_ref, pair_ref,
):
    tokens, width = pair_ref.shape
    kv = width // 2
    lanes = ek_ref.shape[0]
    normed = norm_forward(x_ref[...].astype(F32), gain_ref[...]).astype(BF)
    normed_ref[...] = normed
    mix = token_mask(tokens, lanes, seqs)
    narrow = mm(normed, shrink_ref[...])
    narrow_k = (narrow[:, :lanes] * mix).astype(BF)
    narrow_v = (narrow[:, lanes:] * mix).astype(BF)
    nk_ref[...] = narrow_k
    nv_ref[...] = narrow_v
    raw = mm(normed, w_ref[...]) + bias_ref[...]
    keys = raw[:, :kv] + mm(narrow_k, ek_ref[...])
    vals = raw[:, kv:] + mm(narrow_v, ev_ref[...])
    cosine = cos_ref[...]
    sine = sin_ref[...]
    for h in range(kv // HEAD_DIM):
        at = slice(h * HEAD_DIM, (h + 1) * HEAD_DIM)
        pair_ref[:, at] = turned(keys[:, at], cosine, sine).astype(BF)
    pair_ref[:, kv:] = vals.astype(BF)


def keys_values(x, gain, w_kv, shrink, expand_k, expand_v, bias, cosine, sine, seqs):
    tokens, model = x.shape
    lanes = expand_k.shape[0]
    low = lambda n: jax.ShapeDtypeStruct((tokens, n), BF)
    return pl.pallas_call(
        functools.partial(keys_kernel, seqs),
        out_shape=[low(model), low(lanes), low(lanes), low(w_kv.shape[1])],
        name="keys_values",
        cost_estimate=pl.CostEstimate(
            flops=2 * tokens * model * w_kv.shape[1],
            bytes_accessed=8 * tokens * model,
            transcendentals=tokens,
        ),
    )(x, gain, w_kv, shrink, expand_k, expand_v, bias, cosine, sine)


def queries_kernel(
    seqs, count, info, normed_ref, shrink_ref, eq_ref, bias_ref, cos_ref, sin_ref, *refs
):
    blocks = refs[:count]
    query_ref, narrow_ref, w_ref, sems = refs[count:]
    copies = fetch_rows(info[0], blocks, w_ref, sems)
    for copy in copies:
        copy.start()
    tokens, model = query_ref.shape
    lanes = eq_ref.shape[0]
    normed = normed_ref[...]
    narrow = (mm(normed, shrink_ref[...]) * token_mask(tokens, lanes, seqs)).astype(BF)
    narrow_ref[...] = narrow
    for copy in copies:
        copy.wait()
    cosine = cos_ref[...]
    sine = sin_ref[...]
    step = 2 * HEAD_DIM
    for c in range(0, model, step):
        raw = mm(normed, w_ref[:, c : c + step]) + bias_ref[:, c : c + step]
        raw = raw + mm(narrow, eq_ref[:, c : c + step])
        for h in range(0, step, HEAD_DIM):
            query_ref[:, c + h : c + h + HEAD_DIM] = turned(
                raw[:, h : h + HEAD_DIM], cosine, sine
            ).astype(BF)


def outputs_kernel(seqs, count, info, attended_ref, x_ref, gain_ref, shrink_ref, eo_ref, *refs):
    blocks = refs[:count]
    middle_ref, normed_ref, top_ref, bottom_ref, narrow_ref, w_ref, sems = refs[count:]
    copies = fetch_rows(info[0], blocks, w_ref, sems)
    for copy in copies:
        copy.start()
    tokens, model = middle_ref.shape
    lanes = eo_ref.shape[0]
    attended = attended_ref[...]
    narrow = (mm(attended, shrink_ref[...]) * token_mask(tokens, lanes, seqs)).astype(BF)
    narrow_ref[...] = narrow
    for copy in copies:
        copy.wait()
    middle = x_ref[...].astype(F32) + (mm(attended, w_ref[...]) + mm(narrow, eo_ref[...]))
    middle_ref[...] = middle
    normed = norm_forward(middle, gain_ref[...]).astype(BF)
    normed_ref[...] = normed
    top_ref[...] = normed[: tokens // 2]
    bottom_ref[...] = normed[tokens // 2 :]


def before_attention_kernel(
    seqs, count, *refs
):
    grad_ref, middle_ref, gain_ref, gs_ref, us_ref, os_ref, oe_ref, w_ref = refs[count : count + 8]
    mg_ref, low_ref, gb_ref, ub_ref, ob_ref, ag_ref = refs[count + 8 :]
    tokens, model = mg_ref.shape
    lanes = oe_ref.shape[0]
    mix = token_mask(tokens, lanes, seqs)
    total = sum(ref[...].astype(F32) for ref in refs[:count])
    gate_back = (total[:, model : model + lanes] * mix).astype(BF)
    up_back = (total[:, model + lanes :] * mix).astype(BF)
    gb_ref[...] = gate_back
    ub_ref[...] = up_back
    normed_grad = total[:, :model] + mm_nt(gate_back, gs_ref[...]) + mm_nt(up_back, us_ref[...])
    middle_grad = grad_ref[...].astype(F32) + norm_backward(
        middle_ref[...], gain_ref[...], normed_grad
    )
    mg_ref[...] = middle_grad
    low = middle_grad.astype(BF)
    low_ref[...] = low
    output_back = (mm_nt(low, oe_ref[...]) * mix).astype(BF)
    ob_ref[...] = output_back
    ag_ref[...] = (mm_nt(low, w_ref[...]) + mm_nt(output_back, os_ref[...])).astype(BF)


def before_attention(parts, grad, middle, gain, gs, us, os, oe, w_output, seqs):
    tokens, model = middle.shape
    lanes = oe.shape[0]
    low = lambda n: jax.ShapeDtypeStruct((tokens, n), BF)
    return pl.pallas_call(
        functools.partial(before_attention_kernel, seqs, len(parts)),
        out_shape=[
            jax.ShapeDtypeStruct((tokens, model), F32),
            low(model), low(lanes), low(lanes), low(lanes), low(model),
        ],
        name="before_attention",
        cost_estimate=pl.CostEstimate(
            flops=2 * tokens * model * model, bytes_accessed=30 * tokens * model, transcendentals=0
        ),
    )(*parts, grad, middle, gain, gs, us, os, oe, w_output)


def last_grads_kernel(
    seqs, rank, info, pair_ref, cos_ref, sin_ref, ke_ref, ve_ref, normed_ref, nk_ref, nv_ref,
    kg_ref, vg_ref, kb_ref, vb_ref, late_ref, rows_ref,
):
    tokens, width = pair_ref.shape
    kv = width // 2
    lanes = ke_ref.shape[0]
    model = normed_ref.shape[1]
    mix = token_mask(tokens, lanes, seqs)
    cosine = cos_ref[...]
    sine = -sin_ref[...]
    for h in range(kv // HEAD_DIM):
        at = slice(h * HEAD_DIM, (h + 1) * HEAD_DIM)
        kg_ref[:, at] = turned(pair_ref[:, at].astype(F32), cosine, sine).astype(BF)
    vg_ref[...] = pair_ref[:, kv:]
    key_grad = kg_ref[...]
    value_grad = vg_ref[...]
    key_back = (mm_nt(key_grad, ke_ref[...]) * mix).astype(BF)
    value_back = (mm_nt(value_grad, ve_ref[...]) * mix).astype(BF)
    kb_ref[...] = key_back
    vb_ref[...] = value_back
    normed = normed_ref[...]
    rows_ref[:, :model] = mm_tn(key_back, normed)[:rank].astype(BF)
    rows_ref[:, model : 2 * model] = mm_tn(value_back, normed)[:rank].astype(BF)
    rows_ref[:, 2 * model : 2 * model + kv] = mm_tn(nk_ref[...], key_grad)[:rank].astype(BF)
    rows_ref[:, 2 * model + kv :] = mm_tn(nv_ref[...], value_grad)[:rank].astype(BF)
    parts = 2 * late_ref.shape[1]
    size = late_ref.shape[3]
    for p in range(parts):
        at = p ^ info[0]
        late_ref[lax.rem(at, 2), at // 2] = rows_ref[:, p * size : (p + 1) * size]


def last_grads(mine, pair_grad, cosine, sine, ke, ve, normed, nk, nv, seqs, rank, parts):
    tokens, width = pair_grad.shape
    lanes = ke.shape[0]
    model = normed.shape[1]
    low = lambda n: jax.ShapeDtypeStruct((tokens, n), BF)
    total = 2 * model + width
    operands = [pair_grad, cosine, sine, ke, ve, normed, nk, nv]
    results = [
        low(width // 2), low(width // 2), low(lanes), low(lanes),
        jax.ShapeDtypeStruct((2, parts // 2, rank, total // parts), BF),
    ]
    return pl.pallas_call(
        functools.partial(last_grads_kernel, seqs, rank),
        grid_spec=pltpu.PrefetchScalarGridSpec(
            num_scalar_prefetch=1,
            grid=(1,),
            in_specs=[pl.BlockSpec(a.shape, lambda g, i, n=a.ndim: (0,) * n) for a in operands],
            out_specs=[
                pl.BlockSpec(r.shape, lambda g, i, n=len(r.shape): (0,) * n) for r in results
            ],
            scratch_shapes=[pltpu.VMEM((rank, total), BF)],
        ),
        out_shape=results,
        name="last_grads",
        cost_estimate=pl.CostEstimate(
            flops=4 * tokens * model * 128, bytes_accessed=6 * tokens * model, transcendentals=0
        ),
    )(mine.reshape(1).astype(jnp.int32), *operands)


def with_blocks(kernel, name, seqs, index, blocks, operands, results):
    count = len(blocks)
    depth, lanes = blocks[0].shape
    inside = pl.BlockSpec(memory_space=pltpu.VMEM)
    results = list(results) + [jax.ShapeDtypeStruct((count * depth, lanes), BF)]
    return pl.pallas_call(
        functools.partial(kernel, seqs, count),
        grid_spec=pltpu.PrefetchScalarGridSpec(
            num_scalar_prefetch=1,
            grid=(1,),
            in_specs=[pl.BlockSpec(a.shape, lambda g, i, n=a.ndim: (0,) * n) for a in operands]
            + [pl.BlockSpec(memory_space=pl.ANY)] * count,
            out_specs=[pl.BlockSpec(r.shape, lambda g, i: (0, 0)) for r in results],
            scratch_shapes=[pltpu.SemaphoreType.DMA((count,))],
        ),
        out_shape=results,
        name=name,
        cost_estimate=pl.CostEstimate(
            flops=2 * operands[0].shape[0] * count * depth * lanes,
            bytes_accessed=4 * count * depth * lanes,
            transcendentals=0,
        ),
    )(index.reshape(1).astype(jnp.int32), *operands, *blocks)


def token_mask(tokens, lanes, seqs):
    row = lax.broadcasted_iota(jnp.int32, (tokens, lanes), 0) // (tokens // seqs)
    lane = lax.broadcasted_iota(jnp.int32, (tokens, lanes), 1) // ADAPTER_RANK
    return jnp.where(row == lane, adapter_scale, 0.0).astype(F32)


def feed_kernel(seqs, kinds, info, *refs):
    count = len(kinds)
    blocks = refs[:count]
    top_ref, bottom_ref, grad_top_ref, grad_bottom_ref = refs[count : count + 4]
    count += 4
    sgu_ref, ed_ref, wd_ref, eg_ref, eu_ref, sd_ref = refs[count : count + 6]
    peg_ref, peu_ref, psd_ref = refs[count + 6 : count + 9]
    out_ref, ng_ref, deg_ref, deu_ref, dsd_ref = refs[count + 9 : count + 14]
    acc_out, acc_ng, acc_nd, acc_bg, acc_bu, nar_g, nar_u, back_d, held, sems = refs[count + 14 :]
    chunk = pl.program_id(0)
    chunks = pl.num_programs(0)
    depth = blocks[0].shape[-2]
    size = wd_ref.shape[0]

    def copies(at, slot):
        found = []
        for n, (j, which) in enumerate(kinds):
            rows = pl.ds(pl.multiple_of((info[0] ^ j) * depth, depth), depth)
            lanes = pl.ds(pl.multiple_of(at * size, 128), size)
            if which is None:
                source, target = blocks[n].at[:, :, lanes], held.at[slot, :, rows, :]
            else:
                source, target = blocks[n].at[:, lanes], held.at[slot, info[1] ^ which, rows, :]
            found.append(pltpu.make_async_copy(source, target, sems.at[slot, n]))
        return found

    slot = lax.rem(chunk, 2)

    @pl.when(chunk == 0)
    def _():
        for copy in copies(chunk, slot):
            copy.start()

    @pl.when(chunk + 1 < chunks)
    def _():
        for copy in copies(chunk + 1, 1 - slot):
            copy.start()

    tokens = out_ref.shape[0]
    model = top_ref.shape[1]
    cols = sd_ref.shape[1]
    n2 = jnp.concatenate([top_ref[...], bottom_ref[...]], axis=0)
    g0 = jnp.concatenate([grad_top_ref[...], grad_bottom_ref[...]], axis=0)
    wg_ref = held.at[slot, 0]
    wu_ref = held.at[slot, 1]

    @pl.when(chunk == 0)
    def _():
        mix = token_mask(tokens, cols, seqs)
        narrow = mm(n2, sgu_ref[...])
        nar_g[...] = (narrow[:, :cols] * mix).astype(BF)
        nar_u[...] = (narrow[:, cols:] * mix).astype(BF)
        back_d[...] = (mm_nt(g0, ed_ref[...]) * mix).astype(BF)
        for acc in (acc_out, acc_ng, acc_nd, acc_bg, acc_bu):
            acc[...] = jnp.zeros(acc.shape, F32)

    for copy in copies(chunk, slot):
        copy.wait()
    narrow_g = nar_g[...]
    narrow_u = nar_u[...]
    narrow_b = back_d[...]
    gate = mm(n2, wg_ref[...]) + mm(narrow_g, eg_ref[...])
    upward = mm(n2, wu_ref[...]) + mm(narrow_u, eu_ref[...])
    sig = jax.nn.sigmoid(gate)
    act = gate * sig
    hidden = (act * upward).astype(BF)
    hidden_grad = mm_nt(g0, wd_ref[...]) + mm_nt(narrow_b, sd_ref[...])
    gate_grad = (hidden_grad * upward * (sig * (1.0 + gate * (1.0 - sig)))).astype(BF)
    up_grad = (hidden_grad * act).astype(BF)
    acc_out[...] += mm(hidden, wd_ref[...])
    acc_nd[...] += mm(hidden, sd_ref[...])
    acc_ng[...] += mm_nt(gate_grad, wg_ref[...]) + mm_nt(up_grad, wu_ref[...])
    acc_bg[...] += mm_nt(gate_grad, eg_ref[...])
    acc_bu[...] += mm_nt(up_grad, eu_ref[...])
    deg_ref[...] = peg_ref[...] + mm_tn(narrow_g, gate_grad)
    deu_ref[...] = peu_ref[...] + mm_tn(narrow_u, up_grad)
    dsd_ref[...] = psd_ref[...] + mm_tn(narrow_b, hidden)

    @pl.when(chunk == chunks - 1)
    def _():
        out_ref[:, :model] = acc_out[...].astype(BF)
        out_ref[:, model:] = jnp.concatenate([acc_nd[...], acc_nd[...]], axis=1).astype(BF)
        ng_ref[:, :model] = acc_ng[...].astype(BF)
        ng_ref[:, model:] = jnp.concatenate([acc_bg[...], acc_bu[...]], axis=1).astype(BF)


def feed(index, kinds, blocks, n2, g0, sgu, ed, wd, eg, eu, sd, previous, seqs, limit=768):
    tokens, model = 2 * n2[0].shape[0], n2[0].shape[1]
    count = len(blocks)
    hidden = wd.shape[0]
    cols = ed.shape[0]
    size = max(c for c in range(128, limit + 1, 128) if hidden % c == 0)
    anywhere = pl.BlockSpec(memory_space=pl.ANY)
    whole = lambda a: pl.BlockSpec(
        a.shape, lambda h, i: (0,) * a.ndim, pipeline_mode=pl.Buffered(1)
    )
    part = lambda a: pl.BlockSpec((a.shape[0], size), lambda h, i: (0, h))
    tall = lambda a: pl.BlockSpec((size, a.shape[1]), lambda h, i: (h, 0))
    fixed = lambda c: pl.BlockSpec((tokens, c), lambda h, i: (0, 0))
    grads = jax.ShapeDtypeStruct((cols, hidden), F32)
    return pl.pallas_call(
        functools.partial(feed_kernel, seqs, tuple(kinds)),
        grid_spec=pltpu.PrefetchScalarGridSpec(
            num_scalar_prefetch=1,
            grid=(hidden // size,),
            in_specs=[anywhere] * count
            + [whole(n2[0]), whole(n2[1]), whole(g0[0]), whole(g0[1]), whole(sgu), whole(ed), tall(wd)]
            + [part(eg), part(eu), tall(sd), part(grads), part(grads), part(grads)],
            out_specs=[fixed(model + 2 * cols), fixed(model + 2 * cols)] + [part(grads)] * 3,
            scratch_shapes=[
                pltpu.VMEM((tokens, model), F32),
                pltpu.VMEM((tokens, model), F32),
                pltpu.VMEM((tokens, cols), F32),
                pltpu.VMEM((tokens, cols), F32),
                pltpu.VMEM((tokens, cols), F32),
                pltpu.VMEM((tokens, cols), BF),
                pltpu.VMEM((tokens, cols), BF),
                pltpu.VMEM((tokens, cols), BF),
                pltpu.VMEM((2, 2, model, size), BF),
                pltpu.SemaphoreType.DMA((2, count)),
            ],
        ),
        out_shape=[
            jax.ShapeDtypeStruct((tokens, model + 2 * cols), BF),
            jax.ShapeDtypeStruct((tokens, model + 2 * cols), BF),
            grads, grads, grads,
        ],
        name="feed",
        cost_estimate=pl.CostEstimate(
            flops=12 * tokens * (model + cols) * hidden,
            bytes_accessed=6 * model * hidden,
            transcendentals=tokens * hidden,
        ),
    )(index, *blocks, *n2, *g0, sgu, ed, wd, eg, eu, sd, *previous)


def assemble_kernel(count, info, *refs):
    blocks = refs[:count]
    out_ref, held, blank, in_sem, out_sem = refs[count:]
    depth = blocks[0].shape[0]
    rest = out_ref.shape[0] - count * depth
    arrive = []
    leave = []
    for j in range(count):
        arrive.append(pltpu.make_async_copy(blocks[j], held.at[j], in_sem.at[j]))
        at = pl.multiple_of((info[0] ^ j) * depth, depth)
        leave.append(
            pltpu.make_async_copy(held.at[j], out_ref.at[pl.ds(at, depth), :], out_sem.at[j])
        )
    for copy in arrive:
        copy.start()
    if rest:
        blank[...] = jnp.zeros(blank.shape, BF)
        last = pltpu.make_async_copy(blank, out_ref.at[count * depth :, :], out_sem.at[count])
        last.start()
    for one, two in zip(arrive, leave):
        one.wait()
        two.start()
    for copy in leave:
        copy.wait()
    if rest:
        last.wait()


def assemble(index, blocks, rows):
    count = len(blocks)
    depth, lanes = blocks[0].shape
    anywhere = pl.BlockSpec(memory_space=pl.ANY)
    return pl.pallas_call(
        functools.partial(assemble_kernel, count),
        grid_spec=pltpu.PrefetchScalarGridSpec(
            num_scalar_prefetch=1,
            grid=(1,),
            in_specs=[anywhere] * count,
            out_specs=anywhere,
            scratch_shapes=[
                pltpu.VMEM((count, depth, lanes), BF),
                pltpu.VMEM((max(rows - count * depth, 16), lanes), BF),
                pltpu.SemaphoreType.DMA((count,)),
                pltpu.SemaphoreType.DMA((count + 1,)),
            ],
        ),
        out_shape=jax.ShapeDtypeStruct((rows, lanes), BF),
        name="assemble",
        cost_estimate=pl.CostEstimate(
            flops=0, bytes_accessed=4 * rows * lanes, transcendentals=0
        ),
    )(index.reshape(1).astype(jnp.int32), *blocks)


def expand_kernel(rank, hidden, padded, seq_n, early, kinds, both_ref, select_ref, *outs):
    pair = pl.program_id(0)
    select = select_ref[...]
    lanes = -(-hidden // 128) * 128
    width = both_ref.shape[2] - early
    for q in range(2):
        for i, out_ref in enumerate(outs[:3]):
            groups = []
            for f in range(2):
                at = i * padded
                left = lanes
                pieces = []
                while left:
                    z, low = divmod(at, width)
                    take = min(left, width - low)
                    device = pair * 4 * seq_n + (q * 2 + f) * seq_n + z
                    pieces.append(both_ref[device, :rank, early + low : early + low + take])
                    at += take
                    left -= take
                groups.append(jnp.concatenate(pieces, axis=1))
            rows = jnp.concatenate(groups, axis=0)
            if i < 2:
                out_ref[:, q * hidden : (q + 1) * hidden] = mm_tn(select, rows)[:, :hidden]
            else:
                out_ref[q * hidden : (q + 1) * hidden, :] = mm_tn(rows, select)[:hidden]

    @pl.when(pair == 0)
    def _():
        half = both_ref.shape[0] // 2
        for i, (out_ref, shrink) in enumerate(zip(outs[3:], kinds)):
            rows = jnp.concatenate(
                [
                    jnp.concatenate(
                        [both_ref[f * half + 2 * i + w, :rank, :early] for w in range(2)], axis=1
                    )
                    for f in range(2)
                ],
                axis=0,
            )
            out_ref[...] = mm_tn(rows, select) if shrink else mm_tn(select, rows)


def expand_all(both, select, rank, hidden, padded, seq_n, chips, early, kinds):
    cols = select.shape[1]
    model = 2 * early
    wide = lambda n: jax.ShapeDtypeStruct((cols, n), F32)
    tall = lambda n: jax.ShapeDtypeStruct((n, cols), F32)
    fixed = [tall(model) if shrink else wide(model) for shrink in kinds]
    return pl.pallas_call(
        functools.partial(expand_kernel, rank, hidden, padded, seq_n, early, kinds),
        grid=(chips // 2,),
        in_specs=[
            pl.BlockSpec(both.shape, lambda p: (0, 0, 0), pipeline_mode=pl.Buffered(1)),
            pl.BlockSpec(select.shape, lambda p: (0, 0)),
        ],
        out_specs=[
            pl.BlockSpec((cols, 2 * hidden), lambda p: (0, p)),
            pl.BlockSpec((cols, 2 * hidden), lambda p: (0, p)),
            pl.BlockSpec((2 * hidden, cols), lambda p: (p, 0)),
        ]
        + [pl.BlockSpec(one.shape, lambda p: (0, 0)) for one in fixed],
        out_shape=[wide(chips * hidden), wide(chips * hidden), tall(chips * hidden)] + fixed,
        name="expand",
        cost_estimate=pl.CostEstimate(
            flops=6 * cols * chips * hidden * select.shape[0],
            bytes_accessed=12 * cols * chips * hidden,
            transcendentals=0,
        ),
    )(both, select)


def after(value, *needed):
    return lax.optimization_barrier((value, needed))[0]


def body(
    inputs, cotangent, span_order, adapter_ids, first_gain, second_gain,
    query_weight, key_weight, value_weight, output_weight, gate_weight, up_weight, down_weight,
    query_bias, key_bias, value_bias,
    query_reduce_factors, query_lift_factors, key_reduce_factors, key_lift_factors,
    value_reduce_factors, value_lift_factors, output_reduce_factors, output_lift_factors,
    gate_reduce_factors, gate_lift_factors, upper_reduce_factors, upper_lift_factors,
    down_reduce_factors, down_lift_factors,
):
    seq_n = lax.axis_size("seq")
    cp_n = lax.axis_size("cp")
    fsdp_n = lax.axis_size("fsdp")
    plane = fsdp_n * cp_n
    chips = plane // 2
    group = lax.axis_index("fsdp")
    me = group * cp_n + lax.axis_index("cp")
    chip = me // 2
    core = me % 2
    seqs, tok_rows, model = inputs.shape
    tokens = seqs * tok_rows
    cols = query_reduce_factors.shape[1]
    kv_width = key_weight.shape[1]
    length = tok_rows * seq_n * cp_n
    spans = span_order.shape[1]
    span_len = length // spans
    hidden_all = gate_weight.shape[1]
    hq = hidden_all // chips
    hp = -(-hq // 256) * 256
    pad = hp - hq
    rank = seqs * ADAPTER_RANK
    lanes = -(-rank // 64) * 64

    def swap(value, k):
        return lax.ppermute(value, PLANE, [(i, i ^ k) for i in range(plane)])

    def swap_seq(value, k):
        return lax.ppermute(value, "seq", [(i, i ^ k) for i in range(seq_n)])

    first_row = (lax.axis_index("cp") * seq_n + lax.axis_index("seq")) * tok_rows
    own = lax.dynamic_slice_in_dim(span_order, first_row // span_len, 1, 1)[:, 0]
    shift = first_row % span_len
    cp_index = lax.axis_index("cp")
    seq_index = lax.axis_index("seq")
    info = jnp.concatenate(
        [span_order.reshape(-1), own, jnp.stack([shift, cp_index])]
    ).astype(jnp.int32)
    places = own[:, None] * span_len + shift + jnp.arange(tok_rows, dtype=jnp.int32)[None, :]
    cosine, sine_table = rotary_tables(places.reshape(tokens))
    sine_signed = jnp.where(
        jnp.arange(HEAD_DIM, dtype=jnp.int32) < HEAD_DIM // 2, -sine_table, sine_table
    )
    flat_cosine = cosine
    cosine = cosine[:, None, :]
    sine_table = sine_table[:, None, :]
    lane = jnp.arange(lanes, dtype=jnp.int32)

    def chosen(ids):
        column = jnp.repeat(ids, ADAPTER_RANK) * ADAPTER_RANK + lane[:rank] % ADAPTER_RANK
        column = jnp.pad(column, (0, lanes - rank), constant_values=-1)
        return (jnp.arange(cols, dtype=jnp.int32)[:, None] == column[None, :]).astype(BF)

    ids_wide = jnp.broadcast_to(
        jnp.pad(adapter_ids, (0, -seqs % 8)).astype(F32)[:, None], (seqs + -seqs % 8, 128)
    )
    select = [chosen(adapter_ids)]
    for f in range(1, fsdp_n):
        select.append(chosen(swap(ids_wide, f * cp_n)[:seqs, 0].astype(jnp.int32)))
    mixing = token_mask(tokens, lanes, seqs)

    def shrink_of(value, f=0):
        return mm(value, select[f]).astype(BF)

    def expand_of(value, f=0):
        return mm_tn(select[f], value).astype(BF)

    w_kv = lax.all_gather(
        jnp.concatenate([key_weight, value_weight], axis=1), PLANE, axis=0, tiled=True
    )
    rows_q = [query_weight] + [swap(query_weight, 2 * k) for k in range(1, chips)]

    def by_chip(value):
        return jnp.stack(
            [
                jnp.pad(value[:, hq * c : hq * (c + 1)], ((0, 0), (0, pad)))
                for c in range(chips)
            ]
        )

    gate_up = jnp.stack([by_chip(gate_weight), by_chip(up_weight)], axis=1)
    depth = gate_weight.shape[0]
    parts = [lax.dynamic_index_in_dim(gate_up, chip ^ k, 0, keepdims=False) for k in range(chips)]

    low_in = inputs.reshape(tokens, model)
    resid_in = low_in.astype(F32)
    first_scales = first_gain.astype(F32)
    second_scales = second_gain.astype(F32)
    grad_low = cotangent.reshape(tokens, model)
    w_kv, parts, rows_q = lax.optimization_barrier((w_kv, parts, rows_q))
    rows_o = [output_weight] + [swap(after(output_weight, rows_q), 2 * k) for k in range(1, chips)]
    blocks = {}
    w_key = w_kv[:, :kv_width]
    w_value = w_kv[:, kv_width:]

    query_shrink, key_shrink, value_shrink, output_shrink = [
        shrink_of(value)
        for value in (
            query_reduce_factors, key_reduce_factors, value_reduce_factors, output_reduce_factors,
        )
    ]
    query_expand, key_expand, value_expand, output_expand = [
        expand_of(value)
        for value in (
            query_lift_factors, key_lift_factors, value_lift_factors, output_lift_factors,
        )
    ]
    grad_halves = (grad_low[: tokens // 2], grad_low[tokens // 2 :])
    w_kv, output_shrink, output_expand, query_shrink, query_expand, grad_halves = (
        lax.optimization_barrier(
            (w_kv, output_shrink, output_expand, query_shrink, query_expand, grad_halves)
        )
    )

    def swap_both(pair, k):
        return tuple(swap(half, k) for half in pair)

    g0_pieces = {
        k: swap_both(after(grad_halves, rows_q), 2 * k) for k in range(1, chips) if 2 * k % cp_n == 0
    }

    def narrowed(value, shrink):
        return (mm(value, shrink) * mixing).astype(BF)

    normed, key_narrow, value_narrow, pair = keys_values(
        low_in, first_scales[None], w_kv, jnp.concatenate([key_shrink, value_shrink], axis=1),
        key_expand, value_expand,
        jnp.concatenate([key_bias, value_bias]).astype(F32)[None], flat_cosine, sine_signed, seqs,
    )
    pair_all = lax.all_gather(
        pair.reshape(seqs, tok_rows, 2 * kv_width), ("cp", "seq"), axis=1, tiled=True
    )

    def both_cores(rows):
        found = []
        for part in rows:
            found += [part, swap(part, 1)]
        return found

    query_rot, query_narrow, w_query = with_blocks(
        queries_kernel, "queries", seqs, me, after(both_cores(rows_q), pair),
        [
            after(normed, rows_o, g0_pieces), query_shrink, query_expand, query_bias.astype(F32)[None], flat_cosine,
            sine_signed,
        ],
        [
            jax.ShapeDtypeStruct((tokens, model), BF),
            jax.ShapeDtypeStruct((tokens, lanes), BF),
        ],
    )

    late_lift = after(
        (
        gate_lift_factors, upper_lift_factors, down_reduce_factors, down_lift_factors,
        gate_reduce_factors, upper_reduce_factors,
        ),
        pair_all,
    )
    gate_shrink, up_shrink = shrink_of(late_lift[4]), shrink_of(late_lift[5])
    down_expand = expand_of(late_lift[3])
    reduce_factors = [
        (
            jnp.concatenate([shrink_of(late_lift[4], f), shrink_of(late_lift[5], f)], axis=1),
            expand_of(late_lift[3], f),
        )
        for f in range(fsdp_n)
    ]
    late_down, late_gate, late_up = late_lift[2], late_lift[0], late_lift[1]
    shrink_d = jnp.pad(
        lax.dynamic_slice_in_dim(late_down, chip * hq, hq, 0), ((0, pad), (0, 0))
    )
    lift_g = lax.dynamic_index_in_dim(by_chip(late_gate), chip, 0, keepdims=False)
    lift_u = lax.dynamic_index_in_dim(by_chip(late_up), chip, 0, keepdims=False)
    lift_factors = [(expand_of(lift_g, f), expand_of(lift_u, f)) for f in range(fsdp_n)]
    feed_factors = [
        reduce_factors[f] + lift_factors[f] + (shrink_of(shrink_d, f),) for f in range(fsdp_n)
    ]
    down_rows = [down_weight, swap(after(down_weight, query_rot), 1)]
    w_down = assemble(core, after(down_rows, query_rot), hp)
    attended, lse = attend(
        info, after(query_rot, w_down, feed_factors, gate_shrink, up_shrink, down_expand),
        pair_all, seqs, spans, span_len,
    )
    for k in range(1, chips):
        blocks[k] = swap(after(parts[k], rows_o), 2 * k)
    output_blocks = both_cores(after(rows_o, query_rot))
    middle, normed_two, normed_top, normed_bottom, output_narrow, w_output = with_blocks(
        outputs_kernel, "outputs", seqs, me, output_blocks,
        [attended, low_in, second_scales[None], output_shrink, output_expand],
        [
            jax.ShapeDtypeStruct((tokens, model), F32),
            jax.ShapeDtypeStruct((tokens, model), BF),
            jax.ShapeDtypeStruct((tokens // 2, model), BF),
            jax.ShapeDtypeStruct((tokens // 2, model), BF),
            jax.ShapeDtypeStruct((tokens, lanes), BF),
        ],
    )

    kinds = [(0, None), (1, None)]
    wide = [parts[0], swap(after(parts[0], query_rot), 1)]
    for k in range(1, chips):
        kinds += [(2 * k, None), (2 * k + 1, None)]
        wide += [blocks[k], swap(after(blocks[k], middle), 1)]
    feed_index = jnp.stack([me, core]).astype(jnp.int32)

    g0_pieces[0] = grad_halves
    normed_halves = (normed_top, normed_bottom)
    n2_pieces = [normed_halves]
    for k in range(1, chips):
        if k < 3:
            n2_pieces.append(swap_both(after(normed_halves, blocks), 2 * k))
            if k not in g0_pieces:
                g0_pieces[k] = swap_both(after(grad_halves, wide), 2 * k)
    zero = jnp.zeros((lanes, hp), F32)
    sums = [(zero, zero, zero)] * fsdp_n
    out_raw = []
    grad_parts = []
    early_first = sorted(range(1, chips), key=lambda k: (k > 2, -k if k < 3 else k)) + [0]
    for k in early_first:
        f = 2 * k // cp_n
        sgu, ed, eg, eu, sd = feed_factors[f]
        if len(out_raw) == 1:
            for other in range(3, chips):
                for pieces in (n2_pieces, g0_pieces):
                    first, second, own_pair = after((pieces[2], pieces[1], pieces[0]), out_raw[-1])
                    if other == 3:
                        piece = (swap(first[0], 2), swap(second[1], 4))
                    else:
                        piece = swap_both(own_pair, 2 * other)
                    if pieces is n2_pieces:
                        n2_pieces.append(piece)
                    else:
                        g0_pieces[other] = piece
        if out_raw:
            sums[f] = after(sums[f], out_raw[-1], [] if k else grad_parts[:-1])
        out_k, ng_k, *sums[f] = feed(
            feed_index, kinds, wide, n2_pieces[k], g0_pieces[k], sgu, ed, w_down, eg, eu, sd, sums[f], seqs
        )
        out_raw.append(out_k)
        grad_parts.append(ng_k if k == 0 else swap(ng_k, 2 * k))

    def pack(values, tiles):
        value = jnp.concatenate([value[:rank].astype(BF) for value in values], axis=1)
        return jnp.pad(value, ((0, 0), (0, -value.shape[1] % (128 * tiles))))

    middle_grad, middle_low, gate_back, up_back, output_back, attended_grad = before_attention(
        grad_parts, grad_low, middle, second_scales[None],
        gate_shrink, up_shrink, output_shrink, output_expand, w_output, seqs,
    )

    def narrowed_back(grad, expand):
        return (mm_nt(grad, expand) * mixing).astype(BF)

    out_raw = after(out_raw, middle_low)
    out_of = dict(zip(early_first, out_raw))
    out_parts = [out_of[0]] + [swap(out_of[k], 2 * k) for k in range(1, min(chips, 3))]
    query_rot_grad, pair_part = attend_back(
        info, query_rot, attended_grad, attended, pair_all, lse, seqs, spans, span_len
    )
    out_parts += [
        swap(after(out_of[k], pair_part), 2 * k) for k in range(3, chips)
    ]
    pair_grad = lax.psum_scatter(
        after(pair_part, out_parts[:3]), ("cp", "seq"), scatter_dimension=1, tiled=True
    ).reshape(tokens, 2 * kv_width)
    out_sum = sum(part.astype(F32) for part in out_parts)

    down_narrow = (out_sum[:, model : model + lanes] * mixing).astype(BF)
    result = middle + (out_sum[:, :model] + mm(down_narrow, down_expand))
    outputs = result.astype(BF).reshape(seqs, tok_rows, model)

    query_rot_grad, sums, middle_late, output_back, gate_back, up_back = after(
        (query_rot_grad, sums, middle_low, output_back, gate_back, up_back), out_parts[:3]
    )
    cosine, sine_table = after((cosine, sine_table), pair_part)
    query_grad = (
        unrotate(
            query_rot_grad.reshape(tokens, -1, HEAD_DIM).astype(F32), cosine, sine_table
        )
        .reshape(tokens, model)
        .astype(BF)
    )
    query_back = narrowed_back(query_grad, query_expand)
    query_in = mm_nt(query_grad, w_query) + mm_nt(query_back, query_shrink)

    def halves(value, index, exchange):
        span = 1
        while value.shape[0] > 1:
            split = value.reshape((value.shape[0] // 2, 2) + value.shape[1:])
            bit = index // span % 2
            keep = lax.dynamic_index_in_dim(split, bit, 1, keepdims=False)
            give = lax.dynamic_index_in_dim(split, 1 - bit, 1, keepdims=False)
            value = (keep.astype(F32) + exchange(give, span).astype(F32)).astype(BF)
            span *= 2
        return value[0]

    stacked = jnp.stack([pack(sums[f], seq_n) for f in range(fsdp_n)])
    feed_wide = stacked.shape[2]

    def groups_of(parity):
        return jnp.stack(
            [
                lax.dynamic_index_in_dim(stacked, (2 * j + parity) ^ group, 0, keepdims=False)
                for j in range(fsdp_n // 2)
            ]
        )

    feed_half = groups_of(core).astype(F32) + swap(groups_of(1 - core), 1).astype(F32)
    feed_half = feed_half.reshape(fsdp_n // 2 * rank, seq_n, feed_wide // seq_n).astype(BF)
    feed_half = feed_half.transpose(1, 0, 2)
    feed_piece = halves(feed_half, seq_index, swap_seq)
    ways = cp_n * seq_n
    early = pack(
        [
            mm_tn(output_back, attended),
            mm_tn(gate_back, normed_two),
            mm_tn(up_back, normed_two),
            mm_tn(output_narrow, middle_late),
            mm_tn(down_narrow, grad_low),
            mm_tn(query_back, normed),
            mm_tn(query_narrow, query_grad),
        ],
        ways,
    )
    early = early.reshape(rank, cp_n, seq_n, -1).transpose(1, 2, 0, 3)
    early = halves(early, cp_index, swap)
    early = halves(early, seq_index, swap_seq)
    early_cols = early.shape[1]
    both = jnp.concatenate([jnp.pad(early, ((0, feed_piece.shape[0] - rank), (0, 0))), feed_piece], axis=1)
    both = lax.all_gather(after(both, pair_grad), EVERY, axis=0, tiled=False)

    key_grad, value_grad, key_back, value_back, late = last_grads(
        cp_index, pair_grad, flat_cosine, sine_signed, key_expand, value_expand, normed,
        key_narrow, value_narrow, seqs, rank, cp_n,
    )
    late_wide = late.shape[3] * cp_n
    total = late[0].astype(F32) + swap(late[1], 1).astype(F32)
    span = 2
    while span < cp_n:
        total = total[0::2] + swap(total[1::2].astype(BF), span).astype(F32)
        span *= 2
    late = total[0].astype(BF)
    total = late.astype(F32)
    for k in range(1, seq_n):
        total = total + swap_seq(late, k).astype(F32)
    late = total.astype(BF)[None]
    for step in [span_k for span_k in (2**i for i in range(1, 30)) if span_k < plane] + [1]:
        late = jnp.concatenate([late, swap(late, step)], axis=0)

    normed_grad = (
        query_in
        + mm_nt(key_grad, w_key)
        + mm_nt(value_grad, w_value)
        + mm_nt(key_back, key_shrink)
        + mm_nt(value_back, value_shrink)
    )
    input_grad = middle_grad + norm_backward(resid_in, first_scales, normed_grad)

    came = [0]
    for step in [span_k for span_k in (2**i for i in range(1, 30)) if span_k < plane] + [1]:
        came = came + [c ^ step for c in came]
    inverse = [came.index(c) for c in range(plane)]
    late = jnp.take(
        late, jnp.asarray(inverse, jnp.int32)[jnp.arange(plane, dtype=jnp.int32) ^ me], axis=0
    )
    late = late.reshape(fsdp_n, cp_n, rank, late_wide // cp_n)
    late = late.transpose(0, 2, 1, 3).reshape(fsdp_n * rank, late_wide)

    order = jnp.arange(fsdp_n, dtype=jnp.int32) ^ group
    select_all = (
        jnp.take(jnp.stack(select), order, axis=0)[:, :, :rank]
        .transpose(0, 2, 1)
        .reshape(fsdp_n * rank, cols)
    )
    shrink_grad = lambda value: mm_tn(value, select_all)
    expand_grad = lambda value: mm_tn(select_all, value)

    late_of = lambda i: late[:, model * i : model * (i + 1)]
    tail_of = lambda i: late[:, model * 2 + kv_width * i : model * 2 + kv_width * (i + 1)]
    order_kinds = (True, True, True, False, False, True, False)
    if fsdp_n == 2 and 2 * hq % 128 == 0 and 2 * early_cols == model:
        expanded = expand_all(
            both, select_all, rank, hq, hp, seq_n, chips, early_cols, order_kinds
        )
    else:
        early_full = both[:, :rank, :early_cols].reshape(fsdp_n, ways, rank, early_cols)
        early_full = early_full.transpose(0, 2, 1, 3).reshape(fsdp_n * rank, ways * early_cols)
        feed_full = both[:, :, early_cols:].reshape(
            fsdp_n, cp_n // 2, 2, seq_n, fsdp_n // 2, rank, feed_wide // seq_n
        ).transpose(4, 2, 5, 0, 1, 3, 6)
        feed_full = feed_full.reshape(fsdp_n * rank, chips, feed_wide)
        expanded = []
        for i, shrink in enumerate((False, False, True) + order_kinds):
            if i < 3:
                rows = feed_full[:, :, i * hp : i * hp + hq].reshape(fsdp_n * rank, hidden_all)
            else:
                rows = early_full[:, model * (i - 3) : model * (i - 2)]
            expanded.append(shrink_grad(rows) if shrink else expand_grad(rows))

    return (
        outputs,
        input_grad.reshape(seqs, tok_rows, model),
        expanded[8],
        expanded[9],
        shrink_grad(late_of(0)),
        expand_grad(tail_of(0)),
        shrink_grad(late_of(1)),
        expand_grad(tail_of(1)),
        expanded[3],
        expanded[6],
        expanded[4],
        expanded[0],
        expanded[5],
        expanded[1],
        expanded[2],
        expanded[7],
    )


def solution(mesh):
    tokens_spec = P("fsdp", ("cp", "seq"), None)
    weight_spec = P(("fsdp", "cp"), None)
    placed = (
        (tokens_spec, tokens_spec, P("fsdp", None), P("fsdp"), P(), P())
        + (weight_spec,) * 7
        + (P(),) * 17
    )
    return jax.shard_map(
        body,
        mesh=mesh,
        in_specs=placed,
        out_specs=(tokens_spec, tokens_spec) + (P(),) * 14,
        check_vma=False,
    )
```

```python
import functools
import math

import jax
import jax.numpy as jnp
from jax import lax
from jax.experimental import pallas as pl
from jax.experimental.pallas import tpu as pltpu
from jax.sharding import PartitionSpec as P

HEAD_DIM = 128
ADAPTER_RANK = 16
epsilon = 1e-06
adapter_scale = 0.5
rotary_base = 1000000.0
masked_score = -1e30
PLANE = ("fsdp", "cp")
EVERY = ("fsdp", "cp", "seq")
BF = jnp.bfloat16
F32 = jnp.float32


def rotary_tables(positions):
    halfway = HEAD_DIM // 2
    frequency = jnp.exp(
        jnp.arange(halfway, dtype=jnp.float32) * (-2.0 * math.log(rotary_base) / HEAD_DIM)
    )
    angles = positions.astype(jnp.float32)[..., None] * frequency
    angles = jnp.concatenate([angles, angles], axis=-1)
    return (jnp.cos(angles), jnp.sin(angles))


def rotate(values, cosine, sine_table):
    halfway = values.shape[-1] // 2
    turned = jnp.concatenate([-values[..., halfway:], values[..., :halfway]], axis=-1)
    return values * cosine + turned * sine_table


def unrotate(gradient, cosine, sine_table):
    halfway = gradient.shape[-1] // 2
    scaled = gradient * sine_table
    turned = jnp.concatenate([scaled[..., halfway:], -scaled[..., :halfway]], axis=-1)
    return gradient * cosine + turned


def mm(left, right):
    return jnp.dot(left, right, preferred_element_type=jnp.float32)


def mm_nt(left, right):
    return lax.dot_general(
        left, right, (((1,), (1,)), ((), ())), preferred_element_type=jnp.float32
    )


def mm_tn(left, right):
    return lax.dot_general(
        left, right, (((0,), (0,)), ((), ())), preferred_element_type=jnp.float32
    )


def norm_forward(values, scales):
    return values * lax.rsqrt(jnp.mean(values * values, axis=-1, keepdims=True) + epsilon) * scales


def norm_backward(values, scales, gradient):
    inverse = lax.rsqrt(jnp.mean(values * values, axis=-1, keepdims=True) + epsilon)
    weighted = gradient * scales
    inner_sum = jnp.mean(weighted * values, axis=-1, keepdims=True)
    return inverse * weighted - values * (inverse * inverse * inverse) * inner_sum


def heads_to_rows(block):
    count = block.shape[1] // HEAD_DIM
    return jnp.concatenate(
        [block[:, HEAD_DIM * j : HEAD_DIM * (j + 1)] for j in range(count)], axis=0
    )


def rows_to_heads(rows, tokens):
    count = rows.shape[0] // tokens
    return jnp.concatenate([rows[tokens * j : tokens * (j + 1)] for j in range(count)], axis=1)


def attend_kernel(spans, span_len, tokens, info, q_ref, k_ref, v_ref, o_ref, lse_ref, m_ref, l_ref, acc_ref):
    seq = pl.program_id(0)
    seqs = pl.num_programs(0)
    own = info[seqs * spans + seq]
    shift = info[seqs * spans + seqs]
    scale = math.log2(math.e) / math.sqrt(HEAD_DIM)
    queries = heads_to_rows(q_ref[...])
    m_ref[...] = jnp.full(m_ref.shape, masked_score, F32)
    l_ref[...] = jnp.zeros(l_ref.shape, F32)
    acc_ref[...] = jnp.zeros(acc_ref.shape, F32)

    def update(j, masked):
        rows = pl.ds(pl.multiple_of(j * span_len, span_len), span_len)
        scores = mm_nt(k_ref[0, rows, :], queries) * scale
        if masked:
            key_at = lax.broadcasted_iota(jnp.int32, scores.shape, 0)
            query_at = shift + lax.rem(lax.broadcasted_iota(jnp.int32, scores.shape, 1), tokens)
            scores = jnp.where(key_at <= query_at, scores, masked_score)
        old = m_ref[...]
        top = jnp.maximum(old, jnp.max(scores, axis=0, keepdims=True))
        expo = jnp.exp2(scores - top)
        alpha = jnp.exp2(old - top)
        l_ref[...] = l_ref[...] * alpha + jnp.sum(expo, axis=0, keepdims=True)
        acc_ref[...] = acc_ref[...] * alpha + mm_tn(v_ref[0, rows, :], expo.astype(BF))
        m_ref[...] = top

    def step(j, carry):
        other = info[seq * spans + j]

        @pl.when(other < own)
        def _():
            update(j, False)

        @pl.when(other == own)
        def _():
            update(j, True)

        return carry

    lax.fori_loop(0, spans, step, 0)
    total = l_ref[...]
    out = jnp.transpose(acc_ref[...] / total)
    o_ref[...] = rows_to_heads(out.astype(BF), tokens)
    lse_ref[0] = jnp.broadcast_to(m_ref[...] + jnp.log2(total), lse_ref.shape[1:])


def attend(info, queries, pairs, seqs, spans, span_len):
    tokens = queries.shape[0] // seqs
    length = pairs.shape[1]
    kv_heads = pairs.shape[2] // (2 * HEAD_DIM)
    width = queries.shape[1] // kv_heads
    rows = tokens * (width // HEAD_DIM)
    grid_spec = pltpu.PrefetchScalarGridSpec(
        num_scalar_prefetch=1,
        grid=(seqs, kv_heads),
        in_specs=[
            pl.BlockSpec((tokens, width), lambda s, h, i: (s, h)),
            pl.BlockSpec((1, length, HEAD_DIM), lambda s, h, i: (s, 0, h)),
            pl.BlockSpec((1, length, HEAD_DIM), lambda s, h, i: (s, 0, kv_heads + h)),
        ],
        out_specs=[
            pl.BlockSpec((tokens, width), lambda s, h, i: (s, h)),
            pl.BlockSpec((1, 8, rows), lambda s, h, i: (s * kv_heads + h, 0, 0)),
        ],
        scratch_shapes=[pltpu.VMEM((1, rows), F32)] * 2 + [pltpu.VMEM((HEAD_DIM, rows), F32)],
    )
    work = seqs * kv_heads * rows * length
    return pl.pallas_call(
        functools.partial(attend_kernel, spans, span_len, tokens),
        grid_spec=grid_spec,
        out_shape=[
            jax.ShapeDtypeStruct(queries.shape, BF),
            jax.ShapeDtypeStruct((seqs * kv_heads, 8, rows), F32),
        ],
        name="attend",
        cost_estimate=pl.CostEstimate(
            flops=4 * work * HEAD_DIM, bytes_accessed=pairs.size * 2, transcendentals=work
        ),
    )(info, queries, pairs, pairs)


def attend_back_kernel(
    spans, span_len, tokens, kv_heads,
    info, q_ref, do_ref, o_ref, k_ref, v_ref, lse_ref, dq_ref, dkv_ref, acc_ref,
):
    seq = pl.program_id(0)
    head = pl.program_id(1)
    seqs = pl.num_programs(0)
    own = info[seqs * spans + seq]
    shift = info[seqs * spans + seqs]
    root = 1.0 / math.sqrt(HEAD_DIM)
    scale = math.log2(math.e) * root
    queries = heads_to_rows(q_ref[...])
    grads = heads_to_rows(do_ref[...])
    results = heads_to_rows(o_ref[...])
    inner = jnp.sum(
        jnp.transpose(grads.astype(F32) * results.astype(F32)), axis=0, keepdims=True
    )
    lse = lse_ref[0, :1, :]
    acc_ref[...] = jnp.zeros(acc_ref.shape, F32)
    key_lane = pl.multiple_of(head * HEAD_DIM, HEAD_DIM)
    val_lane = pl.multiple_of((kv_heads + head) * HEAD_DIM, HEAD_DIM)

    def store(j, key_grad, value_grad):
        rows = pl.ds(pl.multiple_of(j * span_len, span_len), span_len)
        dkv_ref[0, rows, pl.ds(key_lane, HEAD_DIM)] = key_grad
        dkv_ref[0, rows, pl.ds(val_lane, HEAD_DIM)] = value_grad

    def update(j, masked):
        rows = pl.ds(pl.multiple_of(j * span_len, span_len), span_len)
        keys = k_ref[0, rows, :]
        prob = jnp.exp2(mm_nt(keys, queries) * scale - lse)
        if masked:
            key_at = lax.broadcasted_iota(jnp.int32, prob.shape, 0)
            query_at = shift + lax.rem(lax.broadcasted_iota(jnp.int32, prob.shape, 1), tokens)
            prob = jnp.where(key_at <= query_at, prob, 0.0)
        prob_grad = mm_nt(v_ref[0, rows, :], grads)
        score_grad = (prob * (prob_grad - inner)).astype(BF)
        acc_ref[...] += mm_tn(score_grad, keys)
        store(
            j, (mm(score_grad, queries) * root).astype(BF), mm(prob.astype(BF), grads).astype(BF)
        )

    def step(j, carry):
        other = info[seq * spans + j]

        @pl.when(other < own)
        def _():
            update(j, False)

        @pl.when(other == own)
        def _():
            update(j, True)

        @pl.when(other > own)
        def _():
            zero = jnp.zeros((span_len, HEAD_DIM), BF)
            store(j, zero, zero)

        return carry

    lax.fori_loop(0, spans, step, 0)
    dq_ref[...] = rows_to_heads((acc_ref[...] * root).astype(BF), tokens)


def attend_back(info, queries, grads, results, pairs, lse, seqs, spans, span_len):
    tokens = queries.shape[0] // seqs
    length = pairs.shape[1]
    kv_heads = pairs.shape[2] // (2 * HEAD_DIM)
    width = queries.shape[1] // kv_heads
    rows = tokens * (width // HEAD_DIM)
    row = pl.BlockSpec((tokens, width), lambda s, h, i: (s, h))
    block = (1, length, pairs.shape[2])
    grid_spec = pltpu.PrefetchScalarGridSpec(
        num_scalar_prefetch=1,
        grid=(seqs, kv_heads),
        in_specs=[
            row,
            row,
            row,
            pl.BlockSpec((1, length, HEAD_DIM), lambda s, h, i: (s, 0, h)),
            pl.BlockSpec((1, length, HEAD_DIM), lambda s, h, i: (s, 0, kv_heads + h)),
            pl.BlockSpec((1, 8, rows), lambda s, h, i: (s * kv_heads + h, 0, 0)),
        ],
        out_specs=[row, pl.BlockSpec(block, lambda s, h, i: (s, 0, 0))],
        scratch_shapes=[pltpu.VMEM((rows, HEAD_DIM), F32)],
    )
    work = seqs * kv_heads * rows * length
    return pl.pallas_call(
        functools.partial(attend_back_kernel, spans, span_len, tokens, kv_heads),
        grid_spec=grid_spec,
        out_shape=[
            jax.ShapeDtypeStruct(queries.shape, BF),
            jax.ShapeDtypeStruct(pairs.shape, BF),
        ],
        name="attend_back",
        cost_estimate=pl.CostEstimate(
            flops=10 * work * HEAD_DIM, bytes_accessed=pairs.size * 4, transcendentals=work
        ),
    )(info, queries, grads, results, pairs, pairs, lse)


def turned(values, cosine, sine_signed):
    return values * cosine + pltpu.roll(values, HEAD_DIM // 2, axis=1) * sine_signed


def fetch_rows(index, blocks, out_ref, sems):
    depth = blocks[0].shape[0]
    return [
        pltpu.make_async_copy(
            block,
            out_ref.at[pl.ds(pl.multiple_of((index ^ j) * depth, depth), depth), :],
            sems.at[j],
        )
        for j, block in enumerate(blocks)
    ]


def keys_kernel(
    seqs, x_ref, gain_ref, w_ref, shrink_ref, ek_ref, ev_ref, bias_ref, cos_ref, sin_ref,
    normed_ref, nk_ref, nv_ref, pair_ref,
):
    tokens, width = pair_ref.shape
    kv = width // 2
    lanes = ek_ref.shape[0]
    normed = norm_forward(x_ref[...].astype(F32), gain_ref[...]).astype(BF)
    normed_ref[...] = normed
    mix = token_mask(tokens, lanes, seqs)
    narrow = mm(normed, shrink_ref[...])
    narrow_k = (narrow[:, :lanes] * mix).astype(BF)
    narrow_v = (narrow[:, lanes:] * mix).astype(BF)
    nk_ref[...] = narrow_k
    nv_ref[...] = narrow_v
    raw = mm(normed, w_ref[...]) + bias_ref[...]
    keys = raw[:, :kv] + mm(narrow_k, ek_ref[...])
    vals = raw[:, kv:] + mm(narrow_v, ev_ref[...])
    cosine = cos_ref[...]
    sine = sin_ref[...]
    for h in range(kv // HEAD_DIM):
        at = slice(h * HEAD_DIM, (h + 1) * HEAD_DIM)
        pair_ref[:, at] = turned(keys[:, at], cosine, sine).astype(BF)
    pair_ref[:, kv:] = vals.astype(BF)


def keys_values(x, gain, w_kv, shrink, expand_k, expand_v, bias, cosine, sine, seqs):
    tokens, model = x.shape
    lanes = expand_k.shape[0]
    low = lambda n: jax.ShapeDtypeStruct((tokens, n), BF)
    return pl.pallas_call(
        functools.partial(keys_kernel, seqs),
        out_shape=[low(model), low(lanes), low(lanes), low(w_kv.shape[1])],
        name="keys_values",
        cost_estimate=pl.CostEstimate(
            flops=2 * tokens * model * w_kv.shape[1],
            bytes_accessed=8 * tokens * model,
            transcendentals=tokens,
        ),
    )(x, gain, w_kv, shrink, expand_k, expand_v, bias, cosine, sine)


def queries_kernel(
    seqs, count, info, normed_ref, shrink_ref, eq_ref, bias_ref, cos_ref, sin_ref, *refs
):
    blocks = refs[:count]
    query_ref, narrow_ref, w_ref, sems = refs[count:]
    copies = fetch_rows(info[0], blocks, w_ref, sems)
    for copy in copies:
        copy.start()
    tokens, model = query_ref.shape
    lanes = eq_ref.shape[0]
    normed = normed_ref[...]
    narrow = (mm(normed, shrink_ref[...]) * token_mask(tokens, lanes, seqs)).astype(BF)
    narrow_ref[...] = narrow
    for copy in copies:
        copy.wait()
    cosine = cos_ref[...]
    sine = sin_ref[...]
    step = 2 * HEAD_DIM
    for c in range(0, model, step):
        raw = mm(normed, w_ref[:, c : c + step]) + bias_ref[:, c : c + step]
        raw = raw + mm(narrow, eq_ref[:, c : c + step])
        for h in range(0, step, HEAD_DIM):
            query_ref[:, c + h : c + h + HEAD_DIM] = turned(
                raw[:, h : h + HEAD_DIM], cosine, sine
            ).astype(BF)


def outputs_kernel(seqs, count, info, attended_ref, x_ref, gain_ref, shrink_ref, eo_ref, *refs):
    blocks = refs[:count]
    middle_ref, normed_ref, top_ref, bottom_ref, narrow_ref, w_ref, sems = refs[count:]
    copies = fetch_rows(info[0], blocks, w_ref, sems)
    for copy in copies:
        copy.start()
    tokens, model = middle_ref.shape
    lanes = eo_ref.shape[0]
    attended = attended_ref[...]
    narrow = (mm(attended, shrink_ref[...]) * token_mask(tokens, lanes, seqs)).astype(BF)
    narrow_ref[...] = narrow
    for copy in copies:
        copy.wait()
    middle = x_ref[...].astype(F32) + (mm(attended, w_ref[...]) + mm(narrow, eo_ref[...]))
    middle_ref[...] = middle
    normed = norm_forward(middle, gain_ref[...]).astype(BF)
    normed_ref[...] = normed
    top_ref[...] = normed[: tokens // 2]
    bottom_ref[...] = normed[tokens // 2 :]


def before_attention_kernel(
    seqs, most_ref, last_ref, grad_ref, middle_ref, gain_ref, gs_ref, us_ref, os_ref, oe_ref, w_ref,
    mg_ref, low_ref, gb_ref, ub_ref, ob_ref, ag_ref,
):
    tokens, model = mg_ref.shape
    lanes = oe_ref.shape[0]
    mix = token_mask(tokens, lanes, seqs)
    total = most_ref[...] + last_ref[...].astype(F32)
    gate_back = (total[:, model : model + lanes] * mix).astype(BF)
    up_back = (total[:, model + lanes :] * mix).astype(BF)
    gb_ref[...] = gate_back
    ub_ref[...] = up_back
    normed_grad = total[:, :model] + mm_nt(gate_back, gs_ref[...]) + mm_nt(up_back, us_ref[...])
    middle_grad = grad_ref[...].astype(F32) + norm_backward(
        middle_ref[...], gain_ref[...], normed_grad
    )
    mg_ref[...] = middle_grad
    low = middle_grad.astype(BF)
    low_ref[...] = low
    output_back = (mm_nt(low, oe_ref[...]) * mix).astype(BF)
    ob_ref[...] = output_back
    ag_ref[...] = (mm_nt(low, w_ref[...]) + mm_nt(output_back, os_ref[...])).astype(BF)


def before_attention(most, last, grad, middle, gain, gs, us, os, oe, w_output, seqs):
    tokens, model = middle.shape
    lanes = oe.shape[0]
    low = lambda n: jax.ShapeDtypeStruct((tokens, n), BF)
    return pl.pallas_call(
        functools.partial(before_attention_kernel, seqs),
        out_shape=[
            jax.ShapeDtypeStruct((tokens, model), F32),
            low(model), low(lanes), low(lanes), low(lanes), low(model),
        ],
        name="before_attention",
        cost_estimate=pl.CostEstimate(
            flops=2 * tokens * model * model, bytes_accessed=30 * tokens * model, transcendentals=0
        ),
    )(most, last, grad, middle, gain, gs, us, os, oe, w_output)


def last_grads_kernel(
    seqs, rank, info, pair_ref, cos_ref, sin_ref, ke_ref, ve_ref, normed_ref, nk_ref, nv_ref,
    kg_ref, vg_ref, kb_ref, vb_ref, late_ref, rows_ref,
):
    tokens, width = pair_ref.shape
    kv = width // 2
    lanes = ke_ref.shape[0]
    model = normed_ref.shape[1]
    mix = token_mask(tokens, lanes, seqs)
    cosine = cos_ref[...]
    sine = -sin_ref[...]
    for h in range(kv // HEAD_DIM):
        at = slice(h * HEAD_DIM, (h + 1) * HEAD_DIM)
        kg_ref[:, at] = turned(pair_ref[:, at].astype(F32), cosine, sine).astype(BF)
    vg_ref[...] = pair_ref[:, kv:]
    key_grad = kg_ref[...]
    value_grad = vg_ref[...]
    key_back = (mm_nt(key_grad, ke_ref[...]) * mix).astype(BF)
    value_back = (mm_nt(value_grad, ve_ref[...]) * mix).astype(BF)
    kb_ref[...] = key_back
    vb_ref[...] = value_back
    normed = normed_ref[...]
    rows_ref[:, :model] = mm_tn(key_back, normed)[:rank].astype(BF)
    rows_ref[:, model : 2 * model] = mm_tn(value_back, normed)[:rank].astype(BF)
    rows_ref[:, 2 * model : 2 * model + kv] = mm_tn(nk_ref[...], key_grad)[:rank].astype(BF)
    rows_ref[:, 2 * model + kv :] = mm_tn(nv_ref[...], value_grad)[:rank].astype(BF)
    parts = 2 * late_ref.shape[1]
    size = late_ref.shape[3]
    for p in range(parts):
        at = p ^ info[0]
        late_ref[lax.rem(at, 2), at // 2] = rows_ref[:, p * size : (p + 1) * size]


def last_grads(mine, pair_grad, cosine, sine, ke, ve, normed, nk, nv, seqs, rank, parts):
    tokens, width = pair_grad.shape
    lanes = ke.shape[0]
    model = normed.shape[1]
    low = lambda n: jax.ShapeDtypeStruct((tokens, n), BF)
    total = 2 * model + width
    operands = [pair_grad, cosine, sine, ke, ve, normed, nk, nv]
    results = [
        low(width // 2), low(width // 2), low(lanes), low(lanes),
        jax.ShapeDtypeStruct((2, parts // 2, rank, total // parts), BF),
    ]
    return pl.pallas_call(
        functools.partial(last_grads_kernel, seqs, rank),
        grid_spec=pltpu.PrefetchScalarGridSpec(
            num_scalar_prefetch=1,
            grid=(1,),
            in_specs=[pl.BlockSpec(a.shape, lambda g, i, n=a.ndim: (0,) * n) for a in operands],
            out_specs=[
                pl.BlockSpec(r.shape, lambda g, i, n=len(r.shape): (0,) * n) for r in results
            ],
            scratch_shapes=[pltpu.VMEM((rank, total), BF)],
        ),
        out_shape=results,
        name="last_grads",
        cost_estimate=pl.CostEstimate(
            flops=4 * tokens * model * 128, bytes_accessed=6 * tokens * model, transcendentals=0
        ),
    )(mine.reshape(1).astype(jnp.int32), *operands)


def with_blocks(kernel, name, seqs, index, blocks, operands, results):
    count = len(blocks)
    depth, lanes = blocks[0].shape
    inside = pl.BlockSpec(memory_space=pltpu.VMEM)
    results = list(results) + [jax.ShapeDtypeStruct((count * depth, lanes), BF)]
    return pl.pallas_call(
        functools.partial(kernel, seqs, count),
        grid_spec=pltpu.PrefetchScalarGridSpec(
            num_scalar_prefetch=1,
            grid=(1,),
            in_specs=[pl.BlockSpec(a.shape, lambda g, i, n=a.ndim: (0,) * n) for a in operands]
            + [pl.BlockSpec(memory_space=pl.ANY)] * count,
            out_specs=[pl.BlockSpec(r.shape, lambda g, i: (0, 0)) for r in results],
            scratch_shapes=[pltpu.SemaphoreType.DMA((count,))],
        ),
        out_shape=results,
        name=name,
        cost_estimate=pl.CostEstimate(
            flops=2 * operands[0].shape[0] * count * depth * lanes,
            bytes_accessed=4 * count * depth * lanes,
            transcendentals=0,
        ),
    )(index.reshape(1).astype(jnp.int32), *operands, *blocks)


def token_mask(tokens, lanes, seqs):
    row = lax.broadcasted_iota(jnp.int32, (tokens, lanes), 0) // (tokens // seqs)
    lane = lax.broadcasted_iota(jnp.int32, (tokens, lanes), 1) // ADAPTER_RANK
    return jnp.where(row == lane, adapter_scale, 0.0).astype(F32)


def feed_kernel(seqs, kinds, info, *refs):
    count = len(kinds)
    blocks = refs[:count]
    top_ref, bottom_ref, grad_top_ref, grad_bottom_ref = refs[count : count + 4]
    count += 4
    sgu_ref, ed_ref, wd_ref, eg_ref, eu_ref, sd_ref = refs[count : count + 6]
    peg_ref, peu_ref, psd_ref = refs[count + 6 : count + 9]
    out_ref, ng_ref, deg_ref, deu_ref, dsd_ref = refs[count + 9 : count + 14]
    acc_out, acc_ng, acc_nd, acc_bg, acc_bu, nar_g, nar_u, back_d, held, sems = refs[count + 14 :]
    chunk = pl.program_id(0)
    chunks = pl.num_programs(0)
    depth = blocks[0].shape[-2]
    size = wd_ref.shape[0]

    def copies(at, slot):
        found = []
        for n, (j, which) in enumerate(kinds):
            rows = pl.ds(pl.multiple_of((info[0] ^ j) * depth, depth), depth)
            lanes = pl.ds(pl.multiple_of(at * size, 128), size)
            if which is None:
                source, target = blocks[n].at[:, :, lanes], held.at[slot, :, rows, :]
            else:
                source, target = blocks[n].at[:, lanes], held.at[slot, info[1] ^ which, rows, :]
            found.append(pltpu.make_async_copy(source, target, sems.at[slot, n]))
        return found

    slot = lax.rem(chunk, 2)

    @pl.when(chunk == 0)
    def _():
        for copy in copies(chunk, slot):
            copy.start()

    @pl.when(chunk + 1 < chunks)
    def _():
        for copy in copies(chunk + 1, 1 - slot):
            copy.start()

    tokens = out_ref.shape[0]
    model = top_ref.shape[1]
    cols = sd_ref.shape[1]
    n2 = jnp.concatenate([top_ref[...], bottom_ref[...]], axis=0)
    g0 = jnp.concatenate([grad_top_ref[...], grad_bottom_ref[...]], axis=0)
    wg_ref = held.at[slot, 0]
    wu_ref = held.at[slot, 1]

    @pl.when(chunk == 0)
    def _():
        mix = token_mask(tokens, cols, seqs)
        narrow = mm(n2, sgu_ref[...])
        nar_g[...] = (narrow[:, :cols] * mix).astype(BF)
        nar_u[...] = (narrow[:, cols:] * mix).astype(BF)
        back_d[...] = (mm_nt(g0, ed_ref[...]) * mix).astype(BF)
        for acc in (acc_out, acc_ng, acc_nd, acc_bg, acc_bu):
            acc[...] = jnp.zeros(acc.shape, F32)

    for copy in copies(chunk, slot):
        copy.wait()
    narrow_g = nar_g[...]
    narrow_u = nar_u[...]
    narrow_b = back_d[...]
    gate = mm(n2, wg_ref[...]) + mm(narrow_g, eg_ref[...])
    upward = mm(n2, wu_ref[...]) + mm(narrow_u, eu_ref[...])
    sig = jax.nn.sigmoid(gate)
    act = gate * sig
    hidden = (act * upward).astype(BF)
    hidden_grad = mm_nt(g0, wd_ref[...]) + mm_nt(narrow_b, sd_ref[...])
    gate_grad = (hidden_grad * upward * (sig * (1.0 + gate * (1.0 - sig)))).astype(BF)
    up_grad = (hidden_grad * act).astype(BF)
    acc_out[...] += mm(hidden, wd_ref[...])
    acc_nd[...] += mm(hidden, sd_ref[...])
    acc_ng[...] += mm_nt(gate_grad, wg_ref[...]) + mm_nt(up_grad, wu_ref[...])
    acc_bg[...] += mm_nt(gate_grad, eg_ref[...])
    acc_bu[...] += mm_nt(up_grad, eu_ref[...])
    deg_ref[...] = peg_ref[...] + mm_tn(narrow_g, gate_grad)
    deu_ref[...] = peu_ref[...] + mm_tn(narrow_u, up_grad)
    dsd_ref[...] = psd_ref[...] + mm_tn(narrow_b, hidden)

    @pl.when(chunk == chunks - 1)
    def _():
        out_ref[:, :model] = acc_out[...].astype(BF)
        out_ref[:, model:] = jnp.concatenate([acc_nd[...], acc_nd[...]], axis=1).astype(BF)
        ng_ref[:, :model] = acc_ng[...].astype(BF)
        ng_ref[:, model:] = jnp.concatenate([acc_bg[...], acc_bu[...]], axis=1).astype(BF)


def feed(index, kinds, blocks, n2, g0, sgu, ed, wd, eg, eu, sd, previous, seqs, limit=768):
    tokens, model = 2 * n2[0].shape[0], n2[0].shape[1]
    count = len(blocks)
    hidden = wd.shape[0]
    cols = ed.shape[0]
    size = max(c for c in range(128, limit + 1, 128) if hidden % c == 0)
    anywhere = pl.BlockSpec(memory_space=pl.ANY)
    whole = lambda a: pl.BlockSpec(
        a.shape, lambda h, i: (0,) * a.ndim, pipeline_mode=pl.Buffered(1)
    )
    part = lambda a: pl.BlockSpec((a.shape[0], size), lambda h, i: (0, h))
    tall = lambda a: pl.BlockSpec((size, a.shape[1]), lambda h, i: (h, 0))
    fixed = lambda c: pl.BlockSpec((tokens, c), lambda h, i: (0, 0))
    grads = jax.ShapeDtypeStruct((cols, hidden), F32)
    return pl.pallas_call(
        functools.partial(feed_kernel, seqs, tuple(kinds)),
        grid_spec=pltpu.PrefetchScalarGridSpec(
            num_scalar_prefetch=1,
            grid=(hidden // size,),
            in_specs=[anywhere] * count
            + [whole(n2[0]), whole(n2[1]), whole(g0[0]), whole(g0[1]), whole(sgu), whole(ed), tall(wd)]
            + [part(eg), part(eu), tall(sd), part(grads), part(grads), part(grads)],
            out_specs=[fixed(model + 2 * cols), fixed(model + 2 * cols)] + [part(grads)] * 3,
            scratch_shapes=[
                pltpu.VMEM((tokens, model), F32),
                pltpu.VMEM((tokens, model), F32),
                pltpu.VMEM((tokens, cols), F32),
                pltpu.VMEM((tokens, cols), F32),
                pltpu.VMEM((tokens, cols), F32),
                pltpu.VMEM((tokens, cols), BF),
                pltpu.VMEM((tokens, cols), BF),
                pltpu.VMEM((tokens, cols), BF),
                pltpu.VMEM((2, 2, model, size), BF),
                pltpu.SemaphoreType.DMA((2, count)),
            ],
        ),
        out_shape=[
            jax.ShapeDtypeStruct((tokens, model + 2 * cols), BF),
            jax.ShapeDtypeStruct((tokens, model + 2 * cols), BF),
            grads, grads, grads,
        ],
        name="feed",
        cost_estimate=pl.CostEstimate(
            flops=12 * tokens * (model + cols) * hidden,
            bytes_accessed=6 * model * hidden,
            transcendentals=tokens * hidden,
        ),
    )(index, *blocks, *n2, *g0, sgu, ed, wd, eg, eu, sd, *previous)


def assemble_kernel(count, info, *refs):
    blocks = refs[:count]
    out_ref, held, blank, in_sem, out_sem = refs[count:]
    depth = blocks[0].shape[0]
    rest = out_ref.shape[0] - count * depth
    arrive = []
    leave = []
    for j in range(count):
        arrive.append(pltpu.make_async_copy(blocks[j], held.at[j], in_sem.at[j]))
        at = pl.multiple_of((info[0] ^ j) * depth, depth)
        leave.append(
            pltpu.make_async_copy(held.at[j], out_ref.at[pl.ds(at, depth), :], out_sem.at[j])
        )
    for copy in arrive:
        copy.start()
    if rest:
        blank[...] = jnp.zeros(blank.shape, BF)
        last = pltpu.make_async_copy(blank, out_ref.at[count * depth :, :], out_sem.at[count])
        last.start()
    for one, two in zip(arrive, leave):
        one.wait()
        two.start()
    for copy in leave:
        copy.wait()
    if rest:
        last.wait()


def assemble(index, blocks, rows):
    count = len(blocks)
    depth, lanes = blocks[0].shape
    anywhere = pl.BlockSpec(memory_space=pl.ANY)
    return pl.pallas_call(
        functools.partial(assemble_kernel, count),
        grid_spec=pltpu.PrefetchScalarGridSpec(
            num_scalar_prefetch=1,
            grid=(1,),
            in_specs=[anywhere] * count,
            out_specs=anywhere,
            scratch_shapes=[
                pltpu.VMEM((count, depth, lanes), BF),
                pltpu.VMEM((max(rows - count * depth, 16), lanes), BF),
                pltpu.SemaphoreType.DMA((count,)),
                pltpu.SemaphoreType.DMA((count + 1,)),
            ],
        ),
        out_shape=jax.ShapeDtypeStruct((rows, lanes), BF),
        name="assemble",
        cost_estimate=pl.CostEstimate(
            flops=0, bytes_accessed=4 * rows * lanes, transcendentals=0
        ),
    )(index.reshape(1).astype(jnp.int32), *blocks)


def expand_kernel(rank, hidden, padded, seq_n, early, kinds, both_ref, select_ref, *outs):
    pair = pl.program_id(0)
    select = select_ref[...]
    lanes = -(-hidden // 128) * 128
    width = both_ref.shape[2] - early
    for q in range(2):
        for i, out_ref in enumerate(outs[:3]):
            groups = []
            for f in range(2):
                at = i * padded
                left = lanes
                pieces = []
                while left:
                    z, low = divmod(at, width)
                    take = min(left, width - low)
                    device = pair * 4 * seq_n + (q * 2 + f) * seq_n + z
                    pieces.append(both_ref[device, :rank, early + low : early + low + take])
                    at += take
                    left -= take
                groups.append(jnp.concatenate(pieces, axis=1))
            rows = jnp.concatenate(groups, axis=0)
            if i < 2:
                out_ref[:, q * hidden : (q + 1) * hidden] = mm_tn(select, rows)[:, :hidden]
            else:
                out_ref[q * hidden : (q + 1) * hidden, :] = mm_tn(rows, select)[:hidden]

    @pl.when(pair == 0)
    def _():
        half = both_ref.shape[0] // 2
        for i, (out_ref, shrink) in enumerate(zip(outs[3:], kinds)):
            rows = jnp.concatenate(
                [
                    jnp.concatenate(
                        [both_ref[f * half + 2 * i + w, :rank, :early] for w in range(2)], axis=1
                    )
                    for f in range(2)
                ],
                axis=0,
            )
            out_ref[...] = mm_tn(rows, select) if shrink else mm_tn(select, rows)


def expand_all(both, select, rank, hidden, padded, seq_n, chips, early, kinds):
    cols = select.shape[1]
    model = 2 * early
    wide = lambda n: jax.ShapeDtypeStruct((cols, n), F32)
    tall = lambda n: jax.ShapeDtypeStruct((n, cols), F32)
    fixed = [tall(model) if shrink else wide(model) for shrink in kinds]
    return pl.pallas_call(
        functools.partial(expand_kernel, rank, hidden, padded, seq_n, early, kinds),
        grid=(chips // 2,),
        in_specs=[
            pl.BlockSpec(both.shape, lambda p: (0, 0, 0), pipeline_mode=pl.Buffered(1)),
            pl.BlockSpec(select.shape, lambda p: (0, 0)),
        ],
        out_specs=[
            pl.BlockSpec((cols, 2 * hidden), lambda p: (0, p)),
            pl.BlockSpec((cols, 2 * hidden), lambda p: (0, p)),
            pl.BlockSpec((2 * hidden, cols), lambda p: (p, 0)),
        ]
        + [pl.BlockSpec(one.shape, lambda p: (0, 0)) for one in fixed],
        out_shape=[wide(chips * hidden), wide(chips * hidden), tall(chips * hidden)] + fixed,
        name="expand",
        cost_estimate=pl.CostEstimate(
            flops=6 * cols * chips * hidden * select.shape[0],
            bytes_accessed=12 * cols * chips * hidden,
            transcendentals=0,
        ),
    )(both, select)


def after(value, *needed):
    return lax.optimization_barrier((value, needed))[0]


def body(
    inputs, cotangent, span_order, adapter_ids, first_gain, second_gain,
    query_weight, key_weight, value_weight, output_weight, gate_weight, up_weight, down_weight,
    query_bias, key_bias, value_bias,
    query_reduce_factors, query_lift_factors, key_reduce_factors, key_lift_factors,
    value_reduce_factors, value_lift_factors, output_reduce_factors, output_lift_factors,
    gate_reduce_factors, gate_lift_factors, upper_reduce_factors, upper_lift_factors,
    down_reduce_factors, down_lift_factors,
):
    seq_n = lax.axis_size("seq")
    cp_n = lax.axis_size("cp")
    fsdp_n = lax.axis_size("fsdp")
    plane = fsdp_n * cp_n
    chips = plane // 2
    group = lax.axis_index("fsdp")
    me = group * cp_n + lax.axis_index("cp")
    chip = me // 2
    core = me % 2
    seqs, tok_rows, model = inputs.shape
    tokens = seqs * tok_rows
    cols = query_reduce_factors.shape[1]
    kv_width = key_weight.shape[1]
    length = tok_rows * seq_n * cp_n
    spans = span_order.shape[1]
    span_len = length // spans
    hidden_all = gate_weight.shape[1]
    hq = hidden_all // chips
    hp = -(-hq // 256) * 256
    pad = hp - hq
    rank = seqs * ADAPTER_RANK
    lanes = -(-rank // 64) * 64

    def swap(value, k):
        return lax.ppermute(value, PLANE, [(i, i ^ k) for i in range(plane)])

    def swap_seq(value, k):
        return lax.ppermute(value, "seq", [(i, i ^ k) for i in range(seq_n)])

    first_row = (lax.axis_index("cp") * seq_n + lax.axis_index("seq")) * tok_rows
    own = lax.dynamic_slice_in_dim(span_order, first_row // span_len, 1, 1)[:, 0]
    shift = first_row % span_len
    cp_index = lax.axis_index("cp")
    seq_index = lax.axis_index("seq")
    info = jnp.concatenate(
        [span_order.reshape(-1), own, jnp.stack([shift, cp_index])]
    ).astype(jnp.int32)
    places = own[:, None] * span_len + shift + jnp.arange(tok_rows, dtype=jnp.int32)[None, :]
    cosine, sine_table = rotary_tables(places.reshape(tokens))
    sine_signed = jnp.where(
        jnp.arange(HEAD_DIM, dtype=jnp.int32) < HEAD_DIM // 2, -sine_table, sine_table
    )
    flat_cosine = cosine
    cosine = cosine[:, None, :]
    sine_table = sine_table[:, None, :]
    lane = jnp.arange(lanes, dtype=jnp.int32)

    def chosen(ids):
        column = jnp.repeat(ids, ADAPTER_RANK) * ADAPTER_RANK + lane[:rank] % ADAPTER_RANK
        column = jnp.pad(column, (0, lanes - rank), constant_values=-1)
        return (jnp.arange(cols, dtype=jnp.int32)[:, None] == column[None, :]).astype(BF)

    ids_wide = jnp.broadcast_to(
        jnp.pad(adapter_ids, (0, -seqs % 8)).astype(F32)[:, None], (seqs + -seqs % 8, 128)
    )
    select = [chosen(adapter_ids)]
    for f in range(1, fsdp_n):
        select.append(chosen(swap(ids_wide, f * cp_n)[:seqs, 0].astype(jnp.int32)))
    mixing = token_mask(tokens, lanes, seqs)

    def shrink_of(value, f=0):
        return mm(value, select[f]).astype(BF)

    def expand_of(value, f=0):
        return mm_tn(select[f], value).astype(BF)

    w_kv = lax.all_gather(
        jnp.concatenate([key_weight, value_weight], axis=1), PLANE, axis=0, tiled=True
    )
    rows_q = [query_weight] + [swap(query_weight, 2 * k) for k in range(1, chips)]

    def by_chip(value):
        return jnp.stack(
            [
                jnp.pad(value[:, hq * c : hq * (c + 1)], ((0, 0), (0, pad)))
                for c in range(chips)
            ]
        )

    gate_up = jnp.stack([by_chip(gate_weight), by_chip(up_weight)], axis=1)
    depth = gate_weight.shape[0]
    parts = [lax.dynamic_index_in_dim(gate_up, chip ^ k, 0, keepdims=False) for k in range(chips)]

    low_in = inputs.reshape(tokens, model)
    resid_in = low_in.astype(F32)
    first_scales = first_gain.astype(F32)
    second_scales = second_gain.astype(F32)
    grad_low = cotangent.reshape(tokens, model)
    w_kv, parts, rows_q = lax.optimization_barrier((w_kv, parts, rows_q))
    rows_o = [output_weight] + [swap(after(output_weight, rows_q), 2 * k) for k in range(1, chips)]
    blocks = {}
    w_key = w_kv[:, :kv_width]
    w_value = w_kv[:, kv_width:]

    query_shrink, key_shrink, value_shrink, output_shrink = [
        shrink_of(value)
        for value in (
            query_reduce_factors, key_reduce_factors, value_reduce_factors, output_reduce_factors,
        )
    ]
    query_expand, key_expand, value_expand, output_expand = [
        expand_of(value)
        for value in (
            query_lift_factors, key_lift_factors, value_lift_factors, output_lift_factors,
        )
    ]
    grad_halves = (grad_low[: tokens // 2], grad_low[tokens // 2 :])
    w_kv, output_shrink, output_expand, query_shrink, query_expand, grad_halves = (
        lax.optimization_barrier(
            (w_kv, output_shrink, output_expand, query_shrink, query_expand, grad_halves)
        )
    )

    def swap_both(pair, k):
        return tuple(swap(half, k) for half in pair)

    g0_pieces = {
        k: swap_both(after(grad_halves, rows_q), 2 * k) for k in range(1, chips) if 2 * k % cp_n == 0
    }

    def narrowed(value, shrink):
        return (mm(value, shrink) * mixing).astype(BF)

    normed, key_narrow, value_narrow, pair = keys_values(
        low_in, first_scales[None], w_kv, jnp.concatenate([key_shrink, value_shrink], axis=1),
        key_expand, value_expand,
        jnp.concatenate([key_bias, value_bias]).astype(F32)[None], flat_cosine, sine_signed, seqs,
    )
    pair_all = lax.all_gather(
        pair.reshape(seqs, tok_rows, 2 * kv_width), ("cp", "seq"), axis=1, tiled=True
    )

    def both_cores(rows):
        found = []
        for part in rows:
            found += [part, swap(part, 1)]
        return found

    query_rot, query_narrow, w_query = with_blocks(
        queries_kernel, "queries", seqs, me, after(both_cores(rows_q), pair),
        [
            after(normed, rows_o, g0_pieces), query_shrink, query_expand, query_bias.astype(F32)[None], flat_cosine,
            sine_signed,
        ],
        [
            jax.ShapeDtypeStruct((tokens, model), BF),
            jax.ShapeDtypeStruct((tokens, lanes), BF),
        ],
    )

    late_lift = after(
        (
        gate_lift_factors, upper_lift_factors, down_reduce_factors, down_lift_factors,
        gate_reduce_factors, upper_reduce_factors,
        ),
        query_rot,
    )
    gate_shrink, up_shrink = shrink_of(late_lift[4]), shrink_of(late_lift[5])
    down_expand = expand_of(late_lift[3])
    reduce_factors = [
        (
            jnp.concatenate([shrink_of(late_lift[4], f), shrink_of(late_lift[5], f)], axis=1),
            expand_of(late_lift[3], f),
        )
        for f in range(fsdp_n)
    ]
    late_down, late_gate, late_up = late_lift[2], late_lift[0], late_lift[1]
    shrink_d = jnp.pad(
        lax.dynamic_slice_in_dim(late_down, chip * hq, hq, 0), ((0, pad), (0, 0))
    )
    lift_g = lax.dynamic_index_in_dim(by_chip(late_gate), chip, 0, keepdims=False)
    lift_u = lax.dynamic_index_in_dim(by_chip(late_up), chip, 0, keepdims=False)
    lift_factors = [(expand_of(lift_g, f), expand_of(lift_u, f)) for f in range(fsdp_n)]
    feed_factors = [
        reduce_factors[f] + lift_factors[f] + (shrink_of(shrink_d, f),) for f in range(fsdp_n)
    ]
    down_rows = [down_weight, swap(after(down_weight, query_rot), 1)]
    w_down = assemble(core, after(down_rows, query_rot), hp)
    attended, lse = attend(
        info, after(query_rot, w_down, feed_factors, gate_shrink, up_shrink, down_expand),
        pair_all, seqs, spans, span_len,
    )
    for k in range(1, chips):
        blocks[k] = swap(after(parts[k], rows_o), 2 * k)
    output_blocks = both_cores(after(rows_o, query_rot))
    middle, normed_two, normed_top, normed_bottom, output_narrow, w_output = with_blocks(
        outputs_kernel, "outputs", seqs, me, output_blocks,
        [attended, low_in, second_scales[None], output_shrink, output_expand],
        [
            jax.ShapeDtypeStruct((tokens, model), F32),
            jax.ShapeDtypeStruct((tokens, model), BF),
            jax.ShapeDtypeStruct((tokens // 2, model), BF),
            jax.ShapeDtypeStruct((tokens // 2, model), BF),
            jax.ShapeDtypeStruct((tokens, lanes), BF),
        ],
    )

    kinds = [(0, None), (1, None)]
    wide = [parts[0], swap(after(parts[0], query_rot), 1)]
    for k in range(1, chips):
        kinds += [(2 * k, None), (2 * k + 1, None)]
        wide += [blocks[k], swap(after(blocks[k], middle), 1)]
    feed_index = jnp.stack([me, core]).astype(jnp.int32)

    g0_pieces[0] = grad_halves
    normed_halves = (normed_top, normed_bottom)
    n2_pieces = [normed_halves]
    for k in range(1, chips):
        if k < 3:
            n2_pieces.append(swap_both(after(normed_halves, wide[:-1]), 2 * k))
    if chips > 2:
        n2_pieces[1:3] = lax.optimization_barrier(n2_pieces[1:3])
    zero = jnp.zeros((lanes, hp), F32)
    sums = [(zero, zero, zero)] * fsdp_n
    out_raw = []
    grad_parts = []
    early_first = [0] + sorted(range(1, chips), key=lambda k: (k > 2, -k if k < 3 else k))
    for k in early_first:
        f = 2 * k // cp_n
        sgu, ed, eg, eu, sd = feed_factors[f]
        if len(out_raw) == 1:
            for other in range(1, min(chips, 3)):
                if other not in g0_pieces:
                    g0_pieces[other] = swap_both(after(grad_halves, out_raw[0]), 2 * other)
        if len(out_raw) == 2:
            for other in range(3, chips):
                for pieces in (n2_pieces, g0_pieces):
                    first, second, own_pair = after((pieces[2], pieces[1], pieces[0]), out_raw[-1])
                    if other == 3:
                        piece = (swap(first[0], 2), swap(second[1], 4))
                    else:
                        piece = swap_both(own_pair, 2 * other)
                    if pieces is n2_pieces:
                        n2_pieces.append(piece)
                    else:
                        g0_pieces[other] = piece
        if out_raw:
            sums[f] = after(sums[f], out_raw[-1])
        out_k, ng_k, *sums[f] = feed(
            feed_index, kinds, wide, n2_pieces[k], g0_pieces[k], sgu, ed, w_down, eg, eu, sd, sums[f], seqs
        )
        out_raw.append(out_k)
        grad_parts.append(ng_k if k == 0 else swap(ng_k, 2 * k))

    grad_most = grad_parts[0].astype(F32)
    for part in grad_parts[1:-1]:
        grad_most = lax.optimization_barrier(grad_most) + part.astype(F32)

    def pack(values, tiles):
        value = jnp.concatenate([value[:rank].astype(BF) for value in values], axis=1)
        return jnp.pad(value, ((0, 0), (0, -value.shape[1] % (128 * tiles))))

    middle_grad, middle_low, gate_back, up_back, output_back, attended_grad = before_attention(
        grad_most, grad_parts[-1], grad_low, middle, second_scales[None],
        gate_shrink, up_shrink, output_shrink, output_expand, w_output, seqs,
    )

    def narrowed_back(grad, expand):
        return (mm_nt(grad, expand) * mixing).astype(BF)

    out_raw = after(out_raw, middle_low)
    out_parts = [swap(part, 2 * k) if k else part for k, part in zip(early_first[:3], out_raw)]
    query_rot_grad, pair_part = attend_back(
        info, query_rot, attended_grad, attended, pair_all, lse, seqs, spans, span_len
    )
    out_parts += [
        swap(after(part, pair_part), 2 * k) for k, part in zip(early_first[3:], out_raw[3:])
    ]
    pair_grad = lax.psum_scatter(
        after(pair_part, out_parts[:3]), ("cp", "seq"), scatter_dimension=1, tiled=True
    ).reshape(tokens, 2 * kv_width)
    out_sum = sum(part.astype(F32) for part in out_parts)

    down_narrow = (out_sum[:, model : model + lanes] * mixing).astype(BF)
    result = middle + (out_sum[:, :model] + mm(down_narrow, down_expand))
    outputs = result.astype(BF).reshape(seqs, tok_rows, model)

    query_rot_grad, sums, middle_late, output_back, gate_back, up_back = after(
        (query_rot_grad, sums, middle_low, output_back, gate_back, up_back), out_parts[:3]
    )
    cosine, sine_table = after((cosine, sine_table), pair_part)
    query_grad = (
        unrotate(
            query_rot_grad.reshape(tokens, -1, HEAD_DIM).astype(F32), cosine, sine_table
        )
        .reshape(tokens, model)
        .astype(BF)
    )
    query_back = narrowed_back(query_grad, query_expand)
    query_in = mm_nt(query_grad, w_query) + mm_nt(query_back, query_shrink)

    def halves(value, index, exchange):
        span = 1
        while value.shape[0] > 1:
            split = value.reshape((value.shape[0] // 2, 2) + value.shape[1:])
            bit = index // span % 2
            keep = lax.dynamic_index_in_dim(split, bit, 1, keepdims=False)
            give = lax.dynamic_index_in_dim(split, 1 - bit, 1, keepdims=False)
            value = (keep.astype(F32) + exchange(give, span).astype(F32)).astype(BF)
            span *= 2
        return value[0]

    stacked = jnp.stack([pack(sums[f], seq_n) for f in range(fsdp_n)])
    feed_wide = stacked.shape[2]

    def groups_of(parity):
        return jnp.stack(
            [
                lax.dynamic_index_in_dim(stacked, (2 * j + parity) ^ group, 0, keepdims=False)
                for j in range(fsdp_n // 2)
            ]
        )

    feed_half = groups_of(core).astype(F32) + swap(groups_of(1 - core), 1).astype(F32)
    feed_half = feed_half.reshape(fsdp_n // 2 * rank, seq_n, feed_wide // seq_n).astype(BF)
    feed_half = feed_half.transpose(1, 0, 2)
    feed_piece = halves(feed_half, seq_index, swap_seq)
    ways = cp_n * seq_n
    early = pack(
        [
            mm_tn(output_back, attended),
            mm_tn(gate_back, normed_two),
            mm_tn(up_back, normed_two),
            mm_tn(output_narrow, middle_late),
            mm_tn(down_narrow, grad_low),
            mm_tn(query_back, normed),
            mm_tn(query_narrow, query_grad),
        ],
        ways,
    )
    early = early.reshape(rank, cp_n, seq_n, -1).transpose(1, 2, 0, 3)
    early = halves(early, cp_index, swap)
    early = halves(early, seq_index, swap_seq)
    early_cols = early.shape[1]
    both = jnp.concatenate([jnp.pad(early, ((0, feed_piece.shape[0] - rank), (0, 0))), feed_piece], axis=1)
    both = lax.all_gather(after(both, pair_grad), EVERY, axis=0, tiled=False)

    key_grad, value_grad, key_back, value_back, late = last_grads(
        cp_index, pair_grad, flat_cosine, sine_signed, key_expand, value_expand, normed,
        key_narrow, value_narrow, seqs, rank, cp_n,
    )
    late_wide = late.shape[3] * cp_n
    total = late[0].astype(F32) + swap(late[1], 1).astype(F32)
    span = 2
    while span < cp_n:
        total = total[0::2] + swap(total[1::2].astype(BF), span).astype(F32)
        span *= 2
    late = total[0].astype(BF)
    total = late.astype(F32)
    for k in range(1, seq_n):
        total = total + swap_seq(late, k).astype(F32)
    late = total.astype(BF)[None]
    for step in [span_k for span_k in (2**i for i in range(1, 30)) if span_k < plane] + [1]:
        late = jnp.concatenate([late, swap(late, step)], axis=0)

    normed_grad = (
        query_in
        + mm_nt(key_grad, w_key)
        + mm_nt(value_grad, w_value)
        + mm_nt(key_back, key_shrink)
        + mm_nt(value_back, value_shrink)
    )
    input_grad = middle_grad + norm_backward(resid_in, first_scales, normed_grad)

    came = [0]
    for step in [span_k for span_k in (2**i for i in range(1, 30)) if span_k < plane] + [1]:
        came = came + [c ^ step for c in came]
    inverse = [came.index(c) for c in range(plane)]
    late = jnp.take(
        late, jnp.asarray(inverse, jnp.int32)[jnp.arange(plane, dtype=jnp.int32) ^ me], axis=0
    )
    late = late.reshape(fsdp_n, cp_n, rank, late_wide // cp_n)
    late = late.transpose(0, 2, 1, 3).reshape(fsdp_n * rank, late_wide)

    order = jnp.arange(fsdp_n, dtype=jnp.int32) ^ group
    select_all = (
        jnp.take(jnp.stack(select), order, axis=0)[:, :, :rank]
        .transpose(0, 2, 1)
        .reshape(fsdp_n * rank, cols)
    )
    shrink_grad = lambda value: mm_tn(value, select_all)
    expand_grad = lambda value: mm_tn(select_all, value)

    late_of = lambda i: late[:, model * i : model * (i + 1)]
    tail_of = lambda i: late[:, model * 2 + kv_width * i : model * 2 + kv_width * (i + 1)]
    order_kinds = (True, True, True, False, False, True, False)
    if fsdp_n == 2 and 2 * hq % 128 == 0 and 2 * early_cols == model:
        expanded = expand_all(
            both, select_all, rank, hq, hp, seq_n, chips, early_cols, order_kinds
        )
    else:
        early_full = both[:, :rank, :early_cols].reshape(fsdp_n, ways, rank, early_cols)
        early_full = early_full.transpose(0, 2, 1, 3).reshape(fsdp_n * rank, ways * early_cols)
        feed_full = both[:, :, early_cols:].reshape(
            fsdp_n, cp_n // 2, 2, seq_n, fsdp_n // 2, rank, feed_wide // seq_n
        ).transpose(4, 2, 5, 0, 1, 3, 6)
        feed_full = feed_full.reshape(fsdp_n * rank, chips, feed_wide)
        expanded = []
        for i, shrink in enumerate((False, False, True) + order_kinds):
            if i < 3:
                rows = feed_full[:, :, i * hp : i * hp + hq].reshape(fsdp_n * rank, hidden_all)
            else:
                rows = early_full[:, model * (i - 3) : model * (i - 2)]
            expanded.append(shrink_grad(rows) if shrink else expand_grad(rows))

    return (
        outputs,
        input_grad.reshape(seqs, tok_rows, model),
        expanded[8],
        expanded[9],
        shrink_grad(late_of(0)),
        expand_grad(tail_of(0)),
        shrink_grad(late_of(1)),
        expand_grad(tail_of(1)),
        expanded[3],
        expanded[6],
        expanded[4],
        expanded[0],
        expanded[5],
        expanded[1],
        expanded[2],
        expanded[7],
    )


def solution(mesh):
    tokens_spec = P("fsdp", ("cp", "seq"), None)
    weight_spec = P(("fsdp", "cp"), None)
    placed = (
        (tokens_spec, tokens_spec, P("fsdp", None), P("fsdp"), P(), P())
        + (weight_spec,) * 7
        + (P(),) * 17
    )
    return jax.shard_map(
        body,
        mesh=mesh,
        in_specs=placed,
        out_specs=(tokens_spec, tokens_spec) + (P(),) * 14,
        check_vma=False,
    )
```
